32 devices in a mesh: seq: 16 (over z, y, x), mlp: 2 (over core).
Axes of the slice: x: 2, y: 2, z: 4, core: 2. Of those that a mesh axis runs over, the one named last changes fastest.
Arguments:
- block_input: bfloat16 [2, 4096, 1024], P('mlp', 'seq'), may hold values from -6 to 6
- out_cotangent: bfloat16 [2, 4096, 1024], P('mlp', 'seq'), may hold values from -6 to 6
- attend_gain: bfloat16 [1024], replicated, may hold values from 0.5 to 1.5
- attend_shift: bfloat16 [1024], replicated, may hold values from -1.25 to 1.25
- query_key_value_weight: bfloat16 [1024, 3072], replicated, may hold values from -0.1875 to 0.1875
- query_key_value_bias: bfloat16 [3072], replicated, may hold values from -1.25 to 1.25
- attention_out_weight: bfloat16 [1024, 1024], replicated, may hold values from -1.5 to 1.5
- attention_out_bias: bfloat16 [1024], replicated, may hold values from -3 to 3
- feed_gain: bfloat16 [1024], replicated, may hold values from 0.5 to 1.5
- feed_shift: bfloat16 [1024], replicated, may hold values from -1.25 to 1.25
- expand_weight: bfloat16 [1024, 4096], P(None, 'mlp'), may hold values from -0.1875 to 0.1875
- expand_bias: bfloat16 [4096], P('mlp'), may hold values from -3 to 3
- contract_weight: bfloat16 [4096, 1024], P('mlp'), may hold values from -0.1875 to 0.1875
- contract_bias: bfloat16 [1024], replicated, may hold values from -3 to 3
Outputs:
- block_output: bfloat16 [2, 4096, 1024], P('mlp', 'seq')
- grad_input: float32 [2, 4096, 1024], P('mlp', 'seq')
- grad_attend_gain: float32 [1024], P(('seq', 'mlp'))
- grad_attend_shift: float32 [1024], P(('seq', 'mlp'))
- grad_merged_weight: float32 [1024, 3072], P(('seq', 'mlp'))
- grad_merged_bias: float32 [3072], P(('seq', 'mlp'))
- grad_dense_weight: float32 [1024, 1024], P(('seq', 'mlp'))
- grad_dense_bias: float32 [1024], P(('seq', 'mlp'))
- grad_feed_gain: float32 [1024], P(('seq', 'mlp'))
- grad_feed_shift: float32 [1024], P(('seq', 'mlp'))
- grad_hidden_weight: float32 [1024, 4096], P('seq', 'mlp')
- grad_hidden_bias: float32 [4096], P(('seq', 'mlp'))
- grad_output_weight: float32 [4096, 1024], P('mlp', 'seq')
- grad_output_bias: float32 [1024], P(('seq', 'mlp'))
The draws below stay inside these ranges and needn't reach their ends.
All inputs are finite; a program needn't handle non-finite values.
Results may differ from the reference program's by a relative error of at most 0.03.
Values may be sent and summed in bfloat16 or wider, within the bound.
No kernel may reach another device: no remote copies, remote signals or barrier semaphores. Data moves between devices by JAX's collectives and lax.ppermute only.
A program may use at most 256 MiB of HBM per device.

```python
import math
import jax
import jax.numpy as jnp
from jax import lax

D = 1024
HEADS = 16
HEAD = 64
ROT = 16
FF = 4096
SEQS = 2
LEN = 4096


def shard_levels(key, dims, shards, smallest, largest):
    def one(position, parts):
        draws = jax.random.uniform(jax.random.fold_in(jax.random.fold_in(key, 6), position), (parts,), jnp.float32, smallest / len(shards), largest / len(shards))
        return jnp.repeat(jnp.exp(draws), dims[position] // parts).reshape((-1,) + (1,) * (len(dims) - position - 1))

    level = one(*shards[0])
    for cut in shards[1:]:
        level = level * one(*cut)
    return level


def normal_values(own_key, shape, deviation, reach, split=(), kind=jnp.bfloat16):
    drawn = deviation * jax.random.normal(own_key, shape, jnp.float32)
    if split:
        drawn = drawn * shard_levels(own_key, shape, split, -0.22, 0.18)
    return jnp.clip(drawn, -reach, reach).astype(kind)


def setup_inputs(seed: int = 0) -> dict:
    key_list = jax.random.split(jax.random.key(seed), 15)
    return {
        "block_input": normal_values(key_list[0], (SEQS, LEN, D), 1.0, 6.0, ((0, 2), (1, 16))),
        "out_cotangent": normal_values(key_list[1], (SEQS, LEN, D), 1.0, 6.0, ((0, 2), (1, 16))),
        "attend_gain": jnp.clip(1.0 + 0.1 * jax.random.normal(key_list[2], (D,), jnp.float32), 0.5, 1.5).astype(jnp.bfloat16),
        "attend_shift": normal_values(key_list[3], (D,), 0.2, 1.25),
        "query_key_value_weight": normal_values(key_list[4], (D, 3 * D), D ** -0.5, 0.1875),
        "query_key_value_bias": normal_values(key_list[5], (3 * D,), 0.2, 1.25),
        "attention_out_weight": normal_values(key_list[6], (D, D), (D // 64) ** -0.5, 1.5),
        "attention_out_bias": normal_values(key_list[7], (D,), 0.5, 3.0),
        "feed_gain": jnp.clip(1.0 + 0.1 * jax.random.normal(key_list[8], (D,), jnp.float32), 0.5, 1.5).astype(jnp.bfloat16),
        "feed_shift": normal_values(key_list[9], (D,), 0.2, 1.25),
        "expand_weight": normal_values(key_list[10], (D, FF), D ** -0.5, 0.1875, ((1, 2),)),
        "expand_bias": normal_values(key_list[11], (FF,), 0.5, 3.0, ((0, 2),)),
        "contract_weight": normal_values(key_list[12], (FF, D), (FF // 4) ** -0.5, 0.1875, ((0, 2),)),
        "contract_bias": normal_values(key_list[13], (D,), 0.5, 3.0),
    }


@jax.custom_vjp
def low(v):
    return lax.optimization_barrier(v.astype(jnp.bfloat16)).astype(jnp.float32)

@jax.custom_vjp
def lowered_gradient(v):
    return v

def low_keep(v):
    return (low(v), None)

def low_pass(kept, grad):
    return (grad,)

def back_keep(v):
    return (v, None)

def back_low(kept, grad):
    return (low(grad),)
low.defvjp(low_keep, low_pass)
lowered_gradient.defvjp(back_keep, back_low)
FULL_PRECISION = lax.Precision.HIGHEST
EPS = 1e-05
NEGATIVE = -1e+30

def layer_norm(values, scales, offsets):
    average = lax.optimization_barrier(jnp.mean(values, -1, keepdims=True))
    centred = values - average
    spread = lax.optimization_barrier(jnp.mean(centred * centred, -1, keepdims=True))
    return centred * lax.rsqrt(spread + EPS) * scales + offsets

def rotary_tables(positions):
    half_dims = ROT // 2
    inverse = 10000.0 ** (-(jnp.arange(half_dims, dtype=jnp.float32) * 2.0 / ROT))
    angles = positions[:, None] * inverse[None, :]
    return (jnp.cos(angles)[:, None, :], jnp.sin(angles)[:, None, :])

def rotate(values, cosine, sine):
    half_dims = ROT // 2
    first_half = values[..., :half_dims]
    second_half = values[..., half_dims:ROT]
    return jnp.concatenate([first_half * cosine - second_half * sine, second_half * cosine + first_half * sine, values[..., ROT:]], -1)

def sequence_attention(operands):
    queries, keys, values = operands
    seq_length = queries.shape[0]
    row_block = math.gcd(seq_length, 512)
    score_scale = float(HEAD) ** (-0.5)
    key_pos = jnp.arange(seq_length)

    def rows_block(pair):
        query_block, first_row = pair
        scores = jnp.einsum('qhd,khd->hqk', query_block, keys, precision=FULL_PRECISION) * score_scale
        scores = lowered_gradient(scores)
        query_pos = first_row + jnp.arange(row_block)
        allowed = key_pos[None, :] <= query_pos[:, None]
        scores = jnp.where(allowed[None], scores, NEGATIVE)
        top_score = lax.optimization_barrier(jnp.max(scores, -1, keepdims=True))
        weights = jnp.exp(scores - top_score)
        probs = weights / lax.optimization_barrier(jnp.sum(weights, -1, keepdims=True))
        return jnp.einsum('hqk,khd->qhd', low(probs), values, precision=FULL_PRECISION)
    query_blocks = queries.reshape(seq_length // row_block, row_block, HEADS, HEAD)
    first_rows = jnp.arange(seq_length // row_block) * row_block
    result = lax.map(jax.checkpoint(rows_block), (query_blocks, first_rows))
    return result.reshape(seq_length, HEADS, HEAD)

def forward(inputs, attend_gain, attend_shift, query_key_value_weight, query_key_value_bias, attention_out_weight, attention_out_bias, feed_gain, feed_shift, expand_weight, expand_bias, contract_weight, contract_bias):
    seq_total, seq_length, model_width = inputs.shape
    attention_normed_input = low(layer_norm(inputs, attend_gain, attend_shift))
    query_key_value = jnp.einsum('uqz,zy->uqy', attention_normed_input, query_key_value_weight, precision=FULL_PRECISION) + query_key_value_bias
    query_key_value = lowered_gradient(query_key_value)
    shape_heads = (seq_total, seq_length, HEADS, HEAD)
    query_lin = query_key_value[..., :model_width].reshape(shape_heads)
    key_lin = query_key_value[..., model_width:2 * model_width].reshape(shape_heads)
    value_lin = query_key_value[..., 2 * model_width:].reshape(shape_heads)
    cosine, sine = rotary_tables(jnp.arange(seq_length, dtype=jnp.float32))
    queries = low(rotate(query_lin, cosine, sine))
    keys = low(rotate(key_lin, cosine, sine))
    values = low(value_lin)
    attention_result = lax.map(sequence_attention, (queries, keys, values))
    attention_result = low(lowered_gradient(attention_result.reshape(seq_total, seq_length, model_width)))
    attention_output = jnp.einsum('uqz,zy->uqy', attention_result, attention_out_weight, precision=FULL_PRECISION) + attention_out_bias
    feedforward_normed_input = low(layer_norm(inputs, feed_gain, feed_shift))
    before_activation = lowered_gradient(jnp.einsum('pkn,nu->pku', feedforward_normed_input, expand_weight, precision=FULL_PRECISION) + expand_bias)
    hidden_activation = low(jax.nn.gelu(before_activation, approximate=False))
    feedforward_output = jnp.einsum('hay,ye->hae', hidden_activation, contract_weight, precision=FULL_PRECISION) + contract_bias
    return inputs + attention_output + feedforward_output

def reference(block_input, out_cotangent, attend_gain, attend_shift, query_key_value_weight, query_key_value_bias, attention_out_weight, attention_out_bias, feed_gain, feed_shift, expand_weight, expand_bias, contract_weight, contract_bias):
    operands = (block_input, attend_gain, attend_shift, query_key_value_weight, query_key_value_bias, attention_out_weight, attention_out_bias, feed_gain, feed_shift, expand_weight, expand_bias, contract_weight, contract_bias)
    operands = tuple((item.astype(jnp.float32) for item in operands))
    result, pullback = jax.vjp(forward, *operands)
    grads_all = pullback(out_cotangent.astype(jnp.float32))
    return (result.astype(jnp.bfloat16), grads_all[0], grads_all[1], grads_all[2], grads_all[3], grads_all[4], grads_all[5], grads_all[6], grads_all[7], grads_all[8], grads_all[9], grads_all[10], grads_all[11], grads_all[12])
```

```python
from functools import partial

import jax
import jax.numpy as jnp
from jax import lax
from jax.experimental import pallas as pl
from jax.experimental.pallas import tpu as pltpu
from jax.sharding import PartitionSpec as P

HEADS = 16
HEAD = 64
ROT = 16
EPS = 1e-05
NEGATIVE = -1e30

NT = (((1,), (1,)), ((), ()))
NN = (((1,), (0,)), ((), ()))


def dot32(a, b, dims=NN):
    return lax.dot_general(a, b, dims, preferred_element_type=jnp.float32)


def gelu_exact(before_activation):
    return jax.nn.gelu(before_activation, approximate=False)


def rotary_tables(positions):
    half_dims = ROT // 2
    inverse = 10000.0 ** (-(jnp.arange(half_dims, dtype=jnp.float32) * 2.0 / ROT))
    angles = positions[:, None] * inverse[None, :]
    return (jnp.cos(angles)[:, None, :], jnp.sin(angles)[:, None, :])


def rotate(values, cosine, sine):
    half_dims = ROT // 2
    first_half = values[..., :half_dims]
    second_half = values[..., half_dims:ROT]
    return jnp.concatenate(
        [
            first_half * cosine - second_half * sine,
            second_half * cosine + first_half * sine,
            values[..., ROT:],
        ],
        -1,
    )


def head_kernel(part_ref, x_ref, y_ref, s_ref, p_ref, dkv_ref, *, group, key_rows, query_rows):
    blocks = x_ref.shape[0] // group
    keys = group * key_rows
    rows = group * query_rows
    scale = float(HEAD) ** -0.5
    lane = lax.broadcasted_iota(jnp.int32, (rows, 2 * HEAD), 1)
    low = lane < HEAD
    row = lax.broadcasted_iota(jnp.int32, (rows, keys), 0)
    col = lax.broadcasted_iota(jnp.int32, (rows, keys), 1)
    row_pos = (row // query_rows) * key_rows + row % query_rows + part_ref[0] * query_rows
    allowed = col <= row_pos

    dkv_ref[...] = jnp.zeros_like(dkv_ref)

    def key_value(j):
        return x_ref[pl.ds(j * group, group), :key_rows, :].reshape(keys, 2 * HEAD)

    def lanes_max(mx, s):
        for c in range(keys // 128):
            mx = jnp.maximum(mx, s[:, c * 128 : (c + 1) * 128])
        return mx

    def one_block(i, unused):
        qdo = x_ref[pl.ds(i * group, group), key_rows:, :].reshape(rows, 2 * HEAD)
        qdo32 = qdo.astype(jnp.float32)
        zero = jnp.zeros_like(qdo32)
        query = jnp.where(low, qdo32 * scale, zero).astype(jnp.bfloat16)

        def first(j, mx):
            s = dot32(query, key_value(j), NT)
            s_ref[j] = s
            return lanes_max(mx, s)

        mx = lax.fori_loop(0, i, first, jnp.full((rows, 128), NEGATIVE, jnp.float32))
        s = jnp.where(allowed, dot32(query, key_value(i), NT), NEGATIVE)
        s_ref[i] = s
        top = jnp.max(lanes_max(mx, s), -1, keepdims=True)

        def second(j, state):
            total, acc = state
            p = jnp.exp(s_ref[j] - top)
            for c in range(keys // 128):
                total = total + p[:, c * 128 : (c + 1) * 128]
            low_p = p.astype(jnp.bfloat16)
            p_ref[j] = low_p
            return (total, acc + dot32(low_p, key_value(j)))

        total, acc = lax.fori_loop(
            0,
            i + 1,
            second,
            (jnp.zeros((rows, 128), jnp.float32), jnp.zeros((rows, 2 * HEAD), jnp.float32)),
        )
        inverse = 1.0 / jnp.sum(total, -1, keepdims=True)
        attended = acc * inverse
        grad = jnp.where(low, zero, qdo32 * inverse).astype(jnp.bfloat16)
        delta = jnp.sum(grad.astype(jnp.float32) * attended, -1, keepdims=True)
        query_t = jnp.transpose(query.astype(jnp.float32))[:HEAD].astype(jnp.bfloat16)
        grad_t = jnp.transpose(grad.astype(jnp.float32))[HEAD:].astype(jnp.bfloat16)

        def third(j, acc):
            kv = key_value(j)
            low_p = p_ref[j]
            dp = dot32(grad, kv, NT)
            ds = (low_p.astype(jnp.float32) * (dp - delta)).astype(jnp.bfloat16)
            dkv_ref[j, :HEAD] += dot32(query_t, ds)
            dkv_ref[j, HEAD:] += dot32(grad_t, low_p)
            return acc + dot32(ds, kv)

        acc = lax.fori_loop(0, i + 1, third, jnp.zeros((rows, 2 * HEAD), jnp.float32))
        done = jnp.where(low, acc * scale, attended).astype(jnp.bfloat16)
        y_ref[pl.ds(i * group, group), key_rows:, :] = done.reshape(group, query_rows, 2 * HEAD)
        return unused

    lax.fori_loop(0, blocks, one_block, 0)

    def finish(i, unused):
        grads = jnp.transpose(dkv_ref[i]).astype(jnp.bfloat16)
        y_ref[pl.ds(i * group, group), :key_rows, :] = grads.reshape(group, key_rows, 2 * HEAD)
        return unused

    lax.fori_loop(0, blocks, finish, 0)


def one_head(x, part, key_rows, query_rows):
    count = x.shape[0]
    group = 2 if count % 2 == 0 else 1
    blocks = count // group
    keys, rows = group * key_rows, group * query_rows
    pairs = count * key_rows * count * query_rows // 2
    return pl.pallas_call(
        partial(head_kernel, group=group, key_rows=key_rows, query_rows=query_rows),
        out_shape=jax.ShapeDtypeStruct(x.shape, jnp.bfloat16),
        in_specs=[
            pl.BlockSpec(memory_space=pltpu.SMEM),
            pl.BlockSpec(memory_space=pltpu.VMEM),
        ],
        out_specs=pl.BlockSpec(memory_space=pltpu.VMEM),
        scratch_shapes=[
            pltpu.VMEM((blocks, rows, keys), jnp.float32),
            pltpu.VMEM((blocks, rows, keys), jnp.bfloat16),
            pltpu.VMEM((blocks, 2 * HEAD, keys), jnp.float32),
        ],
        cost_estimate=pl.CostEstimate(
            flops=pairs * 2 * 256 * 6, bytes_accessed=4 * x.size, transcendentals=pairs
        ),
        compiler_params=pltpu.CompilerParams(vmem_limit_bytes=56 * 1024 * 1024),
        name="one_head",
    )(part, x)


def pair_swap(x):
    return lax.ppermute(x, "mlp", [(0, 1), (1, 0)])


def mlp_rows(x):
    members = lax.axis_size("mlp")
    if members == 2:
        return jnp.concatenate([x, pair_swap(x)], 0)
    return lax.all_gather(x, "mlp", axis=0, tiled=True)


def mlp_columns(pieces):
    members = lax.axis_size("mlp")
    if members == 2:
        me = lax.axis_index("mlp")
        mine = lax.dynamic_index_in_dim(pieces, me, 0, False)
        other = lax.dynamic_index_in_dim(pieces, 1 - me, 0, False)
        return jnp.stack([mine, pair_swap(other)], 0)
    return lax.all_to_all(pieces, "mlp", 0, 0, tiled=False)


def mlp_sum(partial_rows):
    members = lax.axis_size("mlp")
    if members == 2:
        half = partial_rows.shape[0] // 2
        came = pair_swap(partial_rows[half:].astype(jnp.bfloat16))
        return partial_rows[:half] + came.astype(jnp.float32)
    return lax.psum_scatter(
        partial_rows.astype(jnp.bfloat16), "mlp", scatter_dimension=0, tiled=True
    ).astype(jnp.float32)


def seq_sum(pieces, order):
    members = lax.axis_size("seq")
    me = lax.axis_index("seq")
    bits = members.bit_length() - 1
    order = [b for b in order if b < bits] + [b for b in range(bits) if b not in order]
    shape = pieces.shape[1:]
    held = pieces.reshape((2,) * bits + shape)
    left = list(range(bits - 1, -1, -1))
    for bit in order:
        axis = left.index(bit)
        mine = (me >> bit) & 1
        sent = lax.dynamic_index_in_dim(held, 1 - mine, axis, False)
        kept = lax.dynamic_index_in_dim(held, mine, axis, False)
        came = lax.ppermute(
            sent.astype(jnp.bfloat16), "seq", [(s, s ^ (1 << bit)) for s in range(members)]
        )
        held = kept.astype(jnp.float32) + came.astype(jnp.float32)
        left.pop(axis)
        if left:
            held = held.astype(jnp.bfloat16)
    return held


def per_device(
    block_input,
    out_cotangent,
    attend_gain,
    attend_shift,
    query_key_value_weight,
    query_key_value_bias,
    attention_out_weight,
    attention_out_bias,
    feed_gain,
    feed_shift,
    expand_weight,
    expand_bias,
    contract_weight,
    contract_bias,
):
    seq_count, tok_count, width = block_input.shape
    members = lax.axis_size("seq")
    pairs = lax.axis_size("mlp")
    parts = members // HEADS
    query_rows = tok_count // parts
    me = lax.axis_index("seq")
    pair_me = lax.axis_index("mlp")
    f32, bf16 = jnp.float32, jnp.bfloat16
    first_query = me * tok_count

    inputs = block_input.astype(f32).reshape(tok_count, width)
    cot = out_cotangent.reshape(tok_count, width)
    cot_float = cot.astype(f32)

    average = jnp.mean(inputs, -1, keepdims=True)
    centred = inputs - average
    spread = jnp.mean(centred * centred, -1, keepdims=True)
    root = lax.rsqrt(spread + EPS)
    unit = centred * root
    gain_one, gain_two = attend_gain.astype(f32), feed_gain.astype(f32)
    normed_one = (unit * gain_one + attend_shift.astype(f32)).astype(bf16)
    normed_two = (unit * gain_two + feed_shift.astype(f32)).astype(bf16)

    merged = dot32(normed_one, query_key_value_weight) + query_key_value_bias.astype(f32)
    grad_attended = dot32(cot, attention_out_weight, NT).astype(bf16)
    heads = (tok_count, HEADS, HEAD)
    cosine, sine = rotary_tables((first_query + jnp.arange(tok_count)).astype(f32))
    queries = rotate(merged[:, :width].reshape(heads), cosine, sine).astype(bf16)
    keys = rotate(merged[:, width : 2 * width].reshape(heads), cosine, sine).astype(bf16)
    values = merged[:, 2 * width :].astype(bf16).reshape(heads)
    key_value = jnp.transpose(jnp.concatenate([keys, values], -1), (1, 0, 2))
    query_grad = jnp.transpose(
        jnp.concatenate([queries, grad_attended.reshape(heads)], -1), (1, 0, 2)
    )
    outgoing = jnp.concatenate(
        [
            jnp.broadcast_to(
                key_value[:, None], (HEADS, parts, tok_count, 2 * HEAD)
            ).reshape(members, tok_count, 2 * HEAD),
            query_grad.reshape(members, query_rows, 2 * HEAD),
        ],
        1,
    )
    at_head = lax.all_to_all(outgoing, "seq", 0, 0, tiled=True)
    part = (me % parts).astype(jnp.int32).reshape(1)
    from_head = one_head(at_head, part, tok_count, query_rows)

    rows_all = mlp_rows(normed_two)
    cot_all = mlp_rows(cot)
    pre = dot32(rows_all, expand_weight) + expand_bias.astype(f32)
    hidden, gelu_back = jax.vjp(gelu_exact, pre)
    hidden = hidden.astype(bf16)
    feed_out = mlp_sum(dot32(hidden, contract_weight))
    grad_hidden = dot32(cot_all, contract_weight, NT)
    grad_pre = gelu_back(grad_hidden)[0].astype(bf16)
    TN = (((0,), (0,)), ((), ()))
    slice_width = expand_weight.shape[1]
    own = width // members
    grad_out_weight = dot32(cot_all, hidden, TN).astype(bf16).reshape(members, own, slice_width)
    grad_out_weight = jnp.transpose(seq_sum(grad_out_weight, (0, 1, 2, 3, 4)))
    grad_hid_weight = dot32(rows_all, grad_pre, TN).astype(bf16).reshape(members, own, slice_width)
    grad_hid_weight = seq_sum(grad_hid_weight, (1, 0, 2, 3, 4))
    grad_hid_bias = jnp.sum(grad_pre.astype(f32), 0)
    grad_normed_feed = mlp_sum(dot32(grad_pre, expand_weight, NT))

    back = lax.all_to_all(from_head, "seq", 0, 0, tiled=True)
    grad_kv = back[:, :tok_count].reshape(HEADS, parts, tok_count, 2 * HEAD)
    if parts > 1:
        grad_kv = jnp.sum(grad_kv.astype(f32), 1)
    grad_kv = jnp.transpose(grad_kv.reshape(HEADS, tok_count, 2 * HEAD), (1, 0, 2)).astype(f32)
    query_side = jnp.transpose(
        back[:, tok_count:].reshape(HEADS, tok_count, 2 * HEAD), (1, 0, 2)
    )
    attended = query_side[..., HEAD:].reshape(tok_count, width)
    attention_output = dot32(attended, attention_out_weight) + attention_out_bias.astype(f32)
    result = inputs + attention_output + feed_out + contract_bias.astype(f32)
    block_output = result.astype(bf16).reshape(seq_count, tok_count, width)

    grad_q = rotate(query_side[..., :HEAD].astype(f32), cosine, -sine).astype(bf16)
    grad_k = rotate(grad_kv[..., :HEAD], cosine, -sine).astype(bf16)
    grad_v = grad_kv[..., HEAD:].astype(bf16)
    grad_merged = jnp.concatenate(
        [g.reshape(tok_count, width) for g in (grad_q, grad_k, grad_v)], -1
    )
    normed_all = mlp_rows(normed_one)
    attended_all = mlp_rows(attended)
    share = 3 * width // pairs
    merged_part = mlp_columns(
        jnp.transpose(grad_merged.reshape(tok_count, pairs, share), (1, 0, 2))
    ).reshape(pairs * tok_count, share)
    dense_share = width // pairs
    cot_part = lax.dynamic_slice_in_dim(cot_all, pair_me * dense_share, dense_share, 1)
    grad_merged_weight = dot32(normed_all, merged_part, TN).astype(bf16)
    grad_dense_weight = dot32(attended_all, cot_part, TN).astype(bf16)
    weights = jnp.concatenate([grad_merged_weight, grad_dense_weight], -1)
    weights = seq_sum(weights.reshape(members, own, share + dense_share), (0, 1, 2, 3, 4))
    weights = mlp_columns(weights.reshape(pairs, own // pairs, share + dense_share))
    if pairs == 2:
        weights = jnp.where(pair_me == 0, weights, weights[::-1])
    weights = jnp.transpose(weights, (1, 0, 2))
    rows_own = own // pairs
    out_merged_weight = weights[..., :share].reshape(rows_own, 3 * width)
    out_dense_weight = weights[..., share:].reshape(rows_own, width)

    grad_normed_attend = dot32(grad_merged, query_key_value_weight, NT)
    down = grad_normed_attend * gain_one + grad_normed_feed * gain_two
    grad_x = root * (
        down
        - jnp.mean(down, -1, keepdims=True)
        - unit * jnp.mean(down * unit, -1, keepdims=True)
    )
    grad_input = (cot_float + grad_x).reshape(seq_count, tok_count, width)

    bias_full = lax.dynamic_update_slice_in_dim(
        jnp.zeros((pairs * slice_width,), f32), grad_hid_bias, pair_me * slice_width, 0
    )
    vectors = (
        jnp.sum(grad_normed_attend * unit, 0),
        jnp.sum(grad_normed_attend, 0),
        jnp.sum(grad_merged.astype(f32), 0),
        jnp.sum(cot_float, 0),
        jnp.sum(grad_normed_feed * unit, 0),
        jnp.sum(grad_normed_feed, 0),
        bias_full,
    )
    packed = jnp.concatenate([v.reshape(members, pairs, -1) for v in vectors], -1)
    packed = jnp.sum(lax.all_to_all(packed, "seq", 0, 0, tiled=True), 0)
    if pairs == 2:
        mine = lax.dynamic_index_in_dim(packed, pair_me, 0, False)
        other = lax.dynamic_index_in_dim(packed, 1 - pair_me, 0, False)
        packed = mine + pair_swap(other)
    else:
        packed = lax.psum_scatter(packed, "mlp", scatter_dimension=0, tiled=False)
    outs, start = [], 0
    for v in vectors:
        size = v.shape[0] // (members * pairs)
        outs.append(lax.slice_in_dim(packed, start, start + size))
        start += size
    (
        grad_gain_one,
        grad_shift_one,
        grad_merged_bias,
        grad_dense_bias,
        grad_gain_two,
        grad_shift_two,
        out_hid_bias,
    ) = outs
    return (
        block_output,
        grad_input,
        grad_gain_one,
        grad_shift_one,
        out_merged_weight,
        grad_merged_bias,
        out_dense_weight,
        grad_dense_bias,
        grad_gain_two,
        grad_shift_two,
        grad_hid_weight,
        out_hid_bias,
        grad_out_weight,
        grad_dense_bias,
    )


def solution(mesh):
    in_specs = (
        P("mlp", "seq", None),
        P("mlp", "seq", None),
        P(),
        P(),
        P(),
        P(),
        P(),
        P(),
        P(),
        P(),
        P(None, "mlp"),
        P("mlp"),
        P("mlp", None),
        P(),
    )
    out_specs = (
        P("mlp", "seq", None),
        P("mlp", "seq", None),
        P(("seq", "mlp")),
        P(("seq", "mlp")),
        P(("seq", "mlp"), None),
        P(("seq", "mlp")),
        P(("seq", "mlp"), None),
        P(("seq", "mlp")),
        P(("seq", "mlp")),
        P(("seq", "mlp")),
        P("seq", "mlp"),
        P(("seq", "mlp")),
        P("mlp", "seq"),
        P(("seq", "mlp")),
    )
    return jax.shard_map(
        per_device, mesh=mesh, in_specs=in_specs, out_specs=out_specs, check_vma=False
    )
```

```python
from functools import partial

import jax
import jax.numpy as jnp
from jax import lax
from jax.experimental import pallas as pl
from jax.experimental.pallas import tpu as pltpu
from jax.sharding import PartitionSpec as P

HEADS = 16
HEAD = 64
ROT = 16
PAIR = 2 * HEAD
GROUPS = HEADS // 2
EPS = 1e-05
NEGATIVE = -1e30

F32 = jnp.float32
BF16 = jnp.bfloat16
NT = (((1,), (1,)), ((), ()))
NN = (((1,), (0,)), ((), ()))
VMEM_LIMIT = 60 * 1024 * 1024


def dot32(a, b, dims=NN):
    return lax.dot_general(a, b, dims, preferred_element_type=F32)


def shape_of(shape, dtype):
    return jax.ShapeDtypeStruct(shape, dtype)


def fixed(shape):
    return pl.BlockSpec(shape, lambda *i: (0,) * len(shape))


def vector_row(ref):
    return ref[...].astype(F32).reshape(1, -1)


def two_heads(pair_a, pair_b, low):
    even = jnp.where(low, pair_a, pltpu.roll(pair_b, HEAD, 1))
    odd = jnp.where(low, pltpu.roll(pair_a, HEAD, 1), pair_b)
    return (even, odd)


def rotary_lanes(first, rows, inverse):
    shape = (rows, PAIR)
    lane = lax.broadcasted_iota(jnp.int32, shape, 1) % HEAD
    position = (lax.broadcasted_iota(jnp.int32, shape, 0) + first).astype(F32)
    angle = position * inverse
    cosine, sine = jnp.cos(angle), jnp.sin(angle)
    zero = jnp.zeros_like(sine)
    return (
        jnp.where(lane < ROT, cosine, 1.0),
        jnp.where(lane < ROT // 2, -sine, zero),
        jnp.where((lane >= ROT // 2) & (lane < ROT), sine, zero),
    )


def rotate_lanes(x, cosine, to_first, to_second):
    ahead = pltpu.roll(x, PAIR - ROT // 2, 1)
    behind = pltpu.roll(x, ROT // 2, 1)
    return x * cosine + ahead * to_first + behind * to_second


def unit_rows(x):
    average = jnp.mean(x, -1, keepdims=True)
    centred = x - average
    spread = jnp.mean(centred * centred, -1, keepdims=True)
    root = lax.rsqrt(spread + EPS)
    return (centred * root, root)


def open_kernel(
    first_ref, x_ref, g_ref, inv_ref, ga_ref, sa_ref, gf_ref, sf_ref, b_ref,
    wq_ref, wk_ref, wv_ref, wo_ref,
    out_ref, n1_ref, n2_ref, table_ref, n1t_ref, n2t_ref, gt_ref, bias_ref, *, parts,
):
    rows, width = x_ref.shape
    step = pl.program_id(0)
    cols = wq_ref.shape[1]

    @pl.when(step == 0)
    def _():
        unit, root = unit_rows(x_ref[...].astype(F32))
        n1_ref[...] = (unit * vector_row(ga_ref) + vector_row(sa_ref)).astype(BF16)
        n2_ref[...] = (unit * vector_row(gf_ref) + vector_row(sf_ref)).astype(BF16)
        for t, table in enumerate(rotary_lanes(first_ref[0], rows, inv_ref[...])):
            table_ref[t] = table
        bias_ref[...] = vector_row(b_ref)

    for at, source, target in ((1, n1_ref, n1t_ref), (2, n2_ref, n2t_ref), (3, g_ref, gt_ref)):

        @pl.when(step == at)
        def _(source=source, target=target):
            target[...] = jnp.transpose(source[...])

    def bias(third):
        return bias_ref[:, pl.ds(pl.multiple_of(third * width + step * cols, cols), cols)]

    normed = n1_ref[...]
    query = dot32(normed, wq_ref[...]) + bias(0)
    key = dot32(normed, wk_ref[...]) + bias(1)
    value = dot32(normed, wv_ref[...]) + bias(2)
    grad = dot32(g_ref[...], wo_ref[...], NT)
    tables = (table_ref[0], table_ref[1], table_ref[2])
    low = lax.broadcasted_iota(jnp.int32, (rows, PAIR), 1) < HEAD
    query_rows = rows // parts
    for c in range(cols // PAIR):
        cut = slice(c * PAIR, (c + 1) * PAIR)
        kv = two_heads(rotate_lanes(key[:, cut], *tables), value[:, cut], low)
        qg = two_heads(rotate_lanes(query[:, cut], *tables), grad[:, cut], low)
        for h in range(2):
            kv_h, qg_h = kv[h].astype(BF16), qg[h].astype(BF16)
            for p in range(parts):
                out_ref[2 * c + h, p, :rows] = kv_h
                out_ref[2 * c + h, p, rows:] = qg_h[p * query_rows : (p + 1) * query_rows]


def open_layer(x, g, first, vectors, weight, bias, out_weight, parts):
    rows, width = x.shape
    steps = 4
    cols = width // steps
    per = HEADS // steps
    inverse = 10000.0 ** (-(jnp.arange(ROT // 2, dtype=F32) * 2.0 / ROT))
    inverse = jnp.tile(inverse, PAIR // (ROT // 2)).reshape(1, PAIR)
    chunk = rows + rows // parts

    def third(t):
        return pl.BlockSpec((width, cols), lambda i: (0, t * steps + i))

    out, *others = pl.pallas_call(
        partial(open_kernel, parts=parts),
        grid=(steps,),
        out_shape=(
            shape_of((HEADS, parts, chunk, PAIR), BF16),
            shape_of((rows, width), BF16),
            shape_of((rows, width), BF16),
            shape_of((3, rows, PAIR), F32),
            shape_of((width, rows), BF16),
            shape_of((width, rows), BF16),
            shape_of((width, rows), BF16),
        ),
        in_specs=[
            pl.BlockSpec(memory_space=pltpu.SMEM),
            fixed((rows, width)),
            fixed((rows, width)),
            fixed((1, PAIR)),
            *[fixed((width,))] * 4,
            fixed((3 * width,)),
            third(0), third(1), third(2),
            pl.BlockSpec((cols, width), lambda i: (i, 0)),
        ],
        out_specs=(
            pl.BlockSpec((per, parts, chunk, PAIR), lambda i: (i, 0, 0, 0)),
            fixed((rows, width)),
            fixed((rows, width)),
            fixed((3, rows, PAIR)),
            fixed((width, rows)),
            fixed((width, rows)),
            fixed((width, rows)),
        ),
        scratch_shapes=[pltpu.VMEM((1, 3 * width), F32)],
        cost_estimate=pl.CostEstimate(
            flops=8 * rows * width * width,
            bytes_accessed=8 * width * width + 18 * rows * width,
            transcendentals=0,
        ),
        compiler_params=pltpu.CompilerParams(vmem_limit_bytes=VMEM_LIMIT),
        name="open_layer",
    )(first, x, g, inverse, *vectors, bias, weight, weight, weight, out_weight)
    return (out.reshape(HEADS * parts, chunk, PAIR), *others)


def head_kernel(part_ref, x_ref, y_ref, s_ref, p_ref, dkv_ref, *, group, key_rows, query_rows):
    blocks = x_ref.shape[0] // group
    keys = group * key_rows
    rows = group * query_rows
    scale = float(HEAD) ** -0.5
    lane = lax.broadcasted_iota(jnp.int32, (rows, PAIR), 1)
    low = lane < HEAD
    row = lax.broadcasted_iota(jnp.int32, (rows, keys), 0)
    col = lax.broadcasted_iota(jnp.int32, (rows, keys), 1)
    row_pos = (row // query_rows) * key_rows + row % query_rows + part_ref[0] * query_rows
    allowed = col <= row_pos

    dkv_ref[...] = jnp.zeros_like(dkv_ref)

    def key_value(j):
        return x_ref[pl.ds(j * group, group), :key_rows, :].reshape(keys, PAIR)

    def lanes_max(mx, s):
        for c in range(keys // 128):
            mx = jnp.maximum(mx, s[:, c * 128 : (c + 1) * 128])
        return mx

    def one_block(i, unused):
        qdo = x_ref[pl.ds(i * group, group), key_rows:, :].reshape(rows, PAIR)
        qdo32 = qdo.astype(F32)
        zero = jnp.zeros_like(qdo32)
        query = jnp.where(low, qdo32 * scale, zero).astype(BF16)

        def first(j, mx):
            s = dot32(query, key_value(j), NT)
            s_ref[j] = s
            return lanes_max(mx, s)

        mx = lax.fori_loop(0, i, first, jnp.full((rows, 128), NEGATIVE, F32))
        s = jnp.where(allowed, dot32(query, key_value(i), NT), NEGATIVE)
        s_ref[i] = s
        top = jnp.max(lanes_max(mx, s), -1, keepdims=True)

        def second(j, state):
            total, acc = state
            p = jnp.exp(s_ref[j] - top)
            for c in range(keys // 128):
                total = total + p[:, c * 128 : (c + 1) * 128]
            low_p = p.astype(BF16)
            p_ref[j] = low_p
            return (total, acc + dot32(low_p, key_value(j)))

        total, acc = lax.fori_loop(
            0,
            i + 1,
            second,
            (jnp.zeros((rows, 128), F32), jnp.zeros((rows, PAIR), F32)),
        )
        inverse = 1.0 / jnp.sum(total, -1, keepdims=True)
        attended = acc * inverse
        grad = jnp.where(low, zero, qdo32 * inverse).astype(BF16)
        delta = jnp.sum(grad.astype(F32) * attended, -1, keepdims=True)
        query_t = jnp.transpose(query.astype(F32))[:HEAD].astype(BF16)
        grad_t = jnp.transpose(grad.astype(F32))[HEAD:].astype(BF16)

        def third(j, acc):
            kv = key_value(j)
            low_p = p_ref[j]
            dp = dot32(grad, kv, NT)
            ds = (low_p.astype(F32) * (dp - delta)).astype(BF16)
            dkv_ref[j, :HEAD] += dot32(query_t, ds)
            dkv_ref[j, HEAD:] += dot32(grad_t, low_p)
            return acc + dot32(ds, kv)

        acc = lax.fori_loop(0, i + 1, third, jnp.zeros((rows, PAIR), F32))
        done = jnp.where(low, acc * scale, attended).astype(BF16)
        y_ref[pl.ds(i * group, group), key_rows:, :] = done.reshape(group, query_rows, PAIR)
        return unused

    lax.fori_loop(0, blocks, one_block, 0)

    def finish(i, unused):
        grads = jnp.transpose(dkv_ref[i]).astype(BF16)
        y_ref[pl.ds(i * group, group), :key_rows, :] = grads.reshape(group, key_rows, PAIR)
        return unused

    lax.fori_loop(0, blocks, finish, 0)


def one_head(x, part, key_rows, query_rows):
    count = x.shape[0]
    group = 2 if count % 2 == 0 else 1
    blocks = count // group
    keys, rows = group * key_rows, group * query_rows
    pairs = count * key_rows * count * query_rows // 2
    return pl.pallas_call(
        partial(head_kernel, group=group, key_rows=key_rows, query_rows=query_rows),
        out_shape=jax.ShapeDtypeStruct(x.shape, BF16),
        in_specs=[
            pl.BlockSpec(memory_space=pltpu.SMEM),
            pl.BlockSpec(memory_space=pltpu.VMEM),
        ],
        out_specs=pl.BlockSpec(memory_space=pltpu.VMEM),
        scratch_shapes=[
            pltpu.VMEM((blocks, rows, keys), F32),
            pltpu.VMEM((blocks, rows, keys), BF16),
            pltpu.VMEM((blocks, PAIR, keys), F32),
        ],
        cost_estimate=pl.CostEstimate(
            flops=pairs * 2 * 256 * 6, bytes_accessed=4 * x.size, transcendentals=pairs
        ),
        compiler_params=pltpu.CompilerParams(vmem_limit_bytes=56 * 1024 * 1024),
        name="one_head",
    )(part, x)


def feed_kernel(*refs, count, keep):
    rows_refs, cot_refs = refs[:count], refs[count : 2 * count]
    w1_ref, b1_ref, w2_ref = refs[2 * count : 2 * count + 3]
    hid_ref, gpre_ref, gb_ref = refs[2 * count + 3 : 2 * count + 6]
    outs = refs[2 * count + 6 : -2]
    out_acc, grad_acc = refs[-2:]
    step = pl.program_id(0)

    @pl.when(step == 0)
    def _():
        out_acc[...] = jnp.zeros_like(out_acc)
        grad_acc[...] = jnp.zeros_like(grad_acc)

    bias = b1_ref[...]
    sums = jnp.zeros_like(bias)
    rows = rows_refs[0].shape[0]
    for r in range(count):
        here = slice(r * rows, (r + 1) * rows)
        pre = dot32(rows_refs[r][...], w1_ref[...]) + bias
        grad = dot32(cot_refs[r][...], w2_ref[...], NT)
        cdf = 0.5 + 0.5 * lax.erf(pre * (0.5**0.5))
        density = jnp.exp(-0.5 * pre * pre) * 0.3989422804014327
        hidden = (pre * cdf).astype(BF16)
        grad_pre = (grad * (cdf + pre * density)).astype(BF16)
        hid_ref[here] = hidden
        gpre_ref[here] = grad_pre
        sums = sums + jnp.sum(grad_pre.astype(F32), 0, keepdims=True)
        out_acc[here] += dot32(hidden, w2_ref[...])
        grad_acc[here] += dot32(grad_pre, w1_ref[...], NT)
    gb_ref[...] = sums

    @pl.when(step == pl.num_programs(0) - 1)
    def _():
        if keep:
            own_out, own_grad, other_out, other_grad = outs
            own_out[...] = out_acc[:rows]
            own_grad[...] = grad_acc[:rows]
            other_out[...] = out_acc[rows:].astype(BF16)
            other_grad[...] = grad_acc[rows:].astype(BF16)
        else:
            outs[0][...] = out_acc[...].astype(BF16)
            outs[1][...] = grad_acc[...].astype(BF16)


def feed(rows_list, cot_list, w1, b1, w2):
    width, hidden = w1.shape
    count = len(rows_list)
    rows = rows_list[0].shape[0]
    total = rows * count
    block = 256
    keep = count > 1
    sides = (
        [(rows, F32), (rows, F32), (total - rows, BF16), (total - rows, BF16)]
        if keep
        else [(total, BF16), (total, BF16)]
    )
    once = pl.Buffered(1)
    whole = pl.BlockSpec((rows, width), lambda i: (0, 0), pipeline_mode=once)
    return pl.pallas_call(
        partial(feed_kernel, count=count, keep=keep),
        grid=(hidden // block,),
        out_shape=(
            shape_of((total, hidden), BF16),
            shape_of((total, hidden), BF16),
            shape_of((1, hidden), F32),
            *[shape_of((r, width), d) for r, d in sides],
        ),
        in_specs=[
            *[whole] * (2 * count),
            pl.BlockSpec((width, block), lambda i: (0, i)),
            pl.BlockSpec((1, block), lambda i: (0, i)),
            pl.BlockSpec((block, width), lambda i: (i, 0)),
        ],
        out_specs=(
            pl.BlockSpec((total, block), lambda i: (0, i)),
            pl.BlockSpec((total, block), lambda i: (0, i)),
            pl.BlockSpec((1, block), lambda i: (0, i)),
            *[
                pl.BlockSpec((r, width), lambda i: (0, 0), pipeline_mode=once) for r, d in sides
            ],
        ),
        scratch_shapes=[pltpu.VMEM((total, width), F32), pltpu.VMEM((total, width), F32)],
        cost_estimate=pl.CostEstimate(
            flops=8 * total * width * hidden,
            bytes_accessed=4 * width * hidden + 4 * total * hidden,
            transcendentals=2 * total * hidden,
        ),
        compiler_params=pltpu.CompilerParams(vmem_limit_bytes=VMEM_LIMIT),
        name="feed",
    )(*rows_list, *cot_list, w1, b1.astype(F32).reshape(1, hidden), w2)


def chunk_at(k, bit, value):
    return ((k >> bit) << (bit + 1)) + (value << bit) + (k & ((1 << bit) - 1))


def weight_kernel(me_ref, at_ref, *refs, bit, count):
    b_refs, (send_ref, keep_ref, chunk_ref) = refs[:count], refs[count:]
    rows = b_refs[0].shape[0]
    acc = dot32(at_ref[:, :rows], b_refs[0][...])
    for m in range(1, count):
        acc = acc + dot32(at_ref[:, m * rows : (m + 1) * rows], b_refs[m][...])
    chunk_ref[...] = acc.astype(BF16).reshape(chunk_ref.shape)
    mine = (me_ref[0] >> bit) & 1
    for k in range(send_ref.shape[0]):
        send_ref[k] = chunk_ref[chunk_at(k, bit, 1 - mine)]
        keep_ref[k] = chunk_ref[chunk_at(k, bit, mine)]


def weight_halves(me, at, parts, steps, block, members, bit):
    width, tokens = at.shape
    rows = width // members
    half = (members // 2, rows, steps * block)
    out = pl.BlockSpec((members // 2, rows, block), lambda i: (0, 0, i))
    return pl.pallas_call(
        partial(weight_kernel, bit=bit, count=len(parts)),
        grid=(steps,),
        out_shape=(shape_of(half, BF16), shape_of(half, BF16)),
        in_specs=[
            pl.BlockSpec(memory_space=pltpu.SMEM),
            fixed((width, tokens)),
            *[pl.BlockSpec(shape, index) for _, shape, index in parts],
        ],
        out_specs=(out, out),
        scratch_shapes=[pltpu.VMEM((members, rows, block), BF16)],
        cost_estimate=pl.CostEstimate(
            flops=2 * width * tokens * steps * block,
            bytes_accessed=2 * width * tokens + 2 * (width + tokens) * steps * block,
            transcendentals=0,
        ),
        compiler_params=pltpu.CompilerParams(vmem_limit_bytes=VMEM_LIMIT),
        name="weight_halves",
    )(me, at, *[array for array, _, _ in parts])


def add_kernel(me_ref, a0_ref, b0_ref, a1_ref, b1_ref, send_ref, keep_ref):
    send_ref[...] = (a0_ref[...].astype(F32) + b0_ref[...].astype(F32)).astype(BF16)
    keep_ref[...] = (a1_ref[...].astype(F32) + b1_ref[...].astype(F32)).astype(BF16)


def add_halves(me, held, came, ring_bit, bit):
    chunks, rows, cols = held.shape
    block = (1, rows, cols)

    def at(flip):
        return pl.BlockSpec(
            block, lambda k, me: (chunk_at(k, bit, ((me[0] >> ring_bit) & 1) ^ flip), 0, 0)
        )

    out = pl.BlockSpec(block, lambda k, me: (k, 0, 0))
    half = shape_of((chunks // 2, rows, cols), BF16)
    return pl.pallas_call(
        add_kernel,
        grid_spec=pltpu.PrefetchScalarGridSpec(
            num_scalar_prefetch=1,
            grid=(chunks // 2,),
            in_specs=[at(1), at(1), at(0), at(0)],
            out_specs=(out, out),
        ),
        out_shape=(half, half),
        cost_estimate=pl.CostEstimate(
            flops=held.size, bytes_accessed=6 * held.size, transcendentals=0
        ),
        name="add_halves",
    )(me, held, came, held, came)


def seq_move(x, bit):
    members = lax.axis_size("seq")
    return lax.ppermute(x, "seq", [(s, s ^ (1 << bit)) for s in range(members)])


class Ring:
    def __init__(self, me, send, keep, order):
        self.me, self.keep = me, keep
        members = lax.axis_size("seq")
        bits = members.bit_length() - 1
        order = [b for b in order if b < bits] + [b for b in range(bits) if b not in order]
        self.left = sorted(order, reverse=True)
        self.order = list(order)
        self.send = send
        self.travel()

    def travel(self):
        bit = self.order.pop(0)
        self.left.remove(bit)
        self.came = seq_move(self.send, bit)

    def step(self):
        bit = self.order[0]
        lower = len([b for b in self.left if b < bit])
        self.send, self.keep = add_halves(self.me, self.keep, self.came, bit, lower)
        self.travel()

    def total(self):
        while self.order:
            self.step()
        return self.keep[0].astype(F32) + self.came[0].astype(F32)


def regroup_kernel(back_ref, table_ref, gm_ref, att_ref, *, rows):
    heads, parts = back_ref.shape[:2]
    low = lax.broadcasted_iota(jnp.int32, (rows, PAIR), 1) < HEAD
    kv, qo = [], []
    for h in range(heads):
        kv.append(sum(back_ref[h, p, :rows].astype(F32) for p in range(parts)))
        qo.append(jnp.concatenate([back_ref[h, p, rows:].astype(F32) for p in range(parts)], 0))
    grad_k, grad_v = two_heads(kv[0], kv[1], low)
    grad_q, attended = two_heads(qo[0], qo[1], low)
    tables = (table_ref[0], -table_ref[1], -table_ref[2])
    gm_ref[0, :, :PAIR] = rotate_lanes(grad_q, *tables).astype(BF16)
    gm_ref[0, :, PAIR : 2 * PAIR] = rotate_lanes(grad_k, *tables).astype(BF16)
    gm_ref[0, :, 2 * PAIR :] = grad_v.astype(BF16)
    att_ref[...] = attended.astype(BF16)


def regroup(back, table, rows, parts):
    chunk = back.shape[1]
    return pl.pallas_call(
        partial(regroup_kernel, rows=rows),
        grid=(GROUPS,),
        out_shape=(
            shape_of((GROUPS, rows, 3 * PAIR), BF16),
            shape_of((rows, HEADS * HEAD), BF16),
        ),
        in_specs=[
            pl.BlockSpec((2, parts, chunk, PAIR), lambda i: (i, 0, 0, 0)),
            fixed(table.shape),
        ],
        out_specs=(
            pl.BlockSpec((1, rows, 3 * PAIR), lambda i: (i, 0, 0)),
            pl.BlockSpec((rows, PAIR), lambda i: (0, i)),
        ),
        cost_estimate=pl.CostEstimate(
            flops=back.size, bytes_accessed=4 * back.size, transcendentals=0
        ),
        name="regroup",
    )(back.reshape(HEADS, parts, chunk, PAIR), table)


def close_kernel(
    x_ref, g_ref, ga_ref, gf_ref, bo_ref, bc_ref, gm_ref, att_ref,
    wq_ref, wk_ref, wv_ref, wo_ref, *refs, sides,
):
    feeds, grads = refs[:sides], refs[sides : 2 * sides]
    out_ref, gin_ref, vec_ref, gmb_ref, out_acc, grad_acc = refs[2 * sides :]
    step = pl.program_id(0)

    @pl.when(step == 0)
    def _():
        out_acc[...] = jnp.zeros_like(out_acc)
        grad_acc[...] = jnp.zeros_like(grad_acc)

    out_acc[...] += dot32(att_ref[...], wo_ref[...])
    count = gm_ref.shape[0]
    for third, w_ref in enumerate((wq_ref, wk_ref, wv_ref)):
        grad = jnp.concatenate(
            [gm_ref[c, :, third * PAIR : (third + 1) * PAIR] for c in range(count)], 1
        )
        grad_acc[...] += dot32(grad, w_ref[...], NT)
    for c in range(count):
        gmb_ref[c] = jnp.sum(gm_ref[c].astype(F32), 0, keepdims=True)

    @pl.when(step == pl.num_programs(0) - 1)
    def _():
        x = x_ref[...].astype(F32)
        g = g_ref[...].astype(F32)
        total = x + out_acc[...] + vector_row(bo_ref) + vector_row(bc_ref)
        for ref in feeds:
            total = total + ref[...].astype(F32)
        out_ref[...] = total.astype(BF16)
        unit, root = unit_rows(x)
        one = grad_acc[...]
        two = grads[0][...].astype(F32)
        for ref in grads[1:]:
            two = two + ref[...].astype(F32)
        down = one * vector_row(ga_ref) + two * vector_row(gf_ref)
        mean = jnp.mean(down, -1, keepdims=True)
        slope = jnp.mean(down * unit, -1, keepdims=True)
        gin_ref[...] = g + root * (down - mean - unit * slope)
        for r, rows in enumerate((one * unit, one, g, two * unit, two)):
            vec_ref[r : r + 1] = jnp.sum(rows, 0, keepdims=True)


def close_layer(x, g, vectors, gm, attended, weight, out_weight, feeds, grads):
    rows, width = x.shape
    steps = 4
    cols = width // steps
    per = GROUPS // steps

    def third(t):
        return pl.BlockSpec((width, cols), lambda i: (0, t * steps + i))

    return pl.pallas_call(
        partial(close_kernel, sides=len(feeds)),
        grid=(steps,),
        out_shape=(
            shape_of((rows, width), BF16),
            shape_of((rows, width), F32),
            shape_of((5, width), F32),
            shape_of((GROUPS, 1, 3 * PAIR), F32),
        ),
        in_specs=[
            fixed((rows, width)),
            fixed((rows, width)),
            *[fixed((width,))] * 4,
            pl.BlockSpec((per, rows, 3 * PAIR), lambda i: (i, 0, 0)),
            pl.BlockSpec((rows, cols), lambda i: (0, i)),
            third(0), third(1), third(2),
            pl.BlockSpec((cols, width), lambda i: (i, 0)),
            *[fixed((rows, width))] * (2 * len(feeds)),
        ],
        out_specs=(
            fixed((rows, width)),
            fixed((rows, width)),
            fixed((5, width)),
            pl.BlockSpec((per, 1, 3 * PAIR), lambda i: (i, 0, 0)),
        ),
        scratch_shapes=[pltpu.VMEM((rows, width), F32), pltpu.VMEM((rows, width), F32)],
        cost_estimate=pl.CostEstimate(
            flops=8 * rows * width * width,
            bytes_accessed=8 * width * width + 24 * rows * width,
            transcendentals=0,
        ),
        compiler_params=pltpu.CompilerParams(vmem_limit_bytes=VMEM_LIMIT),
        name="close_layer",
    )(x, g, *vectors, gm, attended, weight, weight, weight, out_weight, *feeds, *grads)


def pair_swap(x):
    return lax.ppermute(x, "mlp", [(0, 1), (1, 0)])


def mlp_list(x, axis=0):
    if lax.axis_size("mlp") == 2:
        return [x, pair_swap(x)]
    return [lax.all_gather(x, "mlp", axis=axis, tiled=True)]


def mlp_pieces(pieces):
    members = lax.axis_size("mlp")
    if members == 2:
        me = lax.axis_index("mlp")
        came = pair_swap(lax.dynamic_index_in_dim(pieces, 1 - me, 0, False))
        return [lax.dynamic_index_in_dim(pieces, me, 0, False), came]
    got = lax.all_to_all(pieces, "mlp", 0, 0, tiled=False)
    return [got[m] for m in range(members)]


def after(value, *others):
    return lax.optimization_barrier((value, *others))[0]


def per_device(
    block_input,
    out_cotangent,
    attend_gain,
    attend_shift,
    query_key_value_weight,
    query_key_value_bias,
    attention_out_weight,
    attention_out_bias,
    feed_gain,
    feed_shift,
    expand_weight,
    expand_bias,
    contract_weight,
    contract_bias,
):
    seq_count, rows, width = block_input.shape
    members = lax.axis_size("seq")
    pairs = lax.axis_size("mlp")
    parts = members // HEADS
    own = width // members
    me = lax.axis_index("seq").astype(jnp.int32).reshape(1)
    pair_me = lax.axis_index("mlp")
    inputs = block_input.reshape(rows, width)
    cot = out_cotangent.reshape(rows, width)

    outgoing, normed_one, normed_two, table, one_t, two_t, cot_t = open_layer(
        inputs,
        cot,
        me * rows,
        (attend_gain, attend_shift, feed_gain, feed_shift),
        query_key_value_weight,
        query_key_value_bias,
        attention_out_weight,
        parts,
    )
    at_head = lax.all_to_all(outgoing, "seq", 0, 0, tiled=True)

    rows_list, cot_list = mlp_list(normed_two), mlp_list(cot)
    two_t, cot_t, one_t = (
        jnp.concatenate(mlp_list(v, 1), 1) if pairs == 2 else mlp_list(v, 1)[0]
        for v in (two_t, cot_t, one_t)
    )
    hidden, grad_pre, grad_hid_bias, *sides = feed(
        rows_list, cot_list, expand_weight, expand_bias, contract_weight
    )
    if pairs == 2:
        feeds = [sides[0], pair_swap(sides[2])]
        grads = [sides[1], pair_swap(sides[3])]
    else:
        feeds, grads = (
            [lax.psum_scatter(v, "mlp", scatter_dimension=0, tiled=True)] for v in sides
        )
    slice_width = expand_weight.shape[1]
    block = min(512, slice_width)

    def ring_of(at, b, order):
        parts_b = [
            (b, (rows, block), lambda i, m=m: (m, i)) for m in range(pairs)
        ]
        send, keep = weight_halves(
            me, at, parts_b, slice_width // block, block, members, order[0]
        )
        return Ring(me, send, keep, order)

    ring_out = ring_of(cot_t, hidden, (0, 1, 2, 3))
    ring_hid = ring_of(two_t, grad_pre, (1, 0, 2, 3))

    part = (me % parts).astype(jnp.int32)
    at_head = after(at_head, ring_out.send, ring_hid.send, *feeds, *grads)
    from_head = one_head(at_head, part, rows, rows // parts)
    back = lax.all_to_all(from_head, "seq", 0, 0, tiled=True)

    ring_out.came, ring_hid.came, from_head = lax.optimization_barrier(
        (ring_out.came, ring_hid.came, from_head)
    )
    ring_out.step()
    ring_hid.step()
    gm, attended = regroup(back, table, rows, parts)
    per = GROUPS // pairs
    gm_pieces = mlp_pieces(gm.reshape(pairs, per, rows, 3 * PAIR))
    att_t = jnp.transpose(attended)
    att_t = jnp.concatenate(mlp_list(att_t, 1), 1) if pairs == 2 else mlp_list(att_t, 1)[0]
    dense_share = width // pairs

    rings = []
    cuts = [(0, per // 2, (0, 1, 2, 3)), (per // 2, per, (1, 0, 2, 3))] if per > 1 else [
        (0, per, (0, 1, 2, 3))
    ]
    for low, high, order in cuts:
        parts_b = [
            (piece, (None, rows, 3 * PAIR), lambda i, low=low: (low + i, 0, 0))
            for piece in gm_pieces
        ]
        send, keep = weight_halves(
            me, one_t, parts_b, high - low, 3 * PAIR, members, order[0]
        )
        rings.append(Ring(me, send, keep, order))
    parts_b = [
        (piece, (rows, dense_share), lambda i: (0, 0))
        for piece in [
            lax.dynamic_slice_in_dim(c, pair_me * dense_share, dense_share, 1)
            for c in (
                cot_list
                if pairs == 2
                else [cot_list[0][m * rows : (m + 1) * rows] for m in range(pairs)]
            )
        ]
    ]
    send, keep = weight_halves(me, att_t, parts_b, 1, dense_share, members, 2)
    rings.append(Ring(me, send, keep, (2, 0, 1, 3)))

    block_output, grad_input, vec, gm_bias = close_layer(
        inputs,
        cot,
        (attend_gain, feed_gain, attention_out_bias, contract_bias),
        gm,
        attended,
        query_key_value_weight,
        attention_out_weight,
        feeds,
        grads,
    )

    bias_full = lax.dynamic_update_slice_in_dim(
        jnp.zeros((pairs * slice_width,), F32), grad_hid_bias[0], pair_me * slice_width, 0
    )
    gm_bias = jnp.transpose(gm_bias.reshape(GROUPS, 3, PAIR), (1, 0, 2)).reshape(-1)
    vectors = [*[vec[r] for r in range(5)], gm_bias, bias_full]
    packed = jnp.concatenate([v.reshape(members, pairs, -1) for v in vectors], -1)
    packed = jnp.sum(lax.all_to_all(packed, "seq", 0, 0, tiled=True), 0)
    if pairs == 2:
        mine = lax.dynamic_index_in_dim(packed, pair_me, 0, False)
        other = lax.dynamic_index_in_dim(packed, 1 - pair_me, 0, False)
        packed = mine + pair_swap(other)
    else:
        packed = lax.psum_scatter(packed, "mlp", scatter_dimension=0, tiled=False)
    outs, start = [], 0
    for v in vectors:
        size = v.shape[0] // (members * pairs)
        outs.append(lax.slice_in_dim(packed, start, start + size))
        start += size
    grad_gain_one, grad_shift_one, grad_dense_bias, grad_gain_two, grad_shift_two = outs[:5]
    grad_merged_bias, out_hid_bias = outs[5:]

    out_weight = jnp.transpose(ring_out.total())
    hid_weight = ring_hid.total()

    totals = jnp.concatenate([r.total() for r in rings], -1)
    pieces = mlp_pieces(totals.reshape(pairs, own // pairs, totals.shape[-1]))
    if pairs == 2:
        first = pair_me == 0
        pieces = [jnp.where(first, pieces[0], pieces[1]), jnp.where(first, pieces[1], pieces[0])]
    share = per * 3 * PAIR
    merged = jnp.stack([p[:, :share].reshape(-1, per, 3, PAIR) for p in pieces], 1)
    merged = jnp.transpose(merged, (0, 3, 1, 2, 4)).reshape(own // pairs, 3 * width)
    dense = jnp.concatenate([p[:, share:] for p in pieces], -1)
    return (
        block_output.reshape(seq_count, rows, width),
        grad_input.reshape(seq_count, rows, width),
        grad_gain_one,
        grad_shift_one,
        merged,
        grad_merged_bias,
        dense,
        grad_dense_bias,
        grad_gain_two,
        grad_shift_two,
        hid_weight,
        out_hid_bias,
        out_weight,
        grad_dense_bias,
    )


def solution(mesh):
    in_specs = (
        P("mlp", "seq", None),
        P("mlp", "seq", None),
        P(),
        P(),
        P(),
        P(),
        P(),
        P(),
        P(),
        P(),
        P(None, "mlp"),
        P("mlp"),
        P("mlp", None),
        P(),
    )
    out_specs = (
        P("mlp", "seq", None),
        P("mlp", "seq", None),
        P(("seq", "mlp")),
        P(("seq", "mlp")),
        P(("seq", "mlp"), None),
        P(("seq", "mlp")),
        P(("seq", "mlp"), None),
        P(("seq", "mlp")),
        P(("seq", "mlp")),
        P(("seq", "mlp")),
        P("seq", "mlp"),
        P(("seq", "mlp")),
        P("mlp", "seq"),
        P(("seq", "mlp")),
    )
    return jax.shard_map(
        per_device, mesh=mesh, in_specs=in_specs, out_specs=out_specs, check_vma=False
    )
```

```python
from functools import partial

import jax
import jax.numpy as jnp
from jax import lax
from jax.experimental import pallas as pl
from jax.experimental.pallas import tpu as pltpu
from jax.sharding import PartitionSpec as P

HEADS = 16
HEAD = 64
ROT = 16
PAIR = 2 * HEAD
EPS = 1e-05
NEGATIVE = -1e30

F32 = jnp.float32
BF16 = jnp.bfloat16
NT = (((1,), (1,)), ((), ()))
NN = (((1,), (0,)), ((), ()))
VMEM_LIMIT = 60 * 1024 * 1024
COST_SHARE = 16


def dot32(a, b, dims=NN):
    return lax.dot_general(a, b, dims, preferred_element_type=F32)


def cost(flops, bytes_accessed, transcendentals):
    return pl.CostEstimate(
        flops=flops // COST_SHARE,
        bytes_accessed=bytes_accessed // COST_SHARE,
        transcendentals=transcendentals // COST_SHARE,
    )


def shape_of(shape, dtype):
    return jax.ShapeDtypeStruct(shape, dtype)


def fixed(shape):
    return pl.BlockSpec(shape, lambda *i: (0,) * len(shape))


def vector_row(ref):
    return ref[...].astype(F32).reshape(1, -1)


def two_heads(pair_a, pair_b, low):
    even = jnp.where(low, pair_a, pltpu.roll(pair_b, HEAD, 1))
    odd = jnp.where(low, pltpu.roll(pair_a, HEAD, 1), pair_b)
    return (even, odd)


def rotary_lanes(first, rows, inverse):
    shape = (rows, PAIR)
    lane = lax.broadcasted_iota(jnp.int32, shape, 1) % HEAD
    position = (lax.broadcasted_iota(jnp.int32, shape, 0) + first).astype(F32)
    angle = position * inverse
    cosine, sine = jnp.cos(angle), jnp.sin(angle)
    zero = jnp.zeros_like(sine)
    return (
        jnp.where(lane < ROT, cosine, 1.0),
        jnp.where(lane < ROT // 2, -sine, zero),
        jnp.where((lane >= ROT // 2) & (lane < ROT), sine, zero),
    )


def rotate_lanes(x, cosine, to_first, to_second):
    ahead = pltpu.roll(x, PAIR - ROT // 2, 1)
    behind = pltpu.roll(x, ROT // 2, 1)
    return x * cosine + ahead * to_first + behind * to_second


def unit_rows(x):
    average = jnp.mean(x, -1, keepdims=True)
    centred = x - average
    spread = jnp.mean(centred * centred, -1, keepdims=True)
    root = lax.rsqrt(spread + EPS)
    return (centred * root, root)


def open_kernel(
    first_ref, x_ref, g_ref, inv_ref, ga_ref, sa_ref, gf_ref, sf_ref, b_ref,
    wq_ref, wk_ref, wv_ref, wo_ref,
    out_ref, n1_ref, n2_ref, table_ref, n1t_ref, n2t_ref, gt_ref, bias_ref, *, parts,
):
    rows, width = x_ref.shape
    step = pl.program_id(0)
    cols = wq_ref.shape[1]

    @pl.when(step == 0)
    def _():
        unit, root = unit_rows(x_ref[...].astype(F32))
        n1_ref[...] = (unit * vector_row(ga_ref) + vector_row(sa_ref)).astype(BF16)
        n2_ref[...] = (unit * vector_row(gf_ref) + vector_row(sf_ref)).astype(BF16)
        for t, table in enumerate(rotary_lanes(first_ref[0], rows, inv_ref[...])):
            table_ref[t] = table
        bias_ref[...] = vector_row(b_ref)

    for at, source, target in ((1, n1_ref, n1t_ref), (2, n2_ref, n2t_ref), (3, g_ref, gt_ref)):

        @pl.when(step == at)
        def _(source=source, target=target):
            target[...] = jnp.transpose(source[...])

    def bias(third):
        return bias_ref[:, pl.ds(pl.multiple_of(third * width + step * cols, cols), cols)]

    normed = n1_ref[...]
    query = dot32(normed, wq_ref[...]) + bias(0)
    key = dot32(normed, wk_ref[...]) + bias(1)
    value = dot32(normed, wv_ref[...]) + bias(2)
    grad = dot32(g_ref[...], wo_ref[...], NT)
    tables = (table_ref[0], table_ref[1], table_ref[2])
    low = lax.broadcasted_iota(jnp.int32, (rows, PAIR), 1) < HEAD
    query_rows = rows // parts
    for c in range(cols // PAIR):
        cut = slice(c * PAIR, (c + 1) * PAIR)
        kv = two_heads(rotate_lanes(key[:, cut], *tables), value[:, cut], low)
        qg = two_heads(rotate_lanes(query[:, cut], *tables), grad[:, cut], low)
        for h in range(2):
            kv_h, qg_h = kv[h].astype(BF16), qg[h].astype(BF16)
            for p in range(parts):
                out_ref[2 * c + h, p, :rows] = kv_h
                out_ref[2 * c + h, p, rows:] = qg_h[p * query_rows : (p + 1) * query_rows]


def open_layer(x, g, first, vectors, weight, bias, out_weight, parts):
    rows, width = x.shape
    steps = 4
    cols = width // steps
    per = HEADS // steps
    inverse = 10000.0 ** (-(jnp.arange(ROT // 2, dtype=F32) * 2.0 / ROT))
    inverse = jnp.tile(inverse, PAIR // (ROT // 2)).reshape(1, PAIR)
    chunk = rows + rows // parts

    def third(t):
        return pl.BlockSpec((width, cols), lambda i: (0, t * steps + i))

    out, *others = pl.pallas_call(
        partial(open_kernel, parts=parts),
        grid=(steps,),
        out_shape=(
            shape_of((HEADS, parts, chunk, PAIR), BF16),
            shape_of((rows, width), BF16),
            shape_of((rows, width), BF16),
            shape_of((3, rows, PAIR), F32),
            shape_of((width, rows), BF16),
            shape_of((width, rows), BF16),
            shape_of((width, rows), BF16),
        ),
        in_specs=[
            pl.BlockSpec(memory_space=pltpu.SMEM),
            fixed((rows, width)),
            fixed((rows, width)),
            fixed((1, PAIR)),
            *[fixed((width,))] * 4,
            fixed((3 * width,)),
            third(0), third(1), third(2),
            pl.BlockSpec((cols, width), lambda i: (i, 0)),
        ],
        out_specs=(
            pl.BlockSpec((per, parts, chunk, PAIR), lambda i: (i, 0, 0, 0)),
            fixed((rows, width)),
            fixed((rows, width)),
            fixed((3, rows, PAIR)),
            fixed((width, rows)),
            fixed((width, rows)),
            fixed((width, rows)),
        ),
        scratch_shapes=[pltpu.VMEM((1, 3 * width), F32)],
        cost_estimate=cost(
            flops=8 * rows * width * width,
            bytes_accessed=8 * width * width + 18 * rows * width,
            transcendentals=0,
        ),
        compiler_params=pltpu.CompilerParams(vmem_limit_bytes=VMEM_LIMIT),
        name="open_layer",
    )(first, x, g, inverse, *vectors, bias, weight, weight, weight, out_weight)
    return (out.reshape(HEADS * parts, chunk, PAIR), *others)


ROW_GROUP = 4
ONES = 16
CUTS = 4
KEY_GROUP = 2


def first_tile(i):
    return i * (i + 1)


def column_chunks(x):
    return [x[:, c : c + 128] for c in range(0, x.shape[1], 128)]


def forward_kernel(
    part_ref, x_ref, y_ref, g_ref, d_ref, p_hbm,
    s_ref, p_ref, dv_ref, vt_ref, mx_ref, top_ref, acc_ref, sem,
    *, key_rows, query_rows,
):
    blocks = x_ref.shape[0] // ROW_GROUP
    keys, rows = KEY_GROUP * key_rows, ROW_GROUP * query_rows
    low = lax.broadcasted_iota(jnp.int32, (rows, PAIR), 1) < HEAD
    key_low = lax.broadcasted_iota(jnp.int32, (keys, PAIR), 1) < HEAD
    cuts = [slice(r, r + rows // CUTS) for r in range(0, rows, rows // CUTS)]

    def key_value(j):
        return x_ref[pl.ds(j * KEY_GROUP, KEY_GROUP), :key_rows, :].reshape(keys, PAIR)

    def query_rows_of(i):
        return x_ref[pl.ds(i * ROW_GROUP, ROW_GROUP), key_rows:, :].reshape(rows, PAIR)

    def query_of(i):
        return jnp.where(low, query_rows_of(i).astype(F32) * HEAD**-0.5, 0.0).astype(BF16)

    def copy_out(i, j):
        return pltpu.make_async_copy(p_ref.at[j], p_hbm.at[first_tile(i) + j], sem.at[j])

    def ones_and_values(j, unused):
        turned = jnp.transpose(key_value(j).astype(F32))
        vt_ref[j, :HEAD] = turned[HEAD:].astype(BF16)
        vt_ref[j, HEAD:] = jnp.ones((ONES, keys), BF16)
        return unused

    def raise_max(cut, s):
        mx = mx_ref[cut]
        for chunk in column_chunks(s):
            mx = jnp.maximum(mx, chunk)
        mx_ref[cut] = mx

    def last_scores(i, query):
        row = lax.broadcasted_iota(jnp.int32, (rows, keys), 0)
        col = lax.broadcasted_iota(jnp.int32, (rows, keys), 1)
        row_pos = (row // query_rows) * key_rows + row % query_rows + part_ref[0] * query_rows
        for d in range(ROW_GROUP // KEY_GROUP):
            j = 2 * i + d
            s = dot32(query, key_value(j), NT)
            s = jnp.where(col + d * keys <= row_pos, s, NEGATIVE)
            s_ref[j] = s
            raise_max(slice(None), s)

    def tile(i, j, query, grad_t):
        kv = key_value(j)
        grads = None
        for cut in cuts:
            if grad_t is not None:
                part = dot32(grad_t[:, cut], p_ref[j, cut])
                grads = part if grads is None else grads + part
            top = top_ref[cut]
            p = jnp.concatenate(
                [jnp.exp(c - top) for c in column_chunks(s_ref[j, cut])], 1
            ).astype(BF16)
            p_ref[j, cut] = p
            acc_ref[:, cut] += dot32(vt_ref[j], p, NT)
            if query is not None:
                s = dot32(query[cut], kv, NT)
                s_ref[j, cut] = s
                raise_max(cut, s)
        if grads is not None:
            dv_ref[j, HEAD:] += grads
        copy_out(i, j).start()

    def block(i, grad_t, ahead):
        query = query_of(i + 1) if ahead else None
        top_ref[...] = jnp.broadcast_to(jnp.max(mx_ref[...], -1, keepdims=True), (rows, PAIR))
        mx_ref[...] = jnp.full_like(mx_ref, NEGATIVE)
        acc_ref[...] = jnp.zeros_like(acc_ref)

        def step(j, unused):
            copy_out(i - 1, j).wait()
            tile(i, j, query, grad_t)
            return unused

        lax.fori_loop(0, 2 * i, step, 0)
        for d in range(2):
            tile(i, 2 * i + d, query, None)
        if ahead:
            last_scores(i + 1, query)
        inverse = 1.0 / acc_ref[HEAD : HEAD + 1]
        attended_t = acc_ref[:HEAD] * inverse
        rows_t = jnp.transpose(query_rows_of(i).astype(F32))
        grad_t = (rows_t[HEAD:] * inverse).astype(BF16)
        both = jnp.transpose(jnp.concatenate([attended_t, grad_t.astype(F32)], 0))
        delta = jnp.sum(grad_t.astype(F32) * attended_t, 0, keepdims=True)
        d_ref[i] = jnp.transpose(jnp.broadcast_to(delta, (PAIR, rows)))
        g_ref[i] = jnp.where(low, 0.0, both).astype(BF16)
        here = pl.ds(i * ROW_GROUP, ROW_GROUP)
        y_ref[here, :query_rows, :] = both.astype(BF16).reshape(ROW_GROUP, query_rows, PAIR)
        if query_rows < key_rows:
            y_ref[here, query_rows:, :] = jnp.zeros(
                (ROW_GROUP, key_rows - query_rows, PAIR), BF16
            )
        return grad_t

    dv_ref[...] = jnp.zeros_like(dv_ref)
    lax.fori_loop(0, 2 * blocks, ones_and_values, 0)
    mx_ref[...] = jnp.full_like(mx_ref, NEGATIVE)
    last_scores(0, query_of(0))
    grad_t = lax.fori_loop(
        0, blocks - 1, lambda i, g: block(i, g, True), jnp.zeros((HEAD, rows), BF16)
    )
    grad_t = block(jnp.int32(blocks - 1), grad_t, False)

    def finish(j, unused):
        here = pl.ds(j * KEY_GROUP, KEY_GROUP)
        held = y_ref[here].reshape(keys, PAIR)
        dv_ref[j, HEAD:] += dot32(grad_t, p_ref[j])
        grads = jnp.transpose(dv_ref[j]).astype(BF16)
        y_ref[here] = jnp.where(key_low, held, grads).reshape(KEY_GROUP, key_rows, PAIR)
        copy_out(blocks - 1, j).wait()
        return unused

    lax.fori_loop(0, 2 * blocks, finish, 0)


def backward_kernel(
    x_ref, g_ref, d_ref, p_hbm, y_ref, p_ref, dp0_ref, dp1_ref, dk_ref, acc_ref, sem,
    *, key_rows, query_rows,
):
    blocks = x_ref.shape[0] // ROW_GROUP
    keys, rows = KEY_GROUP * key_rows, ROW_GROUP * query_rows
    tiles = first_tile(blocks)
    slots = p_ref.shape[0]
    low = lax.broadcasted_iota(jnp.int32, (rows, PAIR), 1) < HEAD
    dp_refs = (dp0_ref, dp1_ref)

    def copy_in(t):
        return pltpu.make_async_copy(p_hbm.at[t], p_ref.at[t % slots], sem.at[t % slots])

    def refill(t):
        @pl.when(t + slots < tiles)
        def _():
            copy_in(t + slots).start()

    for t in range(min(slots, tiles)):
        copy_in(t).start()
    dk_ref[...] = jnp.zeros_like(dk_ref)

    def key_value(j):
        return x_ref[pl.ds(j * KEY_GROUP, KEY_GROUP), :key_rows, :].reshape(keys, PAIR)

    def one_block(i, unused):
        here = pl.ds(i * ROW_GROUP, ROW_GROUP)
        query = x_ref[here, key_rows:, :].reshape(rows, PAIR).astype(F32) * HEAD**-0.5
        query_t = jnp.transpose(query)[:HEAD].astype(BF16)
        grad = g_ref[i]
        first = first_tile(i)
        acc_ref[...] = jnp.zeros_like(acc_ref)

        def raise_probs(j, side):
            dp_refs[side][...] = dot32(grad, key_value(j), NT)

        def tile(j, side):
            delta = d_ref[i]
            p = column_chunks(p_ref[(first + j) % slots].astype(F32))
            dp = column_chunks(dp_refs[side][...])
            ds = jnp.concatenate([a * (b - delta) for a, b in zip(p, dp)], 1).astype(BF16)
            dk_ref[j, HEAD:] += dot32(query_t, ds)
            acc_ref[...] += dot32(ds, key_value(j))

        def two_tiles(m, unused, more=True):
            j = 2 * m
            copy_in(first + j).wait()
            copy_in(first + j + 1).wait()
            raise_probs(j + 1, 1)
            tile(j, 0)
            if more:
                raise_probs(j + 2, 0)
            tile(j + 1, 1)
            refill(first + j)
            refill(first + j + 1)
            return unused

        raise_probs(0, 0)
        lax.fori_loop(0, i, two_tiles, 0)
        two_tiles(i, 0, False)
        done = jnp.where(low, acc_ref[...] * HEAD**-0.5, 0.0).astype(BF16)
        y_ref[here, :query_rows, :] = done.reshape(ROW_GROUP, query_rows, PAIR)
        if query_rows < key_rows:
            y_ref[here, query_rows:, :] = jnp.zeros(
                (ROW_GROUP, key_rows - query_rows, PAIR), BF16
            )
        return unused

    lax.fori_loop(0, blocks, one_block, 0)
    key_low = lax.broadcasted_iota(jnp.int32, (keys, PAIR), 1) < HEAD

    def finish(j, unused):
        here = pl.ds(j * KEY_GROUP, KEY_GROUP)
        held = y_ref[here].reshape(keys, PAIR)
        grads = jnp.transpose(dk_ref[j]).astype(BF16)
        y_ref[here] = jnp.where(key_low, held, grads).reshape(KEY_GROUP, key_rows, PAIR)
        return unused

    lax.fori_loop(0, 2 * blocks, finish, 0)


def head_sizes(x, key_rows, query_rows):
    count = x.shape[0]
    blocks = count // ROW_GROUP
    return count, blocks, KEY_GROUP * key_rows, ROW_GROUP * query_rows


def forward_head(x, part, key_rows, query_rows, behind):
    count, blocks, keys, rows = head_sizes(x, key_rows, query_rows)
    tiles = first_tile(blocks)
    vmem = pl.BlockSpec(memory_space=pltpu.VMEM)
    return pl.pallas_call(
        without(
            partial(forward_kernel, key_rows=key_rows, query_rows=query_rows), 2, len(behind)
        ),
        out_shape=(
            shape_of((count, key_rows, PAIR), BF16),
            shape_of((blocks, rows, PAIR), BF16),
            shape_of((blocks, rows, PAIR), F32),
            shape_of((tiles, rows, keys), BF16),
        ),
        in_specs=[pl.BlockSpec(memory_space=pltpu.SMEM), vmem]
        + [pl.BlockSpec(memory_space=pl.ANY)] * len(behind),
        out_specs=(vmem, vmem, vmem, pl.BlockSpec(memory_space=pl.ANY)),
        scratch_shapes=[
            pltpu.VMEM((2 * blocks, rows, keys), F32),
            pltpu.VMEM((2 * blocks, rows, keys), BF16),
            pltpu.VMEM((2 * blocks, PAIR, keys), F32),
            pltpu.VMEM((2 * blocks, HEAD + ONES, keys), BF16),
            pltpu.VMEM((rows, PAIR), F32),
            pltpu.VMEM((rows, PAIR), F32),
            pltpu.VMEM((HEAD + ONES, rows), F32),
            pltpu.SemaphoreType.DMA((2 * blocks,)),
        ],
        cost_estimate=cost(
            flops=tiles * rows * keys * 2 * 256 * 3,
            bytes_accessed=4 * x.size + 2 * tiles * rows * keys,
            transcendentals=tiles * rows * keys,
        ),
        compiler_params=pltpu.CompilerParams(vmem_limit_bytes=VMEM_LIMIT),
        name="forward_head",
    )(part, x, *behind)


def backward_head(x, grad, delta, probs, key_rows, query_rows):
    count, blocks, keys, rows = head_sizes(x, key_rows, query_rows)
    tiles = first_tile(blocks)
    slots = 6
    vmem = pl.BlockSpec(memory_space=pltpu.VMEM)
    return pl.pallas_call(
        partial(backward_kernel, key_rows=key_rows, query_rows=query_rows),
        out_shape=shape_of((count, key_rows, PAIR), BF16),
        in_specs=[vmem, vmem, vmem, pl.BlockSpec(memory_space=pl.ANY)],
        out_specs=vmem,
        scratch_shapes=[
            pltpu.VMEM((slots, rows, keys), BF16),
            pltpu.VMEM((rows, keys), F32),
            pltpu.VMEM((rows, keys), F32),
            pltpu.VMEM((2 * blocks, PAIR, keys), F32),
            pltpu.VMEM((rows, PAIR), F32),
            pltpu.SemaphoreType.DMA((slots,)),
        ],
        cost_estimate=cost(
            flops=tiles * rows * keys * 2 * 256 * 3,
            bytes_accessed=4 * x.size + 2 * tiles * rows * keys,
            transcendentals=0,
        ),
        compiler_params=pltpu.CompilerParams(vmem_limit_bytes=VMEM_LIMIT),
        name="backward_head",
    )(x, grad, delta, probs)


def feed_kernel(*refs, count, keep):
    rows_refs, cot_refs = refs[:count], refs[count : 2 * count]
    w1_ref, b1_ref, w2_ref = refs[2 * count : 2 * count + 3]
    hid_ref, gpre_ref, gb_ref = refs[2 * count + 3 : 2 * count + 6]
    outs = refs[2 * count + 6 : -2]
    out_acc, grad_acc = refs[-2:]
    step = pl.program_id(0)

    @pl.when(step == 0)
    def _():
        out_acc[...] = jnp.zeros_like(out_acc)
        grad_acc[...] = jnp.zeros_like(grad_acc)

    bias = b1_ref[...]
    sums = jnp.zeros_like(bias)
    rows = rows_refs[0].shape[0]
    for r in range(count):
        here = slice(r * rows, (r + 1) * rows)
        pre = dot32(rows_refs[r][...], w1_ref[...]) + bias
        grad = dot32(cot_refs[r][...], w2_ref[...], NT)
        cdf = 0.5 + 0.5 * lax.erf(pre * (0.5**0.5))
        density = jnp.exp(-0.5 * pre * pre) * 0.3989422804014327
        hidden = (pre * cdf).astype(BF16)
        grad_pre = (grad * (cdf + pre * density)).astype(BF16)
        hid_ref[here] = hidden
        gpre_ref[here] = grad_pre
        sums = sums + jnp.sum(grad_pre.astype(F32), 0, keepdims=True)
        out_acc[here] += dot32(hidden, w2_ref[...])
        grad_acc[here] += dot32(grad_pre, w1_ref[...], NT)
    gb_ref[...] = sums

    @pl.when(step == pl.num_programs(0) - 1)
    def _():
        if keep:
            own_out, own_grad, other_out, other_grad = outs
            own_out[...] = out_acc[:rows]
            own_grad[...] = grad_acc[:rows]
            other_out[...] = out_acc[rows:].astype(BF16)
            other_grad[...] = grad_acc[rows:].astype(BF16)
        else:
            outs[0][...] = out_acc[...].astype(BF16)
            outs[1][...] = grad_acc[...].astype(BF16)


def feed(rows_list, cot_list, w1, b1, w2):
    width, hidden = w1.shape
    count = len(rows_list)
    rows = rows_list[0].shape[0]
    total = rows * count
    block = 256
    keep = count > 1
    sides = (
        [(rows, F32), (rows, F32), (total - rows, BF16), (total - rows, BF16)]
        if keep
        else [(total, BF16), (total, BF16)]
    )
    once = pl.Buffered(1)
    whole = pl.BlockSpec((rows, width), lambda i: (0, 0), pipeline_mode=once)
    return pl.pallas_call(
        partial(feed_kernel, count=count, keep=keep),
        grid=(hidden // block,),
        out_shape=(
            shape_of((total, hidden), BF16),
            shape_of((total, hidden), BF16),
            shape_of((1, hidden), F32),
            *[shape_of((r, width), d) for r, d in sides],
        ),
        in_specs=[
            *[whole] * (2 * count),
            pl.BlockSpec((width, block), lambda i: (0, i)),
            pl.BlockSpec((1, block), lambda i: (0, i)),
            pl.BlockSpec((block, width), lambda i: (i, 0)),
        ],
        out_specs=(
            pl.BlockSpec((total, block), lambda i: (0, i)),
            pl.BlockSpec((total, block), lambda i: (0, i)),
            pl.BlockSpec((1, block), lambda i: (0, i)),
            *[
                pl.BlockSpec((r, width), lambda i: (0, 0), pipeline_mode=once) for r, d in sides
            ],
        ),
        scratch_shapes=[pltpu.VMEM((total, width), F32), pltpu.VMEM((total, width), F32)],
        cost_estimate=cost(
            flops=8 * total * width * hidden,
            bytes_accessed=4 * width * hidden + 4 * total * hidden,
            transcendentals=2 * total * hidden,
        ),
        compiler_params=pltpu.CompilerParams(vmem_limit_bytes=VMEM_LIMIT),
        name="feed",
    )(*rows_list, *cot_list, w1, b1.astype(F32).reshape(1, hidden), w2)


def insert_bits(k, positions, values):
    for position, value in zip(positions, values):
        k = ((k >> position) << (position + 1)) + (value << position) + (k & ((1 << position) - 1))
    return k


def part_chunk(k, p, me, ring_bits, positions):
    values = [((me >> bit) & 1) ^ ((p >> n) & 1) for n, bit in enumerate(ring_bits)]
    return insert_bits(k, positions, values)


def weight_kernel(me_ref, *refs, bits, counts):
    total = sum(counts)
    a_refs, b_refs, parts = refs[:total], refs[total : 2 * total], refs[2 * total :]

    def product(first, count):
        b = jnp.concatenate([r[...] for r in b_refs[first : first + count]], 0)
        for p, ref in enumerate(parts):
            chunks, rows, cols = ref.shape
            a = []
            for k in range(chunks):
                start = part_chunk(k, p, me_ref[0], bits, bits) * rows
                here = pl.ds(pl.multiple_of(start, rows), rows)
                a.append(
                    jnp.concatenate([r[here, :] for r in a_refs[first : first + count]], 1)
                )
            ref[...] = dot32(jnp.concatenate(a, 0), b).astype(BF16).reshape(ref.shape)

    if len(counts) == 1:
        product(0, total)
    else:
        for n, count in enumerate(counts):
            pl.when(pl.program_id(0) == n)(partial(product, sum(counts[:n]), count))


def weight_parts(scalars, products, steps, block, members, bits):
    a_runs = [run for a, _ in products for run in a]
    b_runs = [run for _, b in products for run in b]
    width = a_runs[0][1][0]
    rows = width // members
    tokens = sum(shape[1] for _, shape, _ in products[0][0])
    count = 1 << len(bits)
    each = (members // count, rows, steps * block)
    out = pl.BlockSpec((members // count, rows, block), lambda i, me: (0, 0, i))
    return pl.pallas_call(
        partial(weight_kernel, bits=bits, counts=[len(a) for a, _ in products]),
        grid_spec=pltpu.PrefetchScalarGridSpec(
            num_scalar_prefetch=1,
            grid=(steps,),
            in_specs=[pl.BlockSpec(shape, index) for _, shape, index in (*a_runs, *b_runs)],
            out_specs=[out] * count,
        ),
        out_shape=[shape_of(each, BF16)] * count,
        cost_estimate=cost(
            flops=2 * width * tokens * steps * block,
            bytes_accessed=2 * width * tokens + 2 * (width + tokens) * steps * block,
            transcendentals=0,
        ),
        compiler_params=pltpu.CompilerParams(vmem_limit_bytes=VMEM_LIMIT),
        name="weight_parts",
    )(scalars, *[array for array, _, _ in (*a_runs, *b_runs)])


def weight_once_kernel(me_ref, *refs, bits, forms):
    total = len(forms)
    a_refs, b_refs, parts = refs[:total], refs[total : 2 * total], refs[2 * total : -1]
    cols = parts[0].shape[2]
    for n in range(2):
        refs[-1][n] = me_ref[n]

    def run(ref, form):
        if form == "turned":
            return ref[...]
        start = pl.multiple_of(form(me_ref) * cols, cols)
        return ref[:, pl.ds(start, cols)]

    turned = forms[0] == "turned"
    b = jnp.concatenate([run(r, f) for r, f in zip(b_refs, forms)], 1 if turned else 0)
    for p, ref in enumerate(parts):
        chunks, rows, _ = ref.shape
        a = []
        for k in range(chunks):
            start = part_chunk(k, p, me_ref[0], bits, bits) * rows
            here = pl.ds(pl.multiple_of(start, rows), rows)
            a.append(jnp.concatenate([r[here, :] for r in a_refs], 1))
        product = dot32(jnp.concatenate(a, 0), b, NT if turned else NN)
        ref[...] = product.astype(BF16).reshape(ref.shape)


def weight_once(scalars, a_list, b_list, forms, cols, members, bits, behind=()):
    width = a_list[0].shape[0]
    count = 1 << len(bits)
    each = shape_of((members // count, width // members, cols), BF16)
    return vmem_call(
        partial(weight_once_kernel, bits=bits, forms=forms),
        [each] * count + [shape_of((2,), jnp.int32)],
        scalars,
        [*a_list, *b_list],
        "weight_once",
        behind,
    )


def column_sums(refs, counts):
    groups, start = [], 0
    for count in counts:
        groups.append(refs[start : start + count])
        start += count

    def total(group, c):
        value = group[0][c].astype(F32)
        for ref in group[1:]:
            value = value + ref[c].astype(F32)
        return value

    return [partial(total, group) for group in groups]


def add_kernel(me_ref, *refs, counts, bits, positions):
    ins, outs = refs[: sum(counts)], refs[sum(counts) :]
    at = 0
    for group, total in zip(counts, column_sums(ins, counts)):
        cols = ins[0].shape[2]
        for p, ref in enumerate(outs):
            for k in range(ref.shape[0]):
                c = part_chunk(k, p, me_ref[0], bits, positions)
                ref[k, :, at : at + cols] = total(c).astype(BF16)
        at += cols
        ins = ins[group:]


def last_kernel(me_ref, *refs, count, form):
    value = column_sums(refs[:count], [count])[0](0)
    outs = refs[count:]
    if form == "pair":
        half = value.shape[0] // 2
        first = me_ref[1] == 0
        outs[0][...] = jnp.where(first, value[:half], value[half:])
        outs[1][...] = jnp.where(first, value[half:], value[:half]).astype(BF16)
    else:
        at = 0
        for ref in outs:
            ref[...] = value[:, at : at + ref.shape[1]]
            at += ref.shape[1]


def without(kernel, first, count):
    if not count:
        return kernel
    return lambda *refs: kernel(*refs[:first], *refs[first + count :])


def vmem_call(kernel, out_shape, scalars, arrays, name, behind=()):
    vmem = pl.BlockSpec(memory_space=pltpu.VMEM)
    size = sum(a.size for a in arrays)
    return pl.pallas_call(
        without(kernel, 1 + len(arrays), len(behind)),
        in_specs=[pl.BlockSpec(memory_space=pltpu.SMEM)]
        + [vmem] * len(arrays)
        + [pl.BlockSpec(memory_space=pl.ANY)] * len(behind),
        out_specs=[
            pl.BlockSpec(memory_space=pltpu.SMEM) if o.dtype == jnp.int32 else vmem
            for o in out_shape
        ],
        out_shape=out_shape,
        cost_estimate=cost(flops=size, bytes_accessed=3 * size, transcendentals=0),
        compiler_params=pltpu.CompilerParams(vmem_limit_bytes=VMEM_LIMIT),
        name=name,
    )(scalars, *arrays, *behind)


def seq_move(x, mask):
    members = lax.axis_size("seq")
    return lax.ppermute(x, "seq", [(s, s ^ mask) for s in range(members)])


def ring_stages(stages):
    bits = lax.axis_size("seq").bit_length() - 1
    named = [b for stage in stages for b in stage]
    stages = [tuple(b for b in stage if b < bits) for stage in stages]
    stages[-1] = stages[-1] + tuple(b for b in range(bits) if b not in named)
    return [stage for stage in stages if stage]


class Ring:
    def __init__(self, scalars, parts, stages):
        self.scalars, self.stages, self.behind = scalars, list(stages), ()
        self.me = scalars[0]
        self.left = sorted(b for stage in stages for b in stage)
        self.travel(parts)

    def travel(self, parts):
        stage = self.stages.pop(0)
        self.left = [b for b in self.left if b not in stage]
        self.keep, self.sent = parts[0], parts[1:]
        self.came = [
            seq_move(part, sum(1 << b for n, b in enumerate(stage) if (p >> n) & 1))
            for p, part in enumerate(parts)
            if p
        ]

    def hold(self, *others):
        self.behind = others

    def step(self, *others):
        stage = self.stages[0]
        positions = [self.left.index(b) for b in stage]
        rings = (self, *others)
        chunks, rows = self.keep.shape[:2]
        cols = sum(ring.keep.shape[2] for ring in rings)
        count = 1 << len(stage)
        arrays = [[ring.keep, *ring.came] for ring in rings]
        self.travel(
            vmem_call(
                partial(
                    add_kernel, counts=[len(a) for a in arrays], bits=stage, positions=positions
                ),
                [shape_of((chunks // count, rows, cols), BF16)] * count,
                self.scalars,
                [a for group in arrays for a in group],
                "add_parts",
                self.behind,
            )
        )
        self.behind = ()

    def pass_on(self, me):
        stage = self.stages[0]
        bits = self.left
        shape = self.keep.shape[1:]
        arrays = [a.reshape((2,) * len(bits) + shape) for a in (self.keep, *self.came)]
        parts = []
        for p in range(1 << len(stage)):
            total = None
            for a in arrays:
                for n, bit in reversed(list(enumerate(stage))):
                    axis = len(bits) - 1 - bits.index(bit)
                    index = ((me >> bit) & 1) ^ ((p >> n) & 1)
                    a = lax.dynamic_index_in_dim(a, index, axis, True)
                a = a.reshape((-1,) + shape).astype(F32)
                total = a if total is None else total + a
            parts.append(total.astype(BF16))
        self.travel(parts)

    def total(self, widths=None):
        while self.stages:
            self.step()
        rows, cols = self.keep.shape[1:]
        shapes = (
            [shape_of((rows, w), F32) for w in widths]
            if widths
            else [shape_of((rows // 2, cols), F32), shape_of((rows // 2, cols), BF16)]
        )
        arrays = [self.keep, *self.came]
        return vmem_call(
            partial(last_kernel, count=len(arrays), form="rows" if widths else "pair"),
            shapes,
            self.scalars,
            arrays,
            "last_sum",
        )


def regroup_kernel(me_ref, back_ref, *refs, key_rows, query_rows, turned):
    heads, parts = back_ref.shape[:2]
    low = lax.broadcasted_iota(jnp.int32, (key_rows, PAIR), 1) < HEAD
    if turned:
        one_ref, two_ref, one_t_ref, *sides = refs
    else:
        table_ref, one_ref, two_ref, *sides = refs
        tables = (table_ref[0], -table_ref[1], -table_ref[2])
    first = pl.program_id(0) == 0
    for t in range(heads // 2):
        pair = []
        for h in (2 * t, 2 * t + 1):
            if parts == 1:
                pair.append(back_ref[h, 0].astype(F32))
                continue
            keys = sum(back_ref[h, p].astype(F32) for p in range(parts))
            queries = jnp.concatenate(
                [back_ref[h, p, :query_rows].astype(F32) for p in range(parts)], 0
            )
            pair.append(jnp.where(low, queries, keys))
        one, two = two_heads(pair[0], pair[1], low)
        if not turned:
            one, two = rotate_lanes(one, *tables), rotate_lanes(two, *tables)
        one, two = one.astype(BF16), two.astype(BF16)
        here = slice(t * PAIR, (t + 1) * PAIR)
        one_ref[:, here] = one
        two_ref[:, here] = two
        if turned:
            one_t_ref[here] = jnp.transpose(one)
        if sides:
            half = one_ref.shape[1]
            for n, value in enumerate((two,) if turned else (one, two)):
                there = slice(n * half + t * PAIR, n * half + (t + 1) * PAIR)
                pl.when(first)(partial(sides[1].__setitem__, (slice(None), there), value))
                pl.when(~first)(partial(sides[0].__setitem__, (slice(None), there), value))


def regroup(back, table, scalars, rows, query_rows, split):
    turned = table is None
    chunk = back.shape[1]
    parts = back.shape[0] // HEADS
    half = HEADS * HEAD // 2
    full = shape_of((rows, 2 * half), BF16)

    def side(i, me):
        return (i + me[1] + 1) % 2 if split else i

    whole = pl.BlockSpec((rows, half), lambda i, me: (0, side(i, me)))
    tall = pl.BlockSpec((half, rows), lambda i, me: (side(i, me), 0))
    cols = half * (1 if turned else 2)
    own = pl.BlockSpec((rows, cols), lambda i, me: (0, 0))
    return pl.pallas_call(
        partial(regroup_kernel, key_rows=rows, query_rows=query_rows, turned=turned),
        grid_spec=pltpu.PrefetchScalarGridSpec(
            num_scalar_prefetch=1,
            grid=(2,),
            in_specs=[
                pl.BlockSpec(
                    (HEADS // 2, parts, chunk, PAIR), lambda i, me: (side(i, me), 0, 0, 0)
                )
            ]
            + ([] if turned else [pl.BlockSpec(table.shape, lambda i, me: (0, 0, 0))]),
            out_specs=[whole, whole] + ([tall] if turned else []) + ([own, own] if split else []),
        ),
        out_shape=[full, full]
        + ([shape_of((2 * half, rows), BF16)] if turned else [])
        + ([shape_of((rows, cols), BF16)] * 2 if split else []),
        cost_estimate=cost(
            flops=back.size, bytes_accessed=4 * back.size, transcendentals=0
        ),
        name="regroup",
    )(
        scalars,
        back.reshape(HEADS, parts, chunk, PAIR),
        *([] if turned else [table]),
    )


def regroup_once_kernel(me_ref, *refs, turned):
    if turned:
        back_ref, att_ref, v_ref, send_ref, own_a_ref, own_v_ref = refs
    else:
        back_ref, table_ref, q_ref, k_ref, send_ref, own_ref = refs
        tables = (table_ref[0], -table_ref[1], -table_ref[2])
    heads, rows = back_ref.shape[:2]
    half = heads // 2
    low = lax.broadcasted_iota(jnp.int32, (rows, PAIR), 1) < HEAD
    for side in range(2):
        first = ((me_ref[1] + side) % 2) * half
        for t in range(half // 2):
            pair = [back_ref[first + 2 * t + n].astype(F32) for n in range(2)]
            one, two = two_heads(pair[0], pair[1], low)
            if not turned:
                one, two = rotate_lanes(one, *tables), rotate_lanes(two, *tables)
            one, two = one.astype(BF16), two.astype(BF16)
            start = pl.multiple_of((first // 2 + t) * PAIR, PAIR)
            here = pl.ds(start, PAIR)
            local = slice(t * PAIR, (t + 1) * PAIR)
            width = half * HEAD
            if turned:
                att_ref[:, here] = one
                v_ref[:, here] = two
                turned_one, turned_two = jnp.transpose(one), jnp.transpose(two)
                own_a_ref[here] = turned_one
                send_ref[here] = turned_one
                if side == 0:
                    own_v_ref[local] = turned_two
                else:
                    send_ref[2 * width + t * PAIR : 2 * width + (t + 1) * PAIR] = turned_two
            else:
                q_ref[:, here] = one
                k_ref[:, here] = two
                ref = own_ref if side == 0 else send_ref
                ref[:, local] = one
                ref[:, width + t * PAIR : width + (t + 1) * PAIR] = two


def regroup_once(back, table, scalars, behind=()):
    rows = back.shape[1]
    full = shape_of((rows, HEADS * HEAD), BF16)
    half = HEADS * HEAD // 2
    if table is None:
        sides = [
            shape_of((3 * half, rows), BF16),
            shape_of((2 * half, rows), BF16),
            shape_of((half, rows), BF16),
        ]
    else:
        sides = [shape_of((rows, 2 * half), BF16)] * 2
    return vmem_call(
        partial(regroup_once_kernel, turned=table is None),
        [full, full, *sides],
        scalars,
        [back] if table is None else [back, table],
        "regroup_once",
        behind,
    )


def close_kernel(
    x_ref, g_ref, ga_ref, gf_ref, bo_ref, bc_ref, gq_ref, gk_ref, gv_ref, att_ref,
    wq_ref, wk_ref, wv_ref, wo_ref, me_ref, *refs, sides,
):
    feeds, grads = refs[:sides], refs[sides : 2 * sides]
    out_ref, gin_ref, vec_ref, gb_ref, after_ref, out_acc, grad_acc = refs[2 * sides :]
    step = pl.program_id(0)
    for n in range(2):
        after_ref[n] = me_ref[n]

    @pl.when(step == 0)
    def _():
        out_acc[...] = jnp.zeros_like(out_acc)
        grad_acc[...] = jnp.zeros_like(grad_acc)

    out_acc[...] += dot32(att_ref[...], wo_ref[...])
    total = None
    for third, (g_third, w_ref) in enumerate(
        ((gq_ref, wq_ref), (gk_ref, wk_ref), (gv_ref, wv_ref))
    ):
        grad = g_third[...]
        part = dot32(grad, w_ref[...], NT)
        total = part if total is None else total + part
        gb_ref[third : third + 1] = jnp.sum(grad.astype(F32), 0, keepdims=True)
    grad_acc[...] += total

    @pl.when(step == pl.num_programs(0) - 1)
    def _():
        x = x_ref[...].astype(F32)
        g = g_ref[...].astype(F32)
        total = x + out_acc[...] + vector_row(bo_ref) + vector_row(bc_ref)
        for ref in feeds:
            total = total + ref[...].astype(F32)
        out_ref[...] = total.astype(BF16)
        unit, root = unit_rows(x)
        one = grad_acc[...]
        two = grads[0][...].astype(F32)
        for ref in grads[1:]:
            two = two + ref[...].astype(F32)
        down = one * vector_row(ga_ref) + two * vector_row(gf_ref)
        mean = jnp.mean(down, -1, keepdims=True)
        slope = jnp.mean(down * unit, -1, keepdims=True)
        gin_ref[...] = g + root * (down - mean - unit * slope)
        for r, rows in enumerate((one * unit, one, g, two * unit, two)):
            vec_ref[r : r + 1] = jnp.sum(rows, 0, keepdims=True)


def close_layer(x, g, vectors, gm, attended, weight, out_weight, feeds, grads, scalars, behind):
    rows, width = x.shape
    steps = 4
    cols = width // steps

    def third(t):
        return pl.BlockSpec((width, cols), lambda i: (0, t * steps + i))

    part = pl.BlockSpec((rows, cols), lambda i: (0, i))
    return pl.pallas_call(
        without(partial(close_kernel, sides=len(feeds)), 15 + 2 * len(feeds), len(behind)),
        grid=(steps,),
        out_shape=(
            shape_of((rows, width), BF16),
            shape_of((rows, width), F32),
            shape_of((5, width), F32),
            shape_of((3, width), F32),
            shape_of((2,), jnp.int32),
        ),
        in_specs=[
            fixed((rows, width)),
            fixed((rows, width)),
            *[fixed((width,))] * 4,
            part, part, part, part,
            third(0), third(1), third(2),
            pl.BlockSpec((cols, width), lambda i: (i, 0)),
            pl.BlockSpec(memory_space=pltpu.SMEM),
            *[fixed((rows, width))] * (2 * len(feeds)),
            *[pl.BlockSpec(memory_space=pl.ANY)] * len(behind),
        ],
        out_specs=(
            fixed((rows, width)),
            fixed((rows, width)),
            fixed((5, width)),
            pl.BlockSpec((3, cols), lambda i: (0, i)),
            pl.BlockSpec(memory_space=pltpu.SMEM),
        ),
        scratch_shapes=[pltpu.VMEM((rows, width), F32), pltpu.VMEM((rows, width), F32)],
        cost_estimate=cost(
            flops=8 * rows * width * width,
            bytes_accessed=8 * width * width + 24 * rows * width,
            transcendentals=0,
        ),
        compiler_params=pltpu.CompilerParams(vmem_limit_bytes=VMEM_LIMIT),
        name="close_layer",
    )(x, g, *vectors, *gm, attended, weight, weight, weight, out_weight, scalars, *feeds, *grads, *behind)


def place_kernel(me_ref, own_ref, came_ref, merged_ref, dense_ref):
    half = dense_ref.shape[1] // 2
    for side, ref in enumerate((own_ref, came_ref)):
        at = ((me_ref[1] + side) % 2) * half
        for third in range(3):
            start = pl.multiple_of(third * 2 * half + at, half)
            value = ref[:, third * half : (third + 1) * half]
            merged_ref[:, pl.ds(start, half)] = value.astype(F32)
        dense_ref[:, pl.ds(pl.multiple_of(at, half), half)] = ref[:, 3 * half :].astype(F32)


def pair_swap(x):
    return lax.ppermute(x, "mlp", [(0, 1), (1, 0)])


def mlp_list(x, axis=0):
    if lax.axis_size("mlp") == 2:
        return [x, pair_swap(x)]
    return [lax.all_gather(x, "mlp", axis=axis, tiled=True)]


def after(value, *others):
    return lax.optimization_barrier((value, *others))[0]


def per_device(
    block_input,
    out_cotangent,
    attend_gain,
    attend_shift,
    query_key_value_weight,
    query_key_value_bias,
    attention_out_weight,
    attention_out_bias,
    feed_gain,
    feed_shift,
    expand_weight,
    expand_bias,
    contract_weight,
    contract_bias,
):
    seq_count, rows, width = block_input.shape
    members = lax.axis_size("seq")
    pairs = lax.axis_size("mlp")
    parts = members // HEADS
    own = width // members
    me = lax.axis_index("seq").astype(jnp.int32).reshape(1)
    pair_me = lax.axis_index("mlp")
    scalars = jnp.stack([me[0], pair_me.astype(jnp.int32)])
    inputs = block_input.reshape(rows, width)
    cot = out_cotangent.reshape(rows, width)

    outgoing, normed_one, normed_two, table, one_t, two_t, cot_t = open_layer(
        inputs,
        cot,
        me * rows,
        (attend_gain, attend_shift, feed_gain, feed_shift),
        query_key_value_weight,
        query_key_value_bias,
        attention_out_weight,
        parts,
    )
    at_head = lax.all_to_all(outgoing, "seq", 0, 0, tiled=True)

    rows_list, cot_list = mlp_list(normed_two), mlp_list(cot)
    two_t, cot_t, one_t = (mlp_list(v, 1) for v in (two_t, cot_t, one_t))
    hidden, grad_pre, grad_hid_bias, *sides = feed(
        rows_list, cot_list, expand_weight, expand_bias, contract_weight
    )
    if pairs == 2:
        feeds = [sides[0], pair_swap(sides[2])]
        grads = [sides[1], pair_swap(sides[3])]
    else:
        feeds, grads = (
            [lax.psum_scatter(v, "mlp", scatter_dimension=0, tiled=True)] for v in sides
        )
    slice_width = expand_weight.shape[1]
    block = min(512, slice_width)

    def runs(arrays, shape, index):
        if pairs == 2:
            return [(a, shape, lambda i, me: index(0, i, me)) for a in arrays]
        return [(arrays[0], shape, lambda i, me, m=m: index(m, i, me)) for m in range(pairs)]

    def sides_of(arrays):
        return runs(arrays, (width, rows), lambda m, i, me: (0, m))

    def ring_of(products, steps, block, stages):
        stages = ring_stages(stages)
        parts = weight_parts(scalars, products, steps, block, members, stages[0])
        return Ring(scalars, parts, stages)

    def feed_ring(at, b, stages):
        b_runs = [(b, (rows, block), lambda i, me, m=m: (m, i)) for m in range(pairs)]
        return ring_of([(sides_of(at), b_runs)], slice_width // block, block, stages)

    ring_out = feed_ring(cot_t, hidden, [(0,), (1,), (2,), (3,)])
    ring_hid = feed_ring(two_t, grad_pre, [(1,), (0,), (2,), (3,)])

    part = (me % parts).astype(jnp.int32)
    query_rows = rows // parts
    from_first, head_grad, head_delta, probs = forward_head(
        at_head, part, rows, query_rows, (*ring_out.sent, *ring_hid.sent, *feeds, *grads)
    )
    back_first = lax.all_to_all(from_first, "seq", 0, 0, tiled=True)
    from_second = backward_head(at_head, head_grad, head_delta, probs, rows, query_rows)
    from_second, ring_out.came, ring_hid.came = lax.optimization_barrier(
        (from_second, ring_out.came, ring_hid.came)
    )
    back_second = lax.all_to_all(from_second, "seq", 0, 0, tiled=True)
    ring_out.hold(from_second)
    ring_hid.hold(from_second)
    ring_out.step()
    ring_hid.step()

    split = pairs == 2 and parts == 1
    share = width // pairs
    x_first, y_first = [(0,), (1,), (2,), (3,)], [(1,), (0,), (2,), (3,)]

    def pieces_of(arrays):
        stacked = jnp.stack([a.reshape(rows, pairs, share) for a in arrays], 2)
        stacked = jnp.transpose(stacked, (1, 0, 2, 3)).reshape(pairs, rows, len(arrays) * share)
        if pairs == 2:
            mine = lax.dynamic_index_in_dim(stacked, pair_me, 0, False)
            return [mine, pair_swap(lax.dynamic_index_in_dim(stacked, 1 - pair_me, 0, False))]
        got = lax.all_to_all(stacked, "mlp", 0, 0, tiled=True)
        return [got.reshape(pairs * rows, len(arrays) * share)]

    if split:

        def ring_once(a_list, b_list, forms, stages, behind=()):
            stages = ring_stages(stages)
            *sums, after_it = weight_once(
                scalars, a_list, b_list, forms, share, members, stages[0], behind
            )
            ring = Ring(scalars, sums, stages)
            ring.me = after_it[0]
            return ring

        attended, grad_v, sent, own_a, own_v = regroup_once(
            back_first, None, scalars, (*ring_out.sent, *ring_hid.sent)
        )
        came = pair_swap(sent)
        ring_v = ring_once(one_t, [own_v, came[width:]], ["turned"] * 2, x_first)
        ring_d = ring_once(
            [own_a, came[:width]], cot_list, [lambda me_ref: me_ref[1]] * 2, y_first
        )
        grad_q, grad_k, sent, own_qk = regroup_once(
            back_second, table, scalars, (*ring_v.sent, *ring_d.sent)
        )
        came = pair_swap(sent)
        ring_q = ring_once(one_t, [own_qk, came], [lambda me_ref: 0] * 2, x_first)
        ring_k = ring_once(
            one_t, [own_qk, came], [lambda me_ref: 1] * 2, y_first, tuple(ring_q.sent)
        )
    else:
        attended, grad_v, att_t = regroup(back_first, None, scalars, rows, query_rows, False)
        att_t = mlp_list(att_t, 1)
        v_runs = runs(pieces_of([grad_v]), (rows, share), lambda m, i, me: (m, 0))
        ring_v = ring_of([(sides_of(one_t), v_runs)], 1, share, x_first)
        cot_runs = runs(cot_list, (rows, share), lambda m, i, me: (m, me[1]))
        ring_d = ring_of([(sides_of(att_t), cot_runs)], 1, share, y_first)
        grad_q, grad_k = regroup(back_second, table, scalars, rows, query_rows, False)
        pieces = pieces_of([grad_q, grad_k])
        ring_q, ring_k = (
            ring_of(
                [(sides_of(one_t), runs(pieces, (rows, share), lambda m, i, me, n=n: (m, n)))],
                1,
                share,
                stages,
            )
            for n, stages in enumerate((x_first, y_first))
        )

    for ring in (ring_out, ring_v, ring_d):
        ring.hold(*ring_k.sent)
    ring_v.pass_on(ring_k.me)
    ring_d.pass_on(ring_k.me)
    ring_out.step(ring_hid)
    block_output, grad_input, vec, gm_bias, closed = close_layer(
        inputs,
        cot,
        (attend_gain, feed_gain, attention_out_bias, contract_bias),
        (grad_q, grad_k, grad_v),
        attended,
        query_key_value_weight,
        attention_out_weight,
        feeds,
        grads,
        scalars,
        (*ring_v.sent, *ring_d.sent, *ring_out.sent),
    )
    for ring in (ring_q, ring_k, ring_out):
        ring.hold(vec)
    ring_q.pass_on(closed[0])
    ring_k.pass_on(closed[0])
    ring_out.pass_on(closed[0])

    bias_full = lax.dynamic_update_slice_in_dim(
        jnp.zeros((pairs * slice_width,), F32), grad_hid_bias[0], pair_me * slice_width, 0
    )
    vectors = [*[vec[r] for r in range(5)], gm_bias.reshape(-1), bias_full]
    packed = jnp.concatenate([v.reshape(members, pairs, -1) for v in vectors], -1)
    if pairs == 2:
        mine = lax.dynamic_index_in_dim(packed, pair_me, 1, False)
        other = lax.dynamic_index_in_dim(packed, 1 - pair_me, 1, False)
        packed = mine + pair_swap(other)
    else:
        packed = lax.psum_scatter(packed, "mlp", scatter_dimension=1, tiled=False)
    packed = jnp.sum(lax.all_to_all(packed, "seq", 0, 0, tiled=True), 0)
    ring_q.hold(packed)
    ring_q.step(ring_k, ring_v, ring_d)
    outs, start = [], 0
    for v in vectors:
        size = v.shape[0] // (members * pairs)
        outs.append(lax.slice_in_dim(packed, start, start + size))
        start += size
    grad_gain_one, grad_shift_one, grad_dense_bias, grad_gain_two, grad_shift_two = outs[:5]
    grad_merged_bias, out_hid_bias = outs[5:]

    out_weight, hid_weight = ring_out.total([slice_width, slice_width])
    out_weight = jnp.transpose(out_weight)

    if pairs == 2:
        mine, other = ring_q.total()
        merged, dense = vmem_call(
            place_kernel,
            [shape_of((own // pairs, 3 * width), F32), shape_of((own // pairs, width), F32)],
            scalars,
            [mine, pair_swap(other)],
            "place",
        )
    else:
        got = ring_q.total([4 * share])[0].reshape(pairs, own // pairs, 4 * share)
        got = lax.all_to_all(got, "mlp", 0, 0, tiled=True)
        got = jnp.transpose(got.reshape(pairs, own // pairs, 4, share), (1, 2, 0, 3))
        got = got.reshape(own // pairs, 4 * width)
        merged, dense = got[:, : 3 * width], got[:, 3 * width :]
    return (
        block_output.reshape(seq_count, rows, width),
        grad_input.reshape(seq_count, rows, width),
        grad_gain_one,
        grad_shift_one,
        merged,
        grad_merged_bias,
        dense,
        grad_dense_bias,
        grad_gain_two,
        grad_shift_two,
        hid_weight,
        out_hid_bias,
        out_weight,
        grad_dense_bias,
    )


def solution(mesh):
    in_specs = (
        P("mlp", "seq", None),
        P("mlp", "seq", None),
        P(),
        P(),
        P(),
        P(),
        P(),
        P(),
        P(),
        P(),
        P(None, "mlp"),
        P("mlp"),
        P("mlp", None),
        P(),
    )
    out_specs = (
        P("mlp", "seq", None),
        P("mlp", "seq", None),
        P(("seq", "mlp")),
        P(("seq", "mlp")),
        P(("seq", "mlp"), None),
        P(("seq", "mlp")),
        P(("seq", "mlp"), None),
        P(("seq", "mlp")),
        P(("seq", "mlp")),
        P(("seq", "mlp")),
        P("seq", "mlp"),
        P(("seq", "mlp")),
        P("mlp", "seq"),
        P(("seq", "mlp")),
    )
    return jax.shard_map(
        per_device, mesh=mesh, in_specs=in_specs, out_specs=out_specs, check_vma=False
    )
```

```python
from functools import partial

import jax
import jax.numpy as jnp
from jax import lax
from jax.experimental import pallas as pl
from jax.experimental.pallas import tpu as pltpu
from jax.sharding import PartitionSpec as P

HEADS = 16
HEAD = 64
ROT = 16
PAIR = 2 * HEAD
EPS = 1e-05
NEGATIVE = -1e30

F32 = jnp.float32
BF16 = jnp.bfloat16
NT = (((1,), (1,)), ((), ()))
NN = (((1,), (0,)), ((), ()))
VMEM_LIMIT = 60 * 1024 * 1024
COST_SHARE = 16


def dot32(a, b, dims=NN):
    return lax.dot_general(a, b, dims, preferred_element_type=F32)


def cost(flops, bytes_accessed, transcendentals, share=COST_SHARE):
    return pl.CostEstimate(
        flops=flops // share,
        bytes_accessed=bytes_accessed // share,
        transcendentals=transcendentals // share,
    )


def shape_of(shape, dtype):
    return jax.ShapeDtypeStruct(shape, dtype)


def fixed(shape):
    return pl.BlockSpec(shape, lambda *i: (0,) * len(shape))


def vector_row(ref):
    return ref[...].astype(F32).reshape(1, -1)


def two_heads(pair_a, pair_b, low):
    even = jnp.where(low, pair_a, pltpu.roll(pair_b, HEAD, 1))
    odd = jnp.where(low, pltpu.roll(pair_a, HEAD, 1), pair_b)
    return (even, odd)


def rotary_lanes(first, rows, inverse):
    shape = (rows, PAIR)
    lane = lax.broadcasted_iota(jnp.int32, shape, 1) % HEAD
    position = (lax.broadcasted_iota(jnp.int32, shape, 0) + first).astype(F32)
    angle = position * inverse
    cosine, sine = jnp.cos(angle), jnp.sin(angle)
    zero = jnp.zeros_like(sine)
    return (
        jnp.where(lane < ROT, cosine, 1.0),
        jnp.where(lane < ROT // 2, -sine, zero),
        jnp.where((lane >= ROT // 2) & (lane < ROT), sine, zero),
    )


def rotate_lanes(x, cosine, to_first, to_second):
    ahead = pltpu.roll(x, PAIR - ROT // 2, 1)
    behind = pltpu.roll(x, ROT // 2, 1)
    return x * cosine + ahead * to_first + behind * to_second


def unit_rows(x):
    average = jnp.mean(x, -1, keepdims=True)
    centred = x - average
    spread = jnp.mean(centred * centred, -1, keepdims=True)
    root = lax.rsqrt(spread + EPS)
    return (centred * root, root)


def open_kernel(
    first_ref, x_ref, g_ref, inv_ref, ga_ref, sa_ref, gf_ref, sf_ref, b_ref,
    wq_ref, wk_ref, wv_ref, wo_ref,
    out_ref, n1_ref, n2_ref, table_ref, turned_ref, bias_ref, *, parts,
):
    rows, width = x_ref.shape
    step = pl.program_id(0)
    cols = wq_ref.shape[1]

    @pl.when(step == 0)
    def _():
        unit, root = unit_rows(x_ref[...].astype(F32))
        n1_ref[...] = (unit * vector_row(ga_ref) + vector_row(sa_ref)).astype(BF16)
        n2_ref[...] = (unit * vector_row(gf_ref) + vector_row(sf_ref)).astype(BF16)
        for t, table in enumerate(rotary_lanes(first_ref[0], rows, inv_ref[...])):
            table_ref[t] = table
        bias_ref[...] = vector_row(b_ref)

    for n, source in enumerate((n1_ref, n2_ref, g_ref)):

        @pl.when(step == n + 1)
        def _(n=n, source=source):
            turned_ref[n * width : (n + 1) * width] = jnp.transpose(source[...])

    def bias(third):
        return bias_ref[:, pl.ds(pl.multiple_of(third * width + step * cols, cols), cols)]

    normed = n1_ref[...]
    query = dot32(normed, wq_ref[...]) + bias(0)
    key = dot32(normed, wk_ref[...]) + bias(1)
    value = dot32(normed, wv_ref[...]) + bias(2)
    grad = dot32(g_ref[...], wo_ref[...], NT)
    tables = (table_ref[0], table_ref[1], table_ref[2])
    low = lax.broadcasted_iota(jnp.int32, (rows, PAIR), 1) < HEAD
    query_rows = rows // parts
    for c in range(cols // PAIR):
        cut = slice(c * PAIR, (c + 1) * PAIR)
        kv = two_heads(rotate_lanes(key[:, cut], *tables), value[:, cut], low)
        qg = two_heads(rotate_lanes(query[:, cut], *tables), grad[:, cut], low)
        for h in range(2):
            kv_h, qg_h = kv[h].astype(BF16), qg[h].astype(BF16)
            for p in range(parts):
                out_ref[2 * c + h, p, :rows] = kv_h
                out_ref[2 * c + h, p, rows:] = qg_h[p * query_rows : (p + 1) * query_rows]


def open_layer(x, g, first, vectors, weight, bias, out_weight, parts):
    rows, width = x.shape
    steps = 4
    cols = width // steps
    per = HEADS // steps
    inverse = 10000.0 ** (-(jnp.arange(ROT // 2, dtype=F32) * 2.0 / ROT))
    inverse = jnp.tile(inverse, PAIR // (ROT // 2)).reshape(1, PAIR)
    chunk = rows + rows // parts

    def third(t):
        return pl.BlockSpec((width, cols), lambda i: (0, t * steps + i))

    out, *others = pl.pallas_call(
        partial(open_kernel, parts=parts),
        grid=(steps,),
        out_shape=(
            shape_of((HEADS, parts, chunk, PAIR), BF16),
            shape_of((rows, width), BF16),
            shape_of((rows, width), BF16),
            shape_of((3, rows, PAIR), F32),
            shape_of((3 * width, rows), BF16),
        ),
        in_specs=[
            pl.BlockSpec(memory_space=pltpu.SMEM),
            fixed((rows, width)),
            fixed((rows, width)),
            fixed((1, PAIR)),
            *[fixed((width,))] * 4,
            fixed((3 * width,)),
            third(0), third(1), third(2),
            pl.BlockSpec((cols, width), lambda i: (i, 0)),
        ],
        out_specs=(
            pl.BlockSpec((per, parts, chunk, PAIR), lambda i: (i, 0, 0, 0)),
            fixed((rows, width)),
            fixed((rows, width)),
            fixed((3, rows, PAIR)),
            fixed((3 * width, rows)),
        ),
        scratch_shapes=[pltpu.VMEM((1, 3 * width), F32)],
        cost_estimate=cost(
            flops=8 * rows * width * width,
            bytes_accessed=8 * width * width + 18 * rows * width,
            transcendentals=0,
        ),
        compiler_params=pltpu.CompilerParams(vmem_limit_bytes=VMEM_LIMIT),
        name="open_layer",
    )(first, x, g, inverse, *vectors, bias, weight, weight, weight, out_weight)
    return (out.reshape(HEADS * parts, chunk, PAIR), *others)


ROW_GROUP = 4
ONES = 16
CUTS = 4
KEY_GROUP = 2


def first_tile(i):
    return i * (i + 1)


def column_chunks(x):
    return [x[:, c : c + 128] for c in range(0, x.shape[1], 128)]


def forward_kernel(
    part_ref, x_ref, y_ref, g_ref, d_ref, p_hbm, after_ref,
    s_ref, p_ref, dv_ref, vt_ref, mx_ref, top_ref, acc_ref, sem,
    *, key_rows, query_rows,
):
    after_ref[0] = part_ref[1]
    blocks = x_ref.shape[0] // ROW_GROUP
    keys, rows = KEY_GROUP * key_rows, ROW_GROUP * query_rows
    low = lax.broadcasted_iota(jnp.int32, (rows, PAIR), 1) < HEAD
    key_low = lax.broadcasted_iota(jnp.int32, (keys, PAIR), 1) < HEAD
    cuts = [slice(r, r + rows // CUTS) for r in range(0, rows, rows // CUTS)]

    def key_value(j):
        return x_ref[pl.ds(j * KEY_GROUP, KEY_GROUP), :key_rows, :].reshape(keys, PAIR)

    def query_rows_of(i):
        return x_ref[pl.ds(i * ROW_GROUP, ROW_GROUP), key_rows:, :].reshape(rows, PAIR)

    def query_of(i):
        return jnp.where(low, query_rows_of(i).astype(F32) * HEAD**-0.5, 0.0).astype(BF16)

    def copy_out(i, j):
        return pltpu.make_async_copy(p_ref.at[j], p_hbm.at[first_tile(i) + j], sem.at[j])

    def ones_and_values(j, unused):
        turned = jnp.transpose(key_value(j).astype(F32))
        vt_ref[j, :HEAD] = turned[HEAD:].astype(BF16)
        vt_ref[j, HEAD:] = jnp.ones((ONES, keys), BF16)
        return unused

    def raise_max(cut, s):
        mx = mx_ref[cut]
        for chunk in column_chunks(s):
            mx = jnp.maximum(mx, chunk)
        mx_ref[cut] = mx

    def last_scores(i, query):
        row = lax.broadcasted_iota(jnp.int32, (rows, keys), 0)
        col = lax.broadcasted_iota(jnp.int32, (rows, keys), 1)
        row_pos = (row // query_rows) * key_rows + row % query_rows + part_ref[0] * query_rows
        for d in range(ROW_GROUP // KEY_GROUP):
            j = 2 * i + d
            s = dot32(query, key_value(j), NT)
            s = jnp.where(col + d * keys <= row_pos, s, NEGATIVE)
            s_ref[j] = s
            raise_max(slice(None), s)

    def tile(i, j, query, grad_t):
        kv = key_value(j)
        grads = None
        for cut in cuts:
            if grad_t is not None:
                part = dot32(grad_t[:, cut], p_ref[j, cut])
                grads = part if grads is None else grads + part
            top = top_ref[cut]
            p = jnp.concatenate(
                [jnp.exp(c - top) for c in column_chunks(s_ref[j, cut])], 1
            ).astype(BF16)
            p_ref[j, cut] = p
            acc_ref[:, cut] += dot32(vt_ref[j], p, NT)
            if query is not None:
                s = dot32(query[cut], kv, NT)
                s_ref[j, cut] = s
                raise_max(cut, s)
        if grads is not None:
            dv_ref[j, HEAD:] += grads
        copy_out(i, j).start()

    def block(i, grad_t, ahead):
        query = query_of(i + 1) if ahead else None
        top_ref[...] = jnp.broadcast_to(jnp.max(mx_ref[...], -1, keepdims=True), (rows, PAIR))
        mx_ref[...] = jnp.full_like(mx_ref, NEGATIVE)
        acc_ref[...] = jnp.zeros_like(acc_ref)

        def step(j, unused):
            copy_out(i - 1, j).wait()
            tile(i, j, query, grad_t)
            return unused

        lax.fori_loop(0, 2 * i, step, 0)
        for d in range(2):
            tile(i, 2 * i + d, query, None)
        if ahead:
            last_scores(i + 1, query)
        inverse = 1.0 / acc_ref[HEAD : HEAD + 1]
        attended_t = acc_ref[:HEAD] * inverse
        rows_t = jnp.transpose(query_rows_of(i).astype(F32))
        grad_t = (rows_t[HEAD:] * inverse).astype(BF16)
        both = jnp.transpose(jnp.concatenate([attended_t, grad_t.astype(F32)], 0))
        delta = jnp.sum(grad_t.astype(F32) * attended_t, 0, keepdims=True)
        d_ref[i] = jnp.transpose(jnp.broadcast_to(delta, (PAIR, rows)))
        g_ref[i] = jnp.where(low, 0.0, both).astype(BF16)
        here = pl.ds(i * ROW_GROUP, ROW_GROUP)
        y_ref[here, :query_rows, :] = both.astype(BF16).reshape(ROW_GROUP, query_rows, PAIR)
        if query_rows < key_rows:
            y_ref[here, query_rows:, :] = jnp.zeros(
                (ROW_GROUP, key_rows - query_rows, PAIR), BF16
            )
        return grad_t

    dv_ref[...] = jnp.zeros_like(dv_ref)
    lax.fori_loop(0, 2 * blocks, ones_and_values, 0)
    mx_ref[...] = jnp.full_like(mx_ref, NEGATIVE)
    last_scores(0, query_of(0))
    grad_t = lax.fori_loop(
        0, blocks - 1, lambda i, g: block(i, g, True), jnp.zeros((HEAD, rows), BF16)
    )
    grad_t = block(jnp.int32(blocks - 1), grad_t, False)

    def finish(j, unused):
        here = pl.ds(j * KEY_GROUP, KEY_GROUP)
        held = y_ref[here].reshape(keys, PAIR)
        dv_ref[j, HEAD:] += dot32(grad_t, p_ref[j])
        grads = jnp.transpose(dv_ref[j]).astype(BF16)
        y_ref[here] = jnp.where(key_low, held, grads).reshape(KEY_GROUP, key_rows, PAIR)
        copy_out(blocks - 1, j).wait()
        return unused

    lax.fori_loop(0, 2 * blocks, finish, 0)


def backward_kernel(
    me_ref, x_ref, g_ref, d_ref, p_hbm, y_ref, after_ref,
    p_ref, dp0_ref, dp1_ref, dk_ref, acc_ref, sem,
    *, key_rows, query_rows,
):
    after_ref[0] = me_ref[0]
    blocks = x_ref.shape[0] // ROW_GROUP
    keys, rows = KEY_GROUP * key_rows, ROW_GROUP * query_rows
    tiles = first_tile(blocks)
    slots = p_ref.shape[0]
    low = lax.broadcasted_iota(jnp.int32, (rows, PAIR), 1) < HEAD
    dp_refs = (dp0_ref, dp1_ref)

    def copy_in(t):
        return pltpu.make_async_copy(p_hbm.at[t], p_ref.at[t % slots], sem.at[t % slots])

    def refill(t):
        @pl.when(t + slots < tiles)
        def _():
            copy_in(t + slots).start()

    for t in range(min(slots, tiles)):
        copy_in(t).start()
    dk_ref[...] = jnp.zeros_like(dk_ref)

    def key_value(j):
        return x_ref[pl.ds(j * KEY_GROUP, KEY_GROUP), :key_rows, :].reshape(keys, PAIR)

    def one_block(i, unused):
        here = pl.ds(i * ROW_GROUP, ROW_GROUP)
        query = x_ref[here, key_rows:, :].reshape(rows, PAIR).astype(F32) * HEAD**-0.5
        query_t = jnp.transpose(query)[:HEAD].astype(BF16)
        grad = g_ref[i]
        first = first_tile(i)
        acc_ref[...] = jnp.zeros_like(acc_ref)

        def raise_probs(j, side):
            dp_refs[side][...] = dot32(grad, key_value(j), NT)

        def tile(j, side):
            delta = d_ref[i]
            p = column_chunks(p_ref[(first + j) % slots].astype(F32))
            dp = column_chunks(dp_refs[side][...])
            ds = jnp.concatenate([a * (b - delta) for a, b in zip(p, dp)], 1).astype(BF16)
            dk_ref[j, HEAD:] += dot32(query_t, ds)
            acc_ref[...] += dot32(ds, key_value(j))

        def two_tiles(m, unused, more=True):
            j = 2 * m
            copy_in(first + j).wait()
            copy_in(first + j + 1).wait()
            raise_probs(j + 1, 1)
            tile(j, 0)
            if more:
                raise_probs(j + 2, 0)
            tile(j + 1, 1)
            refill(first + j)
            refill(first + j + 1)
            return unused

        raise_probs(0, 0)
        lax.fori_loop(0, i, two_tiles, 0)
        two_tiles(i, 0, False)
        done = jnp.where(low, acc_ref[...] * HEAD**-0.5, 0.0).astype(BF16)
        y_ref[here, :query_rows, :] = done.reshape(ROW_GROUP, query_rows, PAIR)
        if query_rows < key_rows:
            y_ref[here, query_rows:, :] = jnp.zeros(
                (ROW_GROUP, key_rows - query_rows, PAIR), BF16
            )
        return unused

    lax.fori_loop(0, blocks, one_block, 0)
    key_low = lax.broadcasted_iota(jnp.int32, (keys, PAIR), 1) < HEAD

    def finish(j, unused):
        here = pl.ds(j * KEY_GROUP, KEY_GROUP)
        held = y_ref[here].reshape(keys, PAIR)
        grads = jnp.transpose(dk_ref[j]).astype(BF16)
        y_ref[here] = jnp.where(key_low, held, grads).reshape(KEY_GROUP, key_rows, PAIR)
        return unused

    lax.fori_loop(0, 2 * blocks, finish, 0)


def head_sizes(x, key_rows, query_rows):
    count = x.shape[0]
    blocks = count // ROW_GROUP
    return count, blocks, KEY_GROUP * key_rows, ROW_GROUP * query_rows


def forward_head(x, part, key_rows, query_rows, behind):
    count, blocks, keys, rows = head_sizes(x, key_rows, query_rows)
    tiles = first_tile(blocks)
    vmem = pl.BlockSpec(memory_space=pltpu.VMEM)
    return pl.pallas_call(
        without(
            partial(forward_kernel, key_rows=key_rows, query_rows=query_rows), 2, len(behind)
        ),
        out_shape=(
            shape_of((count, key_rows, PAIR), BF16),
            shape_of((blocks, rows, PAIR), BF16),
            shape_of((blocks, rows, PAIR), F32),
            shape_of((tiles, rows, keys), BF16),
            shape_of((1,), jnp.int32),
        ),
        in_specs=[pl.BlockSpec(memory_space=pltpu.SMEM), vmem]
        + [pl.BlockSpec(memory_space=pl.ANY)] * len(behind),
        out_specs=(
            vmem, vmem, vmem, pl.BlockSpec(memory_space=pl.ANY),
            pl.BlockSpec(memory_space=pltpu.SMEM),
        ),
        scratch_shapes=[
            pltpu.VMEM((2 * blocks, rows, keys), F32),
            pltpu.VMEM((2 * blocks, rows, keys), BF16),
            pltpu.VMEM((2 * blocks, PAIR, keys), F32),
            pltpu.VMEM((2 * blocks, HEAD + ONES, keys), BF16),
            pltpu.VMEM((rows, PAIR), F32),
            pltpu.VMEM((rows, PAIR), F32),
            pltpu.VMEM((HEAD + ONES, rows), F32),
            pltpu.SemaphoreType.DMA((2 * blocks,)),
        ],
        cost_estimate=cost(
            flops=tiles * rows * keys * 2 * 256 * 3,
            bytes_accessed=4 * x.size + 2 * tiles * rows * keys,
            transcendentals=tiles * rows * keys,
            share=1,
        ),
        compiler_params=pltpu.CompilerParams(vmem_limit_bytes=VMEM_LIMIT),
        name="forward_head",
    )(part, x, *behind)


def backward_head(scalars, x, grad, delta, probs, key_rows, query_rows, behind):
    count, blocks, keys, rows = head_sizes(x, key_rows, query_rows)
    tiles = first_tile(blocks)
    slots = 6
    vmem = pl.BlockSpec(memory_space=pltpu.VMEM)
    return pl.pallas_call(
        without(
            partial(backward_kernel, key_rows=key_rows, query_rows=query_rows), 5, len(behind)
        ),
        out_shape=(shape_of((count, key_rows, PAIR), BF16), shape_of((1,), jnp.int32)),
        in_specs=[pl.BlockSpec(memory_space=pltpu.SMEM), vmem, vmem, vmem]
        + [pl.BlockSpec(memory_space=pl.ANY)] * (1 + len(behind)),
        out_specs=(vmem, pl.BlockSpec(memory_space=pltpu.SMEM)),
        scratch_shapes=[
            pltpu.VMEM((slots, rows, keys), BF16),
            pltpu.VMEM((rows, keys), F32),
            pltpu.VMEM((rows, keys), F32),
            pltpu.VMEM((2 * blocks, PAIR, keys), F32),
            pltpu.VMEM((rows, PAIR), F32),
            pltpu.SemaphoreType.DMA((slots,)),
        ],
        cost_estimate=cost(
            flops=tiles * rows * keys * 2 * 256 * 3,
            bytes_accessed=4 * x.size + 2 * tiles * rows * keys,
            transcendentals=0,
            share=1,
        ),
        compiler_params=pltpu.CompilerParams(vmem_limit_bytes=VMEM_LIMIT),
        name="backward_head",
    )(scalars, x, grad, delta, probs, *behind)


def feed_kernel(*refs, count, keep):
    rows_refs, cot_refs = refs[:count], refs[count : 2 * count]
    w1_ref, b1_ref, w2_ref = refs[2 * count : 2 * count + 3]
    hid_ref, gpre_ref, gb_ref = refs[2 * count + 3 : 2 * count + 6]
    outs = refs[2 * count + 6 : -2]
    out_acc, grad_acc = refs[-2:]
    step = pl.program_id(0)

    @pl.when(step == 0)
    def _():
        out_acc[...] = jnp.zeros_like(out_acc)
        grad_acc[...] = jnp.zeros_like(grad_acc)

    bias = b1_ref[...]
    sums = jnp.zeros_like(bias)
    rows = rows_refs[0].shape[0]
    for r in range(count):
        here = slice(r * rows, (r + 1) * rows)
        pre = dot32(rows_refs[r][...], w1_ref[...]) + bias
        grad = dot32(cot_refs[r][...], w2_ref[...], NT)
        cdf = 0.5 + 0.5 * lax.erf(pre * (0.5**0.5))
        density = jnp.exp(-0.5 * pre * pre) * 0.3989422804014327
        hidden = (pre * cdf).astype(BF16)
        grad_pre = (grad * (cdf + pre * density)).astype(BF16)
        hid_ref[here] = hidden
        gpre_ref[here] = grad_pre
        sums = sums + jnp.sum(grad_pre.astype(F32), 0, keepdims=True)
        out_acc[here] += dot32(hidden, w2_ref[...])
        grad_acc[here] += dot32(grad_pre, w1_ref[...], NT)
    gb_ref[...] = sums

    @pl.when(step == pl.num_programs(0) - 1)
    def _():
        if keep:
            own_out, own_grad, other = outs
            own_out[...] = out_acc[:rows]
            own_grad[...] = grad_acc[:rows]
            other[:rows] = out_acc[rows:].astype(BF16)
            other[rows:] = grad_acc[rows:].astype(BF16)
        else:
            outs[0][...] = out_acc[...].astype(BF16)
            outs[1][...] = grad_acc[...].astype(BF16)


def feed(rows_list, cot_list, w1, b1, w2):
    width, hidden = w1.shape
    count = len(rows_list)
    rows = rows_list[0].shape[0]
    total = rows * count
    block = 256
    keep = count > 1
    sides = (
        [(rows, F32), (rows, F32), (total, BF16)]
        if keep
        else [(total, BF16), (total, BF16)]
    )
    once = pl.Buffered(1)
    whole = pl.BlockSpec((rows, width), lambda i: (0, 0), pipeline_mode=once)
    return pl.pallas_call(
        partial(feed_kernel, count=count, keep=keep),
        grid=(hidden // block,),
        out_shape=(
            shape_of((total, hidden), BF16),
            shape_of((total, hidden), BF16),
            shape_of((1, hidden), F32),
            *[shape_of((r, width), d) for r, d in sides],
        ),
        in_specs=[
            *[whole] * (2 * count),
            pl.BlockSpec((width, block), lambda i: (0, i)),
            pl.BlockSpec((1, block), lambda i: (0, i)),
            pl.BlockSpec((block, width), lambda i: (i, 0)),
        ],
        out_specs=(
            pl.BlockSpec((total, block), lambda i: (0, i)),
            pl.BlockSpec((total, block), lambda i: (0, i)),
            pl.BlockSpec((1, block), lambda i: (0, i)),
            *[
                pl.BlockSpec((r, width), lambda i: (0, 0), pipeline_mode=once) for r, d in sides
            ],
        ),
        scratch_shapes=[pltpu.VMEM((total, width), F32), pltpu.VMEM((total, width), F32)],
        cost_estimate=cost(
            flops=8 * total * width * hidden,
            bytes_accessed=4 * width * hidden + 4 * total * hidden,
            transcendentals=2 * total * hidden,
        ),
        compiler_params=pltpu.CompilerParams(vmem_limit_bytes=VMEM_LIMIT),
        name="feed",
    )(*rows_list, *cot_list, w1, b1.astype(F32).reshape(1, hidden), w2)


def insert_bits(k, positions, values):
    for position, value in zip(positions, values):
        k = ((k >> position) << (position + 1)) + (value << position) + (k & ((1 << position) - 1))
    return k


def part_chunk(k, p, me, ring_bits, positions):
    values = [((me >> bit) & 1) ^ ((p >> n) & 1) for n, bit in enumerate(ring_bits)]
    return insert_bits(k, positions, values)


def weight_kernel(me_ref, *refs, bits, counts):
    total = sum(counts)
    a_refs, b_refs, parts = refs[:total], refs[total : 2 * total], refs[2 * total :]

    def product(first, count):
        b = jnp.concatenate([r[...] for r in b_refs[first : first + count]], 0)
        for p, ref in enumerate(parts):
            chunks, rows, cols = ref.shape
            a = []
            for k in range(chunks):
                start = part_chunk(k, p, me_ref[0], bits, bits) * rows
                here = pl.ds(pl.multiple_of(start, rows), rows)
                a.append(
                    jnp.concatenate([r[here, :] for r in a_refs[first : first + count]], 1)
                )
            ref[...] = dot32(jnp.concatenate(a, 0), b).astype(BF16).reshape(ref.shape)

    if len(counts) == 1:
        product(0, total)
    else:
        for n, count in enumerate(counts):
            pl.when(pl.program_id(0) == n)(partial(product, sum(counts[:n]), count))


def weight_parts(scalars, products, steps, block, members, bits):
    a_runs = [run for a, _ in products for run in a]
    b_runs = [run for _, b in products for run in b]
    width = a_runs[0][1][0]
    rows = width // members
    tokens = sum(shape[1] for _, shape, _ in products[0][0])
    count = 1 << len(bits)
    each = (members // count, rows, steps * block)
    out = pl.BlockSpec((members // count, rows, block), lambda i, me: (0, 0, i))
    return pl.pallas_call(
        partial(weight_kernel, bits=bits, counts=[len(a) for a, _ in products]),
        grid_spec=pltpu.PrefetchScalarGridSpec(
            num_scalar_prefetch=1,
            grid=(steps,),
            in_specs=[pl.BlockSpec(shape, index) for _, shape, index in (*a_runs, *b_runs)],
            out_specs=[out] * count,
        ),
        out_shape=[shape_of(each, BF16)] * count,
        cost_estimate=cost(
            flops=2 * width * tokens * steps * block,
            bytes_accessed=2 * width * tokens + 2 * (width + tokens) * steps * block,
            transcendentals=0,
        ),
        compiler_params=pltpu.CompilerParams(vmem_limit_bytes=VMEM_LIMIT),
        name="weight_parts",
    )(scalars, *[array for array, _, _ in (*a_runs, *b_runs)])


def weight_once_kernel(me_ref, *refs, products, operands):
    arrays, outs = refs[:operands], refs[operands:-1]
    for n in range(2):
        refs[-1][n] = me_ref[n]
    at = 0
    for blocks, bits in products:
        parts = outs[at : at + (1 << len(bits))]
        at += len(parts)
        cols = parts[0].shape[2] // len(blocks)
        for n, block in enumerate(blocks):
            here = slice(n * cols, (n + 1) * cols)
            if len(block) == len(parts):
                for ref, source in zip(parts, block):
                    ref[:, :, here] = arrays[source][...]
                continue
            a_runs, b_runs, turned = block
            b = jnp.concatenate([run(arrays, me_ref) for run in b_runs], 1 if turned else 0)
            for p, ref in enumerate(parts):
                chunks, rows, _ = ref.shape
                a = []
                for k in range(chunks):
                    start = part_chunk(k, p, me_ref[0], bits, bits) * rows
                    lines = pl.ds(pl.multiple_of(start, rows), rows)
                    a.append(jnp.concatenate([arrays[m][lines, :] for m in a_runs], 1))
                product = dot32(jnp.concatenate(a, 0), b, NT if turned else NN)
                ref[:, :, here] = product.astype(BF16).reshape(chunks, rows, cols)


def rows_run(n, first, count):
    return lambda arrays, me_ref: arrays[n][first : first + count, :]


def columns_run(n, cols, block):
    if block is not None:
        return lambda arrays, me_ref: arrays[n][:, block * cols : (block + 1) * cols]
    return lambda arrays, me_ref: arrays[n][:, pl.ds(pl.multiple_of(me_ref[1] * cols, cols), cols)]


def weight_once(scalars, arrays, products, width, cols, members, behind):
    each = [
        shape_of((members >> len(bits), width // members, cols * len(blocks)), BF16)
        for blocks, bits in products
        for _ in range(1 << len(bits))
    ]
    outs = vmem_call(
        partial(weight_once_kernel, products=products, operands=len(arrays)),
        each + [shape_of((2,), jnp.int32)],
        scalars,
        arrays,
        "weight_once",
        behind,
    )
    return outs[:2], outs[2:4], outs[4]


def column_sums(refs, counts):
    groups, start = [], 0
    for count in counts:
        groups.append(refs[start : start + count])
        start += count

    def total(group, c):
        value = group[0][c].astype(F32)
        for ref in group[1:]:
            value = value + ref[c].astype(F32)
        return value

    return [partial(total, group) for group in groups]


def add_kernel(me_ref, *refs, counts, bits, positions):
    ins, outs = refs[: sum(counts)], refs[sum(counts) :]
    at = 0
    for group, total in zip(counts, column_sums(ins, counts)):
        cols = ins[0].shape[2]
        for p, ref in enumerate(outs):
            for k in range(ref.shape[0]):
                c = part_chunk(k, p, me_ref[0], bits, positions)
                ref[k, :, at : at + cols] = total(c).astype(BF16)
        at += cols
        ins = ins[group:]


def last_kernel(me_ref, *refs, count, form):
    value = column_sums(refs[:count], [count])[0](0)
    outs = refs[count:]
    if form == "pair":
        half = value.shape[0] // 2
        first = me_ref[1] == 0
        outs[0][...] = jnp.where(first, value[:half], value[half:])
        outs[1][...] = jnp.where(first, value[half:], value[:half]).astype(BF16)
    else:
        at = 0
        for ref in outs:
            ref[...] = value[:, at : at + ref.shape[1]]
            at += ref.shape[1]


def without(kernel, first, count):
    if not count:
        return kernel
    return lambda *refs: kernel(*refs[:first], *refs[first + count :])


def vmem_call(kernel, out_shape, scalars, arrays, name, behind=()):
    vmem = pl.BlockSpec(memory_space=pltpu.VMEM)
    size = sum(a.size for a in arrays)
    return pl.pallas_call(
        without(kernel, 1 + len(arrays), len(behind)),
        in_specs=[pl.BlockSpec(memory_space=pltpu.SMEM)]
        + [vmem] * len(arrays)
        + [pl.BlockSpec(memory_space=pl.ANY)] * len(behind),
        out_specs=[
            pl.BlockSpec(memory_space=pltpu.SMEM) if o.dtype == jnp.int32 else vmem
            for o in out_shape
        ],
        out_shape=out_shape,
        cost_estimate=cost(flops=size, bytes_accessed=3 * size, transcendentals=0),
        compiler_params=pltpu.CompilerParams(vmem_limit_bytes=VMEM_LIMIT),
        name=name,
    )(scalars, *arrays, *behind)


def seq_move(x, mask):
    members = lax.axis_size("seq")
    return lax.ppermute(x, "seq", [(s, s ^ mask) for s in range(members)])


def ring_stages(stages):
    bits = lax.axis_size("seq").bit_length() - 1
    named = [b for stage in stages for b in stage]
    stages = [tuple(b for b in stage if b < bits) for stage in stages]
    stages[-1] = stages[-1] + tuple(b for b in range(bits) if b not in named)
    return [stage for stage in stages if stage]


class Ring:
    def __init__(self, scalars, parts, stages):
        self.scalars, self.stages, self.behind = scalars, list(stages), ()
        self.me = scalars[0]
        self.left = sorted(b for stage in stages for b in stage)
        self.travel(parts)

    def travel(self, parts):
        stage = self.stages.pop(0)
        self.left = [b for b in self.left if b not in stage]
        self.keep, self.sent = parts[0], parts[1:]
        self.came = [
            seq_move(part, sum(1 << b for n, b in enumerate(stage) if (p >> n) & 1))
            for p, part in enumerate(parts)
            if p
        ]

    def hold(self, *others):
        self.behind = others

    def step(self, *others):
        stage = self.stages[0]
        positions = [self.left.index(b) for b in stage]
        rings = (self, *others)
        chunks, rows = self.keep.shape[:2]
        cols = sum(ring.keep.shape[2] for ring in rings)
        count = 1 << len(stage)
        arrays = [[ring.keep, *ring.came] for ring in rings]
        self.travel(
            vmem_call(
                partial(
                    add_kernel, counts=[len(a) for a in arrays], bits=stage, positions=positions
                ),
                [shape_of((chunks // count, rows, cols), BF16)] * count,
                self.scalars,
                [a for group in arrays for a in group],
                "add_parts",
                self.behind,
            )
        )
        self.behind = ()

    def pass_on(self, me):
        stage = self.stages[0]
        bits = self.left
        shape = self.keep.shape[1:]
        arrays = [a.reshape((2,) * len(bits) + shape) for a in (self.keep, *self.came)]
        parts = []
        for p in range(1 << len(stage)):
            total = None
            for a in arrays:
                for n, bit in reversed(list(enumerate(stage))):
                    axis = len(bits) - 1 - bits.index(bit)
                    index = ((me >> bit) & 1) ^ ((p >> n) & 1)
                    a = lax.dynamic_index_in_dim(a, index, axis, True)
                a = a.reshape((-1,) + shape).astype(F32)
                total = a if total is None else total + a
            parts.append(total.astype(BF16))
        self.travel(parts)

    def plain_total(self):
        return sum(a[0].astype(F32) for a in (self.keep, *self.came))

    def total(self, widths=None):
        while self.stages:
            self.step()
        rows, cols = self.keep.shape[1:]
        shapes = (
            [shape_of((rows, w), F32) for w in widths]
            if widths
            else [shape_of((rows // 2, cols), F32), shape_of((rows // 2, cols), BF16)]
        )
        arrays = [self.keep, *self.came]
        return vmem_call(
            partial(last_kernel, count=len(arrays), form="rows" if widths else "pair"),
            shapes,
            self.scalars,
            arrays,
            "last_sum",
        )


def regroup_kernel(me_ref, back_ref, *refs, key_rows, query_rows, turned):
    heads, parts = back_ref.shape[:2]
    low = lax.broadcasted_iota(jnp.int32, (key_rows, PAIR), 1) < HEAD
    if turned:
        one_ref, two_ref, one_t_ref, *sides = refs
    else:
        table_ref, one_ref, two_ref, *sides = refs
        tables = (table_ref[0], -table_ref[1], -table_ref[2])
    first = pl.program_id(0) == 0
    for t in range(heads // 2):
        pair = []
        for h in (2 * t, 2 * t + 1):
            if parts == 1:
                pair.append(back_ref[h, 0].astype(F32))
                continue
            keys = sum(back_ref[h, p].astype(F32) for p in range(parts))
            queries = jnp.concatenate(
                [back_ref[h, p, :query_rows].astype(F32) for p in range(parts)], 0
            )
            pair.append(jnp.where(low, queries, keys))
        one, two = two_heads(pair[0], pair[1], low)
        if not turned:
            one, two = rotate_lanes(one, *tables), rotate_lanes(two, *tables)
        one, two = one.astype(BF16), two.astype(BF16)
        here = slice(t * PAIR, (t + 1) * PAIR)
        one_ref[:, here] = one
        two_ref[:, here] = two
        if turned:
            one_t_ref[here] = jnp.transpose(one)
        if sides:
            half = one_ref.shape[1]
            for n, value in enumerate((two,) if turned else (one, two)):
                there = slice(n * half + t * PAIR, n * half + (t + 1) * PAIR)
                pl.when(first)(partial(sides[1].__setitem__, (slice(None), there), value))
                pl.when(~first)(partial(sides[0].__setitem__, (slice(None), there), value))


def regroup(back, table, scalars, rows, query_rows, split):
    turned = table is None
    chunk = back.shape[1]
    parts = back.shape[0] // HEADS
    half = HEADS * HEAD // 2
    full = shape_of((rows, 2 * half), BF16)

    def side(i, me):
        return (i + me[1] + 1) % 2 if split else i

    whole = pl.BlockSpec((rows, half), lambda i, me: (0, side(i, me)))
    tall = pl.BlockSpec((half, rows), lambda i, me: (side(i, me), 0))
    cols = half * (1 if turned else 2)
    own = pl.BlockSpec((rows, cols), lambda i, me: (0, 0))
    return pl.pallas_call(
        partial(regroup_kernel, key_rows=rows, query_rows=query_rows, turned=turned),
        grid_spec=pltpu.PrefetchScalarGridSpec(
            num_scalar_prefetch=1,
            grid=(2,),
            in_specs=[
                pl.BlockSpec(
                    (HEADS // 2, parts, chunk, PAIR), lambda i, me: (side(i, me), 0, 0, 0)
                )
            ]
            + ([] if turned else [pl.BlockSpec(table.shape, lambda i, me: (0, 0, 0))]),
            out_specs=[whole, whole] + ([tall] if turned else []) + ([own, own] if split else []),
        ),
        out_shape=[full, full]
        + ([shape_of((2 * half, rows), BF16)] if turned else [])
        + ([shape_of((rows, cols), BF16)] * 2 if split else []),
        cost_estimate=cost(
            flops=back.size, bytes_accessed=4 * back.size, transcendentals=0
        ),
        name="regroup",
    )(
        scalars,
        back.reshape(HEADS, parts, chunk, PAIR),
        *([] if turned else [table]),
    )


def regroup_once_kernel(me_ref, *refs, turned):
    if turned:
        back_ref, att_ref, v_ref, send_ref, own_a_ref, own_v_ref = refs
    else:
        back_ref, table_ref, q_ref, k_ref, send_ref, own_ref = refs
        tables = (table_ref[0], -table_ref[1], -table_ref[2])
    heads, rows = back_ref.shape[:2]
    half = heads // 2
    low = lax.broadcasted_iota(jnp.int32, (rows, PAIR), 1) < HEAD
    for side in range(2):
        first = ((me_ref[1] + side) % 2) * half
        for t in range(half // 2):
            pair = [back_ref[first + 2 * t + n].astype(F32) for n in range(2)]
            one, two = two_heads(pair[0], pair[1], low)
            if not turned:
                one, two = rotate_lanes(one, *tables), rotate_lanes(two, *tables)
            one, two = one.astype(BF16), two.astype(BF16)
            start = pl.multiple_of((first // 2 + t) * PAIR, PAIR)
            here = pl.ds(start, PAIR)
            local = slice(t * PAIR, (t + 1) * PAIR)
            width = half * HEAD
            if turned:
                att_ref[:, here] = one
                v_ref[:, here] = two
                turned_one, turned_two = jnp.transpose(one), jnp.transpose(two)
                own_a_ref[here] = turned_one
                send_ref[here] = turned_one
                if side == 0:
                    own_v_ref[local] = turned_two
                else:
                    send_ref[2 * width + t * PAIR : 2 * width + (t + 1) * PAIR] = turned_two
            else:
                q_ref[:, here] = one
                k_ref[:, here] = two
                ref = own_ref if side == 0 else send_ref
                ref[:, local] = one
                ref[:, width + t * PAIR : width + (t + 1) * PAIR] = two


def regroup_once(back, table, scalars, behind=()):
    rows = back.shape[1]
    full = shape_of((rows, HEADS * HEAD), BF16)
    half = HEADS * HEAD // 2
    if table is None:
        sides = [
            shape_of((3 * half, rows), BF16),
            shape_of((2 * half, rows), BF16),
            shape_of((half, rows), BF16),
        ]
    else:
        sides = [shape_of((rows, 2 * half), BF16)] * 2
    return vmem_call(
        partial(regroup_once_kernel, turned=table is None),
        [full, full, *sides],
        scalars,
        [back] if table is None else [back, table],
        "regroup_once",
        behind,
    )


def close_kernel(
    x_ref, g_ref, ga_ref, gf_ref, bo_ref, bc_ref, gq_ref, gk_ref, gv_ref, att_ref,
    wq_ref, wk_ref, wv_ref, wo_ref, me_ref, *refs, sides,
):
    feeds, grads = refs[:sides], refs[sides : 2 * sides]
    out_ref, gin_ref, vec_ref, gb_ref, after_ref, out_acc, grad_acc = refs[2 * sides :]
    step = pl.program_id(0)
    for n in range(2):
        after_ref[n] = me_ref[n]

    @pl.when(step == 0)
    def _():
        out_acc[...] = jnp.zeros_like(out_acc)
        grad_acc[...] = jnp.zeros_like(grad_acc)

    out_acc[...] += dot32(att_ref[...], wo_ref[...])
    total = None
    for third, (g_third, w_ref) in enumerate(
        ((gq_ref, wq_ref), (gk_ref, wk_ref), (gv_ref, wv_ref))
    ):
        grad = g_third[...]
        part = dot32(grad, w_ref[...], NT)
        total = part if total is None else total + part
        gb_ref[third : third + 1] = jnp.sum(grad.astype(F32), 0, keepdims=True)
    grad_acc[...] += total

    @pl.when(step == pl.num_programs(0) - 1)
    def _():
        x = x_ref[...].astype(F32)
        g = g_ref[...].astype(F32)
        total = x + out_acc[...] + vector_row(bo_ref) + vector_row(bc_ref)
        for ref in feeds:
            total = total + ref[...].astype(F32)
        out_ref[...] = total.astype(BF16)
        unit, root = unit_rows(x)
        one = grad_acc[...]
        two = grads[0][...].astype(F32)
        for ref in grads[1:]:
            two = two + ref[...].astype(F32)
        down = one * vector_row(ga_ref) + two * vector_row(gf_ref)
        mean = jnp.mean(down, -1, keepdims=True)
        slope = jnp.mean(down * unit, -1, keepdims=True)
        gin_ref[...] = g + root * (down - mean - unit * slope)
        for r, rows in enumerate((one * unit, one, g, two * unit, two)):
            vec_ref[r : r + 1] = jnp.sum(rows, 0, keepdims=True)


def close_layer(x, g, vectors, gm, attended, weight, out_weight, feeds, grads, scalars, behind):
    rows, width = x.shape
    steps = 4
    cols = width // steps

    def third(t):
        return pl.BlockSpec((width, cols), lambda i: (0, t * steps + i))

    part = pl.BlockSpec((rows, cols), lambda i: (0, i))
    return pl.pallas_call(
        without(partial(close_kernel, sides=len(feeds)), 15 + 2 * len(feeds), len(behind)),
        grid=(steps,),
        out_shape=(
            shape_of((rows, width), BF16),
            shape_of((rows, width), F32),
            shape_of((5, width), F32),
            shape_of((3, width), F32),
            shape_of((2,), jnp.int32),
        ),
        in_specs=[
            fixed((rows, width)),
            fixed((rows, width)),
            *[fixed((width,))] * 4,
            part, part, part, part,
            third(0), third(1), third(2),
            pl.BlockSpec((cols, width), lambda i: (i, 0)),
            pl.BlockSpec(memory_space=pltpu.SMEM),
            *[
                pl.BlockSpec((rows, width), lambda i, n=n: (n, 0)) for _, n in (*feeds, *grads)
            ],
            *[pl.BlockSpec(memory_space=pl.ANY)] * len(behind),
        ],
        out_specs=(
            fixed((rows, width)),
            fixed((rows, width)),
            fixed((5, width)),
            pl.BlockSpec((3, cols), lambda i: (0, i)),
            pl.BlockSpec(memory_space=pltpu.SMEM),
        ),
        scratch_shapes=[pltpu.VMEM((rows, width), F32), pltpu.VMEM((rows, width), F32)],
        cost_estimate=cost(
            flops=8 * rows * width * width,
            bytes_accessed=8 * width * width + 24 * rows * width,
            transcendentals=0,
        ),
        compiler_params=pltpu.CompilerParams(vmem_limit_bytes=VMEM_LIMIT),
        name="close_layer",
    )(x, g, *vectors, *gm, attended, weight, weight, weight, out_weight, scalars, *[a for a, _ in (*feeds, *grads)], *behind)


def place_kernel(me_ref, own_ref, came_ref, merged_ref, dense_ref):
    half = dense_ref.shape[1] // 2
    for side, ref in enumerate((own_ref, came_ref)):
        at = ((me_ref[1] + side) % 2) * half
        for third, block in enumerate((0, 2, 1)):
            start = pl.multiple_of(third * 2 * half + at, half)
            value = ref[:, block * half : (block + 1) * half]
            merged_ref[:, pl.ds(start, half)] = value.astype(F32)
        dense_ref[:, pl.ds(pl.multiple_of(at, half), half)] = ref[:, 3 * half :].astype(F32)


def pair_swap(x):
    return lax.ppermute(x, "mlp", [(0, 1), (1, 0)])


def mlp_list(x, axis=0):
    if lax.axis_size("mlp") == 2:
        return [x, pair_swap(x)]
    return [lax.all_gather(x, "mlp", axis=axis, tiled=True)]


def after(value, *others):
    return lax.optimization_barrier((value, *others))[0]


def per_device(
    block_input,
    out_cotangent,
    attend_gain,
    attend_shift,
    query_key_value_weight,
    query_key_value_bias,
    attention_out_weight,
    attention_out_bias,
    feed_gain,
    feed_shift,
    expand_weight,
    expand_bias,
    contract_weight,
    contract_bias,
):
    seq_count, rows, width = block_input.shape
    members = lax.axis_size("seq")
    pairs = lax.axis_size("mlp")
    parts = members // HEADS
    own = width // members
    me = lax.axis_index("seq").astype(jnp.int32).reshape(1)
    pair_me = lax.axis_index("mlp")
    scalars = jnp.stack([me[0], pair_me.astype(jnp.int32)])
    inputs = block_input.reshape(rows, width)
    cot = out_cotangent.reshape(rows, width)

    outgoing, normed_one, normed_two, table, turned = open_layer(
        inputs,
        cot,
        me * rows,
        (attend_gain, attend_shift, feed_gain, feed_shift),
        query_key_value_weight,
        query_key_value_bias,
        attention_out_weight,
        parts,
    )
    at_head = lax.all_to_all(outgoing, "seq", 0, 0, tiled=True)

    rows_list, cot_list = mlp_list(normed_two), mlp_list(cot)
    turned = mlp_list(turned, 1)
    hidden, grad_pre, grad_hid_bias, *sides = feed(
        rows_list, cot_list, expand_weight, expand_bias, contract_weight
    )
    if pairs == 2:
        came = pair_swap(sides[2])
        feeds, grads = [(sides[0], 0), (came, 0)], [(sides[1], 0), (came, 1)]
    else:
        feeds, grads = (
            [(lax.psum_scatter(v, "mlp", scatter_dimension=0, tiled=True), 0)] for v in sides
        )
    slice_width = expand_weight.shape[1]
    block = min(512, slice_width)

    def runs(arrays, shape, index):
        if pairs == 2:
            return [(a, shape, lambda i, me: index(0, i, me)) for a in arrays]
        return [(arrays[0], shape, lambda i, me, m=m: index(m, i, me)) for m in range(pairs)]

    def sides_of(arrays, part=0):
        return runs(arrays, (width, rows), lambda m, i, me: (part, m))

    def ring_of(products, steps, block, stages):
        stages = ring_stages(stages)
        parts = weight_parts(scalars, products, steps, block, members, stages[0])
        return Ring(scalars, parts, stages)

    x_first, y_first = [(0,), (1,), (2,), (3,)], [(1,), (0,), (2,), (3,)]

    def feed_ring(part, b, stages):
        b_runs = [(b, (rows, block), lambda i, me, m=m: (m, i)) for m in range(pairs)]
        return ring_of([(sides_of(turned, part), b_runs)], slice_width // block, block, stages)

    ring_out = feed_ring(2, hidden, x_first)
    ring_hid = feed_ring(1, grad_pre, y_first)

    query_rows = rows // parts
    part = jnp.stack([me[0] % parts, me[0]]).astype(jnp.int32)
    from_first, head_grad, head_delta, probs, _ = forward_head(
        at_head,
        part,
        rows,
        query_rows,
        (*ring_out.sent, *ring_hid.sent, *[a for a, _ in (*feeds, *grads)], *turned),
    )
    back_first = lax.all_to_all(from_first, "seq", 0, 0, tiled=True)
    from_second, after_second = backward_head(
        scalars, at_head, head_grad, head_delta, probs, rows, query_rows, ()
    )
    from_second = after(from_second, *ring_out.came, *ring_hid.came)
    back_second = lax.all_to_all(from_second, "seq", 0, 0, tiled=True)
    x_first, y_first = [(0,), (1,), (2, 3)], [(1,), (0,), (2, 3)]
    split = pairs == 2 and parts == 1
    share = width // pairs

    def pieces_of(arrays):
        stacked = jnp.stack([a.reshape(rows, pairs, share) for a in arrays], 2)
        stacked = jnp.transpose(stacked, (1, 0, 2, 3)).reshape(pairs, rows, len(arrays) * share)
        if pairs == 2:
            mine = lax.dynamic_index_in_dim(stacked, pair_me, 0, False)
            return [mine, pair_swap(lax.dynamic_index_in_dim(stacked, 1 - pair_me, 0, False))]
        got = lax.all_to_all(stacked, "mlp", 0, 0, tiled=True)
        return [got.reshape(pairs * rows, len(arrays) * share)]

    if split:

        attended, grad_v, sent, own_a, own_v = regroup_once(
            back_first, None, scalars, (from_second,)
        )
        came = pair_swap(sent)
        for ring in (ring_out, ring_hid):
            ring.hold(sent)
            ring.step()
        v_parts, d_parts, _ = weight_once(
            scalars,
            [*turned, own_v, came, own_a, *cot_list],
            [
                ([((0, 1), (rows_run(2, 0, share), rows_run(3, width, share)), True)], (0,)),
                (
                    [((4, 3), (columns_run(5, share, None), columns_run(6, share, None)), False)],
                    (1,),
                ),
            ],
            width,
            share,
            members,
            (),
        )
        grad_q, grad_k, sent, own_qk = regroup_once(
            back_second, table, scalars, (*v_parts, *d_parts)
        )
        came = pair_swap(sent)
        qv_parts, kd_parts, weighed = weight_once(
            scalars,
            [*turned, own_qk, came, *v_parts, *d_parts],
            [
                (
                    [
                        ((0, 1), (columns_run(2, share, n), columns_run(3, share, n)), False),
                        (4 + 2 * n, 5 + 2 * n),
                    ],
                    (n,),
                )
                for n in range(2)
            ],
            width,
            share,
            members,
            (),
        )
        ring_qv = Ring(scalars, qv_parts, x_first)
        ring_kd = Ring(scalars, kd_parts, y_first)
    else:
        for ring in (ring_out, ring_hid):
            ring.step()
        attended, grad_v, att_t = regroup(back_first, None, scalars, rows, query_rows, False)
        att_t = mlp_list(att_t, 1)
        grad_q, grad_k = regroup(back_second, table, scalars, rows, query_rows, False)
        pieces = [pieces_of([g]) for g in (grad_q, grad_v, grad_k)]
        q_runs, v_runs, k_runs = (
            runs(p, (rows, share), lambda m, i, me: (m, 0)) for p in pieces
        )
        cot_runs = runs(cot_list, (rows, share), lambda m, i, me: (m, me[1]))
        one = sides_of(turned)
        ring_qv = ring_of([(one, q_runs), (one, v_runs)], 2, share, x_first)
        ring_kd = ring_of([(one, k_runs), (sides_of(att_t), cot_runs)], 2, share, y_first)

    ring_out.hold(*ring_kd.sent)
    ring_out.step(ring_hid)
    block_output, grad_input, vec, gm_bias, closed = close_layer(
        inputs,
        cot,
        (attend_gain, feed_gain, attention_out_bias, contract_bias),
        (grad_q, grad_k, grad_v),
        attended,
        query_key_value_weight,
        attention_out_weight,
        feeds,
        grads,
        scalars,
        ring_out.sent,
    )
    for ring in (ring_qv, ring_kd):
        ring.pass_on(closed[0])
    ring_out.came = [after(x, *ring_qv.sent, *ring_kd.sent) for x in ring_out.came]
    ring_out.pass_on(closed[0])

    bias_full = lax.dynamic_update_slice_in_dim(
        jnp.zeros((pairs * slice_width,), F32), grad_hid_bias[0], pair_me * slice_width, 0
    )
    vectors = [*[vec[r] for r in range(5)], gm_bias.reshape(-1), bias_full]
    packed = jnp.concatenate([v.reshape(members, pairs, -1) for v in vectors], -1)
    if pairs == 2:
        mine = lax.dynamic_index_in_dim(packed, pair_me, 1, False)
        other = lax.dynamic_index_in_dim(packed, 1 - pair_me, 1, False)
        packed = mine + pair_swap(after(other, *ring_out.sent))
    else:
        packed = lax.psum_scatter(packed, "mlp", scatter_dimension=1, tiled=False)
    ring_qv.step(ring_kd)
    packed = after(packed, *ring_qv.sent)
    packed = jnp.sum(lax.all_to_all(packed, "seq", 0, 0, tiled=True), 0)
    outs, start = [], 0
    for v in vectors:
        size = v.shape[0] // (members * pairs)
        outs.append(lax.slice_in_dim(packed, start, start + size))
        start += size
    grad_gain_one, grad_shift_one, grad_dense_bias, grad_gain_two, grad_shift_two = outs[:5]
    grad_merged_bias, out_hid_bias = outs[5:]

    feed_total = ring_out.plain_total()
    out_weight = jnp.transpose(feed_total[:, :slice_width])
    hid_weight = feed_total[:, slice_width:]

    if pairs == 2:
        mine, other = ring_qv.total()
        merged, dense = vmem_call(
            place_kernel,
            [shape_of((own // pairs, 3 * width), F32), shape_of((own // pairs, width), F32)],
            scalars,
            [mine, pair_swap(other)],
            "place",
        )
    else:
        got = ring_qv.total([4 * share])[0].reshape(pairs, own // pairs, 4 * share)
        got = lax.all_to_all(got, "mlp", 0, 0, tiled=True)
        got = jnp.transpose(got.reshape(pairs, own // pairs, 4, share), (1, 2, 0, 3))
        merged = jnp.concatenate([got[:, n].reshape(-1, width) for n in (0, 2, 1)], -1)
        dense = got[:, 3].reshape(-1, width)
    return (
        block_output.reshape(seq_count, rows, width),
        grad_input.reshape(seq_count, rows, width),
        grad_gain_one,
        grad_shift_one,
        merged,
        grad_merged_bias,
        dense,
        grad_dense_bias,
        grad_gain_two,
        grad_shift_two,
        hid_weight,
        out_hid_bias,
        out_weight,
        grad_dense_bias,
    )


def solution(mesh):
    in_specs = (
        P("mlp", "seq", None),
        P("mlp", "seq", None),
        P(),
        P(),
        P(),
        P(),
        P(),
        P(),
        P(),
        P(),
        P(None, "mlp"),
        P("mlp"),
        P("mlp", None),
        P(),
    )
    out_specs = (
        P("mlp", "seq", None),
        P("mlp", "seq", None),
        P(("seq", "mlp")),
        P(("seq", "mlp")),
        P(("seq", "mlp"), None),
        P(("seq", "mlp")),
        P(("seq", "mlp"), None),
        P(("seq", "mlp")),
        P(("seq", "mlp")),
        P(("seq", "mlp")),
        P("seq", "mlp"),
        P(("seq", "mlp")),
        P("mlp", "seq"),
        P(("seq", "mlp")),
    )
    return jax.shard_map(
        per_device, mesh=mesh, in_specs=in_specs, out_specs=out_specs, check_vma=False
    )
```

```python
from functools import partial

import jax
import jax.numpy as jnp
from jax import lax
from jax.experimental import pallas as pl
from jax.experimental.pallas import tpu as pltpu
from jax.sharding import PartitionSpec as P

HEADS = 16
HEAD = 64
ROT = 16
PAIR = 2 * HEAD
EPS = 1e-05
NEGATIVE = -1e30

F32 = jnp.float32
BF16 = jnp.bfloat16
NT = (((1,), (1,)), ((), ()))
NN = (((1,), (0,)), ((), ()))
VMEM_LIMIT = 60 * 1024 * 1024
COST_SHARE = 16


def dot32(a, b, dims=NN):
    return lax.dot_general(a, b, dims, preferred_element_type=F32)


def cost(flops, bytes_accessed, transcendentals, share=COST_SHARE):
    return pl.CostEstimate(
        flops=flops // share,
        bytes_accessed=bytes_accessed // share,
        transcendentals=transcendentals // share,
    )


def shape_of(shape, dtype):
    return jax.ShapeDtypeStruct(shape, dtype)


def fixed(shape):
    return pl.BlockSpec(shape, lambda *i: (0,) * len(shape))


def vector_row(ref):
    return ref[...].astype(F32).reshape(1, -1)


def two_heads(pair_a, pair_b, low):
    even = jnp.where(low, pair_a, pltpu.roll(pair_b, HEAD, 1))
    odd = jnp.where(low, pltpu.roll(pair_a, HEAD, 1), pair_b)
    return (even, odd)


def rotary_lanes(first, rows, inverse):
    shape = (rows, PAIR)
    lane = lax.broadcasted_iota(jnp.int32, shape, 1) % HEAD
    position = (lax.broadcasted_iota(jnp.int32, shape, 0) + first).astype(F32)
    angle = position * inverse
    cosine, sine = jnp.cos(angle), jnp.sin(angle)
    zero = jnp.zeros_like(sine)
    return (
        jnp.where(lane < ROT, cosine, 1.0),
        jnp.where(lane < ROT // 2, -sine, zero),
        jnp.where((lane >= ROT // 2) & (lane < ROT), sine, zero),
    )


def rotate_lanes(x, cosine, to_first, to_second):
    ahead = pltpu.roll(x, PAIR - ROT // 2, 1)
    behind = pltpu.roll(x, ROT // 2, 1)
    return x * cosine + ahead * to_first + behind * to_second


def unit_rows(x):
    average = jnp.mean(x, -1, keepdims=True)
    centred = x - average
    spread = jnp.mean(centred * centred, -1, keepdims=True)
    root = lax.rsqrt(spread + EPS)
    return (centred * root, root)


def open_kernel(
    first_ref, x_ref, g_ref, inv_ref, ga_ref, sa_ref, gf_ref, sf_ref, b_ref,
    wq_ref, wk_ref, wv_ref, wo_ref,
    out_ref, n1_ref, n2_ref, table_ref, one_ref, turned_ref, bias_ref, *, parts,
):
    rows, width = x_ref.shape
    step = pl.program_id(0)
    cols = wq_ref.shape[1]

    @pl.when(step == 0)
    def _():
        unit, root = unit_rows(x_ref[...].astype(F32))
        n1_ref[...] = (unit * vector_row(ga_ref) + vector_row(sa_ref)).astype(BF16)
        n2_ref[...] = (unit * vector_row(gf_ref) + vector_row(sf_ref)).astype(BF16)
        for t, table in enumerate(rotary_lanes(first_ref[0], rows, inv_ref[...])):
            table_ref[t] = table
        bias_ref[...] = vector_row(b_ref)

    for n, (source, target) in enumerate(
        (
            (n1_ref, one_ref),
            (n2_ref, turned_ref.at[:width]),
            (g_ref, turned_ref.at[width:]),
        )
    ):

        @pl.when(step == pl.num_programs(0) - 1)
        def _(source=source, target=target):
            target[...] = jnp.transpose(source[...])

    def bias(third):
        return bias_ref[:, pl.ds(pl.multiple_of(third * width + step * cols, cols), cols)]

    normed = n1_ref[...]
    query = dot32(normed, wq_ref[...]) + bias(0)
    key = dot32(normed, wk_ref[...]) + bias(1)
    value = dot32(normed, wv_ref[...]) + bias(2)
    grad = dot32(g_ref[...], wo_ref[...], NT)
    tables = (table_ref[0], table_ref[1], table_ref[2])
    low = lax.broadcasted_iota(jnp.int32, (rows, PAIR), 1) < HEAD
    query_rows = rows // parts
    for c in range(cols // PAIR):
        cut = slice(c * PAIR, (c + 1) * PAIR)
        kv = two_heads(rotate_lanes(key[:, cut], *tables), value[:, cut], low)
        qg = two_heads(rotate_lanes(query[:, cut], *tables), grad[:, cut], low)
        for h in range(2):
            kv_h, qg_h = kv[h].astype(BF16), qg[h].astype(BF16)
            for p in range(parts):
                out_ref[2 * c + h, p, :rows] = kv_h
                out_ref[2 * c + h, p, rows:] = qg_h[p * query_rows : (p + 1) * query_rows]


def open_layer(x, g, first, vectors, weight, bias, out_weight, parts):
    rows, width = x.shape
    steps = 2
    cols = width // steps
    per = HEADS // steps
    inverse = 10000.0 ** (-(jnp.arange(ROT // 2, dtype=F32) * 2.0 / ROT))
    inverse = jnp.tile(inverse, PAIR // (ROT // 2)).reshape(1, PAIR)
    chunk = rows + rows // parts

    def third(t):
        return pl.BlockSpec((width, cols), lambda i: (0, t * steps + i))

    out, *others = pl.pallas_call(
        partial(open_kernel, parts=parts),
        grid=(steps,),
        out_shape=(
            shape_of((HEADS, parts, chunk, PAIR), BF16),
            shape_of((rows, width), BF16),
            shape_of((rows, width), BF16),
            shape_of((3, rows, PAIR), F32),
            shape_of((width, rows), BF16),
            shape_of((2 * width, rows), BF16),
        ),
        in_specs=[
            pl.BlockSpec(memory_space=pltpu.SMEM),
            fixed((rows, width)),
            fixed((rows, width)),
            fixed((1, PAIR)),
            *[fixed((width,))] * 4,
            fixed((3 * width,)),
            third(0), third(1), third(2),
            pl.BlockSpec((cols, width), lambda i: (i, 0)),
        ],
        out_specs=(
            pl.BlockSpec((per, parts, chunk, PAIR), lambda i: (i, 0, 0, 0)),
            fixed((rows, width)),
            fixed((rows, width)),
            fixed((3, rows, PAIR)),
            fixed((width, rows)),
            fixed((2 * width, rows)),
        ),
        scratch_shapes=[pltpu.VMEM((1, 3 * width), F32)],
        cost_estimate=cost(
            flops=8 * rows * width * width,
            bytes_accessed=8 * width * width + 18 * rows * width,
            transcendentals=0,
        ),
        compiler_params=pltpu.CompilerParams(vmem_limit_bytes=VMEM_LIMIT),
        name="open_layer",
    )(first, x, g, inverse, *vectors, bias, weight, weight, weight, out_weight)
    return (out.reshape(HEADS * parts, chunk, PAIR), *others)


ROW_GROUP = 4
ONES = 16
CUTS = 4
KEY_GROUP = 2


def first_tile(i):
    return i * (i + 1)


def column_chunks(x):
    return [x[:, c : c + 128] for c in range(0, x.shape[1], 128)]


def forward_kernel(
    part_ref, x_ref, y_ref, g_ref, d_ref, p_hbm, after_ref,
    s_ref, p_ref, dv_ref, vt_ref, mx_ref, top_ref, acc_ref, sem,
    *, key_rows, query_rows,
):
    after_ref[0] = part_ref[1]
    blocks = x_ref.shape[0] // ROW_GROUP
    keys, rows = KEY_GROUP * key_rows, ROW_GROUP * query_rows
    low = lax.broadcasted_iota(jnp.int32, (rows, PAIR), 1) < HEAD
    key_low = lax.broadcasted_iota(jnp.int32, (keys, PAIR), 1) < HEAD
    cuts = [slice(r, r + rows // CUTS) for r in range(0, rows, rows // CUTS)]

    def key_value(j):
        return x_ref[pl.ds(j * KEY_GROUP, KEY_GROUP), :key_rows, :].reshape(keys, PAIR)

    def query_rows_of(i):
        return x_ref[pl.ds(i * ROW_GROUP, ROW_GROUP), key_rows:, :].reshape(rows, PAIR)

    def query_of(i):
        return jnp.where(low, query_rows_of(i).astype(F32) * HEAD**-0.5, 0.0).astype(BF16)

    def copy_out(i, j):
        return pltpu.make_async_copy(p_ref.at[j], p_hbm.at[first_tile(i) + j], sem.at[j])

    def ones_and_values(j, unused):
        turned = jnp.transpose(key_value(j).astype(F32))
        vt_ref[j, :HEAD] = turned[HEAD:].astype(BF16)
        vt_ref[j, HEAD:] = jnp.ones((ONES, keys), BF16)
        return unused

    def raise_max(cut, s):
        mx = mx_ref[cut]
        for chunk in column_chunks(s):
            mx = jnp.maximum(mx, chunk)
        mx_ref[cut] = mx

    def last_scores(i, query):
        row = lax.broadcasted_iota(jnp.int32, (rows, keys), 0)
        col = lax.broadcasted_iota(jnp.int32, (rows, keys), 1)
        row_pos = (row // query_rows) * key_rows + row % query_rows + part_ref[0] * query_rows
        for d in range(ROW_GROUP // KEY_GROUP):
            j = 2 * i + d
            s = dot32(query, key_value(j), NT)
            s = jnp.where(col + d * keys <= row_pos, s, NEGATIVE)
            s_ref[j] = s
            raise_max(slice(None), s)

    def tile(i, j, query, grad_t):
        kv = key_value(j)
        grads = None
        for cut in cuts:
            if grad_t is not None:
                part = dot32(grad_t[:, cut], p_ref[j, cut])
                grads = part if grads is None else grads + part
            top = top_ref[cut]
            p = jnp.concatenate(
                [jnp.exp(c - top) for c in column_chunks(s_ref[j, cut])], 1
            ).astype(BF16)
            p_ref[j, cut] = p
            acc_ref[:, cut] += dot32(vt_ref[j], p, NT)
            if query is not None:
                s = dot32(query[cut], kv, NT)
                s_ref[j, cut] = s
                raise_max(cut, s)
        if grads is not None:
            dv_ref[j, HEAD:] += grads
        copy_out(i, j).start()

    def block(i, grad_t, ahead):
        query = query_of(i + 1) if ahead else None
        top_ref[...] = jnp.broadcast_to(jnp.max(mx_ref[...], -1, keepdims=True), (rows, PAIR))
        mx_ref[...] = jnp.full_like(mx_ref, NEGATIVE)
        acc_ref[...] = jnp.zeros_like(acc_ref)

        def step(j, unused):
            copy_out(i - 1, j).wait()
            tile(i, j, query, grad_t)
            return unused

        lax.fori_loop(0, 2 * i, step, 0)
        for d in range(2):
            tile(i, 2 * i + d, query, None)
        if ahead:
            last_scores(i + 1, query)
        inverse = 1.0 / acc_ref[HEAD : HEAD + 1]
        attended_t = acc_ref[:HEAD] * inverse
        rows_t = jnp.transpose(query_rows_of(i).astype(F32))
        grad_t = (rows_t[HEAD:] * inverse).astype(BF16)
        both = jnp.transpose(jnp.concatenate([attended_t, grad_t.astype(F32)], 0))
        delta = jnp.sum(grad_t.astype(F32) * attended_t, 0, keepdims=True)
        d_ref[i] = jnp.transpose(jnp.broadcast_to(delta, (PAIR, rows)))
        g_ref[i] = jnp.where(low, 0.0, both).astype(BF16)
        here = pl.ds(i * ROW_GROUP, ROW_GROUP)
        y_ref[here, :query_rows, :] = both.astype(BF16).reshape(ROW_GROUP, query_rows, PAIR)
        if query_rows < key_rows:
            y_ref[here, query_rows:, :] = jnp.zeros(
                (ROW_GROUP, key_rows - query_rows, PAIR), BF16
            )
        return grad_t

    dv_ref[...] = jnp.zeros_like(dv_ref)
    lax.fori_loop(0, 2 * blocks, ones_and_values, 0)
    mx_ref[...] = jnp.full_like(mx_ref, NEGATIVE)
    last_scores(0, query_of(0))
    grad_t = lax.fori_loop(
        0, blocks - 1, lambda i, g: block(i, g, True), jnp.zeros((HEAD, rows), BF16)
    )
    grad_t = block(jnp.int32(blocks - 1), grad_t, False)

    def finish(j, unused):
        here = pl.ds(j * KEY_GROUP, KEY_GROUP)
        held = y_ref[here].reshape(keys, PAIR)
        dv_ref[j, HEAD:] += dot32(grad_t, p_ref[j])
        grads = jnp.transpose(dv_ref[j]).astype(BF16)
        y_ref[here] = jnp.where(key_low, held, grads).reshape(KEY_GROUP, key_rows, PAIR)
        copy_out(blocks - 1, j).wait()
        return unused

    lax.fori_loop(0, 2 * blocks, finish, 0)


def backward_kernel(
    me_ref, x_ref, g_ref, d_ref, p_hbm, y_ref, after_ref,
    p_ref, dp0_ref, dp1_ref, dk_ref, acc_ref, sem,
    *, key_rows, query_rows,
):
    after_ref[0] = me_ref[0]
    blocks = x_ref.shape[0] // ROW_GROUP
    keys, rows = KEY_GROUP * key_rows, ROW_GROUP * query_rows
    tiles = first_tile(blocks)
    slots = p_ref.shape[0]
    low = lax.broadcasted_iota(jnp.int32, (rows, PAIR), 1) < HEAD
    dp_refs = (dp0_ref, dp1_ref)

    def copy_in(t):
        return pltpu.make_async_copy(p_hbm.at[t], p_ref.at[t % slots], sem.at[t % slots])

    def refill(t):
        @pl.when(t + slots < tiles)
        def _():
            copy_in(t + slots).start()

    for t in range(min(slots, tiles)):
        copy_in(t).start()
    dk_ref[...] = jnp.zeros_like(dk_ref)

    def key_value(j):
        return x_ref[pl.ds(j * KEY_GROUP, KEY_GROUP), :key_rows, :].reshape(keys, PAIR)

    def one_block(i, unused):
        here = pl.ds(i * ROW_GROUP, ROW_GROUP)
        query = x_ref[here, key_rows:, :].reshape(rows, PAIR).astype(F32) * HEAD**-0.5
        query_t = jnp.transpose(query)[:HEAD].astype(BF16)
        grad = g_ref[i]
        first = first_tile(i)
        acc_ref[...] = jnp.zeros_like(acc_ref)

        def raise_probs(j, side):
            dp_refs[side][...] = dot32(grad, key_value(j), NT)

        def tile(j, side):
            delta = d_ref[i]
            p = column_chunks(p_ref[(first + j) % slots].astype(F32))
            dp = column_chunks(dp_refs[side][...])
            ds = jnp.concatenate([a * (b - delta) for a, b in zip(p, dp)], 1).astype(BF16)
            dk_ref[j, HEAD:] += dot32(query_t, ds)
            acc_ref[...] += dot32(ds, key_value(j))

        def two_tiles(m, unused, more=True):
            j = 2 * m
            copy_in(first + j).wait()
            copy_in(first + j + 1).wait()
            raise_probs(j + 1, 1)
            tile(j, 0)
            if more:
                raise_probs(j + 2, 0)
            tile(j + 1, 1)
            refill(first + j)
            refill(first + j + 1)
            return unused

        raise_probs(0, 0)
        lax.fori_loop(0, i, two_tiles, 0)
        two_tiles(i, 0, False)
        done = jnp.where(low, acc_ref[...] * HEAD**-0.5, 0.0).astype(BF16)
        y_ref[here, :query_rows, :] = done.reshape(ROW_GROUP, query_rows, PAIR)
        if query_rows < key_rows:
            y_ref[here, query_rows:, :] = jnp.zeros(
                (ROW_GROUP, key_rows - query_rows, PAIR), BF16
            )
        return unused

    lax.fori_loop(0, blocks, one_block, 0)
    key_low = lax.broadcasted_iota(jnp.int32, (keys, PAIR), 1) < HEAD

    def finish(j, unused):
        here = pl.ds(j * KEY_GROUP, KEY_GROUP)
        held = y_ref[here].reshape(keys, PAIR)
        grads = jnp.transpose(dk_ref[j]).astype(BF16)
        y_ref[here] = jnp.where(key_low, held, grads).reshape(KEY_GROUP, key_rows, PAIR)
        return unused

    lax.fori_loop(0, 2 * blocks, finish, 0)


def head_sizes(x, key_rows, query_rows):
    count = x.shape[0]
    blocks = count // ROW_GROUP
    return count, blocks, KEY_GROUP * key_rows, ROW_GROUP * query_rows


def forward_head(x, part, key_rows, query_rows, behind):
    count, blocks, keys, rows = head_sizes(x, key_rows, query_rows)
    tiles = first_tile(blocks)
    vmem = pl.BlockSpec(memory_space=pltpu.VMEM)
    return pl.pallas_call(
        without(
            partial(forward_kernel, key_rows=key_rows, query_rows=query_rows), 2, len(behind)
        ),
        out_shape=(
            shape_of((count, key_rows, PAIR), BF16),
            shape_of((blocks, rows, PAIR), BF16),
            shape_of((blocks, rows, PAIR), F32),
            shape_of((tiles, rows, keys), BF16),
            shape_of((1,), jnp.int32),
        ),
        in_specs=[pl.BlockSpec(memory_space=pltpu.SMEM), vmem]
        + [pl.BlockSpec(memory_space=pl.ANY)] * len(behind),
        out_specs=(
            vmem, vmem, vmem, pl.BlockSpec(memory_space=pl.ANY),
            pl.BlockSpec(memory_space=pltpu.SMEM),
        ),
        scratch_shapes=[
            pltpu.VMEM((2 * blocks, rows, keys), F32),
            pltpu.VMEM((2 * blocks, rows, keys), BF16),
            pltpu.VMEM((2 * blocks, PAIR, keys), F32),
            pltpu.VMEM((2 * blocks, HEAD + ONES, keys), BF16),
            pltpu.VMEM((rows, PAIR), F32),
            pltpu.VMEM((rows, PAIR), F32),
            pltpu.VMEM((HEAD + ONES, rows), F32),
            pltpu.SemaphoreType.DMA((2 * blocks,)),
        ],
        cost_estimate=cost(
            flops=tiles * rows * keys * 2 * 256 * 3,
            bytes_accessed=4 * x.size + 2 * tiles * rows * keys,
            transcendentals=tiles * rows * keys,
            share=1,
        ),
        compiler_params=pltpu.CompilerParams(vmem_limit_bytes=VMEM_LIMIT),
        name="forward_head",
    )(part, x, *behind)


def backward_head(scalars, x, grad, delta, probs, key_rows, query_rows, behind):
    count, blocks, keys, rows = head_sizes(x, key_rows, query_rows)
    tiles = first_tile(blocks)
    slots = 6
    vmem = pl.BlockSpec(memory_space=pltpu.VMEM)
    return pl.pallas_call(
        without(
            partial(backward_kernel, key_rows=key_rows, query_rows=query_rows), 5, len(behind)
        ),
        out_shape=(shape_of((count, key_rows, PAIR), BF16), shape_of((1,), jnp.int32)),
        in_specs=[pl.BlockSpec(memory_space=pltpu.SMEM), vmem, vmem, vmem]
        + [pl.BlockSpec(memory_space=pl.ANY)] * (1 + len(behind)),
        out_specs=(vmem, pl.BlockSpec(memory_space=pltpu.SMEM)),
        scratch_shapes=[
            pltpu.VMEM((slots, rows, keys), BF16),
            pltpu.VMEM((rows, keys), F32),
            pltpu.VMEM((rows, keys), F32),
            pltpu.VMEM((2 * blocks, PAIR, keys), F32),
            pltpu.VMEM((rows, PAIR), F32),
            pltpu.SemaphoreType.DMA((slots,)),
        ],
        cost_estimate=cost(
            flops=tiles * rows * keys * 2 * 256 * 3,
            bytes_accessed=4 * x.size + 2 * tiles * rows * keys,
            transcendentals=0,
            share=1,
        ),
        compiler_params=pltpu.CompilerParams(vmem_limit_bytes=VMEM_LIMIT),
        name="backward_head",
    )(scalars, x, grad, delta, probs, *behind)


def feed_kernel(*refs, count, keep):
    rows_refs, cot_refs = refs[:count], refs[count : 2 * count]
    w1_ref, b1_ref, w2_ref = refs[2 * count : 2 * count + 3]
    hid_ref, gpre_ref, gb_ref = refs[2 * count + 3 : 2 * count + 6]
    outs = refs[2 * count + 6 : -2]
    out_acc, grad_acc = refs[-2:]
    step = pl.program_id(0)

    @pl.when(step == 0)
    def _():
        out_acc[...] = jnp.zeros_like(out_acc)
        grad_acc[...] = jnp.zeros_like(grad_acc)

    bias = b1_ref[...]
    sums = jnp.zeros_like(bias)
    rows = rows_refs[0].shape[0]
    for r in range(count):
        here = slice(r * rows, (r + 1) * rows)
        pre = dot32(rows_refs[r][...], w1_ref[...]) + bias
        grad = dot32(cot_refs[r][...], w2_ref[...], NT)
        cdf = 0.5 + 0.5 * lax.erf(pre * (0.5**0.5))
        density = jnp.exp(-0.5 * pre * pre) * 0.3989422804014327
        hidden = (pre * cdf).astype(BF16)
        grad_pre = (grad * (cdf + pre * density)).astype(BF16)
        hid_ref[here] = hidden
        gpre_ref[here] = grad_pre
        sums = sums + jnp.sum(grad_pre.astype(F32), 0, keepdims=True)
        out_acc[here] += dot32(hidden, w2_ref[...])
        grad_acc[here] += dot32(grad_pre, w1_ref[...], NT)
    gb_ref[...] = sums

    @pl.when(step == pl.num_programs(0) - 1)
    def _():
        if keep:
            own_out, own_grad, other = outs
            own_out[...] = out_acc[:rows]
            own_grad[...] = grad_acc[:rows]
            other[:rows] = out_acc[rows:].astype(BF16)
            other[rows:] = grad_acc[rows:].astype(BF16)
        else:
            outs[0][...] = out_acc[...].astype(BF16)
            outs[1][...] = grad_acc[...].astype(BF16)


def feed(rows_list, cot_list, w1, b1, w2):
    width, hidden = w1.shape
    count = len(rows_list)
    rows = rows_list[0].shape[0]
    total = rows * count
    block = 256
    keep = count > 1
    sides = (
        [(rows, F32), (rows, F32), (total, BF16)]
        if keep
        else [(total, BF16), (total, BF16)]
    )
    once = pl.Buffered(1)
    whole = pl.BlockSpec((rows, width), lambda i: (0, 0), pipeline_mode=once)
    return pl.pallas_call(
        partial(feed_kernel, count=count, keep=keep),
        grid=(hidden // block,),
        out_shape=(
            shape_of((total, hidden), BF16),
            shape_of((total, hidden), BF16),
            shape_of((1, hidden), F32),
            *[shape_of((r, width), d) for r, d in sides],
        ),
        in_specs=[
            *[whole] * (2 * count),
            pl.BlockSpec((width, block), lambda i: (0, i)),
            pl.BlockSpec((1, block), lambda i: (0, i)),
            pl.BlockSpec((block, width), lambda i: (i, 0)),
        ],
        out_specs=(
            pl.BlockSpec((total, block), lambda i: (0, i)),
            pl.BlockSpec((total, block), lambda i: (0, i)),
            pl.BlockSpec((1, block), lambda i: (0, i)),
            *[
                pl.BlockSpec((r, width), lambda i: (0, 0), pipeline_mode=once) for r, d in sides
            ],
        ),
        scratch_shapes=[pltpu.VMEM((total, width), F32), pltpu.VMEM((total, width), F32)],
        cost_estimate=cost(
            flops=8 * total * width * hidden,
            bytes_accessed=4 * width * hidden + 4 * total * hidden,
            transcendentals=2 * total * hidden,
        ),
        compiler_params=pltpu.CompilerParams(vmem_limit_bytes=VMEM_LIMIT),
        name="feed",
    )(*rows_list, *cot_list, w1, b1.astype(F32).reshape(1, hidden), w2)


def insert_bits(k, positions, values):
    for position, value in zip(positions, values):
        k = ((k >> position) << (position + 1)) + (value << position) + (k & ((1 << position) - 1))
    return k


def part_chunk(k, p, me, ring_bits, positions):
    values = [((me >> bit) & 1) ^ ((p >> n) & 1) for n, bit in enumerate(ring_bits)]
    return insert_bits(k, positions, values)


def weight_kernel(me_ref, *refs, bits, counts):
    total = sum(counts)
    a_refs, b_refs, parts = refs[:total], refs[total : 2 * total], refs[2 * total :]

    def product(first, count):
        b = jnp.concatenate([r[...] for r in b_refs[first : first + count]], 0)
        for p, ref in enumerate(parts):
            chunks, rows, cols = ref.shape
            a = []
            for k in range(chunks):
                start = part_chunk(k, p, me_ref[0], bits, bits) * rows
                here = pl.ds(pl.multiple_of(start, rows), rows)
                a.append(
                    jnp.concatenate([r[here, :] for r in a_refs[first : first + count]], 1)
                )
            ref[...] = dot32(jnp.concatenate(a, 0), b).astype(BF16).reshape(ref.shape)

    if len(counts) == 1:
        product(0, total)
    else:
        for n, count in enumerate(counts):
            pl.when(pl.program_id(0) == n)(partial(product, sum(counts[:n]), count))


def weight_parts(scalars, products, steps, block, members, bits):
    a_runs = [run for a, _ in products for run in a]
    b_runs = [run for _, b in products for run in b]
    width = a_runs[0][1][0]
    rows = width // members
    tokens = sum(shape[1] for _, shape, _ in products[0][0])
    count = 1 << len(bits)
    each = (members // count, rows, steps * block)
    out = pl.BlockSpec((members // count, rows, block), lambda i, me: (0, 0, i))
    return pl.pallas_call(
        partial(weight_kernel, bits=bits, counts=[len(a) for a, _ in products]),
        grid_spec=pltpu.PrefetchScalarGridSpec(
            num_scalar_prefetch=1,
            grid=(steps,),
            in_specs=[pl.BlockSpec(shape, index) for _, shape, index in (*a_runs, *b_runs)],
            out_specs=[out] * count,
        ),
        out_shape=[shape_of(each, BF16)] * count,
        cost_estimate=cost(
            flops=2 * width * tokens * steps * block,
            bytes_accessed=2 * width * tokens + 2 * (width + tokens) * steps * block,
            transcendentals=0,
        ),
        compiler_params=pltpu.CompilerParams(vmem_limit_bytes=VMEM_LIMIT),
        name="weight_parts",
    )(scalars, *[array for array, _, _ in (*a_runs, *b_runs)])


def weight_once_kernel(me_ref, *refs, products, operands):
    arrays, outs = refs[:operands], refs[operands:-1]
    for n in range(2):
        refs[-1][n] = me_ref[n]
    at = 0
    for blocks, bits in products:
        parts = outs[at : at + (1 << len(bits))]
        at += len(parts)
        cols = parts[0].shape[2] // len(blocks)
        for n, block in enumerate(blocks):
            here = slice(n * cols, (n + 1) * cols)
            if len(block) == len(parts):
                for ref, source in zip(parts, block):
                    ref[:, :, here] = arrays[source][...]
                continue
            a_runs, b_runs, turned = block
            b = jnp.concatenate([run(arrays, me_ref) for run in b_runs], 1 if turned else 0)
            for p, ref in enumerate(parts):
                chunks, rows, _ = ref.shape
                a = []
                for k in range(chunks):
                    start = part_chunk(k, p, me_ref[0], bits, bits) * rows
                    lines = pl.ds(pl.multiple_of(start, rows), rows)
                    a.append(jnp.concatenate([arrays[m][lines, :] for m in a_runs], 1))
                product = dot32(jnp.concatenate(a, 0), b, NT if turned else NN)
                ref[:, :, here] = product.astype(BF16).reshape(chunks, rows, cols)


def rows_run(n, first, count):
    return lambda arrays, me_ref: arrays[n][first : first + count, :]


def columns_run(n, cols, block):
    if block is not None:
        return lambda arrays, me_ref: arrays[n][:, block * cols : (block + 1) * cols]
    return lambda arrays, me_ref: arrays[n][:, pl.ds(pl.multiple_of(me_ref[1] * cols, cols), cols)]


def weight_once(scalars, arrays, products, width, cols, members, behind):
    each = [
        shape_of((members >> len(bits), width // members, cols * len(blocks)), BF16)
        for blocks, bits in products
        for _ in range(1 << len(bits))
    ]
    outs = vmem_call(
        partial(weight_once_kernel, products=products, operands=len(arrays)),
        each + [shape_of((2,), jnp.int32)],
        scalars,
        arrays,
        "weight_once",
        behind,
    )
    return outs[:2], outs[2:4], outs[4]


def column_sums(refs, counts):
    groups, start = [], 0
    for count in counts:
        groups.append(refs[start : start + count])
        start += count

    def total(group, c):
        value = group[0][c].astype(F32)
        for ref in group[1:]:
            value = value + ref[c].astype(F32)
        return value

    return [partial(total, group) for group in groups]


def add_kernel(me_ref, *refs, counts, bits, positions):
    ins, outs = refs[: sum(counts)], refs[sum(counts) :]
    at = 0
    for group, total in zip(counts, column_sums(ins, counts)):
        cols = ins[0].shape[2]
        for p, ref in enumerate(outs):
            for k in range(ref.shape[0]):
                c = part_chunk(k, p, me_ref[0], bits, positions)
                ref[k, :, at : at + cols] = total(c).astype(BF16)
        at += cols
        ins = ins[group:]


def last_kernel(me_ref, *refs, count, form):
    value = column_sums(refs[:count], [count])[0](0)
    outs = refs[count:]
    if form == "pair":
        half = value.shape[0] // 2
        first = me_ref[1] == 0
        outs[0][...] = jnp.where(first, value[:half], value[half:])
        outs[1][...] = jnp.where(first, value[half:], value[:half]).astype(BF16)
    else:
        at = 0
        for ref in outs:
            ref[...] = value[:, at : at + ref.shape[1]]
            at += ref.shape[1]


def without(kernel, first, count):
    if not count:
        return kernel
    return lambda *refs: kernel(*refs[:first], *refs[first + count :])


def vmem_call(kernel, out_shape, scalars, arrays, name, behind=()):
    vmem = pl.BlockSpec(memory_space=pltpu.VMEM)
    size = sum(a.size for a in arrays)
    return pl.pallas_call(
        without(kernel, 1 + len(arrays), len(behind)),
        in_specs=[pl.BlockSpec(memory_space=pltpu.SMEM)]
        + [vmem] * len(arrays)
        + [pl.BlockSpec(memory_space=pl.ANY)] * len(behind),
        out_specs=[
            pl.BlockSpec(memory_space=pltpu.SMEM) if o.dtype == jnp.int32 else vmem
            for o in out_shape
        ],
        out_shape=out_shape,
        cost_estimate=cost(flops=size, bytes_accessed=3 * size, transcendentals=0),
        compiler_params=pltpu.CompilerParams(vmem_limit_bytes=VMEM_LIMIT),
        name=name,
    )(scalars, *arrays, *behind)


def seq_move(x, mask):
    members = lax.axis_size("seq")
    return lax.ppermute(x, "seq", [(s, s ^ mask) for s in range(members)])


def ring_stages(stages):
    bits = lax.axis_size("seq").bit_length() - 1
    named = [b for stage in stages for b in stage]
    stages = [tuple(b for b in stage if b < bits) for stage in stages]
    stages[-1] = stages[-1] + tuple(b for b in range(bits) if b not in named)
    return [stage for stage in stages if stage]


class Ring:
    def __init__(self, scalars, parts, stages):
        self.scalars, self.stages, self.behind = scalars, list(stages), ()
        self.me = scalars[0]
        self.left = sorted(b for stage in stages for b in stage)
        self.travel(parts)

    def travel(self, parts):
        stage = self.stages.pop(0)
        self.left = [b for b in self.left if b not in stage]
        self.keep, self.sent = parts[0], parts[1:]
        self.came = [
            seq_move(part, sum(1 << b for n, b in enumerate(stage) if (p >> n) & 1))
            for p, part in enumerate(parts)
            if p
        ]

    def hold(self, *others):
        self.behind = others

    def step(self, *others):
        stage = self.stages[0]
        positions = [self.left.index(b) for b in stage]
        rings = (self, *others)
        chunks, rows = self.keep.shape[:2]
        cols = sum(ring.keep.shape[2] for ring in rings)
        count = 1 << len(stage)
        arrays = [[ring.keep, *ring.came] for ring in rings]
        self.travel(
            vmem_call(
                partial(
                    add_kernel, counts=[len(a) for a in arrays], bits=stage, positions=positions
                ),
                [shape_of((chunks // count, rows, cols), BF16)] * count,
                self.scalars,
                [a for group in arrays for a in group],
                "add_parts",
                self.behind,
            )
        )
        self.behind = ()

    def pass_on(self, me):
        stage = self.stages[0]
        bits = self.left
        shape = self.keep.shape[1:]
        arrays = [a.reshape((2,) * len(bits) + shape) for a in (self.keep, *self.came)]
        parts = []
        for p in range(1 << len(stage)):
            total = None
            for a in arrays:
                for n, bit in reversed(list(enumerate(stage))):
                    axis = len(bits) - 1 - bits.index(bit)
                    index = ((me >> bit) & 1) ^ ((p >> n) & 1)
                    a = lax.dynamic_index_in_dim(a, index, axis, True)
                a = a.reshape((-1,) + shape).astype(F32)
                total = a if total is None else total + a
            parts.append(total.astype(BF16))
        self.travel(parts)

    def plain_total(self):
        return sum(a[0].astype(F32) for a in (self.keep, *self.came))

    def total(self, widths=None):
        while self.stages:
            self.step()
        rows, cols = self.keep.shape[1:]
        shapes = (
            [shape_of((rows, w), F32) for w in widths]
            if widths
            else [shape_of((rows // 2, cols), F32), shape_of((rows // 2, cols), BF16)]
        )
        arrays = [self.keep, *self.came]
        return vmem_call(
            partial(last_kernel, count=len(arrays), form="rows" if widths else "pair"),
            shapes,
            self.scalars,
            arrays,
            "last_sum",
        )


def regroup_kernel(me_ref, back_ref, *refs, key_rows, query_rows, turned):
    heads, parts = back_ref.shape[:2]
    low = lax.broadcasted_iota(jnp.int32, (key_rows, PAIR), 1) < HEAD
    if turned:
        one_ref, two_ref, one_t_ref, *sides = refs
    else:
        table_ref, one_ref, two_ref, *sides = refs
        tables = (table_ref[0], -table_ref[1], -table_ref[2])
    first = pl.program_id(0) == 0
    for t in range(heads // 2):
        pair = []
        for h in (2 * t, 2 * t + 1):
            if parts == 1:
                pair.append(back_ref[h, 0].astype(F32))
                continue
            keys = sum(back_ref[h, p].astype(F32) for p in range(parts))
            queries = jnp.concatenate(
                [back_ref[h, p, :query_rows].astype(F32) for p in range(parts)], 0
            )
            pair.append(jnp.where(low, queries, keys))
        one, two = two_heads(pair[0], pair[1], low)
        if not turned:
            one, two = rotate_lanes(one, *tables), rotate_lanes(two, *tables)
        one, two = one.astype(BF16), two.astype(BF16)
        here = slice(t * PAIR, (t + 1) * PAIR)
        one_ref[:, here] = one
        two_ref[:, here] = two
        if turned:
            one_t_ref[here] = jnp.transpose(one)
        if sides:
            half = one_ref.shape[1]
            for n, value in enumerate((two,) if turned else (one, two)):
                there = slice(n * half + t * PAIR, n * half + (t + 1) * PAIR)
                pl.when(first)(partial(sides[1].__setitem__, (slice(None), there), value))
                pl.when(~first)(partial(sides[0].__setitem__, (slice(None), there), value))


def regroup(back, table, scalars, rows, query_rows, split):
    turned = table is None
    chunk = back.shape[1]
    parts = back.shape[0] // HEADS
    half = HEADS * HEAD // 2
    full = shape_of((rows, 2 * half), BF16)

    def side(i, me):
        return (i + me[1] + 1) % 2 if split else i

    whole = pl.BlockSpec((rows, half), lambda i, me: (0, side(i, me)))
    tall = pl.BlockSpec((half, rows), lambda i, me: (side(i, me), 0))
    cols = half * (1 if turned else 2)
    own = pl.BlockSpec((rows, cols), lambda i, me: (0, 0))
    return pl.pallas_call(
        partial(regroup_kernel, key_rows=rows, query_rows=query_rows, turned=turned),
        grid_spec=pltpu.PrefetchScalarGridSpec(
            num_scalar_prefetch=1,
            grid=(2,),
            in_specs=[
                pl.BlockSpec(
                    (HEADS // 2, parts, chunk, PAIR), lambda i, me: (side(i, me), 0, 0, 0)
                )
            ]
            + ([] if turned else [pl.BlockSpec(table.shape, lambda i, me: (0, 0, 0))]),
            out_specs=[whole, whole] + ([tall] if turned else []) + ([own, own] if split else []),
        ),
        out_shape=[full, full]
        + ([shape_of((2 * half, rows), BF16)] if turned else [])
        + ([shape_of((rows, cols), BF16)] * 2 if split else []),
        cost_estimate=cost(
            flops=back.size, bytes_accessed=4 * back.size, transcendentals=0
        ),
        name="regroup",
    )(
        scalars,
        back.reshape(HEADS, parts, chunk, PAIR),
        *([] if turned else [table]),
    )


def regroup_once_kernel(me_ref, *refs, turned):
    if turned:
        back_ref, att_ref, v_ref, send_ref, own_a_ref, own_v_ref = refs
    else:
        back_ref, table_ref, q_ref, k_ref, send_ref, own_ref = refs
        tables = (table_ref[0], -table_ref[1], -table_ref[2])
    heads, rows = back_ref.shape[:2]
    half = heads // 2
    low = lax.broadcasted_iota(jnp.int32, (rows, PAIR), 1) < HEAD
    for side in range(2):
        first = ((me_ref[1] + side) % 2) * half
        for t in range(half // 2):
            pair = [back_ref[first + 2 * t + n].astype(F32) for n in range(2)]
            one, two = two_heads(pair[0], pair[1], low)
            if not turned:
                one, two = rotate_lanes(one, *tables), rotate_lanes(two, *tables)
            one, two = one.astype(BF16), two.astype(BF16)
            start = pl.multiple_of((first // 2 + t) * PAIR, PAIR)
            here = pl.ds(start, PAIR)
            local = slice(t * PAIR, (t + 1) * PAIR)
            width = half * HEAD
            if turned:
                att_ref[:, here] = one
                v_ref[:, here] = two
                turned_one, turned_two = jnp.transpose(one), jnp.transpose(two)
                own_a_ref[here] = turned_one
                send_ref[here] = turned_one
                if side == 0:
                    own_v_ref[local] = turned_two
                else:
                    send_ref[2 * width + t * PAIR : 2 * width + (t + 1) * PAIR] = turned_two
            else:
                q_ref[:, here] = one
                k_ref[:, here] = two
                ref = own_ref if side == 0 else send_ref
                ref[:, local] = one
                ref[:, width + t * PAIR : width + (t + 1) * PAIR] = two


def regroup_once(back, table, scalars, behind=()):
    rows = back.shape[1]
    full = shape_of((rows, HEADS * HEAD), BF16)
    half = HEADS * HEAD // 2
    if table is None:
        sides = [
            shape_of((3 * half, rows), BF16),
            shape_of((2 * half, rows), BF16),
            shape_of((half, rows), BF16),
        ]
    else:
        sides = [shape_of((rows, 2 * half), BF16)] * 2
    return vmem_call(
        partial(regroup_once_kernel, turned=table is None),
        [full, full, *sides],
        scalars,
        [back] if table is None else [back, table],
        "regroup_once",
        behind,
    )


def close_kernel(
    x_ref, g_ref, ga_ref, gf_ref, bo_ref, bc_ref, gq_ref, gk_ref, gv_ref, att_ref,
    wq_ref, wk_ref, wv_ref, wo_ref, me_ref, *refs, sides,
):
    feeds, grads = refs[:sides], refs[sides : 2 * sides]
    out_ref, gin_ref, vec_ref, gb_ref, after_ref, out_acc, grad_acc = refs[2 * sides :]
    step = pl.program_id(0)
    for n in range(2):
        after_ref[n] = me_ref[n]

    @pl.when(step == 0)
    def _():
        out_acc[...] = jnp.zeros_like(out_acc)
        grad_acc[...] = jnp.zeros_like(grad_acc)

    out_acc[...] += dot32(att_ref[...], wo_ref[...])
    total = None
    for third, (g_third, w_ref) in enumerate(
        ((gq_ref, wq_ref), (gk_ref, wk_ref), (gv_ref, wv_ref))
    ):
        grad = g_third[...]
        part = dot32(grad, w_ref[...], NT)
        total = part if total is None else total + part
        gb_ref[third : third + 1] = jnp.sum(grad.astype(F32), 0, keepdims=True)
    grad_acc[...] += total

    @pl.when(step == pl.num_programs(0) - 1)
    def _():
        x = x_ref[...].astype(F32)
        g = g_ref[...].astype(F32)
        total = x + out_acc[...] + vector_row(bo_ref) + vector_row(bc_ref)
        for ref in feeds:
            total = total + ref[...].astype(F32)
        out_ref[...] = total.astype(BF16)
        unit, root = unit_rows(x)
        one = grad_acc[...]
        two = grads[0][...].astype(F32)
        for ref in grads[1:]:
            two = two + ref[...].astype(F32)
        down = one * vector_row(ga_ref) + two * vector_row(gf_ref)
        mean = jnp.mean(down, -1, keepdims=True)
        slope = jnp.mean(down * unit, -1, keepdims=True)
        gin_ref[...] = g + root * (down - mean - unit * slope)
        for r, rows in enumerate((one * unit, one, g, two * unit, two)):
            vec_ref[r : r + 1] = jnp.sum(rows, 0, keepdims=True)


def close_layer(x, g, vectors, gm, attended, weight, out_weight, feeds, grads, scalars, behind):
    rows, width = x.shape
    steps = 4
    cols = width // steps

    def third(t):
        return pl.BlockSpec((width, cols), lambda i: (0, t * steps + i))

    part = pl.BlockSpec((rows, cols), lambda i: (0, i))
    return pl.pallas_call(
        without(partial(close_kernel, sides=len(feeds)), 15 + 2 * len(feeds), len(behind)),
        grid=(steps,),
        out_shape=(
            shape_of((rows, width), BF16),
            shape_of((rows, width), F32),
            shape_of((5, width), F32),
            shape_of((3, width), F32),
            shape_of((2,), jnp.int32),
        ),
        in_specs=[
            fixed((rows, width)),
            fixed((rows, width)),
            *[fixed((width,))] * 4,
            part, part, part, part,
            third(0), third(1), third(2),
            pl.BlockSpec((cols, width), lambda i: (i, 0)),
            pl.BlockSpec(memory_space=pltpu.SMEM),
            *[
                pl.BlockSpec((rows, width), lambda i, n=n: (n, 0)) for _, n in (*feeds, *grads)
            ],
            *[pl.BlockSpec(memory_space=pl.ANY)] * len(behind),
        ],
        out_specs=(
            fixed((rows, width)),
            fixed((rows, width)),
            fixed((5, width)),
            pl.BlockSpec((3, cols), lambda i: (0, i)),
            pl.BlockSpec(memory_space=pltpu.SMEM),
        ),
        scratch_shapes=[pltpu.VMEM((rows, width), F32), pltpu.VMEM((rows, width), F32)],
        cost_estimate=cost(
            flops=8 * rows * width * width,
            bytes_accessed=8 * width * width + 24 * rows * width,
            transcendentals=0,
        ),
        compiler_params=pltpu.CompilerParams(vmem_limit_bytes=VMEM_LIMIT),
        name="close_layer",
    )(x, g, *vectors, *gm, attended, weight, weight, weight, out_weight, scalars, *[a for a, _ in (*feeds, *grads)], *behind)


def place_kernel(me_ref, own_ref, came_ref, merged_ref, dense_ref):
    half = dense_ref.shape[1] // 2
    for side, ref in enumerate((own_ref, came_ref)):
        at = ((me_ref[1] + side) % 2) * half
        for third, block in enumerate((0, 2, 1)):
            start = pl.multiple_of(third * 2 * half + at, half)
            value = ref[:, block * half : (block + 1) * half]
            merged_ref[:, pl.ds(start, half)] = value.astype(F32)
        dense_ref[:, pl.ds(pl.multiple_of(at, half), half)] = ref[:, 3 * half :].astype(F32)


def pair_swap(x):
    return lax.ppermute(x, "mlp", [(0, 1), (1, 0)])


def mlp_list(x, axis=0):
    if lax.axis_size("mlp") == 2:
        return [x, pair_swap(x)]
    return [lax.all_gather(x, "mlp", axis=axis, tiled=True)]


def after(value, *others):
    return lax.optimization_barrier((value, *others))[0]


def per_device(
    block_input,
    out_cotangent,
    attend_gain,
    attend_shift,
    query_key_value_weight,
    query_key_value_bias,
    attention_out_weight,
    attention_out_bias,
    feed_gain,
    feed_shift,
    expand_weight,
    expand_bias,
    contract_weight,
    contract_bias,
):
    seq_count, rows, width = block_input.shape
    members = lax.axis_size("seq")
    pairs = lax.axis_size("mlp")
    parts = members // HEADS
    own = width // members
    me = lax.axis_index("seq").astype(jnp.int32).reshape(1)
    pair_me = lax.axis_index("mlp")
    scalars = jnp.stack([me[0], pair_me.astype(jnp.int32)])
    inputs = block_input.reshape(rows, width)
    cot = out_cotangent.reshape(rows, width)

    outgoing, _, normed_two, table, one_t, turned = open_layer(
        inputs,
        cot,
        me * rows,
        (attend_gain, attend_shift, feed_gain, feed_shift),
        query_key_value_weight,
        query_key_value_bias,
        attention_out_weight,
        parts,
    )
    at_head = lax.all_to_all(outgoing, "seq", 0, 0, tiled=True)

    rows_list, cot_list = mlp_list(normed_two), mlp_list(cot)
    turned = mlp_list(turned, 1)
    one_t = mlp_list(one_t, 1)
    hidden, grad_pre, grad_hid_bias, *sides = feed(
        rows_list, cot_list, expand_weight, expand_bias, contract_weight
    )
    if pairs == 2:
        came = pair_swap(sides[2])
        feeds, grads = [(sides[0], 0), (came, 0)], [(sides[1], 0), (came, 1)]
    else:
        feeds, grads = (
            [(lax.psum_scatter(v, "mlp", scatter_dimension=0, tiled=True), 0)] for v in sides
        )
    slice_width = expand_weight.shape[1]
    block = min(512, slice_width)

    def runs(arrays, shape, index):
        if pairs == 2:
            return [(a, shape, lambda i, me: index(0, i, me)) for a in arrays]
        return [(arrays[0], shape, lambda i, me, m=m: index(m, i, me)) for m in range(pairs)]

    def sides_of(arrays, part=0):
        return runs(arrays, (width, rows), lambda m, i, me: (part, m))

    def ring_of(products, steps, block, stages):
        stages = ring_stages(stages)
        parts = weight_parts(scalars, products, steps, block, members, stages[0])
        return Ring(scalars, parts, stages)

    x_first, y_first = [(0,), (1,), (2,), (3,)], [(1,), (0,), (2,), (3,)]

    def feed_ring(part, b, stages):
        b_runs = [(b, (rows, block), lambda i, me, m=m: (m, i)) for m in range(pairs)]
        return ring_of([(sides_of(turned, part), b_runs)], slice_width // block, block, stages)

    ring_out = feed_ring(1, hidden, x_first)
    ring_hid = feed_ring(0, grad_pre, y_first)

    query_rows = rows // parts
    part = jnp.stack([me[0] % parts, me[0]]).astype(jnp.int32)
    from_first, head_grad, head_delta, probs, _ = forward_head(
        at_head,
        part,
        rows,
        query_rows,
        (*ring_out.sent, *ring_hid.sent, *[a for a, _ in (*feeds, *grads)], *turned, *one_t),
    )
    back_first = lax.all_to_all(from_first, "seq", 0, 0, tiled=True)
    from_second, after_second = backward_head(
        scalars, at_head, head_grad, head_delta, probs, rows, query_rows, ()
    )
    from_second = after(from_second, *ring_out.came, *ring_hid.came)
    back_second = lax.all_to_all(from_second, "seq", 0, 0, tiled=True)
    x_first, y_first = [(0,), (1,), (2, 3)], [(1,), (0,), (2, 3)]
    split = pairs == 2 and parts == 1
    share = width // pairs

    def pieces_of(arrays):
        stacked = jnp.stack([a.reshape(rows, pairs, share) for a in arrays], 2)
        stacked = jnp.transpose(stacked, (1, 0, 2, 3)).reshape(pairs, rows, len(arrays) * share)
        if pairs == 2:
            mine = lax.dynamic_index_in_dim(stacked, pair_me, 0, False)
            return [mine, pair_swap(lax.dynamic_index_in_dim(stacked, 1 - pair_me, 0, False))]
        got = lax.all_to_all(stacked, "mlp", 0, 0, tiled=True)
        return [got.reshape(pairs * rows, len(arrays) * share)]

    if split:

        attended, grad_v, sent, own_a, own_v = regroup_once(
            back_first, None, scalars, (from_second,)
        )
        came = pair_swap(sent)
        for ring in (ring_out, ring_hid):
            ring.hold(sent)
            ring.step()
        v_parts, d_parts, _ = weight_once(
            scalars,
            [*one_t, own_v, came, own_a, *cot_list],
            [
                ([((0, 1), (rows_run(2, 0, share), rows_run(3, width, share)), True)], (0,)),
                (
                    [((4, 3), (columns_run(5, share, None), columns_run(6, share, None)), False)],
                    (1,),
                ),
            ],
            width,
            share,
            members,
            (),
        )
        grad_q, grad_k, sent, own_qk = regroup_once(
            back_second, table, scalars, (*v_parts, *d_parts)
        )
        came = pair_swap(sent)
        qv_parts, kd_parts, weighed = weight_once(
            scalars,
            [*one_t, own_qk, came, *v_parts, *d_parts],
            [
                (
                    [
                        ((0, 1), (columns_run(2, share, n), columns_run(3, share, n)), False),
                        (4 + 2 * n, 5 + 2 * n),
                    ],
                    (n,),
                )
                for n in range(2)
            ],
            width,
            share,
            members,
            (),
        )
        ring_qv = Ring(scalars, qv_parts, x_first)
        ring_kd = Ring(scalars, kd_parts, y_first)
    else:
        for ring in (ring_out, ring_hid):
            ring.step()
        attended, grad_v, att_t = regroup(back_first, None, scalars, rows, query_rows, False)
        att_t = mlp_list(att_t, 1)
        grad_q, grad_k = regroup(back_second, table, scalars, rows, query_rows, False)
        pieces = [pieces_of([g]) for g in (grad_q, grad_v, grad_k)]
        q_runs, v_runs, k_runs = (
            runs(p, (rows, share), lambda m, i, me: (m, 0)) for p in pieces
        )
        cot_runs = runs(cot_list, (rows, share), lambda m, i, me: (m, me[1]))
        one = sides_of(one_t)
        ring_qv = ring_of([(one, q_runs), (one, v_runs)], 2, share, x_first)
        ring_kd = ring_of([(one, k_runs), (sides_of(att_t), cot_runs)], 2, share, y_first)

    ring_out.hold(*ring_kd.sent)
    ring_out.step(ring_hid)
    block_output, grad_input, vec, gm_bias, closed = close_layer(
        inputs,
        cot,
        (attend_gain, feed_gain, attention_out_bias, contract_bias),
        (grad_q, grad_k, grad_v),
        attended,
        query_key_value_weight,
        attention_out_weight,
        feeds,
        grads,
        scalars,
        ring_out.sent,
    )
    for ring in (ring_qv, ring_kd):
        ring.pass_on(closed[0])
    ring_out.came = [after(x, *ring_qv.sent, *ring_kd.sent) for x in ring_out.came]
    ring_out.pass_on(closed[0])

    bias_full = lax.dynamic_update_slice_in_dim(
        jnp.zeros((pairs * slice_width,), F32), grad_hid_bias[0], pair_me * slice_width, 0
    )
    vectors = [*[vec[r] for r in range(5)], gm_bias.reshape(-1), bias_full]
    packed = jnp.concatenate([v.reshape(members, pairs, -1) for v in vectors], -1)
    if pairs == 2:
        mine = lax.dynamic_index_in_dim(packed, pair_me, 1, False)
        other = lax.dynamic_index_in_dim(packed, 1 - pair_me, 1, False)
        packed = mine + pair_swap(after(other, *ring_out.sent))
    else:
        packed = lax.psum_scatter(packed, "mlp", scatter_dimension=1, tiled=False)
    ring_qv.step(ring_kd)
    packed = after(packed, *ring_qv.sent)
    packed = lax.all_to_all(packed, "seq", 0, 0, tiled=True)

    feed_total = ring_out.plain_total()
    out_weight = jnp.transpose(feed_total[:, :slice_width])
    hid_weight = feed_total[:, slice_width:]

    if pairs == 2:
        mine, other = ring_qv.total()
        packed = after(packed, other)
        merged, dense = vmem_call(
            place_kernel,
            [shape_of((own // pairs, 3 * width), F32), shape_of((own // pairs, width), F32)],
            scalars,
            [mine, pair_swap(other)],
            "place",
        )
    else:
        got = ring_qv.total([4 * share])[0].reshape(pairs, own // pairs, 4 * share)
        got = lax.all_to_all(got, "mlp", 0, 0, tiled=True)
        got = jnp.transpose(got.reshape(pairs, own // pairs, 4, share), (1, 2, 0, 3))
        merged = jnp.concatenate([got[:, n].reshape(-1, width) for n in (0, 2, 1)], -1)
        dense = got[:, 3].reshape(-1, width)
    packed = jnp.sum(packed, 0)
    outs, start = [], 0
    for v in vectors:
        size = v.shape[0] // (members * pairs)
        outs.append(lax.slice_in_dim(packed, start, start + size))
        start += size
    grad_gain_one, grad_shift_one, grad_dense_bias, grad_gain_two, grad_shift_two = outs[:5]
    grad_merged_bias, out_hid_bias = outs[5:]
    return (
        block_output.reshape(seq_count, rows, width),
        grad_input.reshape(seq_count, rows, width),
        grad_gain_one,
        grad_shift_one,
        merged,
        grad_merged_bias,
        dense,
        grad_dense_bias,
        grad_gain_two,
        grad_shift_two,
        hid_weight,
        out_hid_bias,
        out_weight,
        grad_dense_bias,
    )


def solution(mesh):
    in_specs = (
        P("mlp", "seq", None),
        P("mlp", "seq", None),
        P(),
        P(),
        P(),
        P(),
        P(),
        P(),
        P(),
        P(),
        P(None, "mlp"),
        P("mlp"),
        P("mlp", None),
        P(),
    )
    out_specs = (
        P("mlp", "seq", None),
        P("mlp", "seq", None),
        P(("seq", "mlp")),
        P(("seq", "mlp")),
        P(("seq", "mlp"), None),
        P(("seq", "mlp")),
        P(("seq", "mlp"), None),
        P(("seq", "mlp")),
        P(("seq", "mlp")),
        P(("seq", "mlp")),
        P("seq", "mlp"),
        P(("seq", "mlp")),
        P("mlp", "seq"),
        P(("seq", "mlp")),
    )
    return jax.shard_map(
        per_device, mesh=mesh, in_specs=in_specs, out_specs=out_specs, check_vma=False
    )
```

```python
from functools import partial

import jax
import jax.numpy as jnp
from jax import lax
from jax.experimental import pallas as pl
from jax.experimental.pallas import tpu as pltpu
from jax.sharding import PartitionSpec as P

HEADS = 16
HEAD = 64
ROT = 16
PAIR = 2 * HEAD
EPS = 1e-05
NEGATIVE = -1e30

F32 = jnp.float32
BF16 = jnp.bfloat16
NT = (((1,), (1,)), ((), ()))
NN = (((1,), (0,)), ((), ()))
VMEM_LIMIT = 60 * 1024 * 1024
COST_SHARE = 16


def dot32(a, b, dims=NN):
    return lax.dot_general(a, b, dims, preferred_element_type=F32)


def cost(flops, bytes_accessed, transcendentals, share=COST_SHARE):
    return pl.CostEstimate(
        flops=flops // share,
        bytes_accessed=bytes_accessed // share,
        transcendentals=transcendentals // share,
    )


def shape_of(shape, dtype):
    return jax.ShapeDtypeStruct(shape, dtype)


def fixed(shape):
    return pl.BlockSpec(shape, lambda *i: (0,) * len(shape))


def vector_row(ref):
    return ref[...].astype(F32).reshape(1, -1)


def two_heads(pair_a, pair_b, low):
    even = jnp.where(low, pair_a, pltpu.roll(pair_b, HEAD, 1))
    odd = jnp.where(low, pltpu.roll(pair_a, HEAD, 1), pair_b)
    return (even, odd)


def rotary_lanes(first, rows, inverse):
    shape = (rows, PAIR)
    lane = lax.broadcasted_iota(jnp.int32, shape, 1) % HEAD
    position = (lax.broadcasted_iota(jnp.int32, shape, 0) + first).astype(F32)
    angle = position * inverse
    cosine, sine = jnp.cos(angle), jnp.sin(angle)
    zero = jnp.zeros_like(sine)
    return (
        jnp.where(lane < ROT, cosine, 1.0),
        jnp.where(lane < ROT // 2, -sine, zero),
        jnp.where((lane >= ROT // 2) & (lane < ROT), sine, zero),
    )


def rotate_lanes(x, cosine, to_first, to_second):
    ahead = pltpu.roll(x, PAIR - ROT // 2, 1)
    behind = pltpu.roll(x, ROT // 2, 1)
    return x * cosine + ahead * to_first + behind * to_second


def unit_rows(x):
    average = jnp.mean(x, -1, keepdims=True)
    centred = x - average
    spread = jnp.mean(centred * centred, -1, keepdims=True)
    root = lax.rsqrt(spread + EPS)
    return (centred * root, root)


def open_kernel(
    first_ref, x_ref, g_ref, inv_ref, ga_ref, sa_ref, gf_ref, sf_ref, b_ref,
    wq_ref, wk_ref, wv_ref, wo_ref,
    out_ref, n1_ref, n2_ref, table_ref, one_ref, turned_ref, bias_ref, *, parts,
):
    rows, width = x_ref.shape
    step = pl.program_id(0)
    cols = wq_ref.shape[1]

    @pl.when(step == 0)
    def _():
        unit, root = unit_rows(x_ref[...].astype(F32))
        n1_ref[...] = (unit * vector_row(ga_ref) + vector_row(sa_ref)).astype(BF16)
        n2_ref[...] = (unit * vector_row(gf_ref) + vector_row(sf_ref)).astype(BF16)
        for t, table in enumerate(rotary_lanes(first_ref[0], rows, inv_ref[...])):
            table_ref[t] = table
        bias_ref[...] = vector_row(b_ref)

    for n, (source, target) in enumerate(
        (
            (n1_ref, one_ref),
            (n2_ref, turned_ref.at[:width]),
            (g_ref, turned_ref.at[width:]),
        )
    ):

        @pl.when(step == pl.num_programs(0) - 1)
        def _(source=source, target=target):
            target[...] = jnp.transpose(source[...])

    def bias(third):
        return bias_ref[:, pl.ds(pl.multiple_of(third * width + step * cols, cols), cols)]

    normed = n1_ref[...]
    query = dot32(normed, wq_ref[...]) + bias(0)
    key = dot32(normed, wk_ref[...]) + bias(1)
    value = dot32(normed, wv_ref[...]) + bias(2)
    grad = dot32(g_ref[...], wo_ref[...], NT)
    tables = (table_ref[0], table_ref[1], table_ref[2])
    low = lax.broadcasted_iota(jnp.int32, (rows, PAIR), 1) < HEAD
    query_rows = rows // parts
    for c in range(cols // PAIR):
        cut = slice(c * PAIR, (c + 1) * PAIR)
        kv = two_heads(rotate_lanes(key[:, cut], *tables), value[:, cut], low)
        qg = two_heads(rotate_lanes(query[:, cut], *tables), grad[:, cut], low)
        for h in range(2):
            kv_h, qg_h = kv[h].astype(BF16), qg[h].astype(BF16)
            for p in range(parts):
                out_ref[2 * c + h, p, :rows] = kv_h
                out_ref[2 * c + h, p, rows:] = qg_h[p * query_rows : (p + 1) * query_rows]


def open_layer(x, g, first, vectors, weight, bias, out_weight, parts):
    rows, width = x.shape
    steps = 2
    cols = width // steps
    per = HEADS // steps
    inverse = 10000.0 ** (-(jnp.arange(ROT // 2, dtype=F32) * 2.0 / ROT))
    inverse = jnp.tile(inverse, PAIR // (ROT // 2)).reshape(1, PAIR)
    chunk = rows + rows // parts

    def third(t):
        return pl.BlockSpec((width, cols), lambda i: (0, t * steps + i))

    out, *others = pl.pallas_call(
        partial(open_kernel, parts=parts),
        grid=(steps,),
        out_shape=(
            shape_of((HEADS, parts, chunk, PAIR), BF16),
            shape_of((rows, width), BF16),
            shape_of((rows, width), BF16),
            shape_of((3, rows, PAIR), F32),
            shape_of((width, rows), BF16),
            shape_of((2 * width, rows), BF16),
        ),
        in_specs=[
            pl.BlockSpec(memory_space=pltpu.SMEM),
            fixed((rows, width)),
            fixed((rows, width)),
            fixed((1, PAIR)),
            *[fixed((width,))] * 4,
            fixed((3 * width,)),
            third(0), third(1), third(2),
            pl.BlockSpec((cols, width), lambda i: (i, 0)),
        ],
        out_specs=(
            pl.BlockSpec((per, parts, chunk, PAIR), lambda i: (i, 0, 0, 0)),
            fixed((rows, width)),
            fixed((rows, width)),
            fixed((3, rows, PAIR)),
            fixed((width, rows)),
            fixed((2 * width, rows)),
        ),
        scratch_shapes=[pltpu.VMEM((1, 3 * width), F32)],
        cost_estimate=cost(
            flops=8 * rows * width * width,
            bytes_accessed=8 * width * width + 18 * rows * width,
            transcendentals=0,
        ),
        compiler_params=pltpu.CompilerParams(vmem_limit_bytes=VMEM_LIMIT),
        name="open_layer",
    )(first, x, g, inverse, *vectors, bias, weight, weight, weight, out_weight)
    return (out.reshape(HEADS * parts, chunk, PAIR), *others)


ROW_GROUP = 4
ONES = 16
CUTS = 4
KEY_GROUP = 2


def first_tile(i):
    return i * (i + 1)


def column_chunks(x):
    return [x[:, c : c + 128] for c in range(0, x.shape[1], 128)]


def forward_kernel(
    part_ref, x_ref, y_ref, g_ref, d_ref, p_hbm, after_ref,
    s_ref, p_ref, dv_ref, vt_ref, mx_ref, top_ref, acc_ref, sem,
    *, key_rows, query_rows,
):
    after_ref[0] = part_ref[1]
    blocks = x_ref.shape[0] // ROW_GROUP
    keys, rows = KEY_GROUP * key_rows, ROW_GROUP * query_rows
    low = lax.broadcasted_iota(jnp.int32, (rows, PAIR), 1) < HEAD
    key_low = lax.broadcasted_iota(jnp.int32, (keys, PAIR), 1) < HEAD
    cuts = [slice(r, r + rows // CUTS) for r in range(0, rows, rows // CUTS)]

    def key_value(j):
        return x_ref[pl.ds(j * KEY_GROUP, KEY_GROUP), :key_rows, :].reshape(keys, PAIR)

    def query_rows_of(i):
        return x_ref[pl.ds(i * ROW_GROUP, ROW_GROUP), key_rows:, :].reshape(rows, PAIR)

    def query_of(i):
        return jnp.where(low, query_rows_of(i).astype(F32) * HEAD**-0.5, 0.0).astype(BF16)

    def copy_out(i, j):
        return pltpu.make_async_copy(p_ref.at[j], p_hbm.at[first_tile(i) + j], sem.at[j])

    def ones_and_values(j, unused):
        turned = jnp.transpose(key_value(j).astype(F32))
        vt_ref[j, :HEAD] = turned[HEAD:].astype(BF16)
        vt_ref[j, HEAD:] = jnp.ones((ONES, keys), BF16)
        return unused

    def raise_max(cut, s):
        mx = mx_ref[cut]
        for chunk in column_chunks(s):
            mx = jnp.maximum(mx, chunk)
        mx_ref[cut] = mx

    def last_scores(i, query):
        row = lax.broadcasted_iota(jnp.int32, (rows, keys), 0)
        col = lax.broadcasted_iota(jnp.int32, (rows, keys), 1)
        row_pos = (row // query_rows) * key_rows + row % query_rows + part_ref[0] * query_rows
        for d in range(ROW_GROUP // KEY_GROUP):
            j = 2 * i + d
            s = dot32(query, key_value(j), NT)
            s = jnp.where(col + d * keys <= row_pos, s, NEGATIVE)
            s_ref[j] = s
            raise_max(slice(None), s)

    def tile(i, j, query, grad_t):
        kv = key_value(j)
        grads = None
        for cut in cuts:
            if grad_t is not None:
                part = dot32(grad_t[:, cut], p_ref[j, cut])
                grads = part if grads is None else grads + part
            top = top_ref[cut]
            p = jnp.concatenate(
                [jnp.exp(c - top) for c in column_chunks(s_ref[j, cut])], 1
            ).astype(BF16)
            p_ref[j, cut] = p
            acc_ref[:, cut] += dot32(vt_ref[j], p, NT)
            if query is not None:
                s = dot32(query[cut], kv, NT)
                s_ref[j, cut] = s
                raise_max(cut, s)
        if grads is not None:
            dv_ref[j, HEAD:] += grads
        copy_out(i, j).start()

    def block(i, grad_t, ahead):
        query = query_of(i + 1) if ahead else None
        top_ref[...] = jnp.broadcast_to(jnp.max(mx_ref[...], -1, keepdims=True), (rows, PAIR))
        mx_ref[...] = jnp.full_like(mx_ref, NEGATIVE)
        acc_ref[...] = jnp.zeros_like(acc_ref)

        def step(j, unused):
            copy_out(i - 1, j).wait()
            tile(i, j, query, grad_t)
            return unused

        lax.fori_loop(0, 2 * i, step, 0)
        for d in range(2):
            tile(i, 2 * i + d, query, None)
        if ahead:
            last_scores(i + 1, query)
        inverse = 1.0 / acc_ref[HEAD : HEAD + 1]
        attended_t = acc_ref[:HEAD] * inverse
        rows_t = jnp.transpose(query_rows_of(i).astype(F32))
        grad_t = (rows_t[HEAD:] * inverse).astype(BF16)
        both = jnp.transpose(jnp.concatenate([attended_t, grad_t.astype(F32)], 0))
        delta = jnp.sum(grad_t.astype(F32) * attended_t, 0, keepdims=True)
        d_ref[i] = jnp.transpose(jnp.broadcast_to(delta, (PAIR, rows)))
        g_ref[i] = jnp.where(low, 0.0, both).astype(BF16)
        here = pl.ds(i * ROW_GROUP, ROW_GROUP)
        y_ref[here, :query_rows, :] = both.astype(BF16).reshape(ROW_GROUP, query_rows, PAIR)
        if query_rows < key_rows:
            y_ref[here, query_rows:, :] = jnp.zeros(
                (ROW_GROUP, key_rows - query_rows, PAIR), BF16
            )
        return grad_t

    dv_ref[...] = jnp.zeros_like(dv_ref)
    lax.fori_loop(0, 2 * blocks, ones_and_values, 0)
    mx_ref[...] = jnp.full_like(mx_ref, NEGATIVE)
    last_scores(0, query_of(0))
    grad_t = lax.fori_loop(
        0, blocks - 1, lambda i, g: block(i, g, True), jnp.zeros((HEAD, rows), BF16)
    )
    grad_t = block(jnp.int32(blocks - 1), grad_t, False)

    def finish(j, unused):
        here = pl.ds(j * KEY_GROUP, KEY_GROUP)
        held = y_ref[here].reshape(keys, PAIR)
        dv_ref[j, HEAD:] += dot32(grad_t, p_ref[j])
        grads = jnp.transpose(dv_ref[j]).astype(BF16)
        y_ref[here] = jnp.where(key_low, held, grads).reshape(KEY_GROUP, key_rows, PAIR)
        copy_out(blocks - 1, j).wait()
        return unused

    lax.fori_loop(0, 2 * blocks, finish, 0)


def backward_kernel(
    me_ref, x_ref, g_ref, d_ref, p_hbm, y_ref, after_ref,
    p_ref, dp0_ref, dp1_ref, dk_ref, acc_ref, sem,
    *, key_rows, query_rows,
):
    after_ref[0] = me_ref[0]
    blocks = x_ref.shape[0] // ROW_GROUP
    keys, rows = KEY_GROUP * key_rows, ROW_GROUP * query_rows
    tiles = first_tile(blocks)
    slots = p_ref.shape[0]
    low = lax.broadcasted_iota(jnp.int32, (rows, PAIR), 1) < HEAD
    dp_refs = (dp0_ref, dp1_ref)

    def copy_in(t):
        return pltpu.make_async_copy(p_hbm.at[t], p_ref.at[t % slots], sem.at[t % slots])

    def refill(t):
        @pl.when(t + slots < tiles)
        def _():
            copy_in(t + slots).start()

    for t in range(min(slots, tiles)):
        copy_in(t).start()
    dk_ref[...] = jnp.zeros_like(dk_ref)

    def key_value(j):
        return x_ref[pl.ds(j * KEY_GROUP, KEY_GROUP), :key_rows, :].reshape(keys, PAIR)

    def one_block(i, unused):
        here = pl.ds(i * ROW_GROUP, ROW_GROUP)
        query = x_ref[here, key_rows:, :].reshape(rows, PAIR).astype(F32) * HEAD**-0.5
        query_t = jnp.transpose(query)[:HEAD].astype(BF16)
        grad = g_ref[i]
        first = first_tile(i)
        acc_ref[...] = jnp.zeros_like(acc_ref)

        def raise_probs(j, side):
            dp_refs[side][...] = dot32(grad, key_value(j), NT)

        def tile(j, side):
            delta = d_ref[i]
            p = column_chunks(p_ref[(first + j) % slots].astype(F32))
            dp = column_chunks(dp_refs[side][...])
            ds = jnp.concatenate([a * (b - delta) for a, b in zip(p, dp)], 1).astype(BF16)
            dk_ref[j, HEAD:] += dot32(query_t, ds)
            acc_ref[...] += dot32(ds, key_value(j))

        def two_tiles(m, unused, more=True):
            j = 2 * m
            copy_in(first + j).wait()
            copy_in(first + j + 1).wait()
            raise_probs(j + 1, 1)
            tile(j, 0)
            if more:
                raise_probs(j + 2, 0)
            tile(j + 1, 1)
            refill(first + j)
            refill(first + j + 1)
            return unused

        raise_probs(0, 0)
        lax.fori_loop(0, i, two_tiles, 0)
        two_tiles(i, 0, False)
        done = jnp.where(low, acc_ref[...] * HEAD**-0.5, 0.0).astype(BF16)
        y_ref[here, :query_rows, :] = done.reshape(ROW_GROUP, query_rows, PAIR)
        if query_rows < key_rows:
            y_ref[here, query_rows:, :] = jnp.zeros(
                (ROW_GROUP, key_rows - query_rows, PAIR), BF16
            )
        return unused

    lax.fori_loop(0, blocks, one_block, 0)
    key_low = lax.broadcasted_iota(jnp.int32, (keys, PAIR), 1) < HEAD

    def finish(j, unused):
        here = pl.ds(j * KEY_GROUP, KEY_GROUP)
        held = y_ref[here].reshape(keys, PAIR)
        grads = jnp.transpose(dk_ref[j]).astype(BF16)
        y_ref[here] = jnp.where(key_low, held, grads).reshape(KEY_GROUP, key_rows, PAIR)
        return unused

    lax.fori_loop(0, 2 * blocks, finish, 0)


def head_sizes(x, key_rows, query_rows):
    count = x.shape[0]
    blocks = count // ROW_GROUP
    return count, blocks, KEY_GROUP * key_rows, ROW_GROUP * query_rows


def forward_head(x, part, key_rows, query_rows, behind):
    count, blocks, keys, rows = head_sizes(x, key_rows, query_rows)
    tiles = first_tile(blocks)
    vmem = pl.BlockSpec(memory_space=pltpu.VMEM)
    return pl.pallas_call(
        without(
            partial(forward_kernel, key_rows=key_rows, query_rows=query_rows), 2, len(behind)
        ),
        out_shape=(
            shape_of((count, key_rows, PAIR), BF16),
            shape_of((blocks, rows, PAIR), BF16),
            shape_of((blocks, rows, PAIR), F32),
            shape_of((tiles, rows, keys), BF16),
            shape_of((1,), jnp.int32),
        ),
        in_specs=[pl.BlockSpec(memory_space=pltpu.SMEM), vmem]
        + [pl.BlockSpec(memory_space=pl.ANY)] * len(behind),
        out_specs=(
            vmem, vmem, vmem, pl.BlockSpec(memory_space=pl.ANY),
            pl.BlockSpec(memory_space=pltpu.SMEM),
        ),
        scratch_shapes=[
            pltpu.VMEM((2 * blocks, rows, keys), F32),
            pltpu.VMEM((2 * blocks, rows, keys), BF16),
            pltpu.VMEM((2 * blocks, PAIR, keys), F32),
            pltpu.VMEM((2 * blocks, HEAD + ONES, keys), BF16),
            pltpu.VMEM((rows, PAIR), F32),
            pltpu.VMEM((rows, PAIR), F32),
            pltpu.VMEM((HEAD + ONES, rows), F32),
            pltpu.SemaphoreType.DMA((2 * blocks,)),
        ],
        cost_estimate=cost(
            flops=tiles * rows * keys * 2 * 256 * 3,
            bytes_accessed=4 * x.size + 2 * tiles * rows * keys,
            transcendentals=tiles * rows * keys,
            share=1,
        ),
        compiler_params=pltpu.CompilerParams(vmem_limit_bytes=VMEM_LIMIT),
        name="forward_head",
    )(part, x, *behind)


def backward_head(scalars, x, grad, delta, probs, key_rows, query_rows, behind):
    count, blocks, keys, rows = head_sizes(x, key_rows, query_rows)
    tiles = first_tile(blocks)
    slots = 6
    vmem = pl.BlockSpec(memory_space=pltpu.VMEM)
    return pl.pallas_call(
        without(
            partial(backward_kernel, key_rows=key_rows, query_rows=query_rows), 5, len(behind)
        ),
        out_shape=(shape_of((count, key_rows, PAIR), BF16), shape_of((1,), jnp.int32)),
        in_specs=[pl.BlockSpec(memory_space=pltpu.SMEM), vmem, vmem, vmem]
        + [pl.BlockSpec(memory_space=pl.ANY)] * (1 + len(behind)),
        out_specs=(vmem, pl.BlockSpec(memory_space=pltpu.SMEM)),
        scratch_shapes=[
            pltpu.VMEM((slots, rows, keys), BF16),
            pltpu.VMEM((rows, keys), F32),
            pltpu.VMEM((rows, keys), F32),
            pltpu.VMEM((2 * blocks, PAIR, keys), F32),
            pltpu.VMEM((rows, PAIR), F32),
            pltpu.SemaphoreType.DMA((slots,)),
        ],
        cost_estimate=cost(
            flops=tiles * rows * keys * 2 * 256 * 3,
            bytes_accessed=4 * x.size + 2 * tiles * rows * keys,
            transcendentals=0,
            share=1,
        ),
        compiler_params=pltpu.CompilerParams(vmem_limit_bytes=VMEM_LIMIT),
        name="backward_head",
    )(scalars, x, grad, delta, probs, *behind)


def feed_kernel(*refs, count, keep):
    rows_refs, cot_refs = refs[:count], refs[count : 2 * count]
    w1_ref, b1_ref, w2_ref = refs[2 * count : 2 * count + 3]
    hid_ref, gpre_ref, gb_ref = refs[2 * count + 3 : 2 * count + 6]
    outs = refs[2 * count + 6 : -2]
    out_acc, grad_acc = refs[-2:]
    step = pl.program_id(0)

    @pl.when(step == 0)
    def _():
        out_acc[...] = jnp.zeros_like(out_acc)
        grad_acc[...] = jnp.zeros_like(grad_acc)

    bias = b1_ref[...]
    sums = jnp.zeros_like(bias)
    rows = rows_refs[0].shape[0]
    for r in range(count):
        here = slice(r * rows, (r + 1) * rows)
        pre = dot32(rows_refs[r][...], w1_ref[...]) + bias
        grad = dot32(cot_refs[r][...], w2_ref[...], NT)
        cdf = 0.5 + 0.5 * lax.erf(pre * (0.5**0.5))
        density = jnp.exp(-0.5 * pre * pre) * 0.3989422804014327
        hidden = (pre * cdf).astype(BF16)
        grad_pre = (grad * (cdf + pre * density)).astype(BF16)
        hid_ref[here] = hidden
        gpre_ref[here] = grad_pre
        sums = sums + jnp.sum(grad_pre.astype(F32), 0, keepdims=True)
        out_acc[here] += dot32(hidden, w2_ref[...])
        grad_acc[here] += dot32(grad_pre, w1_ref[...], NT)
    gb_ref[...] = sums

    @pl.when(step == pl.num_programs(0) - 1)
    def _():
        if keep:
            own_out, own_grad, other = outs
            own_out[...] = out_acc[:rows]
            own_grad[...] = grad_acc[:rows]
            other[:rows] = out_acc[rows:].astype(BF16)
            other[rows:] = grad_acc[rows:].astype(BF16)
        else:
            outs[0][...] = out_acc[...].astype(BF16)
            outs[1][...] = grad_acc[...].astype(BF16)


def feed(rows_list, cot_list, w1, b1, w2):
    width, hidden = w1.shape
    count = len(rows_list)
    rows = rows_list[0].shape[0]
    total = rows * count
    block = 256
    keep = count > 1
    sides = (
        [(rows, F32), (rows, F32), (total, BF16)]
        if keep
        else [(total, BF16), (total, BF16)]
    )
    once = pl.Buffered(1)
    whole = pl.BlockSpec((rows, width), lambda i: (0, 0), pipeline_mode=once)
    return pl.pallas_call(
        partial(feed_kernel, count=count, keep=keep),
        grid=(hidden // block,),
        out_shape=(
            shape_of((total, hidden), BF16),
            shape_of((total, hidden), BF16),
            shape_of((1, hidden), F32),
            *[shape_of((r, width), d) for r, d in sides],
        ),
        in_specs=[
            *[whole] * (2 * count),
            pl.BlockSpec((width, block), lambda i: (0, i)),
            pl.BlockSpec((1, block), lambda i: (0, i)),
            pl.BlockSpec((block, width), lambda i: (i, 0)),
        ],
        out_specs=(
            pl.BlockSpec((total, block), lambda i: (0, i)),
            pl.BlockSpec((total, block), lambda i: (0, i)),
            pl.BlockSpec((1, block), lambda i: (0, i)),
            *[
                pl.BlockSpec((r, width), lambda i: (0, 0), pipeline_mode=once) for r, d in sides
            ],
        ),
        scratch_shapes=[pltpu.VMEM((total, width), F32), pltpu.VMEM((total, width), F32)],
        cost_estimate=cost(
            flops=8 * total * width * hidden,
            bytes_accessed=4 * width * hidden + 4 * total * hidden,
            transcendentals=2 * total * hidden,
        ),
        compiler_params=pltpu.CompilerParams(vmem_limit_bytes=VMEM_LIMIT),
        name="feed",
    )(*rows_list, *cot_list, w1, b1.astype(F32).reshape(1, hidden), w2)


def insert_bits(k, positions, values):
    for position, value in zip(positions, values):
        k = ((k >> position) << (position + 1)) + (value << position) + (k & ((1 << position) - 1))
    return k


def part_chunk(k, p, me, ring_bits, positions):
    values = [((me >> bit) & 1) ^ ((p >> n) & 1) for n, bit in enumerate(ring_bits)]
    return insert_bits(k, positions, values)


def weight_kernel(me_ref, *refs, bits, counts):
    total = sum(counts)
    a_refs, b_refs, parts = refs[:total], refs[total : 2 * total], refs[2 * total :]

    def product(first, count):
        b = jnp.concatenate([r[...] for r in b_refs[first : first + count]], 0)
        for p, ref in enumerate(parts):
            chunks, rows, cols = ref.shape
            a = []
            for k in range(chunks):
                start = part_chunk(k, p, me_ref[0], bits, bits) * rows
                here = pl.ds(pl.multiple_of(start, rows), rows)
                a.append(
                    jnp.concatenate([r[here, :] for r in a_refs[first : first + count]], 1)
                )
            ref[...] = dot32(jnp.concatenate(a, 0), b).astype(BF16).reshape(ref.shape)

    if len(counts) == 1:
        product(0, total)
    else:
        for n, count in enumerate(counts):
            pl.when(pl.program_id(0) == n)(partial(product, sum(counts[:n]), count))


def weight_parts(scalars, products, steps, block, members, bits):
    a_runs = [run for a, _ in products for run in a]
    b_runs = [run for _, b in products for run in b]
    width = a_runs[0][1][0]
    rows = width // members
    tokens = sum(shape[1] for _, shape, _ in products[0][0])
    count = 1 << len(bits)
    each = (members // count, rows, steps * block)
    out = pl.BlockSpec((members // count, rows, block), lambda i, me: (0, 0, i))
    return pl.pallas_call(
        partial(weight_kernel, bits=bits, counts=[len(a) for a, _ in products]),
        grid_spec=pltpu.PrefetchScalarGridSpec(
            num_scalar_prefetch=1,
            grid=(steps,),
            in_specs=[pl.BlockSpec(shape, index) for _, shape, index in (*a_runs, *b_runs)],
            out_specs=[out] * count,
        ),
        out_shape=[shape_of(each, BF16)] * count,
        cost_estimate=cost(
            flops=2 * width * tokens * steps * block,
            bytes_accessed=2 * width * tokens + 2 * (width + tokens) * steps * block,
            transcendentals=0,
        ),
        compiler_params=pltpu.CompilerParams(vmem_limit_bytes=VMEM_LIMIT),
        name="weight_parts",
    )(scalars, *[array for array, _, _ in (*a_runs, *b_runs)])


def weight_once_kernel(me_ref, *refs, products, operands, only):
    arrays, outs = refs[:operands], refs[operands:]
    at = 0
    for blocks, bits in products:
        parts = outs[at : at + len(only)]
        at += len(parts)
        cols = parts[0].shape[2] // len(blocks)
        for n, block in enumerate(blocks):
            here = slice(n * cols, (n + 1) * cols)
            if isinstance(block[0], int):
                for ref, source in zip(parts, block):
                    ref[:, :, here] = arrays[source][...]
                continue
            a_runs, b_runs, turned = block
            b = jnp.concatenate([run(arrays, me_ref) for run in b_runs], 1 if turned else 0)
            for p, ref in zip(only, parts):
                chunks, rows, _ = ref.shape
                a = []
                for k in range(chunks):
                    start = part_chunk(k, p, me_ref[0], bits, bits) * rows
                    lines = pl.ds(pl.multiple_of(start, rows), rows)
                    a.append(jnp.concatenate([arrays[m][lines, :] for m in a_runs], 1))
                product = dot32(jnp.concatenate(a, 0), b, NT if turned else NN)
                ref[:, :, here] = product.astype(BF16).reshape(chunks, rows, cols)


def rows_run(n, first, count):
    return lambda arrays, me_ref: arrays[n][first : first + count, :]


def columns_run(n, cols, block):
    if block is not None:
        return lambda arrays, me_ref: arrays[n][:, block * cols : (block + 1) * cols]
    return lambda arrays, me_ref: arrays[n][:, pl.ds(pl.multiple_of(me_ref[1] * cols, cols), cols)]


def weight_once(scalars, arrays, products, width, cols, members, only, behind=()):
    each = [
        shape_of((members // 2, width // members, cols * len(blocks)), BF16)
        for blocks, bits in products
        for _ in only
    ]
    outs = vmem_call(
        partial(weight_once_kernel, products=products, operands=len(arrays), only=only),
        each,
        scalars,
        arrays,
        "weight_once",
        behind,
    )
    return outs[: len(only)], outs[len(only) :]


def column_sums(refs, counts):
    groups, start = [], 0
    for count in counts:
        groups.append(refs[start : start + count])
        start += count

    def total(group, c):
        value = group[0][c].astype(F32)
        for ref in group[1:]:
            value = value + ref[c].astype(F32)
        return value

    return [partial(total, group) for group in groups]


def add_kernel(me_ref, *refs, counts, bits, positions):
    ins, outs = refs[: sum(counts)], refs[sum(counts) :]
    at = 0
    for group, total in zip(counts, column_sums(ins, counts)):
        cols = ins[0].shape[2]
        for p, ref in enumerate(outs):
            for k in range(ref.shape[0]):
                c = part_chunk(k, p, me_ref[0], bits, positions)
                ref[k, :, at : at + cols] = total(c).astype(BF16)
        at += cols
        ins = ins[group:]


def last_kernel(me_ref, *refs, count, form):
    value = column_sums(refs[:count], [count])[0](0)
    outs = refs[count:]
    if form == "pair":
        half = value.shape[0] // 2
        first = me_ref[1] == 0
        outs[0][...] = jnp.where(first, value[:half], value[half:])
        outs[1][...] = jnp.where(first, value[half:], value[:half]).astype(BF16)
    else:
        at = 0
        for ref in outs:
            ref[...] = value[:, at : at + ref.shape[1]]
            at += ref.shape[1]


def without(kernel, first, count):
    if not count:
        return kernel
    return lambda *refs: kernel(*refs[:first], *refs[first + count :])


def vmem_call(kernel, out_shape, scalars, arrays, name, behind=()):
    vmem = pl.BlockSpec(memory_space=pltpu.VMEM)
    size = sum(a.size for a in arrays)
    return pl.pallas_call(
        without(kernel, 1 + len(arrays), len(behind)),
        in_specs=[pl.BlockSpec(memory_space=pltpu.SMEM)]
        + [vmem] * len(arrays)
        + [pl.BlockSpec(memory_space=pl.ANY)] * len(behind),
        out_specs=[
            pl.BlockSpec(memory_space=pltpu.SMEM) if o.dtype == jnp.int32 else vmem
            for o in out_shape
        ],
        out_shape=out_shape,
        cost_estimate=cost(flops=size, bytes_accessed=3 * size, transcendentals=0),
        compiler_params=pltpu.CompilerParams(vmem_limit_bytes=VMEM_LIMIT),
        name=name,
    )(scalars, *arrays, *behind)


def seq_move(x, mask):
    members = lax.axis_size("seq")
    return lax.ppermute(x, "seq", [(s, s ^ mask) for s in range(members)])


def ring_stages(stages):
    bits = lax.axis_size("seq").bit_length() - 1
    named = [b for stage in stages for b in stage]
    stages = [tuple(b for b in stage if b < bits) for stage in stages]
    stages[-1] = stages[-1] + tuple(b for b in range(bits) if b not in named)
    return [stage for stage in stages if stage]


class Ring:
    def __init__(self, scalars, parts, stages):
        self.scalars, self.stages, self.behind = scalars, list(stages), ()
        self.me = scalars[0]
        self.left = sorted(b for stage in stages for b in stage)
        self.travel(parts)

    def travel(self, parts):
        stage = self.stages.pop(0)
        self.left = [b for b in self.left if b not in stage]
        self.keep, self.sent = parts[0], parts[1:]
        self.came = [
            seq_move(part, sum(1 << b for n, b in enumerate(stage) if (p >> n) & 1))
            for p, part in enumerate(parts)
            if p
        ]

    def hold(self, *others):
        self.behind = others

    def step(self, *others):
        stage = self.stages[0]
        positions = [self.left.index(b) for b in stage]
        rings = (self, *others)
        chunks, rows = self.keep.shape[:2]
        cols = sum(ring.keep.shape[2] for ring in rings)
        count = 1 << len(stage)
        arrays = [[ring.keep, *ring.came] for ring in rings]
        self.travel(
            vmem_call(
                partial(
                    add_kernel, counts=[len(a) for a in arrays], bits=stage, positions=positions
                ),
                [shape_of((chunks // count, rows, cols), BF16)] * count,
                self.scalars,
                [a for group in arrays for a in group],
                "add_parts",
                self.behind,
            )
        )
        self.behind = ()

    def pass_on(self, me):
        stage = self.stages[0]
        bits = self.left
        shape = self.keep.shape[1:]
        arrays = [a.reshape((2,) * len(bits) + shape) for a in (self.keep, *self.came)]
        parts = []
        for p in range(1 << len(stage)):
            total = None
            for a in arrays:
                for n, bit in reversed(list(enumerate(stage))):
                    axis = len(bits) - 1 - bits.index(bit)
                    index = ((me >> bit) & 1) ^ ((p >> n) & 1)
                    a = lax.dynamic_index_in_dim(a, index, axis, True)
                a = a.reshape((-1,) + shape).astype(F32)
                total = a if total is None else total + a
            parts.append(total.astype(BF16))
        self.travel(parts)

    def plain_total(self):
        return sum(a[0].astype(F32) for a in (self.keep, *self.came))

    def total(self, widths=None):
        while self.stages:
            self.step()
        rows, cols = self.keep.shape[1:]
        shapes = (
            [shape_of((rows, w), F32) for w in widths]
            if widths
            else [shape_of((rows // 2, cols), F32), shape_of((rows // 2, cols), BF16)]
        )
        arrays = [self.keep, *self.came]
        return vmem_call(
            partial(last_kernel, count=len(arrays), form="rows" if widths else "pair"),
            shapes,
            self.scalars,
            arrays,
            "last_sum",
        )


def regroup_kernel(me_ref, back_ref, *refs, key_rows, query_rows, turned):
    heads, parts = back_ref.shape[:2]
    low = lax.broadcasted_iota(jnp.int32, (key_rows, PAIR), 1) < HEAD
    if turned:
        one_ref, two_ref, one_t_ref, *sides = refs
    else:
        table_ref, one_ref, two_ref, *sides = refs
        tables = (table_ref[0], -table_ref[1], -table_ref[2])
    first = pl.program_id(0) == 0
    for t in range(heads // 2):
        pair = []
        for h in (2 * t, 2 * t + 1):
            if parts == 1:
                pair.append(back_ref[h, 0].astype(F32))
                continue
            keys = sum(back_ref[h, p].astype(F32) for p in range(parts))
            queries = jnp.concatenate(
                [back_ref[h, p, :query_rows].astype(F32) for p in range(parts)], 0
            )
            pair.append(jnp.where(low, queries, keys))
        one, two = two_heads(pair[0], pair[1], low)
        if not turned:
            one, two = rotate_lanes(one, *tables), rotate_lanes(two, *tables)
        one, two = one.astype(BF16), two.astype(BF16)
        here = slice(t * PAIR, (t + 1) * PAIR)
        one_ref[:, here] = one
        two_ref[:, here] = two
        if turned:
            one_t_ref[here] = jnp.transpose(one)
        if sides:
            half = one_ref.shape[1]
            for n, value in enumerate((two,) if turned else (one, two)):
                there = slice(n * half + t * PAIR, n * half + (t + 1) * PAIR)
                pl.when(first)(partial(sides[1].__setitem__, (slice(None), there), value))
                pl.when(~first)(partial(sides[0].__setitem__, (slice(None), there), value))


def regroup(back, table, scalars, rows, query_rows, split):
    turned = table is None
    chunk = back.shape[1]
    parts = back.shape[0] // HEADS
    half = HEADS * HEAD // 2
    full = shape_of((rows, 2 * half), BF16)

    def side(i, me):
        return (i + me[1] + 1) % 2 if split else i

    whole = pl.BlockSpec((rows, half), lambda i, me: (0, side(i, me)))
    tall = pl.BlockSpec((half, rows), lambda i, me: (side(i, me), 0))
    cols = half * (1 if turned else 2)
    own = pl.BlockSpec((rows, cols), lambda i, me: (0, 0))
    return pl.pallas_call(
        partial(regroup_kernel, key_rows=rows, query_rows=query_rows, turned=turned),
        grid_spec=pltpu.PrefetchScalarGridSpec(
            num_scalar_prefetch=1,
            grid=(2,),
            in_specs=[
                pl.BlockSpec(
                    (HEADS // 2, parts, chunk, PAIR), lambda i, me: (side(i, me), 0, 0, 0)
                )
            ]
            + ([] if turned else [pl.BlockSpec(table.shape, lambda i, me: (0, 0, 0))]),
            out_specs=[whole, whole] + ([tall] if turned else []) + ([own, own] if split else []),
        ),
        out_shape=[full, full]
        + ([shape_of((2 * half, rows), BF16)] if turned else [])
        + ([shape_of((rows, cols), BF16)] * 2 if split else []),
        cost_estimate=cost(
            flops=back.size, bytes_accessed=4 * back.size, transcendentals=0
        ),
        name="regroup",
    )(
        scalars,
        back.reshape(HEADS, parts, chunk, PAIR),
        *([] if turned else [table]),
    )


def regroup_once_kernel(me_ref, *refs, turned):
    if turned:
        back_ref, att_ref, v_ref, send_ref, own_a_ref, own_v_ref = refs
    else:
        back_ref, table_ref, q_ref, k_ref, send_ref, own_ref = refs
        tables = (table_ref[0], -table_ref[1], -table_ref[2])
    heads, rows = back_ref.shape[:2]
    half = heads // 2
    low = lax.broadcasted_iota(jnp.int32, (rows, PAIR), 1) < HEAD
    for side in range(2):
        first = ((me_ref[1] + side) % 2) * half
        for t in range(half // 2):
            pair = [back_ref[first + 2 * t + n].astype(F32) for n in range(2)]
            one, two = two_heads(pair[0], pair[1], low)
            if not turned:
                one, two = rotate_lanes(one, *tables), rotate_lanes(two, *tables)
            one, two = one.astype(BF16), two.astype(BF16)
            start = pl.multiple_of((first // 2 + t) * PAIR, PAIR)
            here = pl.ds(start, PAIR)
            local = slice(t * PAIR, (t + 1) * PAIR)
            width = half * HEAD
            if turned:
                att_ref[:, here] = one
                v_ref[:, here] = two
                turned_one, turned_two = jnp.transpose(one), jnp.transpose(two)
                own_a_ref[here] = turned_one
                send_ref[here] = turned_one
                if side == 0:
                    own_v_ref[local] = turned_two
                else:
                    send_ref[2 * width + t * PAIR : 2 * width + (t + 1) * PAIR] = turned_two
            else:
                q_ref[:, here] = one
                k_ref[:, here] = two
                ref = own_ref if side == 0 else send_ref
                ref[:, local] = one
                ref[:, width + t * PAIR : width + (t + 1) * PAIR] = two


def regroup_once(back, table, scalars, behind=()):
    rows = back.shape[1]
    full = shape_of((rows, HEADS * HEAD), BF16)
    half = HEADS * HEAD // 2
    if table is None:
        sides = [
            shape_of((3 * half, rows), BF16),
            shape_of((2 * half, rows), BF16),
            shape_of((half, rows), BF16),
        ]
    else:
        sides = [shape_of((rows, 2 * half), BF16)] * 2
    return vmem_call(
        partial(regroup_once_kernel, turned=table is None),
        [full, full, *sides],
        scalars,
        [back] if table is None else [back, table],
        "regroup_once",
        behind,
    )


def close_kernel(
    x_ref, g_ref, ga_ref, gf_ref, bo_ref, bc_ref, gq_ref, gk_ref, gv_ref, att_ref,
    wq_ref, wk_ref, wv_ref, wo_ref, me_ref, *refs, sides,
):
    feeds, grads = refs[:sides], refs[sides : 2 * sides]
    out_ref, gin_ref, vec_ref, gb_ref, after_ref, out_acc, grad_acc = refs[2 * sides :]
    step = pl.program_id(0)
    for n in range(2):
        after_ref[n] = me_ref[n]

    @pl.when(step == 0)
    def _():
        out_acc[...] = jnp.zeros_like(out_acc)
        grad_acc[...] = jnp.zeros_like(grad_acc)

    out_acc[...] += dot32(att_ref[...], wo_ref[...])
    total = None
    for third, (g_third, w_ref) in enumerate(
        ((gq_ref, wq_ref), (gk_ref, wk_ref), (gv_ref, wv_ref))
    ):
        grad = g_third[...]
        part = dot32(grad, w_ref[...], NT)
        total = part if total is None else total + part
        gb_ref[third : third + 1] = jnp.sum(grad.astype(F32), 0, keepdims=True)
    grad_acc[...] += total

    @pl.when(step == pl.num_programs(0) - 1)
    def _():
        x = x_ref[...].astype(F32)
        g = g_ref[...].astype(F32)
        total = x + out_acc[...] + vector_row(bo_ref) + vector_row(bc_ref)
        for ref in feeds:
            total = total + ref[...].astype(F32)
        out_ref[...] = total.astype(BF16)
        unit, root = unit_rows(x)
        one = grad_acc[...]
        two = grads[0][...].astype(F32)
        for ref in grads[1:]:
            two = two + ref[...].astype(F32)
        down = one * vector_row(ga_ref) + two * vector_row(gf_ref)
        mean = jnp.mean(down, -1, keepdims=True)
        slope = jnp.mean(down * unit, -1, keepdims=True)
        gin_ref[...] = g + root * (down - mean - unit * slope)
        for r, rows in enumerate((one * unit, one, g, two * unit, two)):
            vec_ref[r : r + 1] = jnp.sum(rows, 0, keepdims=True)


def close_layer(x, g, vectors, gm, attended, weight, out_weight, feeds, grads, scalars, behind):
    rows, width = x.shape
    steps = 4
    cols = width // steps

    def third(t):
        return pl.BlockSpec((width, cols), lambda i: (0, t * steps + i))

    part = pl.BlockSpec((rows, cols), lambda i: (0, i))
    return pl.pallas_call(
        without(partial(close_kernel, sides=len(feeds)), 15 + 2 * len(feeds), len(behind)),
        grid=(steps,),
        out_shape=(
            shape_of((rows, width), BF16),
            shape_of((rows, width), F32),
            shape_of((5, width), F32),
            shape_of((3, width), F32),
            shape_of((2,), jnp.int32),
        ),
        in_specs=[
            fixed((rows, width)),
            fixed((rows, width)),
            *[fixed((width,))] * 4,
            part, part, part, part,
            third(0), third(1), third(2),
            pl.BlockSpec((cols, width), lambda i: (i, 0)),
            pl.BlockSpec(memory_space=pltpu.SMEM),
            *[
                pl.BlockSpec((rows, width), lambda i, n=n: (n, 0)) for _, n in (*feeds, *grads)
            ],
            *[pl.BlockSpec(memory_space=pl.ANY)] * len(behind),
        ],
        out_specs=(
            fixed((rows, width)),
            fixed((rows, width)),
            fixed((5, width)),
            pl.BlockSpec((3, cols), lambda i: (0, i)),
            pl.BlockSpec(memory_space=pltpu.SMEM),
        ),
        scratch_shapes=[pltpu.VMEM((rows, width), F32), pltpu.VMEM((rows, width), F32)],
        cost_estimate=cost(
            flops=8 * rows * width * width,
            bytes_accessed=8 * width * width + 24 * rows * width,
            transcendentals=0,
        ),
        compiler_params=pltpu.CompilerParams(vmem_limit_bytes=VMEM_LIMIT),
        name="close_layer",
    )(x, g, *vectors, *gm, attended, weight, weight, weight, out_weight, scalars, *[a for a, _ in (*feeds, *grads)], *behind)


def place_kernel(me_ref, own_ref, came_ref, merged_ref, dense_ref):
    half = dense_ref.shape[1] // 2
    for side, ref in enumerate((own_ref, came_ref)):
        at = ((me_ref[1] + side) % 2) * half
        for third, block in enumerate((0, 2, 1)):
            start = pl.multiple_of(third * 2 * half + at, half)
            value = ref[:, block * half : (block + 1) * half]
            merged_ref[:, pl.ds(start, half)] = value.astype(F32)
        dense_ref[:, pl.ds(pl.multiple_of(at, half), half)] = ref[:, 3 * half :].astype(F32)


def pair_swap(x):
    return lax.ppermute(x, "mlp", [(0, 1), (1, 0)])


def mlp_list(x, axis=0):
    if lax.axis_size("mlp") == 2:
        return [x, pair_swap(x)]
    return [lax.all_gather(x, "mlp", axis=axis, tiled=True)]


def after(value, *others):
    return lax.optimization_barrier((value, *others))[0]


def per_device(
    block_input,
    out_cotangent,
    attend_gain,
    attend_shift,
    query_key_value_weight,
    query_key_value_bias,
    attention_out_weight,
    attention_out_bias,
    feed_gain,
    feed_shift,
    expand_weight,
    expand_bias,
    contract_weight,
    contract_bias,
):
    seq_count, rows, width = block_input.shape
    members = lax.axis_size("seq")
    pairs = lax.axis_size("mlp")
    parts = members // HEADS
    own = width // members
    me = lax.axis_index("seq").astype(jnp.int32).reshape(1)
    pair_me = lax.axis_index("mlp")
    scalars = jnp.stack([me[0], pair_me.astype(jnp.int32)])
    inputs = block_input.reshape(rows, width)
    cot = out_cotangent.reshape(rows, width)

    outgoing, _, normed_two, table, one_t, turned = open_layer(
        inputs,
        cot,
        me * rows,
        (attend_gain, attend_shift, feed_gain, feed_shift),
        query_key_value_weight,
        query_key_value_bias,
        attention_out_weight,
        parts,
    )
    at_head = lax.all_to_all(outgoing, "seq", 0, 0, tiled=True)

    rows_list, cot_list = mlp_list(normed_two), mlp_list(cot)
    turned = mlp_list(turned, 1)
    one_t = mlp_list(one_t, 1)
    hidden, grad_pre, grad_hid_bias, *sides = feed(
        rows_list, cot_list, expand_weight, expand_bias, contract_weight
    )
    if pairs == 2:
        came = pair_swap(sides[2])
        feeds, grads = [(sides[0], 0), (came, 0)], [(sides[1], 0), (came, 1)]
    else:
        feeds, grads = (
            [(lax.psum_scatter(v, "mlp", scatter_dimension=0, tiled=True), 0)] for v in sides
        )
    slice_width = expand_weight.shape[1]
    block = min(512, slice_width)

    def runs(arrays, shape, index):
        if pairs == 2:
            return [(a, shape, lambda i, me: index(0, i, me)) for a in arrays]
        return [(arrays[0], shape, lambda i, me, m=m: index(m, i, me)) for m in range(pairs)]

    def sides_of(arrays, part=0):
        return runs(arrays, (width, rows), lambda m, i, me: (part, m))

    def ring_of(products, steps, block, stages):
        stages = ring_stages(stages)
        parts = weight_parts(scalars, products, steps, block, members, stages[0])
        return Ring(scalars, parts, stages)

    x_first, y_first = [(0,), (1,), (2,), (3,)], [(1,), (0,), (2,), (3,)]

    def feed_ring(part, b, stages):
        b_runs = [(b, (rows, block), lambda i, me, m=m: (m, i)) for m in range(pairs)]
        return ring_of([(sides_of(turned, part), b_runs)], slice_width // block, block, stages)

    ring_out = feed_ring(1, hidden, x_first)
    ring_hid = feed_ring(0, grad_pre, y_first)

    query_rows = rows // parts
    part = jnp.stack([me[0] % parts, me[0]]).astype(jnp.int32)
    from_first, head_grad, head_delta, probs, _ = forward_head(
        at_head,
        part,
        rows,
        query_rows,
        (*ring_out.sent, *ring_hid.sent, *[a for a, _ in (*feeds, *grads)], *turned, *one_t),
    )
    back_first = lax.all_to_all(from_first, "seq", 0, 0, tiled=True)
    from_second, after_second = backward_head(
        scalars, at_head, head_grad, head_delta, probs, rows, query_rows, ()
    )
    from_second = after(from_second, *ring_out.came, *ring_hid.came)
    back_second = lax.all_to_all(from_second, "seq", 0, 0, tiled=True)
    x_first, y_first = [(0,), (1,), (2, 3)], [(1,), (0,), (2, 3)]
    split = pairs == 2 and parts == 1
    share = width // pairs

    def pieces_of(arrays):
        stacked = jnp.stack([a.reshape(rows, pairs, share) for a in arrays], 2)
        stacked = jnp.transpose(stacked, (1, 0, 2, 3)).reshape(pairs, rows, len(arrays) * share)
        if pairs == 2:
            mine = lax.dynamic_index_in_dim(stacked, pair_me, 0, False)
            return [mine, pair_swap(lax.dynamic_index_in_dim(stacked, 1 - pair_me, 0, False))]
        got = lax.all_to_all(stacked, "mlp", 0, 0, tiled=True)
        return [got.reshape(pairs * rows, len(arrays) * share)]

    if split:

        attended, grad_v, sent, own_a, own_v = regroup_once(
            back_first, None, scalars, (from_second,)
        )
        came = pair_swap(sent)
        for ring in (ring_out, ring_hid):
            ring.hold(sent)
            ring.step()
        v_parts, d_parts = weight_once(
            scalars,
            [*one_t, own_v, came, own_a, *cot_list],
            [
                ([((0, 1), (rows_run(2, 0, share), rows_run(3, width, share)), True)], (0,)),
                (
                    [((4, 3), (columns_run(5, share, None), columns_run(6, share, None)), False)],
                    (1,),
                ),
            ],
            width,
            share,
            members,
            (0, 1),
        )
        grad_q, grad_k, sent, own_qk = regroup_once(
            back_second, table, scalars, (*v_parts, *d_parts)
        )
        came = pair_swap(sent)
        halves = [
            weight_once(
                scalars,
                [*one_t, own_qk, came, v_parts[p], d_parts[p]],
                [
                    (
                        [
                            ((0, 1), (columns_run(2, share, n), columns_run(3, share, n)), False),
                            (4 + n,),
                        ],
                        (n,),
                    )
                    for n in range(2)
                ],
                width,
                share,
                members,
                (p,),
            )
            for p in range(2)
        ]
        qv_parts, kd_parts = ([h[n][0] for h in halves] for n in range(2))
        ring_qv = Ring(scalars, qv_parts, x_first)
        ring_kd = Ring(scalars, kd_parts, y_first)
    else:
        for ring in (ring_out, ring_hid):
            ring.step()
        attended, grad_v, att_t = regroup(back_first, None, scalars, rows, query_rows, False)
        att_t = mlp_list(att_t, 1)
        grad_q, grad_k = regroup(back_second, table, scalars, rows, query_rows, False)
        pieces = [pieces_of([g]) for g in (grad_q, grad_v, grad_k)]
        q_runs, v_runs, k_runs = (
            runs(p, (rows, share), lambda m, i, me: (m, 0)) for p in pieces
        )
        cot_runs = runs(cot_list, (rows, share), lambda m, i, me: (m, me[1]))
        one = sides_of(one_t)
        ring_qv = ring_of([(one, q_runs), (one, v_runs)], 2, share, x_first)
        ring_kd = ring_of([(one, k_runs), (sides_of(att_t), cot_runs)], 2, share, y_first)

    ring_out.hold(*ring_kd.sent)
    ring_out.step(ring_hid)
    block_output, grad_input, vec, gm_bias, closed = close_layer(
        inputs,
        cot,
        (attend_gain, feed_gain, attention_out_bias, contract_bias),
        (grad_q, grad_k, grad_v),
        attended,
        query_key_value_weight,
        attention_out_weight,
        feeds,
        grads,
        scalars,
        ring_out.sent,
    )
    for ring in (ring_qv, ring_kd):
        ring.pass_on(closed[0])
    ring_out.came = [after(x, *ring_qv.sent, *ring_kd.sent) for x in ring_out.came]
    ring_out.pass_on(closed[0])

    bias_full = lax.dynamic_update_slice_in_dim(
        jnp.zeros((pairs * slice_width,), F32), grad_hid_bias[0], pair_me * slice_width, 0
    )
    vectors = [*[vec[r] for r in range(5)], gm_bias.reshape(-1), bias_full]
    packed = jnp.concatenate([v.reshape(members, pairs, -1) for v in vectors], -1)
    if pairs == 2:
        mine = lax.dynamic_index_in_dim(packed, pair_me, 1, False)
        other = lax.dynamic_index_in_dim(packed, 1 - pair_me, 1, False)
        packed = mine + pair_swap(after(other, *ring_out.sent))
    else:
        packed = lax.psum_scatter(packed, "mlp", scatter_dimension=1, tiled=False)
    ring_qv.step(ring_kd)
    packed = after(packed, *ring_qv.sent)
    packed = lax.all_to_all(packed, "seq", 0, 0, tiled=True)

    feed_total = ring_out.plain_total()
    out_weight = jnp.transpose(feed_total[:, :slice_width])
    hid_weight = feed_total[:, slice_width:]

    if pairs == 2:
        mine, other = ring_qv.total()
        packed = after(packed, other)
        merged, dense = vmem_call(
            place_kernel,
            [shape_of((own // pairs, 3 * width), F32), shape_of((own // pairs, width), F32)],
            scalars,
            [mine, pair_swap(other)],
            "place",
        )
    else:
        got = ring_qv.total([4 * share])[0].reshape(pairs, own // pairs, 4 * share)
        got = lax.all_to_all(got, "mlp", 0, 0, tiled=True)
        got = jnp.transpose(got.reshape(pairs, own // pairs, 4, share), (1, 2, 0, 3))
        merged = jnp.concatenate([got[:, n].reshape(-1, width) for n in (0, 2, 1)], -1)
        dense = got[:, 3].reshape(-1, width)
    packed = jnp.sum(packed, 0)
    outs, start = [], 0
    for v in vectors:
        size = v.shape[0] // (members * pairs)
        outs.append(lax.slice_in_dim(packed, start, start + size))
        start += size
    grad_gain_one, grad_shift_one, grad_dense_bias, grad_gain_two, grad_shift_two = outs[:5]
    grad_merged_bias, out_hid_bias = outs[5:]
    return (
        block_output.reshape(seq_count, rows, width),
        grad_input.reshape(seq_count, rows, width),
        grad_gain_one,
        grad_shift_one,
        merged,
        grad_merged_bias,
        dense,
        grad_dense_bias,
        grad_gain_two,
        grad_shift_two,
        hid_weight,
        out_hid_bias,
        out_weight,
        grad_dense_bias,
    )


def solution(mesh):
    in_specs = (
        P("mlp", "seq", None),
        P("mlp", "seq", None),
        P(),
        P(),
        P(),
        P(),
        P(),
        P(),
        P(),
        P(),
        P(None, "mlp"),
        P("mlp"),
        P("mlp", None),
        P(),
    )
    out_specs = (
        P("mlp", "seq", None),
        P("mlp", "seq", None),
        P(("seq", "mlp")),
        P(("seq", "mlp")),
        P(("seq", "mlp"), None),
        P(("seq", "mlp")),
        P(("seq", "mlp"), None),
        P(("seq", "mlp")),
        P(("seq", "mlp")),
        P(("seq", "mlp")),
        P("seq", "mlp"),
        P(("seq", "mlp")),
        P("mlp", "seq"),
        P(("seq", "mlp")),
    )
    return jax.shard_map(
        per_device, mesh=mesh, in_specs=in_specs, out_specs=out_specs, check_vma=False
    )
```

```python
from functools import partial

import jax
import jax.numpy as jnp
from jax import lax
from jax.experimental import pallas as pl
from jax.experimental.pallas import tpu as pltpu
from jax.sharding import PartitionSpec as P

HEADS = 16
HEAD = 64
ROT = 16
PAIR = 2 * HEAD
EPS = 1e-05
NEGATIVE = -1e30

F32 = jnp.float32
BF16 = jnp.bfloat16
NT = (((1,), (1,)), ((), ()))
NN = (((1,), (0,)), ((), ()))
VMEM_LIMIT = 60 * 1024 * 1024
COST_SHARE = 16


def dot32(a, b, dims=NN):
    return lax.dot_general(a, b, dims, preferred_element_type=F32)


def cost(flops, bytes_accessed, transcendentals, share=COST_SHARE):
    return pl.CostEstimate(
        flops=flops // share,
        bytes_accessed=bytes_accessed // share,
        transcendentals=transcendentals // share,
    )


def shape_of(shape, dtype):
    return jax.ShapeDtypeStruct(shape, dtype)


def fixed(shape):
    return pl.BlockSpec(shape, lambda *i: (0,) * len(shape))


def vector_row(ref):
    return ref[...].astype(F32).reshape(1, -1)


def two_heads(pair_a, pair_b, low):
    even = jnp.where(low, pair_a, pltpu.roll(pair_b, HEAD, 1))
    odd = jnp.where(low, pltpu.roll(pair_a, HEAD, 1), pair_b)
    return (even, odd)


def rotary_lanes(first, rows, inverse):
    shape = (rows, PAIR)
    lane = lax.broadcasted_iota(jnp.int32, shape, 1) % HEAD
    position = (lax.broadcasted_iota(jnp.int32, shape, 0) + first).astype(F32)
    angle = position * inverse
    cosine, sine = jnp.cos(angle), jnp.sin(angle)
    zero = jnp.zeros_like(sine)
    return (
        jnp.where(lane < ROT, cosine, 1.0),
        jnp.where(lane < ROT // 2, -sine, zero),
        jnp.where((lane >= ROT // 2) & (lane < ROT), sine, zero),
    )


def rotate_lanes(x, cosine, to_first, to_second):
    ahead = pltpu.roll(x, PAIR - ROT // 2, 1)
    behind = pltpu.roll(x, ROT // 2, 1)
    return x * cosine + ahead * to_first + behind * to_second


def unit_rows(x):
    average = jnp.mean(x, -1, keepdims=True)
    centred = x - average
    spread = jnp.mean(centred * centred, -1, keepdims=True)
    root = lax.rsqrt(spread + EPS)
    return (centred * root, root)


def open_kernel(
    first_ref, x_ref, g_ref, inv_ref, ga_ref, sa_ref, gf_ref, sf_ref, b_ref,
    wq_ref, wk_ref, wv_ref, wo_ref,
    out_ref, n1_ref, n2_ref, table_ref, one_ref, turned_ref, bias_ref, *, parts,
):
    rows, width = x_ref.shape
    step = pl.program_id(0)
    cols = wq_ref.shape[1]

    @pl.when(step == 0)
    def _():
        unit, root = unit_rows(x_ref[...].astype(F32))
        n1_ref[...] = (unit * vector_row(ga_ref) + vector_row(sa_ref)).astype(BF16)
        n2_ref[...] = (unit * vector_row(gf_ref) + vector_row(sf_ref)).astype(BF16)
        for t, table in enumerate(rotary_lanes(first_ref[0], rows, inv_ref[...])):
            table_ref[t] = table
        bias_ref[...] = vector_row(b_ref)

    for n, (source, target) in enumerate(
        (
            (n1_ref, one_ref),
            (n2_ref, turned_ref.at[:width]),
            (g_ref, turned_ref.at[width:]),
        )
    ):

        @pl.when(step == pl.num_programs(0) - 1)
        def _(source=source, target=target):
            target[...] = jnp.transpose(source[...])

    def bias(third):
        return bias_ref[:, pl.ds(pl.multiple_of(third * width + step * cols, cols), cols)]

    normed = n1_ref[...]
    query = dot32(normed, wq_ref[...]) + bias(0)
    key = dot32(normed, wk_ref[...]) + bias(1)
    value = dot32(normed, wv_ref[...]) + bias(2)
    grad = dot32(g_ref[...], wo_ref[...], NT)
    tables = (table_ref[0], table_ref[1], table_ref[2])
    low = lax.broadcasted_iota(jnp.int32, (rows, PAIR), 1) < HEAD
    query_rows = rows // parts
    for c in range(cols // PAIR):
        cut = slice(c * PAIR, (c + 1) * PAIR)
        kv = two_heads(rotate_lanes(key[:, cut], *tables), value[:, cut], low)
        qg = two_heads(rotate_lanes(query[:, cut], *tables), grad[:, cut], low)
        for h in range(2):
            kv_h, qg_h = kv[h].astype(BF16), qg[h].astype(BF16)
            for p in range(parts):
                out_ref[2 * c + h, p, :rows] = kv_h
                out_ref[2 * c + h, p, rows:] = qg_h[p * query_rows : (p + 1) * query_rows]


def open_layer(x, g, first, vectors, weight, bias, out_weight, parts):
    rows, width = x.shape
    steps = 2
    cols = width // steps
    per = HEADS // steps
    inverse = 10000.0 ** (-(jnp.arange(ROT // 2, dtype=F32) * 2.0 / ROT))
    inverse = jnp.tile(inverse, PAIR // (ROT // 2)).reshape(1, PAIR)
    chunk = rows + rows // parts

    def third(t):
        return pl.BlockSpec((width, cols), lambda i: (0, t * steps + i))

    out, *others = pl.pallas_call(
        partial(open_kernel, parts=parts),
        grid=(steps,),
        out_shape=(
            shape_of((HEADS, parts, chunk, PAIR), BF16),
            shape_of((rows, width), BF16),
            shape_of((rows, width), BF16),
            shape_of((3, rows, PAIR), F32),
            shape_of((width, rows), BF16),
            shape_of((2 * width, rows), BF16),
        ),
        in_specs=[
            pl.BlockSpec(memory_space=pltpu.SMEM),
            fixed((rows, width)),
            fixed((rows, width)),
            fixed((1, PAIR)),
            *[fixed((width,))] * 4,
            fixed((3 * width,)),
            third(0), third(1), third(2),
            pl.BlockSpec((cols, width), lambda i: (i, 0)),
        ],
        out_specs=(
            pl.BlockSpec((per, parts, chunk, PAIR), lambda i: (i, 0, 0, 0)),
            fixed((rows, width)),
            fixed((rows, width)),
            fixed((3, rows, PAIR)),
            fixed((width, rows)),
            fixed((2 * width, rows)),
        ),
        scratch_shapes=[pltpu.VMEM((1, 3 * width), F32)],
        cost_estimate=cost(
            flops=8 * rows * width * width,
            bytes_accessed=8 * width * width + 18 * rows * width,
            transcendentals=0,
        ),
        compiler_params=pltpu.CompilerParams(vmem_limit_bytes=VMEM_LIMIT),
        name="open_layer",
    )(first, x, g, inverse, *vectors, bias, weight, weight, weight, out_weight)
    return (out.reshape(HEADS * parts, chunk, PAIR), *others)


ROW_GROUP = 4
ONES = 16
CUTS = 4
KEY_GROUP = 2


def first_tile(i):
    return i * (i + 1)


def column_chunks(x):
    return [x[:, c : c + 128] for c in range(0, x.shape[1], 128)]


def forward_kernel(
    part_ref, x_ref, y_ref, g_ref, d_ref, p_hbm, after_ref,
    s_ref, p_ref, dv_ref, vt_ref, mx_ref, top_ref, acc_ref, sem,
    *, key_rows, query_rows,
):
    after_ref[0] = part_ref[1]
    blocks = x_ref.shape[0] // ROW_GROUP
    keys, rows = KEY_GROUP * key_rows, ROW_GROUP * query_rows
    low = lax.broadcasted_iota(jnp.int32, (rows, PAIR), 1) < HEAD
    key_low = lax.broadcasted_iota(jnp.int32, (keys, PAIR), 1) < HEAD
    cuts = [slice(r, r + rows // CUTS) for r in range(0, rows, rows // CUTS)]

    def key_value(j):
        return x_ref[pl.ds(j * KEY_GROUP, KEY_GROUP), :key_rows, :].reshape(keys, PAIR)

    def query_rows_of(i):
        return x_ref[pl.ds(i * ROW_GROUP, ROW_GROUP), key_rows:, :].reshape(rows, PAIR)

    def query_of(i):
        return jnp.where(low, query_rows_of(i).astype(F32) * HEAD**-0.5, 0.0).astype(BF16)

    def copy_out(i, j):
        return pltpu.make_async_copy(p_ref.at[j], p_hbm.at[first_tile(i) + j], sem.at[j])

    def ones_and_values(j, unused):
        turned = jnp.transpose(key_value(j).astype(F32))
        vt_ref[j, :HEAD] = turned[HEAD:].astype(BF16)
        vt_ref[j, HEAD:] = jnp.ones((ONES, keys), BF16)
        return unused

    def raise_max(cut, s):
        mx = mx_ref[cut]
        for chunk in column_chunks(s):
            mx = jnp.maximum(mx, chunk)
        mx_ref[cut] = mx

    def last_scores(i, query):
        row = lax.broadcasted_iota(jnp.int32, (rows, keys), 0)
        col = lax.broadcasted_iota(jnp.int32, (rows, keys), 1)
        row_pos = (row // query_rows) * key_rows + row % query_rows + part_ref[0] * query_rows
        for d in range(ROW_GROUP // KEY_GROUP):
            j = 2 * i + d
            s = dot32(query, key_value(j), NT)
            s = jnp.where(col + d * keys <= row_pos, s, NEGATIVE)
            s_ref[j] = s
            raise_max(slice(None), s)

    def tile(i, j, query, grad_t):
        kv = key_value(j)
        grads = None
        for cut in cuts:
            if grad_t is not None:
                part = dot32(grad_t[:, cut], p_ref[j, cut])
                grads = part if grads is None else grads + part
            top = top_ref[cut]
            p = jnp.concatenate(
                [jnp.exp(c - top) for c in column_chunks(s_ref[j, cut])], 1
            ).astype(BF16)
            p_ref[j, cut] = p
            acc_ref[:, cut] += dot32(vt_ref[j], p, NT)
            if query is not None:
                s = dot32(query[cut], kv, NT)
                s_ref[j, cut] = s
                raise_max(cut, s)
        if grads is not None:
            dv_ref[j, HEAD:] += grads
        copy_out(i, j).start()

    def block(i, grad_t, ahead):
        query = query_of(i + 1) if ahead else None
        top_ref[...] = jnp.broadcast_to(jnp.max(mx_ref[...], -1, keepdims=True), (rows, PAIR))
        mx_ref[...] = jnp.full_like(mx_ref, NEGATIVE)
        acc_ref[...] = jnp.zeros_like(acc_ref)

        def step(j, unused):
            copy_out(i - 1, j).wait()
            tile(i, j, query, grad_t)
            return unused

        lax.fori_loop(0, 2 * i, step, 0)
        for d in range(2):
            tile(i, 2 * i + d, query, None)
        if ahead:
            last_scores(i + 1, query)
        inverse = 1.0 / acc_ref[HEAD : HEAD + 1]
        attended_t = acc_ref[:HEAD] * inverse
        rows_t = jnp.transpose(query_rows_of(i).astype(F32))
        grad_t = (rows_t[HEAD:] * inverse).astype(BF16)
        both = jnp.transpose(jnp.concatenate([attended_t, grad_t.astype(F32)], 0))
        delta = jnp.sum(grad_t.astype(F32) * attended_t, 0, keepdims=True)
        d_ref[i] = jnp.transpose(jnp.broadcast_to(delta, (PAIR, rows)))
        g_ref[i] = jnp.where(low, 0.0, both).astype(BF16)
        here = pl.ds(i * ROW_GROUP, ROW_GROUP)
        y_ref[here, :query_rows, :] = both.astype(BF16).reshape(ROW_GROUP, query_rows, PAIR)
        if query_rows < key_rows:
            y_ref[here, query_rows:, :] = jnp.zeros(
                (ROW_GROUP, key_rows - query_rows, PAIR), BF16
            )
        return grad_t

    dv_ref[...] = jnp.zeros_like(dv_ref)
    lax.fori_loop(0, 2 * blocks, ones_and_values, 0)
    mx_ref[...] = jnp.full_like(mx_ref, NEGATIVE)
    last_scores(0, query_of(0))
    grad_t = lax.fori_loop(
        0, blocks - 1, lambda i, g: block(i, g, True), jnp.zeros((HEAD, rows), BF16)
    )
    grad_t = block(jnp.int32(blocks - 1), grad_t, False)

    def finish(j, unused):
        here = pl.ds(j * KEY_GROUP, KEY_GROUP)
        held = y_ref[here].reshape(keys, PAIR)
        dv_ref[j, HEAD:] += dot32(grad_t, p_ref[j])
        grads = jnp.transpose(dv_ref[j]).astype(BF16)
        y_ref[here] = jnp.where(key_low, held, grads).reshape(KEY_GROUP, key_rows, PAIR)
        copy_out(blocks - 1, j).wait()
        return unused

    lax.fori_loop(0, 2 * blocks, finish, 0)


def backward_kernel(
    me_ref, x_ref, g_ref, d_ref, p_hbm, y_ref, after_ref,
    p_ref, dp0_ref, dp1_ref, dk_ref, acc_ref, sem,
    *, key_rows, query_rows,
):
    after_ref[0] = me_ref[0]
    blocks = x_ref.shape[0] // ROW_GROUP
    keys, rows = KEY_GROUP * key_rows, ROW_GROUP * query_rows
    tiles = first_tile(blocks)
    slots = p_ref.shape[0]
    low = lax.broadcasted_iota(jnp.int32, (rows, PAIR), 1) < HEAD
    dp_refs = (dp0_ref, dp1_ref)

    def copy_in(t):
        return pltpu.make_async_copy(p_hbm.at[t], p_ref.at[t % slots], sem.at[t % slots])

    def refill(t):
        @pl.when(t + slots < tiles)
        def _():
            copy_in(t + slots).start()

    for t in range(min(slots, tiles)):
        copy_in(t).start()
    dk_ref[...] = jnp.zeros_like(dk_ref)

    def key_value(j):
        return x_ref[pl.ds(j * KEY_GROUP, KEY_GROUP), :key_rows, :].reshape(keys, PAIR)

    def one_block(i, unused):
        here = pl.ds(i * ROW_GROUP, ROW_GROUP)
        query = x_ref[here, key_rows:, :].reshape(rows, PAIR).astype(F32) * HEAD**-0.5
        query_t = jnp.transpose(query)[:HEAD].astype(BF16)
        grad = g_ref[i]
        first = first_tile(i)
        acc_ref[...] = jnp.zeros_like(acc_ref)

        def raise_probs(j, side):
            dp_refs[side][...] = dot32(grad, key_value(j), NT)

        def tile(j, side):
            delta = d_ref[i]
            p = column_chunks(p_ref[(first + j) % slots].astype(F32))
            dp = column_chunks(dp_refs[side][...])
            ds = jnp.concatenate([a * (b - delta) for a, b in zip(p, dp)], 1).astype(BF16)
            dk_ref[j, HEAD:] += dot32(query_t, ds)
            acc_ref[...] += dot32(ds, key_value(j))

        def two_tiles(m, unused, more=True):
            j = 2 * m
            copy_in(first + j).wait()
            copy_in(first + j + 1).wait()
            raise_probs(j + 1, 1)
            tile(j, 0)
            if more:
                raise_probs(j + 2, 0)
            tile(j + 1, 1)
            refill(first + j)
            refill(first + j + 1)
            return unused

        raise_probs(0, 0)
        lax.fori_loop(0, i, two_tiles, 0)
        two_tiles(i, 0, False)
        done = jnp.where(low, acc_ref[...] * HEAD**-0.5, 0.0).astype(BF16)
        y_ref[here, :query_rows, :] = done.reshape(ROW_GROUP, query_rows, PAIR)
        if query_rows < key_rows:
            y_ref[here, query_rows:, :] = jnp.zeros(
                (ROW_GROUP, key_rows - query_rows, PAIR), BF16
            )
        return unused

    lax.fori_loop(0, blocks, one_block, 0)
    key_low = lax.broadcasted_iota(jnp.int32, (keys, PAIR), 1) < HEAD

    def finish(j, unused):
        here = pl.ds(j * KEY_GROUP, KEY_GROUP)
        held = y_ref[here].reshape(keys, PAIR)
        grads = jnp.transpose(dk_ref[j]).astype(BF16)
        y_ref[here] = jnp.where(key_low, held, grads).reshape(KEY_GROUP, key_rows, PAIR)
        return unused

    lax.fori_loop(0, 2 * blocks, finish, 0)


def head_sizes(x, key_rows, query_rows):
    count = x.shape[0]
    blocks = count // ROW_GROUP
    return count, blocks, KEY_GROUP * key_rows, ROW_GROUP * query_rows


def forward_head(x, part, key_rows, query_rows, behind):
    count, blocks, keys, rows = head_sizes(x, key_rows, query_rows)
    tiles = first_tile(blocks)
    vmem = pl.BlockSpec(memory_space=pltpu.VMEM)
    return pl.pallas_call(
        without(
            partial(forward_kernel, key_rows=key_rows, query_rows=query_rows), 2, len(behind)
        ),
        out_shape=(
            shape_of((count, key_rows, PAIR), BF16),
            shape_of((blocks, rows, PAIR), BF16),
            shape_of((blocks, rows, PAIR), F32),
            shape_of((tiles, rows, keys), BF16),
            shape_of((1,), jnp.int32),
        ),
        in_specs=[pl.BlockSpec(memory_space=pltpu.SMEM), vmem]
        + [pl.BlockSpec(memory_space=pl.ANY)] * len(behind),
        out_specs=(
            vmem, vmem, vmem, pl.BlockSpec(memory_space=pl.ANY),
            pl.BlockSpec(memory_space=pltpu.SMEM),
        ),
        scratch_shapes=[
            pltpu.VMEM((2 * blocks, rows, keys), F32),
            pltpu.VMEM((2 * blocks, rows, keys), BF16),
            pltpu.VMEM((2 * blocks, PAIR, keys), F32),
            pltpu.VMEM((2 * blocks, HEAD + ONES, keys), BF16),
            pltpu.VMEM((rows, PAIR), F32),
            pltpu.VMEM((rows, PAIR), F32),
            pltpu.VMEM((HEAD + ONES, rows), F32),
            pltpu.SemaphoreType.DMA((2 * blocks,)),
        ],
        cost_estimate=cost(
            flops=tiles * rows * keys * 2 * 256 * 3,
            bytes_accessed=4 * x.size + 2 * tiles * rows * keys,
            transcendentals=tiles * rows * keys,
            share=1,
        ),
        compiler_params=pltpu.CompilerParams(vmem_limit_bytes=VMEM_LIMIT),
        name="forward_head",
    )(part, x, *behind)


def backward_head(scalars, x, grad, delta, probs, key_rows, query_rows, behind):
    count, blocks, keys, rows = head_sizes(x, key_rows, query_rows)
    tiles = first_tile(blocks)
    slots = 6
    vmem = pl.BlockSpec(memory_space=pltpu.VMEM)
    return pl.pallas_call(
        without(
            partial(backward_kernel, key_rows=key_rows, query_rows=query_rows), 5, len(behind)
        ),
        out_shape=(shape_of((count, key_rows, PAIR), BF16), shape_of((1,), jnp.int32)),
        in_specs=[pl.BlockSpec(memory_space=pltpu.SMEM), vmem, vmem, vmem]
        + [pl.BlockSpec(memory_space=pl.ANY)] * (1 + len(behind)),
        out_specs=(vmem, pl.BlockSpec(memory_space=pltpu.SMEM)),
        scratch_shapes=[
            pltpu.VMEM((slots, rows, keys), BF16),
            pltpu.VMEM((rows, keys), F32),
            pltpu.VMEM((rows, keys), F32),
            pltpu.VMEM((2 * blocks, PAIR, keys), F32),
            pltpu.VMEM((rows, PAIR), F32),
            pltpu.SemaphoreType.DMA((slots,)),
        ],
        cost_estimate=cost(
            flops=tiles * rows * keys * 2 * 256 * 3,
            bytes_accessed=4 * x.size + 2 * tiles * rows * keys,
            transcendentals=0,
            share=1,
        ),
        compiler_params=pltpu.CompilerParams(vmem_limit_bytes=VMEM_LIMIT),
        name="backward_head",
    )(scalars, x, grad, delta, probs, *behind)


def feed_kernel(*refs, count, keep):
    rows_refs, cot_refs = refs[:count], refs[count : 2 * count]
    w1_ref, b1_ref, w2_ref = refs[2 * count : 2 * count + 3]
    hid_ref, gpre_ref, gb_ref = refs[2 * count + 3 : 2 * count + 6]
    outs = refs[2 * count + 6 : -2]
    out_acc, grad_acc = refs[-2:]
    step = pl.program_id(0)

    @pl.when(step == 0)
    def _():
        out_acc[...] = jnp.zeros_like(out_acc)
        grad_acc[...] = jnp.zeros_like(grad_acc)

    bias = b1_ref[...]
    sums = jnp.zeros_like(bias)
    rows = rows_refs[0].shape[0]
    for r in range(count):
        here = slice(r * rows, (r + 1) * rows)
        pre = dot32(rows_refs[r][...], w1_ref[...]) + bias
        grad = dot32(cot_refs[r][...], w2_ref[...], NT)
        cdf = 0.5 + 0.5 * lax.erf(pre * (0.5**0.5))
        density = jnp.exp(-0.5 * pre * pre) * 0.3989422804014327
        hidden = (pre * cdf).astype(BF16)
        grad_pre = (grad * (cdf + pre * density)).astype(BF16)
        hid_ref[here] = hidden
        gpre_ref[here] = grad_pre
        sums = sums + jnp.sum(grad_pre.astype(F32), 0, keepdims=True)
        out_acc[here] += dot32(hidden, w2_ref[...])
        grad_acc[here] += dot32(grad_pre, w1_ref[...], NT)
    gb_ref[...] = sums

    @pl.when(step == pl.num_programs(0) - 1)
    def _():
        if keep:
            own_out, own_grad, other = outs
            own_out[...] = out_acc[:rows]
            own_grad[...] = grad_acc[:rows]
            other[:rows] = out_acc[rows:].astype(BF16)
            other[rows:] = grad_acc[rows:].astype(BF16)
        else:
            outs[0][...] = out_acc[...].astype(BF16)
            outs[1][...] = grad_acc[...].astype(BF16)


def feed(rows_list, cot_list, w1, b1, w2):
    width, hidden = w1.shape
    count = len(rows_list)
    rows = rows_list[0].shape[0]
    total = rows * count
    block = 256
    keep = count > 1
    sides = (
        [(rows, F32), (rows, F32), (total, BF16)]
        if keep
        else [(total, BF16), (total, BF16)]
    )
    once = pl.Buffered(1)
    whole = pl.BlockSpec((rows, width), lambda i: (0, 0), pipeline_mode=once)
    return pl.pallas_call(
        partial(feed_kernel, count=count, keep=keep),
        grid=(hidden // block,),
        out_shape=(
            shape_of((total, hidden), BF16),
            shape_of((total, hidden), BF16),
            shape_of((1, hidden), F32),
            *[shape_of((r, width), d) for r, d in sides],
        ),
        in_specs=[
            *[whole] * (2 * count),
            pl.BlockSpec((width, block), lambda i: (0, i)),
            pl.BlockSpec((1, block), lambda i: (0, i)),
            pl.BlockSpec((block, width), lambda i: (i, 0)),
        ],
        out_specs=(
            pl.BlockSpec((total, block), lambda i: (0, i)),
            pl.BlockSpec((total, block), lambda i: (0, i)),
            pl.BlockSpec((1, block), lambda i: (0, i)),
            *[
                pl.BlockSpec((r, width), lambda i: (0, 0), pipeline_mode=once) for r, d in sides
            ],
        ),
        scratch_shapes=[pltpu.VMEM((total, width), F32), pltpu.VMEM((total, width), F32)],
        cost_estimate=cost(
            flops=8 * total * width * hidden,
            bytes_accessed=4 * width * hidden + 4 * total * hidden,
            transcendentals=2 * total * hidden,
        ),
        compiler_params=pltpu.CompilerParams(vmem_limit_bytes=VMEM_LIMIT),
        name="feed",
    )(*rows_list, *cot_list, w1, b1.astype(F32).reshape(1, hidden), w2)


def insert_bits(k, positions, values):
    for position, value in zip(positions, values):
        k = ((k >> position) << (position + 1)) + (value << position) + (k & ((1 << position) - 1))
    return k


def part_chunk(k, p, me, ring_bits, positions):
    values = [((me >> bit) & 1) ^ ((p >> n) & 1) for n, bit in enumerate(ring_bits)]
    return insert_bits(k, positions, values)


def weight_kernel(me_ref, *refs, bits, counts):
    total = sum(counts)
    a_refs, b_refs, parts = refs[:total], refs[total : 2 * total], refs[2 * total :]

    def product(first, count):
        b = jnp.concatenate([r[...] for r in b_refs[first : first + count]], 0)
        for p, ref in enumerate(parts):
            chunks, rows, cols = ref.shape
            a = []
            for k in range(chunks):
                start = part_chunk(k, p, me_ref[0], bits, bits) * rows
                here = pl.ds(pl.multiple_of(start, rows), rows)
                a.append(
                    jnp.concatenate([r[here, :] for r in a_refs[first : first + count]], 1)
                )
            ref[...] = dot32(jnp.concatenate(a, 0), b).astype(BF16).reshape(ref.shape)

    if len(counts) == 1:
        product(0, total)
    else:
        for n, count in enumerate(counts):
            pl.when(pl.program_id(0) == n)(partial(product, sum(counts[:n]), count))


def weight_parts(scalars, products, steps, block, members, bits):
    a_runs = [run for a, _ in products for run in a]
    b_runs = [run for _, b in products for run in b]
    width = a_runs[0][1][0]
    rows = width // members
    tokens = sum(shape[1] for _, shape, _ in products[0][0])
    count = 1 << len(bits)
    each = (members // count, rows, steps * block)
    out = pl.BlockSpec((members // count, rows, block), lambda i, me: (0, 0, i))
    return pl.pallas_call(
        partial(weight_kernel, bits=bits, counts=[len(a) for a, _ in products]),
        grid_spec=pltpu.PrefetchScalarGridSpec(
            num_scalar_prefetch=1,
            grid=(steps,),
            in_specs=[pl.BlockSpec(shape, index) for _, shape, index in (*a_runs, *b_runs)],
            out_specs=[out] * count,
        ),
        out_shape=[shape_of(each, BF16)] * count,
        cost_estimate=cost(
            flops=2 * width * tokens * steps * block,
            bytes_accessed=2 * width * tokens + 2 * (width + tokens) * steps * block,
            transcendentals=0,
        ),
        compiler_params=pltpu.CompilerParams(vmem_limit_bytes=VMEM_LIMIT),
        name="weight_parts",
    )(scalars, *[array for array, _, _ in (*a_runs, *b_runs)])


def weight_once_kernel(me_ref, *refs, products, operands, only):
    arrays, outs = refs[:operands], refs[operands:]
    at = 0
    for blocks, bits in products:
        parts = outs[at : at + len(only)]
        at += len(parts)
        cols = parts[0].shape[2] // len(blocks)
        for n, block in enumerate(blocks):
            here = slice(n * cols, (n + 1) * cols)
            if isinstance(block[0], int):
                for ref, source in zip(parts, block):
                    ref[:, :, here] = arrays[source][...]
                continue
            a_runs, b_runs, turned = block
            b = jnp.concatenate([run(arrays, me_ref) for run in b_runs], 1 if turned else 0)
            for p, ref in zip(only, parts):
                chunks, rows, _ = ref.shape
                a = []
                for k in range(chunks):
                    start = part_chunk(k, p, me_ref[0], bits, bits) * rows
                    lines = pl.ds(pl.multiple_of(start, rows), rows)
                    a.append(jnp.concatenate([arrays[m][lines, :] for m in a_runs], 1))
                product = dot32(jnp.concatenate(a, 0), b, NT if turned else NN)
                ref[:, :, here] = product.astype(BF16).reshape(chunks, rows, cols)


def rows_run(n, first, count):
    return lambda arrays, me_ref: arrays[n][first : first + count, :]


def columns_run(n, cols, block):
    if block is not None:
        return lambda arrays, me_ref: arrays[n][:, block * cols : (block + 1) * cols]
    return lambda arrays, me_ref: arrays[n][:, pl.ds(pl.multiple_of(me_ref[1] * cols, cols), cols)]


def weight_once(scalars, arrays, products, width, cols, members, only, behind=()):
    each = [
        shape_of((members // 2, width // members, cols * len(blocks)), BF16)
        for blocks, bits in products
        for _ in only
    ]
    outs = vmem_call(
        partial(weight_once_kernel, products=products, operands=len(arrays), only=only),
        each,
        scalars,
        arrays,
        "weight_once",
        behind,
    )
    return outs[: len(only)], outs[len(only) :]


def column_sums(refs, counts):
    groups, start = [], 0
    for count in counts:
        groups.append(refs[start : start + count])
        start += count

    def total(group, c):
        value = group[0][c].astype(F32)
        for ref in group[1:]:
            value = value + ref[c].astype(F32)
        return value

    return [partial(total, group) for group in groups]


def add_kernel(me_ref, *refs, counts, bits, positions, only):
    ins, outs = refs[: sum(counts)], refs[sum(counts) :]
    at = 0
    for group, total in zip(counts, column_sums(ins, counts)):
        cols = ins[0].shape[2]
        for p, ref in zip(only, outs):
            for k in range(ref.shape[0]):
                c = part_chunk(k, p, me_ref[0], bits, positions)
                ref[k, :, at : at + cols] = total(c).astype(BF16)
        at += cols
        ins = ins[group:]


def last_kernel(me_ref, *refs, count, form):
    value = column_sums(refs[:count], [count])[0](0)
    outs = refs[count:]
    if form == "pair":
        half = value.shape[0] // 2
        first = me_ref[1] == 0
        outs[0][...] = jnp.where(first, value[:half], value[half:])
        outs[1][...] = jnp.where(first, value[half:], value[:half]).astype(BF16)
    else:
        at = 0
        for ref in outs:
            ref[...] = value[:, at : at + ref.shape[1]]
            at += ref.shape[1]


def without(kernel, first, count):
    if not count:
        return kernel
    return lambda *refs: kernel(*refs[:first], *refs[first + count :])


def vmem_call(kernel, out_shape, scalars, arrays, name, behind=()):
    vmem = pl.BlockSpec(memory_space=pltpu.VMEM)
    size = sum(a.size for a in arrays)
    return pl.pallas_call(
        without(kernel, 1 + len(arrays), len(behind)),
        in_specs=[pl.BlockSpec(memory_space=pltpu.SMEM)]
        + [vmem] * len(arrays)
        + [pl.BlockSpec(memory_space=pl.ANY)] * len(behind),
        out_specs=[
            pl.BlockSpec(memory_space=pltpu.SMEM) if o.dtype == jnp.int32 else vmem
            for o in out_shape
        ],
        out_shape=out_shape,
        cost_estimate=cost(flops=size, bytes_accessed=3 * size, transcendentals=0),
        compiler_params=pltpu.CompilerParams(vmem_limit_bytes=VMEM_LIMIT),
        name=name,
    )(scalars, *arrays, *behind)


def seq_move(x, mask):
    members = lax.axis_size("seq")
    return lax.ppermute(x, "seq", [(s, s ^ mask) for s in range(members)])


def ring_stages(stages):
    bits = lax.axis_size("seq").bit_length() - 1
    named = [b for stage in stages for b in stage]
    stages = [tuple(b for b in stage if b < bits) for stage in stages]
    stages[-1] = stages[-1] + tuple(b for b in range(bits) if b not in named)
    return [stage for stage in stages if stage]


class Ring:
    def __init__(self, scalars, parts, stages):
        self.scalars, self.stages, self.behind = scalars, list(stages), ()
        self.me = scalars[0]
        self.left = sorted(b for stage in stages for b in stage)
        self.travel(parts)

    def travel(self, parts):
        stage = self.stages.pop(0)
        self.left = [b for b in self.left if b not in stage]
        self.keep, self.sent = parts[0], parts[1:]
        self.came = [
            seq_move(part, sum(1 << b for n, b in enumerate(stage) if (p >> n) & 1))
            for p, part in enumerate(parts)
            if p
        ]

    def hold(self, *others):
        self.behind = others

    def step(self, *others, apart=False):
        stage = self.stages[0]
        positions = [self.left.index(b) for b in stage]
        rings = (self, *others)
        chunks, rows = self.keep.shape[:2]
        cols = sum(ring.keep.shape[2] for ring in rings)
        count = 1 << len(stage)
        arrays = [[ring.keep, *ring.came] for ring in rings]

        def parts(only):
            return vmem_call(
                partial(
                    add_kernel,
                    counts=[len(a) for a in arrays],
                    bits=stage,
                    positions=positions,
                    only=only,
                ),
                [shape_of((chunks // count, rows, cols), BF16)] * len(only),
                self.scalars,
                [a for group in arrays for a in group],
                "add_parts",
                self.behind,
            )

        if apart:
            sent = parts(range(1, count))
            self.travel([*parts((0,)), *sent])
        else:
            self.travel(parts(range(count)))
        self.behind = ()

    def pass_on(self, me):
        stage = self.stages[0]
        bits = self.left
        shape = self.keep.shape[1:]
        arrays = [a.reshape((2,) * len(bits) + shape) for a in (self.keep, *self.came)]
        parts = []
        for p in range(1 << len(stage)):
            total = None
            for a in arrays:
                for n, bit in reversed(list(enumerate(stage))):
                    axis = len(bits) - 1 - bits.index(bit)
                    index = ((me >> bit) & 1) ^ ((p >> n) & 1)
                    a = lax.dynamic_index_in_dim(a, index, axis, True)
                a = a.reshape((-1,) + shape).astype(F32)
                total = a if total is None else total + a
            parts.append(total.astype(BF16))
        self.travel(parts)

    def plain_total(self):
        return sum(a[0].astype(F32) for a in (self.keep, *self.came))

    def total(self, widths=None):
        while self.stages:
            self.step()
        rows, cols = self.keep.shape[1:]
        shapes = (
            [shape_of((rows, w), F32) for w in widths]
            if widths
            else [shape_of((rows // 2, cols), F32), shape_of((rows // 2, cols), BF16)]
        )
        arrays = [self.keep, *self.came]
        return vmem_call(
            partial(last_kernel, count=len(arrays), form="rows" if widths else "pair"),
            shapes,
            self.scalars,
            arrays,
            "last_sum",
        )


def regroup_kernel(me_ref, back_ref, *refs, key_rows, query_rows, turned):
    heads, parts = back_ref.shape[:2]
    low = lax.broadcasted_iota(jnp.int32, (key_rows, PAIR), 1) < HEAD
    if turned:
        one_ref, two_ref, one_t_ref, *sides = refs
    else:
        table_ref, one_ref, two_ref, *sides = refs
        tables = (table_ref[0], -table_ref[1], -table_ref[2])
    first = pl.program_id(0) == 0
    for t in range(heads // 2):
        pair = []
        for h in (2 * t, 2 * t + 1):
            if parts == 1:
                pair.append(back_ref[h, 0].astype(F32))
                continue
            keys = sum(back_ref[h, p].astype(F32) for p in range(parts))
            queries = jnp.concatenate(
                [back_ref[h, p, :query_rows].astype(F32) for p in range(parts)], 0
            )
            pair.append(jnp.where(low, queries, keys))
        one, two = two_heads(pair[0], pair[1], low)
        if not turned:
            one, two = rotate_lanes(one, *tables), rotate_lanes(two, *tables)
        one, two = one.astype(BF16), two.astype(BF16)
        here = slice(t * PAIR, (t + 1) * PAIR)
        one_ref[:, here] = one
        two_ref[:, here] = two
        if turned:
            one_t_ref[here] = jnp.transpose(one)
        if sides:
            half = one_ref.shape[1]
            for n, value in enumerate((two,) if turned else (one, two)):
                there = slice(n * half + t * PAIR, n * half + (t + 1) * PAIR)
                pl.when(first)(partial(sides[1].__setitem__, (slice(None), there), value))
                pl.when(~first)(partial(sides[0].__setitem__, (slice(None), there), value))


def regroup(back, table, scalars, rows, query_rows, split):
    turned = table is None
    chunk = back.shape[1]
    parts = back.shape[0] // HEADS
    half = HEADS * HEAD // 2
    full = shape_of((rows, 2 * half), BF16)

    def side(i, me):
        return (i + me[1] + 1) % 2 if split else i

    whole = pl.BlockSpec((rows, half), lambda i, me: (0, side(i, me)))
    tall = pl.BlockSpec((half, rows), lambda i, me: (side(i, me), 0))
    cols = half * (1 if turned else 2)
    own = pl.BlockSpec((rows, cols), lambda i, me: (0, 0))
    return pl.pallas_call(
        partial(regroup_kernel, key_rows=rows, query_rows=query_rows, turned=turned),
        grid_spec=pltpu.PrefetchScalarGridSpec(
            num_scalar_prefetch=1,
            grid=(2,),
            in_specs=[
                pl.BlockSpec(
                    (HEADS // 2, parts, chunk, PAIR), lambda i, me: (side(i, me), 0, 0, 0)
                )
            ]
            + ([] if turned else [pl.BlockSpec(table.shape, lambda i, me: (0, 0, 0))]),
            out_specs=[whole, whole] + ([tall] if turned else []) + ([own, own] if split else []),
        ),
        out_shape=[full, full]
        + ([shape_of((2 * half, rows), BF16)] if turned else [])
        + ([shape_of((rows, cols), BF16)] * 2 if split else []),
        cost_estimate=cost(
            flops=back.size, bytes_accessed=4 * back.size, transcendentals=0
        ),
        name="regroup",
    )(
        scalars,
        back.reshape(HEADS, parts, chunk, PAIR),
        *([] if turned else [table]),
    )


def regroup_once_kernel(me_ref, *refs, turned):
    if turned:
        back_ref, att_ref, v_ref, send_ref, own_a_ref, own_v_ref = refs
    else:
        back_ref, table_ref, q_ref, k_ref, send_ref, own_ref = refs
        tables = (table_ref[0], -table_ref[1], -table_ref[2])
    heads, rows = back_ref.shape[:2]
    half = heads // 2
    low = lax.broadcasted_iota(jnp.int32, (rows, PAIR), 1) < HEAD
    for side in range(2):
        first = ((me_ref[1] + side) % 2) * half
        for t in range(half // 2):
            pair = [back_ref[first + 2 * t + n].astype(F32) for n in range(2)]
            one, two = two_heads(pair[0], pair[1], low)
            if not turned:
                one, two = rotate_lanes(one, *tables), rotate_lanes(two, *tables)
            one, two = one.astype(BF16), two.astype(BF16)
            start = pl.multiple_of((first // 2 + t) * PAIR, PAIR)
            here = pl.ds(start, PAIR)
            local = slice(t * PAIR, (t + 1) * PAIR)
            width = half * HEAD
            if turned:
                att_ref[:, here] = one
                v_ref[:, here] = two
                turned_one, turned_two = jnp.transpose(one), jnp.transpose(two)
                own_a_ref[here] = turned_one
                send_ref[here] = turned_one
                if side == 0:
                    own_v_ref[local] = turned_two
                else:
                    send_ref[2 * width + t * PAIR : 2 * width + (t + 1) * PAIR] = turned_two
            else:
                q_ref[:, here] = one
                k_ref[:, here] = two
                ref = own_ref if side == 0 else send_ref
                ref[:, local] = one
                ref[:, width + t * PAIR : width + (t + 1) * PAIR] = two


def regroup_once(back, table, scalars, behind=()):
    rows = back.shape[1]
    full = shape_of((rows, HEADS * HEAD), BF16)
    half = HEADS * HEAD // 2
    if table is None:
        sides = [
            shape_of((3 * half, rows), BF16),
            shape_of((2 * half, rows), BF16),
            shape_of((half, rows), BF16),
        ]
    else:
        sides = [shape_of((rows, 2 * half), BF16)] * 2
    return vmem_call(
        partial(regroup_once_kernel, turned=table is None),
        [full, full, *sides],
        scalars,
        [back] if table is None else [back, table],
        "regroup_once",
        behind,
    )


def close_kernel(
    x_ref, g_ref, ga_ref, gf_ref, bo_ref, bc_ref, gq_ref, gk_ref, gv_ref, att_ref,
    wq_ref, wk_ref, wv_ref, wo_ref, me_ref, *refs, sides,
):
    feeds, grads = refs[:sides], refs[sides : 2 * sides]
    out_ref, gin_ref, vec_ref, gb_ref, after_ref, out_acc, grad_acc = refs[2 * sides :]
    step = pl.program_id(0)
    for n in range(2):
        after_ref[n] = me_ref[n]

    @pl.when(step == 0)
    def _():
        out_acc[...] = jnp.zeros_like(out_acc)
        grad_acc[...] = jnp.zeros_like(grad_acc)

    out_acc[...] += dot32(att_ref[...], wo_ref[...])
    total = None
    for third, (g_third, w_ref) in enumerate(
        ((gq_ref, wq_ref), (gk_ref, wk_ref), (gv_ref, wv_ref))
    ):
        grad = g_third[...]
        part = dot32(grad, w_ref[...], NT)
        total = part if total is None else total + part
        gb_ref[third : third + 1] = jnp.sum(grad.astype(F32), 0, keepdims=True)
    grad_acc[...] += total

    @pl.when(step == pl.num_programs(0) - 1)
    def _():
        x = x_ref[...].astype(F32)
        g = g_ref[...].astype(F32)
        total = x + out_acc[...] + vector_row(bo_ref) + vector_row(bc_ref)
        for ref in feeds:
            total = total + ref[...].astype(F32)
        out_ref[...] = total.astype(BF16)
        unit, root = unit_rows(x)
        one = grad_acc[...]
        two = grads[0][...].astype(F32)
        for ref in grads[1:]:
            two = two + ref[...].astype(F32)
        down = one * vector_row(ga_ref) + two * vector_row(gf_ref)
        mean = jnp.mean(down, -1, keepdims=True)
        slope = jnp.mean(down * unit, -1, keepdims=True)
        gin_ref[...] = g + root * (down - mean - unit * slope)
        for r, rows in enumerate((one * unit, one, g, two * unit, two)):
            vec_ref[r : r + 1] = jnp.sum(rows, 0, keepdims=True)


def close_layer(x, g, vectors, gm, attended, weight, out_weight, feeds, grads, scalars, behind):
    rows, width = x.shape
    steps = 4
    cols = width // steps

    def third(t):
        return pl.BlockSpec((width, cols), lambda i: (0, t * steps + i))

    part = pl.BlockSpec((rows, cols), lambda i: (0, i))
    return pl.pallas_call(
        without(partial(close_kernel, sides=len(feeds)), 15 + 2 * len(feeds), len(behind)),
        grid=(steps,),
        out_shape=(
            shape_of((rows, width), BF16),
            shape_of((rows, width), F32),
            shape_of((5, width), F32),
            shape_of((3, width), F32),
            shape_of((2,), jnp.int32),
        ),
        in_specs=[
            fixed((rows, width)),
            fixed((rows, width)),
            *[fixed((width,))] * 4,
            part, part, part, part,
            third(0), third(1), third(2),
            pl.BlockSpec((cols, width), lambda i: (i, 0)),
            pl.BlockSpec(memory_space=pltpu.SMEM),
            *[
                pl.BlockSpec((rows, width), lambda i, n=n: (n, 0)) for _, n in (*feeds, *grads)
            ],
            *[pl.BlockSpec(memory_space=pl.ANY)] * len(behind),
        ],
        out_specs=(
            fixed((rows, width)),
            fixed((rows, width)),
            fixed((5, width)),
            pl.BlockSpec((3, cols), lambda i: (0, i)),
            pl.BlockSpec(memory_space=pltpu.SMEM),
        ),
        scratch_shapes=[pltpu.VMEM((rows, width), F32), pltpu.VMEM((rows, width), F32)],
        cost_estimate=cost(
            flops=8 * rows * width * width,
            bytes_accessed=8 * width * width + 24 * rows * width,
            transcendentals=0,
        ),
        compiler_params=pltpu.CompilerParams(vmem_limit_bytes=VMEM_LIMIT),
        name="close_layer",
    )(x, g, *vectors, *gm, attended, weight, weight, weight, out_weight, scalars, *[a for a, _ in (*feeds, *grads)], *behind)


def place_kernel(me_ref, own_ref, came_ref, merged_ref, dense_ref):
    half = dense_ref.shape[1] // 2
    for side, ref in enumerate((own_ref, came_ref)):
        at = ((me_ref[1] + side) % 2) * half
        for third, block in enumerate((0, 2, 1)):
            start = pl.multiple_of(third * 2 * half + at, half)
            value = ref[:, block * half : (block + 1) * half]
            merged_ref[:, pl.ds(start, half)] = value.astype(F32)
        dense_ref[:, pl.ds(pl.multiple_of(at, half), half)] = ref[:, 3 * half :].astype(F32)


def pair_swap(x):
    return lax.ppermute(x, "mlp", [(0, 1), (1, 0)])


def mlp_list(x, axis=0):
    if lax.axis_size("mlp") == 2:
        return [x, pair_swap(x)]
    return [lax.all_gather(x, "mlp", axis=axis, tiled=True)]


def after(value, *others):
    return lax.optimization_barrier((value, *others))[0]


def per_device(
    block_input,
    out_cotangent,
    attend_gain,
    attend_shift,
    query_key_value_weight,
    query_key_value_bias,
    attention_out_weight,
    attention_out_bias,
    feed_gain,
    feed_shift,
    expand_weight,
    expand_bias,
    contract_weight,
    contract_bias,
):
    seq_count, rows, width = block_input.shape
    members = lax.axis_size("seq")
    pairs = lax.axis_size("mlp")
    parts = members // HEADS
    own = width // members
    me = lax.axis_index("seq").astype(jnp.int32).reshape(1)
    pair_me = lax.axis_index("mlp")
    scalars = jnp.stack([me[0], pair_me.astype(jnp.int32)])
    inputs = block_input.reshape(rows, width)
    cot = out_cotangent.reshape(rows, width)

    outgoing, _, normed_two, table, one_t, turned = open_layer(
        inputs,
        cot,
        me * rows,
        (attend_gain, attend_shift, feed_gain, feed_shift),
        query_key_value_weight,
        query_key_value_bias,
        attention_out_weight,
        parts,
    )
    at_head = lax.all_to_all(outgoing, "seq", 0, 0, tiled=True)

    rows_list, cot_list = mlp_list(normed_two), mlp_list(cot)
    turned = mlp_list(turned, 1)
    one_t = mlp_list(one_t, 1)
    hidden, grad_pre, grad_hid_bias, *sides = feed(
        rows_list, cot_list, expand_weight, expand_bias, contract_weight
    )
    if pairs == 2:
        came = pair_swap(sides[2])
        feeds, grads = [(sides[0], 0), (came, 0)], [(sides[1], 0), (came, 1)]
    else:
        feeds, grads = (
            [(lax.psum_scatter(v, "mlp", scatter_dimension=0, tiled=True), 0)] for v in sides
        )
    slice_width = expand_weight.shape[1]
    block = min(512, slice_width)

    def runs(arrays, shape, index):
        if pairs == 2:
            return [(a, shape, lambda i, me: index(0, i, me)) for a in arrays]
        return [(arrays[0], shape, lambda i, me, m=m: index(m, i, me)) for m in range(pairs)]

    def sides_of(arrays, part=0):
        return runs(arrays, (width, rows), lambda m, i, me: (part, m))

    def ring_of(products, steps, block, stages):
        stages = ring_stages(stages)
        parts = weight_parts(scalars, products, steps, block, members, stages[0])
        return Ring(scalars, parts, stages)

    x_first, y_first = [(0,), (1,), (2,), (3,)], [(1,), (0,), (2,), (3,)]

    def feed_ring(part, b, stages):
        b_runs = [(b, (rows, block), lambda i, me, m=m: (m, i)) for m in range(pairs)]
        return ring_of([(sides_of(turned, part), b_runs)], slice_width // block, block, stages)

    ring_out = feed_ring(1, hidden, x_first)
    ring_hid = feed_ring(0, grad_pre, y_first)

    query_rows = rows // parts
    part = jnp.stack([me[0] % parts, me[0]]).astype(jnp.int32)
    from_first, head_grad, head_delta, probs, _ = forward_head(
        at_head,
        part,
        rows,
        query_rows,
        (*ring_out.sent, *ring_hid.sent, *[a for a, _ in (*feeds, *grads)], *turned, *one_t),
    )
    back_first = lax.all_to_all(from_first, "seq", 0, 0, tiled=True)
    from_second, after_second = backward_head(
        scalars, at_head, head_grad, head_delta, probs, rows, query_rows, ()
    )
    from_second = after(from_second, *ring_out.came, *ring_hid.came)
    back_second = lax.all_to_all(from_second, "seq", 0, 0, tiled=True)
    x_first, y_first = [(0,), (1,), (2, 3)], [(1,), (0,), (2, 3)]
    split = pairs == 2 and parts == 1
    share = width // pairs

    def pieces_of(arrays):
        stacked = jnp.stack([a.reshape(rows, pairs, share) for a in arrays], 2)
        stacked = jnp.transpose(stacked, (1, 0, 2, 3)).reshape(pairs, rows, len(arrays) * share)
        if pairs == 2:
            mine = lax.dynamic_index_in_dim(stacked, pair_me, 0, False)
            return [mine, pair_swap(lax.dynamic_index_in_dim(stacked, 1 - pair_me, 0, False))]
        got = lax.all_to_all(stacked, "mlp", 0, 0, tiled=True)
        return [got.reshape(pairs * rows, len(arrays) * share)]

    if split:

        attended, grad_v, sent, own_a, own_v = regroup_once(
            back_first, None, scalars, (from_second,)
        )
        came = pair_swap(sent)
        for ring in (ring_out, ring_hid):
            ring.hold(sent)
            ring.step(apart=True)
        v_parts, d_parts = weight_once(
            scalars,
            [*one_t, own_v, came, own_a, *cot_list],
            [
                ([((0, 1), (rows_run(2, 0, share), rows_run(3, width, share)), True)], (0,)),
                (
                    [((4, 3), (columns_run(5, share, None), columns_run(6, share, None)), False)],
                    (1,),
                ),
            ],
            width,
            share,
            members,
            (0, 1),
        )
        grad_q, grad_k, sent, own_qk = regroup_once(
            back_second, table, scalars, (*v_parts, *d_parts)
        )
        came = pair_swap(sent)
        halves = [
            weight_once(
                scalars,
                [*one_t, own_qk, came, v_parts[p], d_parts[p]],
                [
                    (
                        [
                            ((0, 1), (columns_run(2, share, n), columns_run(3, share, n)), False),
                            (4 + n,),
                        ],
                        (n,),
                    )
                    for n in range(2)
                ],
                width,
                share,
                members,
                (p,),
            )
            for p in range(2)
        ]
        qv_parts, kd_parts = ([h[n][0] for h in halves] for n in range(2))
        ring_qv = Ring(scalars, qv_parts, x_first)
        ring_kd = Ring(scalars, kd_parts, y_first)
    else:
        for ring in (ring_out, ring_hid):
            ring.step()
        attended, grad_v, att_t = regroup(back_first, None, scalars, rows, query_rows, False)
        att_t = mlp_list(att_t, 1)
        grad_q, grad_k = regroup(back_second, table, scalars, rows, query_rows, False)
        pieces = [pieces_of([g]) for g in (grad_q, grad_v, grad_k)]
        q_runs, v_runs, k_runs = (
            runs(p, (rows, share), lambda m, i, me: (m, 0)) for p in pieces
        )
        cot_runs = runs(cot_list, (rows, share), lambda m, i, me: (m, me[1]))
        one = sides_of(one_t)
        ring_qv = ring_of([(one, q_runs), (one, v_runs)], 2, share, x_first)
        ring_kd = ring_of([(one, k_runs), (sides_of(att_t), cot_runs)], 2, share, y_first)

    ring_out.hold(*ring_kd.sent)
    ring_out.step(ring_hid)
    block_output, grad_input, vec, gm_bias, closed = close_layer(
        inputs,
        cot,
        (attend_gain, feed_gain, attention_out_bias, contract_bias),
        (grad_q, grad_k, grad_v),
        attended,
        query_key_value_weight,
        attention_out_weight,
        feeds,
        grads,
        scalars,
        ring_out.sent,
    )
    for ring in (ring_qv, ring_kd):
        ring.pass_on(closed[0])
    ring_out.came = [after(x, *ring_qv.sent, *ring_kd.sent) for x in ring_out.came]
    ring_out.pass_on(closed[0])

    bias_full = lax.dynamic_update_slice_in_dim(
        jnp.zeros((pairs * slice_width,), F32), grad_hid_bias[0], pair_me * slice_width, 0
    )
    vectors = [*[vec[r] for r in range(5)], gm_bias.reshape(-1), bias_full]
    packed = jnp.concatenate([v.reshape(members, pairs, -1) for v in vectors], -1)
    if pairs == 2:
        mine = lax.dynamic_index_in_dim(packed, pair_me, 1, False)
        other = lax.dynamic_index_in_dim(packed, 1 - pair_me, 1, False)
        packed = mine + pair_swap(after(other, *ring_out.sent))
    else:
        packed = lax.psum_scatter(packed, "mlp", scatter_dimension=1, tiled=False)
    ring_qv.step(ring_kd)
    packed = after(packed, *ring_qv.sent)
    packed = lax.all_to_all(packed, "seq", 0, 0, tiled=True)

    feed_total = ring_out.plain_total()
    out_weight = jnp.transpose(feed_total[:, :slice_width])
    hid_weight = feed_total[:, slice_width:]

    if pairs == 2:
        mine, other = ring_qv.total()
        packed = after(packed, other)
        merged, dense = vmem_call(
            place_kernel,
            [shape_of((own // pairs, 3 * width), F32), shape_of((own // pairs, width), F32)],
            scalars,
            [mine, pair_swap(other)],
            "place",
        )
    else:
        got = ring_qv.total([4 * share])[0].reshape(pairs, own // pairs, 4 * share)
        got = lax.all_to_all(got, "mlp", 0, 0, tiled=True)
        got = jnp.transpose(got.reshape(pairs, own // pairs, 4, share), (1, 2, 0, 3))
        merged = jnp.concatenate([got[:, n].reshape(-1, width) for n in (0, 2, 1)], -1)
        dense = got[:, 3].reshape(-1, width)
    packed = jnp.sum(packed, 0)
    outs, start = [], 0
    for v in vectors:
        size = v.shape[0] // (members * pairs)
        outs.append(lax.slice_in_dim(packed, start, start + size))
        start += size
    grad_gain_one, grad_shift_one, grad_dense_bias, grad_gain_two, grad_shift_two = outs[:5]
    grad_merged_bias, out_hid_bias = outs[5:]
    return (
        block_output.reshape(seq_count, rows, width),
        grad_input.reshape(seq_count, rows, width),
        grad_gain_one,
        grad_shift_one,
        merged,
        grad_merged_bias,
        dense,
        grad_dense_bias,
        grad_gain_two,
        grad_shift_two,
        hid_weight,
        out_hid_bias,
        out_weight,
        grad_dense_bias,
    )


def solution(mesh):
    in_specs = (
        P("mlp", "seq", None),
        P("mlp", "seq", None),
        P(),
        P(),
        P(),
        P(),
        P(),
        P(),
        P(),
        P(),
        P(None, "mlp"),
        P("mlp"),
        P("mlp", None),
        P(),
    )
    out_specs = (
        P("mlp", "seq", None),
        P("mlp", "seq", None),
        P(("seq", "mlp")),
        P(("seq", "mlp")),
        P(("seq", "mlp"), None),
        P(("seq", "mlp")),
        P(("seq", "mlp"), None),
        P(("seq", "mlp")),
        P(("seq", "mlp")),
        P(("seq", "mlp")),
        P("seq", "mlp"),
        P(("seq", "mlp")),
        P("mlp", "seq"),
        P(("seq", "mlp")),
    )
    return jax.shard_map(
        per_device, mesh=mesh, in_specs=in_specs, out_specs=out_specs, check_vma=False
    )
```

```python
from functools import partial

import jax
import jax.numpy as jnp
from jax import lax
from jax.experimental import pallas as pl
from jax.experimental.pallas import tpu as pltpu
from jax.sharding import PartitionSpec as P

HEADS = 16
HEAD = 64
ROT = 16
PAIR = 2 * HEAD
EPS = 1e-05
NEGATIVE = -1e30

F32 = jnp.float32
BF16 = jnp.bfloat16
NT = (((1,), (1,)), ((), ()))
NN = (((1,), (0,)), ((), ()))
VMEM_LIMIT = 60 * 1024 * 1024
COST_SHARE = 16


def dot32(a, b, dims=NN):
    return lax.dot_general(a, b, dims, preferred_element_type=F32)


def cost(flops, bytes_accessed, transcendentals, share=COST_SHARE):
    return pl.CostEstimate(
        flops=flops // share,
        bytes_accessed=bytes_accessed // share,
        transcendentals=transcendentals // share,
    )


def shape_of(shape, dtype):
    return jax.ShapeDtypeStruct(shape, dtype)


def fixed(shape):
    return pl.BlockSpec(shape, lambda *i: (0,) * len(shape))


def vector_row(ref):
    return ref[...].astype(F32).reshape(1, -1)


def two_heads(pair_a, pair_b, low):
    even = jnp.where(low, pair_a, pltpu.roll(pair_b, HEAD, 1))
    odd = jnp.where(low, pltpu.roll(pair_a, HEAD, 1), pair_b)
    return (even, odd)


def rotary_lanes(first, rows, inverse):
    shape = (rows, PAIR)
    lane = lax.broadcasted_iota(jnp.int32, shape, 1) % HEAD
    position = (lax.broadcasted_iota(jnp.int32, shape, 0) + first).astype(F32)
    angle = position * inverse
    cosine, sine = jnp.cos(angle), jnp.sin(angle)
    zero = jnp.zeros_like(sine)
    return (
        jnp.where(lane < ROT, cosine, 1.0),
        jnp.where(lane < ROT // 2, -sine, zero),
        jnp.where((lane >= ROT // 2) & (lane < ROT), sine, zero),
    )


def rotate_lanes(x, cosine, to_first, to_second):
    ahead = pltpu.roll(x, PAIR - ROT // 2, 1)
    behind = pltpu.roll(x, ROT // 2, 1)
    return x * cosine + ahead * to_first + behind * to_second


def unit_rows(x):
    average = jnp.mean(x, -1, keepdims=True)
    centred = x - average
    spread = jnp.mean(centred * centred, -1, keepdims=True)
    root = lax.rsqrt(spread + EPS)
    return (centred * root, root)


def open_kernel(
    first_ref, x_ref, g_ref, inv_ref, ga_ref, sa_ref, gf_ref, sf_ref, b_ref,
    wq_ref, wk_ref, wv_ref, wo_ref,
    out_ref, n1_ref, n2_ref, table_ref, one_ref, turned_ref, bias_ref, *, parts,
):
    rows, width = x_ref.shape
    step = pl.program_id(0)
    cols = wq_ref.shape[1]

    @pl.when(step == 0)
    def _():
        unit, root = unit_rows(x_ref[...].astype(F32))
        n1_ref[...] = (unit * vector_row(ga_ref) + vector_row(sa_ref)).astype(BF16)
        n2_ref[...] = (unit * vector_row(gf_ref) + vector_row(sf_ref)).astype(BF16)
        for t, table in enumerate(rotary_lanes(first_ref[0], rows, inv_ref[...])):
            table_ref[t] = table
        bias_ref[...] = vector_row(b_ref)

    for n, (source, target) in enumerate(
        (
            (n1_ref, one_ref),
            (n2_ref, turned_ref.at[:width]),
            (g_ref, turned_ref.at[width:]),
        )
    ):

        @pl.when(step == pl.num_programs(0) - 1)
        def _(source=source, target=target):
            target[...] = jnp.transpose(source[...])

    def bias(third):
        return bias_ref[:, pl.ds(pl.multiple_of(third * width + step * cols, cols), cols)]

    normed = n1_ref[...]
    query = dot32(normed, wq_ref[...]) + bias(0)
    key = dot32(normed, wk_ref[...]) + bias(1)
    value = dot32(normed, wv_ref[...]) + bias(2)
    grad = dot32(g_ref[...], wo_ref[...], NT)
    tables = (table_ref[0], table_ref[1], table_ref[2])
    low = lax.broadcasted_iota(jnp.int32, (rows, PAIR), 1) < HEAD
    query_rows = rows // parts
    for c in range(cols // PAIR):
        cut = slice(c * PAIR, (c + 1) * PAIR)
        kv = two_heads(rotate_lanes(key[:, cut], *tables), value[:, cut], low)
        qg = two_heads(rotate_lanes(query[:, cut], *tables), grad[:, cut], low)
        for h in range(2):
            kv_h, qg_h = kv[h].astype(BF16), qg[h].astype(BF16)
            for p in range(parts):
                out_ref[2 * c + h, p, :rows] = kv_h
                out_ref[2 * c + h, p, rows:] = qg_h[p * query_rows : (p + 1) * query_rows]


def open_layer(x, g, first, vectors, weight, bias, out_weight, parts):
    rows, width = x.shape
    steps = 2
    cols = width // steps
    per = HEADS // steps
    inverse = 10000.0 ** (-(jnp.arange(ROT // 2, dtype=F32) * 2.0 / ROT))
    inverse = jnp.tile(inverse, PAIR // (ROT // 2)).reshape(1, PAIR)
    chunk = rows + rows // parts

    def third(t):
        return pl.BlockSpec((width, cols), lambda i: (0, t * steps + i))

    out, *others = pl.pallas_call(
        partial(open_kernel, parts=parts),
        grid=(steps,),
        out_shape=(
            shape_of((HEADS, parts, chunk, PAIR), BF16),
            shape_of((rows, width), BF16),
            shape_of((rows, width), BF16),
            shape_of((3, rows, PAIR), F32),
            shape_of((width, rows), BF16),
            shape_of((2 * width, rows), BF16),
        ),
        in_specs=[
            pl.BlockSpec(memory_space=pltpu.SMEM),
            fixed((rows, width)),
            fixed((rows, width)),
            fixed((1, PAIR)),
            *[fixed((width,))] * 4,
            fixed((3 * width,)),
            third(0), third(1), third(2),
            pl.BlockSpec((cols, width), lambda i: (i, 0)),
        ],
        out_specs=(
            pl.BlockSpec((per, parts, chunk, PAIR), lambda i: (i, 0, 0, 0)),
            fixed((rows, width)),
            fixed((rows, width)),
            fixed((3, rows, PAIR)),
            fixed((width, rows)),
            fixed((2 * width, rows)),
        ),
        scratch_shapes=[pltpu.VMEM((1, 3 * width), F32)],
        cost_estimate=cost(
            flops=8 * rows * width * width,
            bytes_accessed=8 * width * width + 18 * rows * width,
            transcendentals=0,
        ),
        compiler_params=pltpu.CompilerParams(vmem_limit_bytes=VMEM_LIMIT),
        name="open_layer",
    )(first, x, g, inverse, *vectors, bias, weight, weight, weight, out_weight)
    return (out.reshape(HEADS * parts, chunk, PAIR), *others)


ROW_GROUP = 4
ONES = 16
CUTS = 4
KEY_GROUP = 2


def first_tile(i):
    return i * (i + 1)


def column_chunks(x):
    return [x[:, c : c + 128] for c in range(0, x.shape[1], 128)]


def forward_kernel(
    part_ref, x_ref, y_ref, g_ref, d_ref, p_hbm, after_ref,
    s_ref, p_ref, dv_ref, vt_ref, mx_ref, top_ref, acc_ref, sem,
    *, key_rows, query_rows,
):
    after_ref[0] = part_ref[1]
    blocks = x_ref.shape[0] // ROW_GROUP
    keys, rows = KEY_GROUP * key_rows, ROW_GROUP * query_rows
    low = lax.broadcasted_iota(jnp.int32, (rows, PAIR), 1) < HEAD
    key_low = lax.broadcasted_iota(jnp.int32, (keys, PAIR), 1) < HEAD
    cuts = [slice(r, r + rows // CUTS) for r in range(0, rows, rows // CUTS)]

    def key_value(j):
        return x_ref[pl.ds(j * KEY_GROUP, KEY_GROUP), :key_rows, :].reshape(keys, PAIR)

    def query_rows_of(i):
        return x_ref[pl.ds(i * ROW_GROUP, ROW_GROUP), key_rows:, :].reshape(rows, PAIR)

    def query_of(i):
        return jnp.where(low, query_rows_of(i).astype(F32) * HEAD**-0.5, 0.0).astype(BF16)

    def copy_out(i, j):
        return pltpu.make_async_copy(p_ref.at[j], p_hbm.at[first_tile(i) + j], sem.at[j])

    def ones_and_values(j, unused):
        turned = jnp.transpose(key_value(j).astype(F32))
        vt_ref[j, :HEAD] = turned[HEAD:].astype(BF16)
        vt_ref[j, HEAD:] = jnp.ones((ONES, keys), BF16)
        return unused

    def raise_max(cut, s):
        mx = mx_ref[cut]
        for chunk in column_chunks(s):
            mx = jnp.maximum(mx, chunk)
        mx_ref[cut] = mx

    def last_scores(i, query):
        row = lax.broadcasted_iota(jnp.int32, (rows, keys), 0)
        col = lax.broadcasted_iota(jnp.int32, (rows, keys), 1)
        row_pos = (row // query_rows) * key_rows + row % query_rows + part_ref[0] * query_rows
        for d in range(ROW_GROUP // KEY_GROUP):
            j = 2 * i + d
            s = dot32(query, key_value(j), NT)
            s = jnp.where(col + d * keys <= row_pos, s, NEGATIVE)
            s_ref[j] = s
            raise_max(slice(None), s)

    def tile(i, j, query, grad_t):
        kv = key_value(j)
        grads = None
        for cut in cuts:
            if grad_t is not None:
                part = dot32(grad_t[:, cut], p_ref[j, cut])
                grads = part if grads is None else grads + part
            top = top_ref[cut]
            p = jnp.concatenate(
                [jnp.exp(c - top) for c in column_chunks(s_ref[j, cut])], 1
            ).astype(BF16)
            p_ref[j, cut] = p
            acc_ref[:, cut] += dot32(vt_ref[j], p, NT)
            if query is not None:
                s = dot32(query[cut], kv, NT)
                s_ref[j, cut] = s
                raise_max(cut, s)
        if grads is not None:
            dv_ref[j, HEAD:] += grads
        copy_out(i, j).start()

    def block(i, grad_t, ahead):
        query = query_of(i + 1) if ahead else None
        top_ref[...] = jnp.broadcast_to(jnp.max(mx_ref[...], -1, keepdims=True), (rows, PAIR))
        mx_ref[...] = jnp.full_like(mx_ref, NEGATIVE)
        acc_ref[...] = jnp.zeros_like(acc_ref)

        def step(j, unused):
            copy_out(i - 1, j).wait()
            tile(i, j, query, grad_t)
            return unused

        lax.fori_loop(0, 2 * i, step, 0)
        for d in range(2):
            tile(i, 2 * i + d, query, None)
        if ahead:
            last_scores(i + 1, query)
        inverse = 1.0 / acc_ref[HEAD : HEAD + 1]
        attended_t = acc_ref[:HEAD] * inverse
        rows_t = jnp.transpose(query_rows_of(i).astype(F32))
        grad_t = (rows_t[HEAD:] * inverse).astype(BF16)
        both = jnp.transpose(jnp.concatenate([attended_t, grad_t.astype(F32)], 0))
        delta = jnp.sum(grad_t.astype(F32) * attended_t, 0, keepdims=True)
        d_ref[i] = jnp.transpose(jnp.broadcast_to(delta, (PAIR, rows)))
        g_ref[i] = jnp.where(low, 0.0, both).astype(BF16)
        here = pl.ds(i * ROW_GROUP, ROW_GROUP)
        y_ref[here, :query_rows, :] = both.astype(BF16).reshape(ROW_GROUP, query_rows, PAIR)
        if query_rows < key_rows:
            y_ref[here, query_rows:, :] = jnp.zeros(
                (ROW_GROUP, key_rows - query_rows, PAIR), BF16
            )
        return grad_t

    dv_ref[...] = jnp.zeros_like(dv_ref)
    lax.fori_loop(0, 2 * blocks, ones_and_values, 0)
    mx_ref[...] = jnp.full_like(mx_ref, NEGATIVE)
    last_scores(0, query_of(0))
    grad_t = lax.fori_loop(
        0, blocks - 1, lambda i, g: block(i, g, True), jnp.zeros((HEAD, rows), BF16)
    )
    grad_t = block(jnp.int32(blocks - 1), grad_t, False)

    def finish(j, unused):
        here = pl.ds(j * KEY_GROUP, KEY_GROUP)
        held = y_ref[here].reshape(keys, PAIR)
        dv_ref[j, HEAD:] += dot32(grad_t, p_ref[j])
        grads = jnp.transpose(dv_ref[j]).astype(BF16)
        y_ref[here] = jnp.where(key_low, held, grads).reshape(KEY_GROUP, key_rows, PAIR)
        copy_out(blocks - 1, j).wait()
        return unused

    lax.fori_loop(0, 2 * blocks, finish, 0)


def backward_kernel(
    me_ref, x_ref, g_ref, d_ref, p_hbm, y_ref, after_ref,
    p_ref, dp0_ref, dp1_ref, dk_ref, acc_ref, sem,
    *, key_rows, query_rows,
):
    after_ref[0] = me_ref[0]
    blocks = x_ref.shape[0] // ROW_GROUP
    keys, rows = KEY_GROUP * key_rows, ROW_GROUP * query_rows
    tiles = first_tile(blocks)
    slots = p_ref.shape[0]
    low = lax.broadcasted_iota(jnp.int32, (rows, PAIR), 1) < HEAD
    dp_refs = (dp0_ref, dp1_ref)

    def copy_in(t):
        return pltpu.make_async_copy(p_hbm.at[t], p_ref.at[t % slots], sem.at[t % slots])

    def refill(t):
        @pl.when(t + slots < tiles)
        def _():
            copy_in(t + slots).start()

    for t in range(min(slots, tiles)):
        copy_in(t).start()
    dk_ref[...] = jnp.zeros_like(dk_ref)

    def key_value(j):
        return x_ref[pl.ds(j * KEY_GROUP, KEY_GROUP), :key_rows, :].reshape(keys, PAIR)

    def one_block(i, unused):
        here = pl.ds(i * ROW_GROUP, ROW_GROUP)
        query = x_ref[here, key_rows:, :].reshape(rows, PAIR).astype(F32) * HEAD**-0.5
        query_t = jnp.transpose(query)[:HEAD].astype(BF16)
        grad = g_ref[i]
        first = first_tile(i)
        acc_ref[...] = jnp.zeros_like(acc_ref)

        def raise_probs(j, side):
            dp_refs[side][...] = dot32(grad, key_value(j), NT)

        def tile(j, side):
            delta = d_ref[i]
            p = column_chunks(p_ref[(first + j) % slots].astype(F32))
            dp = column_chunks(dp_refs[side][...])
            ds = jnp.concatenate([a * (b - delta) for a, b in zip(p, dp)], 1).astype(BF16)
            dk_ref[j, HEAD:] += dot32(query_t, ds)
            acc_ref[...] += dot32(ds, key_value(j))

        def two_tiles(m, unused, more=True):
            j = 2 * m
            copy_in(first + j).wait()
            copy_in(first + j + 1).wait()
            raise_probs(j + 1, 1)
            tile(j, 0)
            if more:
                raise_probs(j + 2, 0)
            tile(j + 1, 1)
            refill(first + j)
            refill(first + j + 1)
            return unused

        raise_probs(0, 0)
        lax.fori_loop(0, i, two_tiles, 0)
        two_tiles(i, 0, False)
        done = jnp.where(low, acc_ref[...] * HEAD**-0.5, 0.0).astype(BF16)
        y_ref[here, :query_rows, :] = done.reshape(ROW_GROUP, query_rows, PAIR)
        if query_rows < key_rows:
            y_ref[here, query_rows:, :] = jnp.zeros(
                (ROW_GROUP, key_rows - query_rows, PAIR), BF16
            )
        return unused

    lax.fori_loop(0, blocks, one_block, 0)
    key_low = lax.broadcasted_iota(jnp.int32, (keys, PAIR), 1) < HEAD

    def finish(j, unused):
        here = pl.ds(j * KEY_GROUP, KEY_GROUP)
        held = y_ref[here].reshape(keys, PAIR)
        grads = jnp.transpose(dk_ref[j]).astype(BF16)
        y_ref[here] = jnp.where(key_low, held, grads).reshape(KEY_GROUP, key_rows, PAIR)
        return unused

    lax.fori_loop(0, 2 * blocks, finish, 0)


def head_sizes(x, key_rows, query_rows):
    count = x.shape[0]
    blocks = count // ROW_GROUP
    return count, blocks, KEY_GROUP * key_rows, ROW_GROUP * query_rows


def forward_head(x, part, key_rows, query_rows, behind):
    count, blocks, keys, rows = head_sizes(x, key_rows, query_rows)
    tiles = first_tile(blocks)
    vmem = pl.BlockSpec(memory_space=pltpu.VMEM)
    return pl.pallas_call(
        without(
            partial(forward_kernel, key_rows=key_rows, query_rows=query_rows), 2, len(behind)
        ),
        out_shape=(
            shape_of((count, key_rows, PAIR), BF16),
            shape_of((blocks, rows, PAIR), BF16),
            shape_of((blocks, rows, PAIR), F32),
            shape_of((tiles, rows, keys), BF16),
            shape_of((1,), jnp.int32),
        ),
        in_specs=[pl.BlockSpec(memory_space=pltpu.SMEM), vmem]
        + [pl.BlockSpec(memory_space=pl.ANY)] * len(behind),
        out_specs=(
            vmem, vmem, vmem, pl.BlockSpec(memory_space=pl.ANY),
            pl.BlockSpec(memory_space=pltpu.SMEM),
        ),
        scratch_shapes=[
            pltpu.VMEM((2 * blocks, rows, keys), F32),
            pltpu.VMEM((2 * blocks, rows, keys), BF16),
            pltpu.VMEM((2 * blocks, PAIR, keys), F32),
            pltpu.VMEM((2 * blocks, HEAD + ONES, keys), BF16),
            pltpu.VMEM((rows, PAIR), F32),
            pltpu.VMEM((rows, PAIR), F32),
            pltpu.VMEM((HEAD + ONES, rows), F32),
            pltpu.SemaphoreType.DMA((2 * blocks,)),
        ],
        cost_estimate=cost(
            flops=tiles * rows * keys * 2 * 256 * 3,
            bytes_accessed=4 * x.size + 2 * tiles * rows * keys,
            transcendentals=tiles * rows * keys,
            share=1,
        ),
        compiler_params=pltpu.CompilerParams(vmem_limit_bytes=VMEM_LIMIT),
        name="forward_head",
    )(part, x, *behind)


def backward_head(scalars, x, grad, delta, probs, key_rows, query_rows, behind):
    count, blocks, keys, rows = head_sizes(x, key_rows, query_rows)
    tiles = first_tile(blocks)
    slots = 6
    vmem = pl.BlockSpec(memory_space=pltpu.VMEM)
    return pl.pallas_call(
        without(
            partial(backward_kernel, key_rows=key_rows, query_rows=query_rows), 5, len(behind)
        ),
        out_shape=(shape_of((count, key_rows, PAIR), BF16), shape_of((1,), jnp.int32)),
        in_specs=[pl.BlockSpec(memory_space=pltpu.SMEM), vmem, vmem, vmem]
        + [pl.BlockSpec(memory_space=pl.ANY)] * (1 + len(behind)),
        out_specs=(vmem, pl.BlockSpec(memory_space=pltpu.SMEM)),
        scratch_shapes=[
            pltpu.VMEM((slots, rows, keys), BF16),
            pltpu.VMEM((rows, keys), F32),
            pltpu.VMEM((rows, keys), F32),
            pltpu.VMEM((2 * blocks, PAIR, keys), F32),
            pltpu.VMEM((rows, PAIR), F32),
            pltpu.SemaphoreType.DMA((slots,)),
        ],
        cost_estimate=cost(
            flops=tiles * rows * keys * 2 * 256 * 3,
            bytes_accessed=4 * x.size + 2 * tiles * rows * keys,
            transcendentals=0,
            share=1,
        ),
        compiler_params=pltpu.CompilerParams(vmem_limit_bytes=VMEM_LIMIT),
        name="backward_head",
    )(scalars, x, grad, delta, probs, *behind)


def feed_kernel(*refs, count, keep):
    rows_refs, cot_refs = refs[:count], refs[count : 2 * count]
    w1_ref, b1_ref, w2_ref = refs[2 * count : 2 * count + 3]
    hid_ref, gpre_ref, gb_ref = refs[2 * count + 3 : 2 * count + 6]
    outs = refs[2 * count + 6 : -2]
    out_acc, grad_acc = refs[-2:]
    step = pl.program_id(0)

    @pl.when(step == 0)
    def _():
        out_acc[...] = jnp.zeros_like(out_acc)
        grad_acc[...] = jnp.zeros_like(grad_acc)

    bias = b1_ref[...]
    sums = jnp.zeros_like(bias)
    rows = rows_refs[0].shape[0]
    for r in range(count):
        here = slice(r * rows, (r + 1) * rows)
        pre = dot32(rows_refs[r][...], w1_ref[...]) + bias
        grad = dot32(cot_refs[r][...], w2_ref[...], NT)
        cdf = 0.5 + 0.5 * lax.erf(pre * (0.5**0.5))
        density = jnp.exp(-0.5 * pre * pre) * 0.3989422804014327
        hidden = (pre * cdf).astype(BF16)
        grad_pre = (grad * (cdf + pre * density)).astype(BF16)
        hid_ref[here] = hidden
        gpre_ref[here] = grad_pre
        sums = sums + jnp.sum(grad_pre.astype(F32), 0, keepdims=True)
        out_acc[here] += dot32(hidden, w2_ref[...])
        grad_acc[here] += dot32(grad_pre, w1_ref[...], NT)
    gb_ref[...] = sums

    @pl.when(step == pl.num_programs(0) - 1)
    def _():
        if keep:
            own_out, own_grad, other = outs
            own_out[...] = out_acc[:rows]
            own_grad[...] = grad_acc[:rows]
            other[:rows] = out_acc[rows:].astype(BF16)
            other[rows:] = grad_acc[rows:].astype(BF16)
        else:
            outs[0][...] = out_acc[...].astype(BF16)
            outs[1][...] = grad_acc[...].astype(BF16)


def feed(rows_list, cot_list, w1, b1, w2):
    width, hidden = w1.shape
    count = len(rows_list)
    rows = rows_list[0].shape[0]
    total = rows * count
    block = 256
    keep = count > 1
    sides = (
        [(rows, F32), (rows, F32), (total, BF16)]
        if keep
        else [(total, BF16), (total, BF16)]
    )
    once = pl.Buffered(1)
    whole = pl.BlockSpec((rows, width), lambda i: (0, 0), pipeline_mode=once)
    return pl.pallas_call(
        partial(feed_kernel, count=count, keep=keep),
        grid=(hidden // block,),
        out_shape=(
            shape_of((total, hidden), BF16),
            shape_of((total, hidden), BF16),
            shape_of((1, hidden), F32),
            *[shape_of((r, width), d) for r, d in sides],
        ),
        in_specs=[
            *[whole] * (2 * count),
            pl.BlockSpec((width, block), lambda i: (0, i)),
            pl.BlockSpec((1, block), lambda i: (0, i)),
            pl.BlockSpec((block, width), lambda i: (i, 0)),
        ],
        out_specs=(
            pl.BlockSpec((total, block), lambda i: (0, i)),
            pl.BlockSpec((total, block), lambda i: (0, i)),
            pl.BlockSpec((1, block), lambda i: (0, i)),
            *[
                pl.BlockSpec((r, width), lambda i: (0, 0), pipeline_mode=once) for r, d in sides
            ],
        ),
        scratch_shapes=[pltpu.VMEM((total, width), F32), pltpu.VMEM((total, width), F32)],
        cost_estimate=cost(
            flops=8 * total * width * hidden,
            bytes_accessed=4 * width * hidden + 4 * total * hidden,
            transcendentals=2 * total * hidden,
        ),
        compiler_params=pltpu.CompilerParams(vmem_limit_bytes=VMEM_LIMIT),
        name="feed",
    )(*rows_list, *cot_list, w1, b1.astype(F32).reshape(1, hidden), w2)


def insert_bits(k, positions, values):
    for position, value in zip(positions, values):
        k = ((k >> position) << (position + 1)) + (value << position) + (k & ((1 << position) - 1))
    return k


def part_chunk(k, p, me, ring_bits, positions):
    values = [((me >> bit) & 1) ^ ((p >> n) & 1) for n, bit in enumerate(ring_bits)]
    return insert_bits(k, positions, values)


def weight_kernel(me_ref, *refs, bits, counts):
    total = sum(counts)
    a_refs, b_refs, parts = refs[:total], refs[total : 2 * total], refs[2 * total :]

    def product(first, count):
        b = jnp.concatenate([r[...] for r in b_refs[first : first + count]], 0)
        for p, ref in enumerate(parts):
            chunks, rows, cols = ref.shape
            a = []
            for k in range(chunks):
                start = part_chunk(k, p, me_ref[0], bits, bits) * rows
                here = pl.ds(pl.multiple_of(start, rows), rows)
                a.append(
                    jnp.concatenate([r[here, :] for r in a_refs[first : first + count]], 1)
                )
            ref[...] = dot32(jnp.concatenate(a, 0), b).astype(BF16).reshape(ref.shape)

    if len(counts) == 1:
        product(0, total)
    else:
        for n, count in enumerate(counts):
            pl.when(pl.program_id(0) == n)(partial(product, sum(counts[:n]), count))


def weight_parts(scalars, products, steps, block, members, bits):
    a_runs = [run for a, _ in products for run in a]
    b_runs = [run for _, b in products for run in b]
    width = a_runs[0][1][0]
    rows = width // members
    tokens = sum(shape[1] for _, shape, _ in products[0][0])
    count = 1 << len(bits)
    each = (members // count, rows, steps * block)
    out = pl.BlockSpec((members // count, rows, block), lambda i, me: (0, 0, i))
    return pl.pallas_call(
        partial(weight_kernel, bits=bits, counts=[len(a) for a, _ in products]),
        grid_spec=pltpu.PrefetchScalarGridSpec(
            num_scalar_prefetch=1,
            grid=(steps,),
            in_specs=[pl.BlockSpec(shape, index) for _, shape, index in (*a_runs, *b_runs)],
            out_specs=[out] * count,
        ),
        out_shape=[shape_of(each, BF16)] * count,
        cost_estimate=cost(
            flops=2 * width * tokens * steps * block,
            bytes_accessed=2 * width * tokens + 2 * (width + tokens) * steps * block,
            transcendentals=0,
        ),
        compiler_params=pltpu.CompilerParams(vmem_limit_bytes=VMEM_LIMIT),
        name="weight_parts",
    )(scalars, *[array for array, _, _ in (*a_runs, *b_runs)])


def weight_once_kernel(me_ref, *refs, products, operands, only):
    arrays, outs = refs[:operands], refs[operands:]
    at = 0
    for blocks, bits in products:
        parts = outs[at : at + len(only)]
        at += len(parts)
        cols = parts[0].shape[2] // len(blocks)
        for n, block in enumerate(blocks):
            here = slice(n * cols, (n + 1) * cols)
            if isinstance(block[0], int):
                for ref, source in zip(parts, block):
                    ref[:, :, here] = arrays[source][...]
                continue
            a_runs, b_runs, turned = block
            b = jnp.concatenate([run(arrays, me_ref) for run in b_runs], 1 if turned else 0)
            for p, ref in zip(only, parts):
                chunks, rows, _ = ref.shape
                a = []
                for k in range(chunks):
                    start = part_chunk(k, p, me_ref[0], bits, bits) * rows
                    lines = pl.ds(pl.multiple_of(start, rows), rows)
                    a.append(jnp.concatenate([arrays[m][lines, :] for m in a_runs], 1))
                product = dot32(jnp.concatenate(a, 0), b, NT if turned else NN)
                ref[:, :, here] = product.astype(BF16).reshape(chunks, rows, cols)


def rows_run(n, first, count):
    return lambda arrays, me_ref: arrays[n][first : first + count, :]


def columns_run(n, cols, block):
    if block is not None:
        return lambda arrays, me_ref: arrays[n][:, block * cols : (block + 1) * cols]
    return lambda arrays, me_ref: arrays[n][:, pl.ds(pl.multiple_of(me_ref[1] * cols, cols), cols)]


def weight_once(scalars, arrays, products, width, cols, members, only, behind=()):
    each = [
        shape_of((members // 2, width // members, cols * len(blocks)), BF16)
        for blocks, bits in products
        for _ in only
    ]
    outs = vmem_call(
        partial(weight_once_kernel, products=products, operands=len(arrays), only=only),
        each,
        scalars,
        arrays,
        "weight_once",
        behind,
    )
    return outs[: len(only)], outs[len(only) :]


def column_sums(refs, counts):
    groups, start = [], 0
    for count in counts:
        groups.append(refs[start : start + count])
        start += count

    def total(group, c):
        value = group[0][c].astype(F32)
        for ref in group[1:]:
            value = value + ref[c].astype(F32)
        return value

    return [partial(total, group) for group in groups]


def add_kernel(me_ref, *refs, counts, bits, positions):
    ins, outs = refs[: sum(counts)], refs[sum(counts) :]
    at = 0
    for group, total in zip(counts, column_sums(ins, counts)):
        cols = ins[0].shape[2]
        for p, ref in enumerate(outs):
            for k in range(ref.shape[0]):
                c = part_chunk(k, p, me_ref[0], bits, positions)
                ref[k, :, at : at + cols] = total(c).astype(BF16)
        at += cols
        ins = ins[group:]


def last_kernel(me_ref, *refs, count, form):
    value = column_sums(refs[:count], [count])[0](0)
    outs = refs[count:]
    if form == "pair":
        half = value.shape[0] // 2
        first = me_ref[1] == 0
        outs[0][...] = jnp.where(first, value[:half], value[half:])
        outs[1][...] = jnp.where(first, value[half:], value[:half]).astype(BF16)
    else:
        at = 0
        for ref in outs:
            ref[...] = value[:, at : at + ref.shape[1]]
            at += ref.shape[1]


def without(kernel, first, count):
    if not count:
        return kernel
    return lambda *refs: kernel(*refs[:first], *refs[first + count :])


def vmem_call(kernel, out_shape, scalars, arrays, name, behind=()):
    vmem = pl.BlockSpec(memory_space=pltpu.VMEM)
    size = sum(a.size for a in arrays)
    return pl.pallas_call(
        without(kernel, 1 + len(arrays), len(behind)),
        in_specs=[pl.BlockSpec(memory_space=pltpu.SMEM)]
        + [vmem] * len(arrays)
        + [pl.BlockSpec(memory_space=pl.ANY)] * len(behind),
        out_specs=[
            pl.BlockSpec(memory_space=pltpu.SMEM) if o.dtype == jnp.int32 else vmem
            for o in out_shape
        ],
        out_shape=out_shape,
        cost_estimate=cost(flops=size, bytes_accessed=3 * size, transcendentals=0),
        compiler_params=pltpu.CompilerParams(vmem_limit_bytes=VMEM_LIMIT),
        name=name,
    )(scalars, *arrays, *behind)


def seq_move(x, mask):
    members = lax.axis_size("seq")
    return lax.ppermute(x, "seq", [(s, s ^ mask) for s in range(members)])


def ring_stages(stages):
    bits = lax.axis_size("seq").bit_length() - 1
    named = [b for stage in stages for b in stage]
    stages = [tuple(b for b in stage if b < bits) for stage in stages]
    stages[-1] = stages[-1] + tuple(b for b in range(bits) if b not in named)
    return [stage for stage in stages if stage]


class Ring:
    def __init__(self, scalars, parts, stages):
        self.scalars, self.stages, self.behind = scalars, list(stages), ()
        self.me = scalars[0]
        self.left = sorted(b for stage in stages for b in stage)
        self.travel(parts)

    def travel(self, parts):
        stage = self.stages.pop(0)
        self.left = [b for b in self.left if b not in stage]
        self.keep, self.sent = parts[0], parts[1:]
        self.came = [
            seq_move(part, sum(1 << b for n, b in enumerate(stage) if (p >> n) & 1))
            for p, part in enumerate(parts)
            if p
        ]

    def hold(self, *others):
        self.behind = others

    def step(self, *others):
        stage = self.stages[0]
        positions = [self.left.index(b) for b in stage]
        rings = (self, *others)
        chunks, rows = self.keep.shape[:2]
        cols = sum(ring.keep.shape[2] for ring in rings)
        count = 1 << len(stage)
        arrays = [[ring.keep, *ring.came] for ring in rings]
        self.travel(
            vmem_call(
                partial(
                    add_kernel, counts=[len(a) for a in arrays], bits=stage, positions=positions
                ),
                [shape_of((chunks // count, rows, cols), BF16)] * count,
                self.scalars,
                [a for group in arrays for a in group],
                "add_parts",
                self.behind,
            )
        )
        self.behind = ()

    def pass_on(self, me):
        stage = self.stages[0]
        bits = self.left
        shape = self.keep.shape[1:]
        arrays = [a.reshape((2,) * len(bits) + shape) for a in (self.keep, *self.came)]
        parts = []
        for p in range(1 << len(stage)):
            total = None
            for a in arrays:
                for n, bit in reversed(list(enumerate(stage))):
                    axis = len(bits) - 1 - bits.index(bit)
                    index = ((me >> bit) & 1) ^ ((p >> n) & 1)
                    a = lax.dynamic_index_in_dim(a, index, axis, True)
                a = a.reshape((-1,) + shape).astype(F32)
                total = a if total is None else total + a
            parts.append(total.astype(BF16))
        self.travel(parts)

    def plain_total(self):
        return sum(a[0].astype(F32) for a in (self.keep, *self.came))

    def total(self, widths=None):
        while self.stages:
            self.step()
        rows, cols = self.keep.shape[1:]
        shapes = (
            [shape_of((rows, w), F32) for w in widths]
            if widths
            else [shape_of((rows // 2, cols), F32), shape_of((rows // 2, cols), BF16)]
        )
        arrays = [self.keep, *self.came]
        return vmem_call(
            partial(last_kernel, count=len(arrays), form="rows" if widths else "pair"),
            shapes,
            self.scalars,
            arrays,
            "last_sum",
        )


def regroup_kernel(me_ref, back_ref, *refs, key_rows, query_rows, turned):
    heads, parts = back_ref.shape[:2]
    low = lax.broadcasted_iota(jnp.int32, (key_rows, PAIR), 1) < HEAD
    if turned:
        one_ref, two_ref, one_t_ref, *sides = refs
    else:
        table_ref, one_ref, two_ref, *sides = refs
        tables = (table_ref[0], -table_ref[1], -table_ref[2])
    first = pl.program_id(0) == 0
    for t in range(heads // 2):
        pair = []
        for h in (2 * t, 2 * t + 1):
            if parts == 1:
                pair.append(back_ref[h, 0].astype(F32))
                continue
            keys = sum(back_ref[h, p].astype(F32) for p in range(parts))
            queries = jnp.concatenate(
                [back_ref[h, p, :query_rows].astype(F32) for p in range(parts)], 0
            )
            pair.append(jnp.where(low, queries, keys))
        one, two = two_heads(pair[0], pair[1], low)
        if not turned:
            one, two = rotate_lanes(one, *tables), rotate_lanes(two, *tables)
        one, two = one.astype(BF16), two.astype(BF16)
        here = slice(t * PAIR, (t + 1) * PAIR)
        one_ref[:, here] = one
        two_ref[:, here] = two
        if turned:
            one_t_ref[here] = jnp.transpose(one)
        if sides:
            half = one_ref.shape[1]
            for n, value in enumerate((two,) if turned else (one, two)):
                there = slice(n * half + t * PAIR, n * half + (t + 1) * PAIR)
                pl.when(first)(partial(sides[1].__setitem__, (slice(None), there), value))
                pl.when(~first)(partial(sides[0].__setitem__, (slice(None), there), value))


def regroup(back, table, scalars, rows, query_rows, split):
    turned = table is None
    chunk = back.shape[1]
    parts = back.shape[0] // HEADS
    half = HEADS * HEAD // 2
    full = shape_of((rows, 2 * half), BF16)

    def side(i, me):
        return (i + me[1] + 1) % 2 if split else i

    whole = pl.BlockSpec((rows, half), lambda i, me: (0, side(i, me)))
    tall = pl.BlockSpec((half, rows), lambda i, me: (side(i, me), 0))
    cols = half * (1 if turned else 2)
    own = pl.BlockSpec((rows, cols), lambda i, me: (0, 0))
    return pl.pallas_call(
        partial(regroup_kernel, key_rows=rows, query_rows=query_rows, turned=turned),
        grid_spec=pltpu.PrefetchScalarGridSpec(
            num_scalar_prefetch=1,
            grid=(2,),
            in_specs=[
                pl.BlockSpec(
                    (HEADS // 2, parts, chunk, PAIR), lambda i, me: (side(i, me), 0, 0, 0)
                )
            ]
            + ([] if turned else [pl.BlockSpec(table.shape, lambda i, me: (0, 0, 0))]),
            out_specs=[whole, whole] + ([tall] if turned else []) + ([own, own] if split else []),
        ),
        out_shape=[full, full]
        + ([shape_of((2 * half, rows), BF16)] if turned else [])
        + ([shape_of((rows, cols), BF16)] * 2 if split else []),
        cost_estimate=cost(
            flops=back.size, bytes_accessed=4 * back.size, transcendentals=0
        ),
        name="regroup",
    )(
        scalars,
        back.reshape(HEADS, parts, chunk, PAIR),
        *([] if turned else [table]),
    )


def regroup_once_kernel(me_ref, *refs, turned):
    if turned:
        back_ref, att_ref, v_ref, send_ref, own_a_ref, own_v_ref = refs
    else:
        back_ref, table_ref, q_ref, k_ref, send_ref, own_ref = refs
        tables = (table_ref[0], -table_ref[1], -table_ref[2])
    heads, rows = back_ref.shape[:2]
    half = heads // 2
    low = lax.broadcasted_iota(jnp.int32, (rows, PAIR), 1) < HEAD
    for side in range(2):
        first = ((me_ref[1] + side) % 2) * half
        for t in range(half // 2):
            pair = [back_ref[first + 2 * t + n].astype(F32) for n in range(2)]
            one, two = two_heads(pair[0], pair[1], low)
            if not turned:
                one, two = rotate_lanes(one, *tables), rotate_lanes(two, *tables)
            one, two = one.astype(BF16), two.astype(BF16)
            start = pl.multiple_of((first // 2 + t) * PAIR, PAIR)
            here = pl.ds(start, PAIR)
            local = slice(t * PAIR, (t + 1) * PAIR)
            width = half * HEAD
            if turned:
                att_ref[:, here] = one
                v_ref[:, here] = two
                turned_one, turned_two = jnp.transpose(one), jnp.transpose(two)
                own_a_ref[here] = turned_one
                send_ref[here] = turned_one
                if side == 0:
                    own_v_ref[local] = turned_two
                else:
                    send_ref[2 * width + t * PAIR : 2 * width + (t + 1) * PAIR] = turned_two
            else:
                q_ref[:, here] = one
                k_ref[:, here] = two
                ref = own_ref if side == 0 else send_ref
                ref[:, local] = one
                ref[:, width + t * PAIR : width + (t + 1) * PAIR] = two


def regroup_once(back, table, scalars, behind=()):
    rows = back.shape[1]
    full = shape_of((rows, HEADS * HEAD), BF16)
    half = HEADS * HEAD // 2
    if table is None:
        sides = [
            shape_of((3 * half, rows), BF16),
            shape_of((2 * half, rows), BF16),
            shape_of((half, rows), BF16),
        ]
    else:
        sides = [shape_of((rows, 2 * half), BF16)] * 2
    return vmem_call(
        partial(regroup_once_kernel, turned=table is None),
        [full, full, *sides],
        scalars,
        [back] if table is None else [back, table],
        "regroup_once",
        behind,
    )


def close_kernel(
    x_ref, g_ref, ga_ref, gf_ref, bo_ref, bc_ref, gq_ref, gk_ref, gv_ref, att_ref,
    wq_ref, wk_ref, wv_ref, wo_ref, me_ref, *refs, sides,
):
    feeds, grads = refs[:sides], refs[sides : 2 * sides]
    out_ref, gin_ref, vec_ref, gb_ref, after_ref, out_acc, grad_acc = refs[2 * sides :]
    step = pl.program_id(0)
    for n in range(2):
        after_ref[n] = me_ref[n]

    @pl.when(step == 0)
    def _():
        out_acc[...] = jnp.zeros_like(out_acc)
        grad_acc[...] = jnp.zeros_like(grad_acc)

    out_acc[...] += dot32(att_ref[...], wo_ref[...])
    total = None
    for third, (g_third, w_ref) in enumerate(
        ((gq_ref, wq_ref), (gk_ref, wk_ref), (gv_ref, wv_ref))
    ):
        grad = g_third[...]
        part = dot32(grad, w_ref[...], NT)
        total = part if total is None else total + part
        gb_ref[third : third + 1] = jnp.sum(grad.astype(F32), 0, keepdims=True)
    grad_acc[...] += total

    @pl.when(step == pl.num_programs(0) - 1)
    def _():
        x = x_ref[...].astype(F32)
        g = g_ref[...].astype(F32)
        total = x + out_acc[...] + vector_row(bo_ref) + vector_row(bc_ref)
        for ref in feeds:
            total = total + ref[...].astype(F32)
        out_ref[...] = total.astype(BF16)
        unit, root = unit_rows(x)
        one = grad_acc[...]
        two = grads[0][...].astype(F32)
        for ref in grads[1:]:
            two = two + ref[...].astype(F32)
        down = one * vector_row(ga_ref) + two * vector_row(gf_ref)
        mean = jnp.mean(down, -1, keepdims=True)
        slope = jnp.mean(down * unit, -1, keepdims=True)
        gin_ref[...] = g + root * (down - mean - unit * slope)
        for r, rows in enumerate((one * unit, one, g, two * unit, two)):
            vec_ref[r : r + 1] = jnp.sum(rows, 0, keepdims=True)


def close_layer(x, g, vectors, gm, attended, weight, out_weight, feeds, grads, scalars, behind):
    rows, width = x.shape
    steps = 4
    cols = width // steps

    def third(t):
        return pl.BlockSpec((width, cols), lambda i: (0, t * steps + i))

    part = pl.BlockSpec((rows, cols), lambda i: (0, i))
    return pl.pallas_call(
        without(partial(close_kernel, sides=len(feeds)), 15 + 2 * len(feeds), len(behind)),
        grid=(steps,),
        out_shape=(
            shape_of((rows, width), BF16),
            shape_of((rows, width), F32),
            shape_of((5, width), F32),
            shape_of((3, width), F32),
            shape_of((2,), jnp.int32),
        ),
        in_specs=[
            fixed((rows, width)),
            fixed((rows, width)),
            *[fixed((width,))] * 4,
            part, part, part, part,
            third(0), third(1), third(2),
            pl.BlockSpec((cols, width), lambda i: (i, 0)),
            pl.BlockSpec(memory_space=pltpu.SMEM),
            *[
                pl.BlockSpec((rows, width), lambda i, n=n: (n, 0)) for _, n in (*feeds, *grads)
            ],
            *[pl.BlockSpec(memory_space=pl.ANY)] * len(behind),
        ],
        out_specs=(
            fixed((rows, width)),
            fixed((rows, width)),
            fixed((5, width)),
            pl.BlockSpec((3, cols), lambda i: (0, i)),
            pl.BlockSpec(memory_space=pltpu.SMEM),
        ),
        scratch_shapes=[pltpu.VMEM((rows, width), F32), pltpu.VMEM((rows, width), F32)],
        cost_estimate=cost(
            flops=8 * rows * width * width,
            bytes_accessed=8 * width * width + 24 * rows * width,
            transcendentals=0,
        ),
        compiler_params=pltpu.CompilerParams(vmem_limit_bytes=VMEM_LIMIT),
        name="close_layer",
    )(x, g, *vectors, *gm, attended, weight, weight, weight, out_weight, scalars, *[a for a, _ in (*feeds, *grads)], *behind)


def place_kernel(me_ref, own_ref, came_ref, merged_ref, dense_ref):
    half = dense_ref.shape[1] // 2
    for side, ref in enumerate((own_ref, came_ref)):
        at = ((me_ref[1] + side) % 2) * half
        for third, block in enumerate((0, 2, 1)):
            start = pl.multiple_of(third * 2 * half + at, half)
            value = ref[:, block * half : (block + 1) * half]
            merged_ref[:, pl.ds(start, half)] = value.astype(F32)
        dense_ref[:, pl.ds(pl.multiple_of(at, half), half)] = ref[:, 3 * half :].astype(F32)


def pair_swap(x):
    return lax.ppermute(x, "mlp", [(0, 1), (1, 0)])


def mlp_list(x, axis=0):
    if lax.axis_size("mlp") == 2:
        return [x, pair_swap(x)]
    return [lax.all_gather(x, "mlp", axis=axis, tiled=True)]


def after(value, *others):
    return lax.optimization_barrier((value, *others))[0]


def per_device(
    block_input,
    out_cotangent,
    attend_gain,
    attend_shift,
    query_key_value_weight,
    query_key_value_bias,
    attention_out_weight,
    attention_out_bias,
    feed_gain,
    feed_shift,
    expand_weight,
    expand_bias,
    contract_weight,
    contract_bias,
):
    seq_count, rows, width = block_input.shape
    members = lax.axis_size("seq")
    pairs = lax.axis_size("mlp")
    parts = members // HEADS
    own = width // members
    me = lax.axis_index("seq").astype(jnp.int32).reshape(1)
    pair_me = lax.axis_index("mlp")
    scalars = jnp.stack([me[0], pair_me.astype(jnp.int32)])
    inputs = block_input.reshape(rows, width)
    cot = out_cotangent.reshape(rows, width)

    outgoing, _, normed_two, table, one_t, turned = open_layer(
        inputs,
        cot,
        me * rows,
        (attend_gain, attend_shift, feed_gain, feed_shift),
        query_key_value_weight,
        query_key_value_bias,
        attention_out_weight,
        parts,
    )
    at_head = lax.all_to_all(outgoing, "seq", 0, 0, tiled=True)

    rows_list, cot_list = mlp_list(normed_two), mlp_list(cot)
    turned = mlp_list(turned, 1)
    one_t = mlp_list(one_t, 1)
    hidden, grad_pre, grad_hid_bias, *sides = feed(
        rows_list, cot_list, expand_weight, expand_bias, contract_weight
    )
    if pairs == 2:
        came = pair_swap(sides[2])
        feeds, grads = [(sides[0], 0), (came, 0)], [(sides[1], 0), (came, 1)]
    else:
        feeds, grads = (
            [(lax.psum_scatter(v, "mlp", scatter_dimension=0, tiled=True), 0)] for v in sides
        )
    slice_width = expand_weight.shape[1]
    block = min(512, slice_width)

    def runs(arrays, shape, index):
        if pairs == 2:
            return [(a, shape, lambda i, me: index(0, i, me)) for a in arrays]
        return [(arrays[0], shape, lambda i, me, m=m: index(m, i, me)) for m in range(pairs)]

    def sides_of(arrays, part=0):
        return runs(arrays, (width, rows), lambda m, i, me: (part, m))

    def ring_of(products, steps, block, stages):
        stages = ring_stages(stages)
        parts = weight_parts(scalars, products, steps, block, members, stages[0])
        return Ring(scalars, parts, stages)

    x_first, y_first = [(0,), (1,), (2,), (3,)], [(1,), (0,), (2,), (3,)]

    def feed_ring(part, b, stages):
        b_runs = [(b, (rows, block), lambda i, me, m=m: (m, i)) for m in range(pairs)]
        return ring_of([(sides_of(turned, part), b_runs)], slice_width // block, block, stages)

    ring_out = feed_ring(1, hidden, x_first)
    ring_hid = feed_ring(0, grad_pre, y_first)

    query_rows = rows // parts
    part = jnp.stack([me[0] % parts, me[0]]).astype(jnp.int32)
    from_first, head_grad, head_delta, probs, _ = forward_head(
        at_head,
        part,
        rows,
        query_rows,
        (*ring_out.sent, *ring_hid.sent, *[a for a, _ in (*feeds, *grads)], *turned, *one_t),
    )
    back_first = lax.all_to_all(from_first, "seq", 0, 0, tiled=True)
    from_second, after_second = backward_head(
        scalars, at_head, head_grad, head_delta, probs, rows, query_rows, ()
    )
    from_second = after(from_second, *ring_out.came, *ring_hid.came)
    back_second = lax.all_to_all(from_second, "seq", 0, 0, tiled=True)
    x_first, y_first = [(0,), (1,), (2, 3)], [(1,), (0,), (2, 3)]
    split = pairs == 2 and parts == 1
    share = width // pairs

    def pieces_of(arrays):
        stacked = jnp.stack([a.reshape(rows, pairs, share) for a in arrays], 2)
        stacked = jnp.transpose(stacked, (1, 0, 2, 3)).reshape(pairs, rows, len(arrays) * share)
        if pairs == 2:
            mine = lax.dynamic_index_in_dim(stacked, pair_me, 0, False)
            return [mine, pair_swap(lax.dynamic_index_in_dim(stacked, 1 - pair_me, 0, False))]
        got = lax.all_to_all(stacked, "mlp", 0, 0, tiled=True)
        return [got.reshape(pairs * rows, len(arrays) * share)]

    if split:

        attended, grad_v, sent, own_a, own_v = regroup_once(
            back_first, None, scalars, (from_second,)
        )
        came = pair_swap(sent)
        for ring in (ring_out, ring_hid):
            ring.hold(sent)
            ring.step()
        v_parts, d_parts = weight_once(
            scalars,
            [*one_t, own_v, came, own_a, *cot_list],
            [
                ([((0, 1), (rows_run(2, 0, share), rows_run(3, width, share)), True)], (0,)),
                (
                    [((4, 3), (columns_run(5, share, None), columns_run(6, share, None)), False)],
                    (1,),
                ),
            ],
            width,
            share,
            members,
            (0, 1),
        )
        grad_q, grad_k, sent, own_qk = regroup_once(
            back_second, table, scalars, (*v_parts, *d_parts)
        )
        came = pair_swap(sent)
        halves = [
            weight_once(
                scalars,
                [*one_t, own_qk, came, v_parts[p], d_parts[p]],
                [
                    (
                        [
                            ((0, 1), (columns_run(2, share, n), columns_run(3, share, n)), False),
                            (4 + n,),
                        ],
                        (n,),
                    )
                    for n in range(2)
                ],
                width,
                share,
                members,
                (p,),
            )
            for p in range(2)
        ]
        qv_parts, kd_parts = ([h[n][0] for h in halves] for n in range(2))
        ring_qv = Ring(scalars, qv_parts, x_first)
        ring_kd = Ring(scalars, kd_parts, y_first)
    else:
        for ring in (ring_out, ring_hid):
            ring.step()
        attended, grad_v, att_t = regroup(back_first, None, scalars, rows, query_rows, False)
        att_t = mlp_list(att_t, 1)
        grad_q, grad_k = regroup(back_second, table, scalars, rows, query_rows, False)
        pieces = [pieces_of([g]) for g in (grad_q, grad_v, grad_k)]
        q_runs, v_runs, k_runs = (
            runs(p, (rows, share), lambda m, i, me: (m, 0)) for p in pieces
        )
        cot_runs = runs(cot_list, (rows, share), lambda m, i, me: (m, me[1]))
        one = sides_of(one_t)
        ring_qv = ring_of([(one, q_runs), (one, v_runs)], 2, share, x_first)
        ring_kd = ring_of([(one, k_runs), (sides_of(att_t), cot_runs)], 2, share, y_first)

    ring_out.hold(*ring_kd.sent)
    ring_out.step(ring_hid)
    block_output, grad_input, vec, gm_bias, closed = close_layer(
        inputs,
        cot,
        (attend_gain, feed_gain, attention_out_bias, contract_bias),
        (grad_q, grad_k, grad_v),
        attended,
        query_key_value_weight,
        attention_out_weight,
        feeds,
        grads,
        scalars,
        ring_out.sent,
    )
    for ring in (ring_qv, ring_kd):
        ring.pass_on(closed[0])
    ring_out.came = [after(x, *ring_qv.sent, *ring_kd.sent) for x in ring_out.came]
    ring_out.pass_on(closed[0])

    bias_full = lax.dynamic_update_slice_in_dim(
        jnp.zeros((pairs * slice_width,), F32), grad_hid_bias[0], pair_me * slice_width, 0
    )
    vectors = [*[vec[r] for r in range(5)], gm_bias.reshape(-1), bias_full]
    packed = jnp.concatenate([v.reshape(members, pairs, -1) for v in vectors], -1)
    if pairs == 2:
        mine = lax.dynamic_index_in_dim(packed, pair_me, 1, False)
        other = lax.dynamic_index_in_dim(packed, 1 - pair_me, 1, False)
        packed = mine + pair_swap(after(other, *ring_out.sent))
    else:
        packed = lax.psum_scatter(packed, "mlp", scatter_dimension=1, tiled=False)
    packed = after(packed, *ring_qv.sent, *ring_kd.sent)
    packed = lax.all_to_all(packed, "seq", 0, 0, tiled=True)
    ring_qv.step(ring_kd)

    feed_total = ring_out.plain_total()
    out_weight = jnp.transpose(feed_total[:, :slice_width])
    hid_weight = feed_total[:, slice_width:]

    if pairs == 2:
        mine, other = ring_qv.total()
        packed = after(packed, other)
        merged, dense = vmem_call(
            place_kernel,
            [shape_of((own // pairs, 3 * width), F32), shape_of((own // pairs, width), F32)],
            scalars,
            [mine, pair_swap(other)],
            "place",
        )
    else:
        got = ring_qv.total([4 * share])[0].reshape(pairs, own // pairs, 4 * share)
        got = lax.all_to_all(got, "mlp", 0, 0, tiled=True)
        got = jnp.transpose(got.reshape(pairs, own // pairs, 4, share), (1, 2, 0, 3))
        merged = jnp.concatenate([got[:, n].reshape(-1, width) for n in (0, 2, 1)], -1)
        dense = got[:, 3].reshape(-1, width)
    packed = jnp.sum(packed, 0)
    outs, start = [], 0
    for v in vectors:
        size = v.shape[0] // (members * pairs)
        outs.append(lax.slice_in_dim(packed, start, start + size))
        start += size
    grad_gain_one, grad_shift_one, grad_dense_bias, grad_gain_two, grad_shift_two = outs[:5]
    grad_merged_bias, out_hid_bias = outs[5:]
    return (
        block_output.reshape(seq_count, rows, width),
        grad_input.reshape(seq_count, rows, width),
        grad_gain_one,
        grad_shift_one,
        merged,
        grad_merged_bias,
        dense,
        grad_dense_bias,
        grad_gain_two,
        grad_shift_two,
        hid_weight,
        out_hid_bias,
        out_weight,
        grad_dense_bias,
    )


def solution(mesh):
    in_specs = (
        P("mlp", "seq", None),
        P("mlp", "seq", None),
        P(),
        P(),
        P(),
        P(),
        P(),
        P(),
        P(),
        P(),
        P(None, "mlp"),
        P("mlp"),
        P("mlp", None),
        P(),
    )
    out_specs = (
        P("mlp", "seq", None),
        P("mlp", "seq", None),
        P(("seq", "mlp")),
        P(("seq", "mlp")),
        P(("seq", "mlp"), None),
        P(("seq", "mlp")),
        P(("seq", "mlp"), None),
        P(("seq", "mlp")),
        P(("seq", "mlp")),
        P(("seq", "mlp")),
        P("seq", "mlp"),
        P(("seq", "mlp")),
        P("mlp", "seq"),
        P(("seq", "mlp")),
    )
    return jax.shard_map(
        per_device, mesh=mesh, in_specs=in_specs, out_specs=out_specs, check_vma=False
    )
```

```python
from functools import partial

import jax
import jax.numpy as jnp
from jax import lax
from jax.experimental import pallas as pl
from jax.experimental.pallas import tpu as pltpu
from jax.sharding import PartitionSpec as P

HEADS = 16
HEAD = 64
ROT = 16
PAIR = 2 * HEAD
EPS = 1e-05
NEGATIVE = -1e30

F32 = jnp.float32
BF16 = jnp.bfloat16
NT = (((1,), (1,)), ((), ()))
NN = (((1,), (0,)), ((), ()))
VMEM_LIMIT = 60 * 1024 * 1024
COST_SHARE = 16


def dot32(a, b, dims=NN):
    return lax.dot_general(a, b, dims, preferred_element_type=F32)


def cost(flops, bytes_accessed, transcendentals, share=COST_SHARE):
    return pl.CostEstimate(
        flops=flops // share,
        bytes_accessed=bytes_accessed // share,
        transcendentals=transcendentals // share,
    )


def shape_of(shape, dtype):
    return jax.ShapeDtypeStruct(shape, dtype)


def fixed(shape):
    return pl.BlockSpec(shape, lambda *i: (0,) * len(shape))


def vector_row(ref):
    return ref[...].astype(F32).reshape(1, -1)


def two_heads(pair_a, pair_b, low):
    even = jnp.where(low, pair_a, pltpu.roll(pair_b, HEAD, 1))
    odd = jnp.where(low, pltpu.roll(pair_a, HEAD, 1), pair_b)
    return (even, odd)


def rotary_lanes(first, rows, inverse):
    shape = (rows, PAIR)
    lane = lax.broadcasted_iota(jnp.int32, shape, 1) % HEAD
    position = (lax.broadcasted_iota(jnp.int32, shape, 0) + first).astype(F32)
    angle = position * inverse
    cosine, sine = jnp.cos(angle), jnp.sin(angle)
    zero = jnp.zeros_like(sine)
    return (
        jnp.where(lane < ROT, cosine, 1.0),
        jnp.where(lane < ROT // 2, -sine, zero),
        jnp.where((lane >= ROT // 2) & (lane < ROT), sine, zero),
    )


def rotate_lanes(x, cosine, to_first, to_second):
    ahead = pltpu.roll(x, PAIR - ROT // 2, 1)
    behind = pltpu.roll(x, ROT // 2, 1)
    return x * cosine + ahead * to_first + behind * to_second


def unit_rows(x):
    average = jnp.mean(x, -1, keepdims=True)
    centred = x - average
    spread = jnp.mean(centred * centred, -1, keepdims=True)
    root = lax.rsqrt(spread + EPS)
    return (centred * root, root)


def open_kernel(
    first_ref, x_ref, g_ref, inv_ref, ga_ref, sa_ref, gf_ref, sf_ref, b_ref,
    wq_ref, wk_ref, wv_ref, wo_ref,
    out_ref, n1_ref, n2_ref, table_ref, one_ref, turned_ref, bias_ref, *, parts,
):
    rows, width = x_ref.shape
    step = pl.program_id(0)
    cols = wq_ref.shape[1]

    @pl.when(step == 0)
    def _():
        unit, root = unit_rows(x_ref[...].astype(F32))
        n1_ref[...] = (unit * vector_row(ga_ref) + vector_row(sa_ref)).astype(BF16)
        n2_ref[...] = (unit * vector_row(gf_ref) + vector_row(sf_ref)).astype(BF16)
        for t, table in enumerate(rotary_lanes(first_ref[0], rows, inv_ref[...])):
            table_ref[t] = table
        bias_ref[...] = vector_row(b_ref)

    for n, (source, target) in enumerate(
        (
            (n1_ref, one_ref),
            (n2_ref, turned_ref.at[:width]),
            (g_ref, turned_ref.at[width:]),
        )
    ):

        @pl.when(step == pl.num_programs(0) - 1)
        def _(source=source, target=target):
            target[...] = jnp.transpose(source[...])

    def bias(third):
        return bias_ref[:, pl.ds(pl.multiple_of(third * width + step * cols, cols), cols)]

    normed = n1_ref[...]
    query = dot32(normed, wq_ref[...]) + bias(0)
    key = dot32(normed, wk_ref[...]) + bias(1)
    value = dot32(normed, wv_ref[...]) + bias(2)
    grad = dot32(g_ref[...], wo_ref[...], NT)
    tables = (table_ref[0], table_ref[1], table_ref[2])
    low = lax.broadcasted_iota(jnp.int32, (rows, PAIR), 1) < HEAD
    query_rows = rows // parts
    for c in range(cols // PAIR):
        cut = slice(c * PAIR, (c + 1) * PAIR)
        kv = two_heads(rotate_lanes(key[:, cut], *tables), value[:, cut], low)
        qg = two_heads(rotate_lanes(query[:, cut], *tables), grad[:, cut], low)
        for h in range(2):
            kv_h, qg_h = kv[h].astype(BF16), qg[h].astype(BF16)
            for p in range(parts):
                out_ref[2 * c + h, p, :rows] = kv_h
                out_ref[2 * c + h, p, rows:] = qg_h[p * query_rows : (p + 1) * query_rows]


def open_layer(x, g, first, vectors, weight, bias, out_weight, parts):
    rows, width = x.shape
    steps = 2
    cols = width // steps
    per = HEADS // steps
    inverse = 10000.0 ** (-(jnp.arange(ROT // 2, dtype=F32) * 2.0 / ROT))
    inverse = jnp.tile(inverse, PAIR // (ROT // 2)).reshape(1, PAIR)
    chunk = rows + rows // parts

    def third(t):
        return pl.BlockSpec((width, cols), lambda i: (0, t * steps + i))

    out, *others = pl.pallas_call(
        partial(open_kernel, parts=parts),
        grid=(steps,),
        out_shape=(
            shape_of((HEADS, parts, chunk, PAIR), BF16),
            shape_of((rows, width), BF16),
            shape_of((rows, width), BF16),
            shape_of((3, rows, PAIR), F32),
            shape_of((width, rows), BF16),
            shape_of((2 * width, rows), BF16),
        ),
        in_specs=[
            pl.BlockSpec(memory_space=pltpu.SMEM),
            fixed((rows, width)),
            fixed((rows, width)),
            fixed((1, PAIR)),
            *[fixed((width,))] * 4,
            fixed((3 * width,)),
            third(0), third(1), third(2),
            pl.BlockSpec((cols, width), lambda i: (i, 0)),
        ],
        out_specs=(
            pl.BlockSpec((per, parts, chunk, PAIR), lambda i: (i, 0, 0, 0)),
            fixed((rows, width)),
            fixed((rows, width)),
            fixed((3, rows, PAIR)),
            fixed((width, rows)),
            fixed((2 * width, rows)),
        ),
        scratch_shapes=[pltpu.VMEM((1, 3 * width), F32)],
        cost_estimate=cost(
            flops=8 * rows * width * width,
            bytes_accessed=8 * width * width + 18 * rows * width,
            transcendentals=0,
        ),
        compiler_params=pltpu.CompilerParams(vmem_limit_bytes=VMEM_LIMIT),
        name="open_layer",
    )(first, x, g, inverse, *vectors, bias, weight, weight, weight, out_weight)
    return (out.reshape(HEADS * parts, chunk, PAIR), *others)


ROW_GROUP = 4
ONES = 16
CUTS = 4
KEY_GROUP = 2


def first_tile(i):
    return i * (i + 1)


def column_chunks(x):
    return [x[:, c : c + 128] for c in range(0, x.shape[1], 128)]


def forward_kernel(
    part_ref, x_ref, y_ref, g_ref, d_ref, p_hbm, after_ref,
    s_ref, p_ref, dv_ref, vt_ref, mx_ref, top_ref, acc_ref, sem,
    *, key_rows, query_rows,
):
    after_ref[0] = part_ref[1]
    blocks = x_ref.shape[0] // ROW_GROUP
    keys, rows = KEY_GROUP * key_rows, ROW_GROUP * query_rows
    low = lax.broadcasted_iota(jnp.int32, (rows, PAIR), 1) < HEAD
    key_low = lax.broadcasted_iota(jnp.int32, (keys, PAIR), 1) < HEAD
    cuts = [slice(r, r + rows // CUTS) for r in range(0, rows, rows // CUTS)]

    def key_value(j):
        return x_ref[pl.ds(j * KEY_GROUP, KEY_GROUP), :key_rows, :].reshape(keys, PAIR)

    def query_rows_of(i):
        return x_ref[pl.ds(i * ROW_GROUP, ROW_GROUP), key_rows:, :].reshape(rows, PAIR)

    def query_of(i):
        return jnp.where(low, query_rows_of(i).astype(F32) * HEAD**-0.5, 0.0).astype(BF16)

    def copy_out(i, j):
        return pltpu.make_async_copy(p_ref.at[j], p_hbm.at[first_tile(i) + j], sem.at[j])

    def ones_and_values(j, unused):
        turned = jnp.transpose(key_value(j).astype(F32))
        vt_ref[j, :HEAD] = turned[HEAD:].astype(BF16)
        vt_ref[j, HEAD:] = jnp.ones((ONES, keys), BF16)
        return unused

    def raise_max(cut, s):
        mx = mx_ref[cut]
        for chunk in column_chunks(s):
            mx = jnp.maximum(mx, chunk)
        mx_ref[cut] = mx

    def last_scores(i, query):
        row = lax.broadcasted_iota(jnp.int32, (rows, keys), 0)
        col = lax.broadcasted_iota(jnp.int32, (rows, keys), 1)
        row_pos = (row // query_rows) * key_rows + row % query_rows + part_ref[0] * query_rows
        for d in range(ROW_GROUP // KEY_GROUP):
            j = 2 * i + d
            s = dot32(query, key_value(j), NT)
            s = jnp.where(col + d * keys <= row_pos, s, NEGATIVE)
            s_ref[j] = s
            raise_max(slice(None), s)

    def tile(i, j, query, grad_t):
        kv = key_value(j)
        grads = None
        for cut in cuts:
            old = s_ref[j, cut]
            if query is not None:
                s = dot32(query[cut], kv, NT)
            if grad_t is not None:
                part = dot32(grad_t[:, cut], p_ref[j, cut])
                grads = part if grads is None else grads + part
            top = top_ref[cut]
            p = jnp.concatenate([jnp.exp(c - top) for c in column_chunks(old)], 1).astype(BF16)
            p_ref[j, cut] = p
            acc_ref[:, cut] += dot32(vt_ref[j], p, NT)
            if query is not None:
                s_ref[j, cut] = s
                raise_max(cut, s)
        if grads is not None:
            dv_ref[j, HEAD:] += grads
        copy_out(i, j).start()

    def block(i, grad_t, ahead):
        query = query_of(i + 1) if ahead else None
        top_ref[...] = jnp.broadcast_to(jnp.max(mx_ref[...], -1, keepdims=True), (rows, PAIR))
        mx_ref[...] = jnp.full_like(mx_ref, NEGATIVE)
        acc_ref[...] = jnp.zeros_like(acc_ref)

        def step(j, unused):
            copy_out(i - 1, j).wait()
            tile(i, j, query, grad_t)
            return unused

        lax.fori_loop(0, 2 * i, step, 0)
        for d in range(2):
            tile(i, 2 * i + d, query, None)
        if ahead:
            last_scores(i + 1, query)
        inverse = 1.0 / acc_ref[HEAD : HEAD + 1]
        attended_t = acc_ref[:HEAD] * inverse
        rows_t = jnp.transpose(query_rows_of(i).astype(F32))
        grad_t = (rows_t[HEAD:] * inverse).astype(BF16)
        both = jnp.transpose(jnp.concatenate([attended_t, grad_t.astype(F32)], 0))
        delta = jnp.sum(grad_t.astype(F32) * attended_t, 0, keepdims=True)
        d_ref[i] = jnp.transpose(jnp.broadcast_to(delta, (PAIR, rows)))
        g_ref[i] = jnp.where(low, 0.0, both).astype(BF16)
        here = pl.ds(i * ROW_GROUP, ROW_GROUP)
        y_ref[here, :query_rows, :] = both.astype(BF16).reshape(ROW_GROUP, query_rows, PAIR)
        if query_rows < key_rows:
            y_ref[here, query_rows:, :] = jnp.zeros(
                (ROW_GROUP, key_rows - query_rows, PAIR), BF16
            )
        return grad_t

    dv_ref[...] = jnp.zeros_like(dv_ref)
    lax.fori_loop(0, 2 * blocks, ones_and_values, 0)
    mx_ref[...] = jnp.full_like(mx_ref, NEGATIVE)
    last_scores(0, query_of(0))
    grad_t = lax.fori_loop(
        0, blocks - 1, lambda i, g: block(i, g, True), jnp.zeros((HEAD, rows), BF16)
    )
    grad_t = block(jnp.int32(blocks - 1), grad_t, False)

    def finish(j, unused):
        here = pl.ds(j * KEY_GROUP, KEY_GROUP)
        held = y_ref[here].reshape(keys, PAIR)
        dv_ref[j, HEAD:] += dot32(grad_t, p_ref[j])
        grads = jnp.transpose(dv_ref[j]).astype(BF16)
        y_ref[here] = jnp.where(key_low, held, grads).reshape(KEY_GROUP, key_rows, PAIR)
        copy_out(blocks - 1, j).wait()
        return unused

    lax.fori_loop(0, 2 * blocks, finish, 0)


def backward_kernel(
    me_ref, x_ref, g_ref, d_ref, p_hbm, y_ref, after_ref,
    p_ref, dp0_ref, dp1_ref, dk_ref, acc_ref, sem,
    *, key_rows, query_rows,
):
    after_ref[0] = me_ref[0]
    blocks = x_ref.shape[0] // ROW_GROUP
    keys, rows = KEY_GROUP * key_rows, ROW_GROUP * query_rows
    tiles = first_tile(blocks)
    slots = p_ref.shape[0]
    low = lax.broadcasted_iota(jnp.int32, (rows, PAIR), 1) < HEAD
    dp_refs = (dp0_ref, dp1_ref)

    def copy_in(t):
        return pltpu.make_async_copy(p_hbm.at[t], p_ref.at[t % slots], sem.at[t % slots])

    def refill(t):
        @pl.when(t + slots < tiles)
        def _():
            copy_in(t + slots).start()

    for t in range(min(slots, tiles)):
        copy_in(t).start()
    dk_ref[...] = jnp.zeros_like(dk_ref)

    def key_value(j):
        return x_ref[pl.ds(j * KEY_GROUP, KEY_GROUP), :key_rows, :].reshape(keys, PAIR)

    def one_block(i, unused):
        here = pl.ds(i * ROW_GROUP, ROW_GROUP)
        query = x_ref[here, key_rows:, :].reshape(rows, PAIR).astype(F32) * HEAD**-0.5
        query_t = jnp.transpose(query)[:HEAD].astype(BF16)
        grad = g_ref[i]
        first = first_tile(i)
        acc_ref[...] = jnp.zeros_like(acc_ref)

        def raise_probs(j, side):
            dp_refs[side][...] = dot32(grad, key_value(j), NT)

        def tile(j, side):
            delta = d_ref[i]
            p = column_chunks(p_ref[(first + j) % slots].astype(F32))
            dp = column_chunks(dp_refs[side][...])
            ds = jnp.concatenate([a * (b - delta) for a, b in zip(p, dp)], 1).astype(BF16)
            dk_ref[j, HEAD:] += dot32(query_t, ds)
            acc_ref[...] += dot32(ds, key_value(j))

        def two_tiles(m, unused, more=True):
            j = 2 * m
            copy_in(first + j).wait()
            copy_in(first + j + 1).wait()
            raise_probs(j + 1, 1)
            tile(j, 0)
            if more:
                raise_probs(j + 2, 0)
            tile(j + 1, 1)
            refill(first + j)
            refill(first + j + 1)
            return unused

        raise_probs(0, 0)
        lax.fori_loop(0, i, two_tiles, 0)
        two_tiles(i, 0, False)
        done = jnp.where(low, acc_ref[...] * HEAD**-0.5, 0.0).astype(BF16)
        y_ref[here, :query_rows, :] = done.reshape(ROW_GROUP, query_rows, PAIR)
        if query_rows < key_rows:
            y_ref[here, query_rows:, :] = jnp.zeros(
                (ROW_GROUP, key_rows - query_rows, PAIR), BF16
            )
        return unused

    lax.fori_loop(0, blocks, one_block, 0)
    key_low = lax.broadcasted_iota(jnp.int32, (keys, PAIR), 1) < HEAD

    def finish(j, unused):
        here = pl.ds(j * KEY_GROUP, KEY_GROUP)
        held = y_ref[here].reshape(keys, PAIR)
        grads = jnp.transpose(dk_ref[j]).astype(BF16)
        y_ref[here] = jnp.where(key_low, held, grads).reshape(KEY_GROUP, key_rows, PAIR)
        return unused

    lax.fori_loop(0, 2 * blocks, finish, 0)


def head_sizes(x, key_rows, query_rows):
    count = x.shape[0]
    blocks = count // ROW_GROUP
    return count, blocks, KEY_GROUP * key_rows, ROW_GROUP * query_rows


def forward_head(x, part, key_rows, query_rows, behind):
    count, blocks, keys, rows = head_sizes(x, key_rows, query_rows)
    tiles = first_tile(blocks)
    vmem = pl.BlockSpec(memory_space=pltpu.VMEM)
    return pl.pallas_call(
        without(
            partial(forward_kernel, key_rows=key_rows, query_rows=query_rows), 2, len(behind)
        ),
        out_shape=(
            shape_of((count, key_rows, PAIR), BF16),
            shape_of((blocks, rows, PAIR), BF16),
            shape_of((blocks, rows, PAIR), F32),
            shape_of((tiles, rows, keys), BF16),
            shape_of((1,), jnp.int32),
        ),
        in_specs=[pl.BlockSpec(memory_space=pltpu.SMEM), vmem]
        + [pl.BlockSpec(memory_space=pl.ANY)] * len(behind),
        out_specs=(
            vmem, vmem, vmem, pl.BlockSpec(memory_space=pl.ANY),
            pl.BlockSpec(memory_space=pltpu.SMEM),
        ),
        scratch_shapes=[
            pltpu.VMEM((2 * blocks, rows, keys), F32),
            pltpu.VMEM((2 * blocks, rows, keys), BF16),
            pltpu.VMEM((2 * blocks, PAIR, keys), F32),
            pltpu.VMEM((2 * blocks, HEAD + ONES, keys), BF16),
            pltpu.VMEM((rows, PAIR), F32),
            pltpu.VMEM((rows, PAIR), F32),
            pltpu.VMEM((HEAD + ONES, rows), F32),
            pltpu.SemaphoreType.DMA((2 * blocks,)),
        ],
        cost_estimate=cost(
            flops=tiles * rows * keys * 2 * 256 * 3,
            bytes_accessed=4 * x.size + 2 * tiles * rows * keys,
            transcendentals=tiles * rows * keys,
            share=1,
        ),
        compiler_params=pltpu.CompilerParams(vmem_limit_bytes=VMEM_LIMIT),
        name="forward_head",
    )(part, x, *behind)


def backward_head(scalars, x, grad, delta, probs, key_rows, query_rows, behind):
    count, blocks, keys, rows = head_sizes(x, key_rows, query_rows)
    tiles = first_tile(blocks)
    slots = 6
    vmem = pl.BlockSpec(memory_space=pltpu.VMEM)
    return pl.pallas_call(
        without(
            partial(backward_kernel, key_rows=key_rows, query_rows=query_rows), 5, len(behind)
        ),
        out_shape=(shape_of((count, key_rows, PAIR), BF16), shape_of((1,), jnp.int32)),
        in_specs=[pl.BlockSpec(memory_space=pltpu.SMEM), vmem, vmem, vmem]
        + [pl.BlockSpec(memory_space=pl.ANY)] * (1 + len(behind)),
        out_specs=(vmem, pl.BlockSpec(memory_space=pltpu.SMEM)),
        scratch_shapes=[
            pltpu.VMEM((slots, rows, keys), BF16),
            pltpu.VMEM((rows, keys), F32),
            pltpu.VMEM((rows, keys), F32),
            pltpu.VMEM((2 * blocks, PAIR, keys), F32),
            pltpu.VMEM((rows, PAIR), F32),
            pltpu.SemaphoreType.DMA((slots,)),
        ],
        cost_estimate=cost(
            flops=tiles * rows * keys * 2 * 256 * 3,
            bytes_accessed=4 * x.size + 2 * tiles * rows * keys,
            transcendentals=0,
            share=1,
        ),
        compiler_params=pltpu.CompilerParams(vmem_limit_bytes=VMEM_LIMIT),
        name="backward_head",
    )(scalars, x, grad, delta, probs, *behind)


def feed_kernel(*refs, count, keep):
    rows_refs, cot_refs = refs[:count], refs[count : 2 * count]
    w1_ref, b1_ref, w2_ref = refs[2 * count : 2 * count + 3]
    hid_ref, gpre_ref, gb_ref = refs[2 * count + 3 : 2 * count + 6]
    outs = refs[2 * count + 6 : -2]
    out_acc, grad_acc = refs[-2:]
    step = pl.program_id(0)

    @pl.when(step == 0)
    def _():
        out_acc[...] = jnp.zeros_like(out_acc)
        grad_acc[...] = jnp.zeros_like(grad_acc)

    bias = b1_ref[...]
    sums = jnp.zeros_like(bias)
    rows = rows_refs[0].shape[0]
    for r in range(count):
        here = slice(r * rows, (r + 1) * rows)
        pre = dot32(rows_refs[r][...], w1_ref[...]) + bias
        grad = dot32(cot_refs[r][...], w2_ref[...], NT)
        cdf = 0.5 + 0.5 * lax.erf(pre * (0.5**0.5))
        density = jnp.exp(-0.5 * pre * pre) * 0.3989422804014327
        hidden = (pre * cdf).astype(BF16)
        grad_pre = (grad * (cdf + pre * density)).astype(BF16)
        hid_ref[here] = hidden
        gpre_ref[here] = grad_pre
        sums = sums + jnp.sum(grad_pre.astype(F32), 0, keepdims=True)
        out_acc[here] += dot32(hidden, w2_ref[...])
        grad_acc[here] += dot32(grad_pre, w1_ref[...], NT)
    gb_ref[...] = sums

    @pl.when(step == pl.num_programs(0) - 1)
    def _():
        if keep:
            own_out, own_grad, other = outs
            own_out[...] = out_acc[:rows]
            own_grad[...] = grad_acc[:rows]
            other[:rows] = out_acc[rows:].astype(BF16)
            other[rows:] = grad_acc[rows:].astype(BF16)
        else:
            outs[0][...] = out_acc[...].astype(BF16)
            outs[1][...] = grad_acc[...].astype(BF16)


def feed(rows_list, cot_list, w1, b1, w2):
    width, hidden = w1.shape
    count = len(rows_list)
    rows = rows_list[0].shape[0]
    total = rows * count
    block = 256
    keep = count > 1
    sides = (
        [(rows, F32), (rows, F32), (total, BF16)]
        if keep
        else [(total, BF16), (total, BF16)]
    )
    once = pl.Buffered(1)
    whole = pl.BlockSpec((rows, width), lambda i: (0, 0), pipeline_mode=once)
    return pl.pallas_call(
        partial(feed_kernel, count=count, keep=keep),
        grid=(hidden // block,),
        out_shape=(
            shape_of((total, hidden), BF16),
            shape_of((total, hidden), BF16),
            shape_of((1, hidden), F32),
            *[shape_of((r, width), d) for r, d in sides],
        ),
        in_specs=[
            *[whole] * (2 * count),
            pl.BlockSpec((width, block), lambda i: (0, i)),
            pl.BlockSpec((1, block), lambda i: (0, i)),
            pl.BlockSpec((block, width), lambda i: (i, 0)),
        ],
        out_specs=(
            pl.BlockSpec((total, block), lambda i: (0, i)),
            pl.BlockSpec((total, block), lambda i: (0, i)),
            pl.BlockSpec((1, block), lambda i: (0, i)),
            *[
                pl.BlockSpec((r, width), lambda i: (0, 0), pipeline_mode=once) for r, d in sides
            ],
        ),
        scratch_shapes=[pltpu.VMEM((total, width), F32), pltpu.VMEM((total, width), F32)],
        cost_estimate=cost(
            flops=8 * total * width * hidden,
            bytes_accessed=4 * width * hidden + 4 * total * hidden,
            transcendentals=2 * total * hidden,
        ),
        compiler_params=pltpu.CompilerParams(vmem_limit_bytes=VMEM_LIMIT),
        name="feed",
    )(*rows_list, *cot_list, w1, b1.astype(F32).reshape(1, hidden), w2)


def insert_bits(k, positions, values):
    for position, value in zip(positions, values):
        k = ((k >> position) << (position + 1)) + (value << position) + (k & ((1 << position) - 1))
    return k


def part_chunk(k, p, me, ring_bits, positions):
    values = [((me >> bit) & 1) ^ ((p >> n) & 1) for n, bit in enumerate(ring_bits)]
    return insert_bits(k, positions, values)


def weight_kernel(me_ref, *refs, bits, counts):
    total = sum(counts)
    a_refs, b_refs, parts = refs[:total], refs[total : 2 * total], refs[2 * total :]

    def product(first, count):
        b = jnp.concatenate([r[...] for r in b_refs[first : first + count]], 0)
        for p, ref in enumerate(parts):
            chunks, rows, cols = ref.shape
            a = []
            for k in range(chunks):
                start = part_chunk(k, p, me_ref[0], bits, bits) * rows
                here = pl.ds(pl.multiple_of(start, rows), rows)
                a.append(
                    jnp.concatenate([r[here, :] for r in a_refs[first : first + count]], 1)
                )
            ref[...] = dot32(jnp.concatenate(a, 0), b).astype(BF16).reshape(ref.shape)

    if len(counts) == 1:
        product(0, total)
    else:
        for n, count in enumerate(counts):
            pl.when(pl.program_id(0) == n)(partial(product, sum(counts[:n]), count))


def weight_parts(scalars, products, steps, block, members, bits):
    a_runs = [run for a, _ in products for run in a]
    b_runs = [run for _, b in products for run in b]
    width = a_runs[0][1][0]
    rows = width // members
    tokens = sum(shape[1] for _, shape, _ in products[0][0])
    count = 1 << len(bits)
    each = (members // count, rows, steps * block)
    out = pl.BlockSpec((members // count, rows, block), lambda i, me: (0, 0, i))
    return pl.pallas_call(
        partial(weight_kernel, bits=bits, counts=[len(a) for a, _ in products]),
        grid_spec=pltpu.PrefetchScalarGridSpec(
            num_scalar_prefetch=1,
            grid=(steps,),
            in_specs=[pl.BlockSpec(shape, index) for _, shape, index in (*a_runs, *b_runs)],
            out_specs=[out] * count,
        ),
        out_shape=[shape_of(each, BF16)] * count,
        cost_estimate=cost(
            flops=2 * width * tokens * steps * block,
            bytes_accessed=2 * width * tokens + 2 * (width + tokens) * steps * block,
            transcendentals=0,
        ),
        compiler_params=pltpu.CompilerParams(vmem_limit_bytes=VMEM_LIMIT),
        name="weight_parts",
    )(scalars, *[array for array, _, _ in (*a_runs, *b_runs)])


def weight_once_kernel(me_ref, *refs, products, operands):
    arrays, outs = refs[:operands], refs[operands:-1]
    for n in range(2):
        refs[-1][n] = me_ref[n]
    at = 0
    for blocks, bits in products:
        parts = outs[at : at + (1 << len(bits))]
        at += len(parts)
        cols = parts[0].shape[2] // len(blocks)
        for n, block in enumerate(blocks):
            here = slice(n * cols, (n + 1) * cols)
            if len(block) == len(parts):
                for ref, source in zip(parts, block):
                    ref[:, :, here] = arrays[source][...]
                continue
            a_runs, b_runs, turned = block
            b = jnp.concatenate([run(arrays, me_ref) for run in b_runs], 1 if turned else 0)
            for p, ref in enumerate(parts):
                chunks, rows, _ = ref.shape
                a = []
                for k in range(chunks):
                    start = part_chunk(k, p, me_ref[0], bits, bits) * rows
                    lines = pl.ds(pl.multiple_of(start, rows), rows)
                    a.append(jnp.concatenate([arrays[m][lines, :] for m in a_runs], 1))
                product = dot32(jnp.concatenate(a, 0), b, NT if turned else NN)
                ref[:, :, here] = product.astype(BF16).reshape(chunks, rows, cols)


def rows_run(n, first, count):
    return lambda arrays, me_ref: arrays[n][first : first + count, :]


def columns_run(n, cols, block):
    if block is not None:
        return lambda arrays, me_ref: arrays[n][:, block * cols : (block + 1) * cols]
    return lambda arrays, me_ref: arrays[n][:, pl.ds(pl.multiple_of(me_ref[1] * cols, cols), cols)]


def weight_once(scalars, arrays, products, width, cols, members, behind):
    each = [
        shape_of((members >> len(bits), width // members, cols * len(blocks)), BF16)
        for blocks, bits in products
        for _ in range(1 << len(bits))
    ]
    outs = vmem_call(
        partial(weight_once_kernel, products=products, operands=len(arrays)),
        each + [shape_of((2,), jnp.int32)],
        scalars,
        arrays,
        "weight_once",
        behind,
    )
    return outs[:2], outs[2:4], outs[4]


def column_sums(refs, counts):
    groups, start = [], 0
    for count in counts:
        groups.append(refs[start : start + count])
        start += count

    def total(group, c):
        value = group[0][c].astype(F32)
        for ref in group[1:]:
            value = value + ref[c].astype(F32)
        return value

    return [partial(total, group) for group in groups]


def add_kernel(me_ref, *refs, counts, bits, positions):
    ins, outs = refs[: sum(counts)], refs[sum(counts) :]
    at = 0
    for group, total in zip(counts, column_sums(ins, counts)):
        cols = ins[0].shape[2]
        for p, ref in enumerate(outs):
            for k in range(ref.shape[0]):
                c = part_chunk(k, p, me_ref[0], bits, positions)
                ref[k, :, at : at + cols] = total(c).astype(BF16)
        at += cols
        ins = ins[group:]


def last_kernel(me_ref, *refs, count, form):
    value = column_sums(refs[:count], [count])[0](0)
    outs = refs[count:]
    if form == "pair":
        half = value.shape[0] // 2
        first = me_ref[1] == 0
        outs[0][...] = jnp.where(first, value[:half], value[half:])
        outs[1][...] = jnp.where(first, value[half:], value[:half]).astype(BF16)
    else:
        at = 0
        for ref in outs:
            ref[...] = value[:, at : at + ref.shape[1]]
            at += ref.shape[1]


def without(kernel, first, count):
    if not count:
        return kernel
    return lambda *refs: kernel(*refs[:first], *refs[first + count :])


def vmem_call(kernel, out_shape, scalars, arrays, name, behind=()):
    vmem = pl.BlockSpec(memory_space=pltpu.VMEM)
    size = sum(a.size for a in arrays)
    return pl.pallas_call(
        without(kernel, 1 + len(arrays), len(behind)),
        in_specs=[pl.BlockSpec(memory_space=pltpu.SMEM)]
        + [vmem] * len(arrays)
        + [pl.BlockSpec(memory_space=pl.ANY)] * len(behind),
        out_specs=[
            pl.BlockSpec(memory_space=pltpu.SMEM) if o.dtype == jnp.int32 else vmem
            for o in out_shape
        ],
        out_shape=out_shape,
        cost_estimate=cost(flops=size, bytes_accessed=3 * size, transcendentals=0),
        compiler_params=pltpu.CompilerParams(vmem_limit_bytes=VMEM_LIMIT),
        name=name,
    )(scalars, *arrays, *behind)


def seq_move(x, mask):
    members = lax.axis_size("seq")
    return lax.ppermute(x, "seq", [(s, s ^ mask) for s in range(members)])


def ring_stages(stages):
    bits = lax.axis_size("seq").bit_length() - 1
    named = [b for stage in stages for b in stage]
    stages = [tuple(b for b in stage if b < bits) for stage in stages]
    stages[-1] = stages[-1] + tuple(b for b in range(bits) if b not in named)
    return [stage for stage in stages if stage]


class Ring:
    def __init__(self, scalars, parts, stages):
        self.scalars, self.stages, self.behind = scalars, list(stages), ()
        self.me = scalars[0]
        self.left = sorted(b for stage in stages for b in stage)
        self.travel(parts)

    def travel(self, parts):
        stage = self.stages.pop(0)
        self.left = [b for b in self.left if b not in stage]
        self.keep, self.sent = parts[0], parts[1:]
        self.came = [
            seq_move(part, sum(1 << b for n, b in enumerate(stage) if (p >> n) & 1))
            for p, part in enumerate(parts)
            if p
        ]

    def hold(self, *others):
        self.behind = others

    def step(self, *others):
        stage = self.stages[0]
        positions = [self.left.index(b) for b in stage]
        rings = (self, *others)
        chunks, rows = self.keep.shape[:2]
        cols = sum(ring.keep.shape[2] for ring in rings)
        count = 1 << len(stage)
        arrays = [[ring.keep, *ring.came] for ring in rings]
        self.travel(
            vmem_call(
                partial(
                    add_kernel, counts=[len(a) for a in arrays], bits=stage, positions=positions
                ),
                [shape_of((chunks // count, rows, cols), BF16)] * count,
                self.scalars,
                [a for group in arrays for a in group],
                "add_parts",
                self.behind,
            )
        )
        self.behind = ()

    def pass_on(self, me):
        stage = self.stages[0]
        bits = self.left
        shape = self.keep.shape[1:]
        arrays = [a.reshape((2,) * len(bits) + shape) for a in (self.keep, *self.came)]
        parts = []
        for p in range(1 << len(stage)):
            total = None
            for a in arrays:
                for n, bit in reversed(list(enumerate(stage))):
                    axis = len(bits) - 1 - bits.index(bit)
                    index = ((me >> bit) & 1) ^ ((p >> n) & 1)
                    a = lax.dynamic_index_in_dim(a, index, axis, True)
                a = a.reshape((-1,) + shape).astype(F32)
                total = a if total is None else total + a
            parts.append(total.astype(BF16))
        self.travel(parts)

    def plain_total(self):
        return sum(a[0].astype(F32) for a in (self.keep, *self.came))

    def total(self, widths=None):
        while self.stages:
            self.step()
        rows, cols = self.keep.shape[1:]
        shapes = (
            [shape_of((rows, w), F32) for w in widths]
            if widths
            else [shape_of((rows // 2, cols), F32), shape_of((rows // 2, cols), BF16)]
        )
        arrays = [self.keep, *self.came]
        return vmem_call(
            partial(last_kernel, count=len(arrays), form="rows" if widths else "pair"),
            shapes,
            self.scalars,
            arrays,
            "last_sum",
        )


def regroup_kernel(me_ref, back_ref, *refs, key_rows, query_rows, turned):
    heads, parts = back_ref.shape[:2]
    low = lax.broadcasted_iota(jnp.int32, (key_rows, PAIR), 1) < HEAD
    if turned:
        one_ref, two_ref, one_t_ref, *sides = refs
    else:
        table_ref, one_ref, two_ref, *sides = refs
        tables = (table_ref[0], -table_ref[1], -table_ref[2])
    first = pl.program_id(0) == 0
    for t in range(heads // 2):
        pair = []
        for h in (2 * t, 2 * t + 1):
            if parts == 1:
                pair.append(back_ref[h, 0].astype(F32))
                continue
            keys = sum(back_ref[h, p].astype(F32) for p in range(parts))
            queries = jnp.concatenate(
                [back_ref[h, p, :query_rows].astype(F32) for p in range(parts)], 0
            )
            pair.append(jnp.where(low, queries, keys))
        one, two = two_heads(pair[0], pair[1], low)
        if not turned:
            one, two = rotate_lanes(one, *tables), rotate_lanes(two, *tables)
        one, two = one.astype(BF16), two.astype(BF16)
        here = slice(t * PAIR, (t + 1) * PAIR)
        one_ref[:, here] = one
        two_ref[:, here] = two
        if turned:
            one_t_ref[here] = jnp.transpose(one)
        if sides:
            half = one_ref.shape[1]
            for n, value in enumerate((two,) if turned else (one, two)):
                there = slice(n * half + t * PAIR, n * half + (t + 1) * PAIR)
                pl.when(first)(partial(sides[1].__setitem__, (slice(None), there), value))
                pl.when(~first)(partial(sides[0].__setitem__, (slice(None), there), value))


def regroup(back, table, scalars, rows, query_rows, split):
    turned = table is None
    chunk = back.shape[1]
    parts = back.shape[0] // HEADS
    half = HEADS * HEAD // 2
    full = shape_of((rows, 2 * half), BF16)

    def side(i, me):
        return (i + me[1] + 1) % 2 if split else i

    whole = pl.BlockSpec((rows, half), lambda i, me: (0, side(i, me)))
    tall = pl.BlockSpec((half, rows), lambda i, me: (side(i, me), 0))
    cols = half * (1 if turned else 2)
    own = pl.BlockSpec((rows, cols), lambda i, me: (0, 0))
    return pl.pallas_call(
        partial(regroup_kernel, key_rows=rows, query_rows=query_rows, turned=turned),
        grid_spec=pltpu.PrefetchScalarGridSpec(
            num_scalar_prefetch=1,
            grid=(2,),
            in_specs=[
                pl.BlockSpec(
                    (HEADS // 2, parts, chunk, PAIR), lambda i, me: (side(i, me), 0, 0, 0)
                )
            ]
            + ([] if turned else [pl.BlockSpec(table.shape, lambda i, me: (0, 0, 0))]),
            out_specs=[whole, whole] + ([tall] if turned else []) + ([own, own] if split else []),
        ),
        out_shape=[full, full]
        + ([shape_of((2 * half, rows), BF16)] if turned else [])
        + ([shape_of((rows, cols), BF16)] * 2 if split else []),
        cost_estimate=cost(
            flops=back.size, bytes_accessed=4 * back.size, transcendentals=0
        ),
        name="regroup",
    )(
        scalars,
        back.reshape(HEADS, parts, chunk, PAIR),
        *([] if turned else [table]),
    )


def regroup_once_kernel(me_ref, *refs, turned):
    if turned:
        back_ref, att_ref, v_ref, send_ref, own_a_ref, own_v_ref = refs
    else:
        back_ref, table_ref, q_ref, k_ref, send_ref, own_ref = refs
        tables = (table_ref[0], -table_ref[1], -table_ref[2])
    heads, rows = back_ref.shape[:2]
    half = heads // 2
    low = lax.broadcasted_iota(jnp.int32, (rows, PAIR), 1) < HEAD
    for side in range(2):
        first = ((me_ref[1] + side) % 2) * half
        for t in range(half // 2):
            pair = [back_ref[first + 2 * t + n].astype(F32) for n in range(2)]
            one, two = two_heads(pair[0], pair[1], low)
            if not turned:
                one, two = rotate_lanes(one, *tables), rotate_lanes(two, *tables)
            one, two = one.astype(BF16), two.astype(BF16)
            start = pl.multiple_of((first // 2 + t) * PAIR, PAIR)
            here = pl.ds(start, PAIR)
            local = slice(t * PAIR, (t + 1) * PAIR)
            width = half * HEAD
            if turned:
                att_ref[:, here] = one
                v_ref[:, here] = two
                turned_one, turned_two = jnp.transpose(one), jnp.transpose(two)
                own_a_ref[here] = turned_one
                send_ref[here] = turned_one
                if side == 0:
                    own_v_ref[local] = turned_two
                else:
                    send_ref[2 * width + t * PAIR : 2 * width + (t + 1) * PAIR] = turned_two
            else:
                q_ref[:, here] = one
                k_ref[:, here] = two
                ref = own_ref if side == 0 else send_ref
                ref[:, local] = one
                ref[:, width + t * PAIR : width + (t + 1) * PAIR] = two


def regroup_once(back, table, scalars, behind=()):
    rows = back.shape[1]
    full = shape_of((rows, HEADS * HEAD), BF16)
    half = HEADS * HEAD // 2
    if table is None:
        sides = [
            shape_of((3 * half, rows), BF16),
            shape_of((2 * half, rows), BF16),
            shape_of((half, rows), BF16),
        ]
    else:
        sides = [shape_of((rows, 2 * half), BF16)] * 2
    return vmem_call(
        partial(regroup_once_kernel, turned=table is None),
        [full, full, *sides],
        scalars,
        [back] if table is None else [back, table],
        "regroup_once",
        behind,
    )


def close_kernel(
    x_ref, g_ref, ga_ref, gf_ref, bo_ref, bc_ref, gq_ref, gk_ref, gv_ref, att_ref,
    wq_ref, wk_ref, wv_ref, wo_ref, me_ref, *refs, sides,
):
    feeds, grads = refs[:sides], refs[sides : 2 * sides]
    out_ref, gin_ref, vec_ref, gb_ref, after_ref, out_acc, grad_acc = refs[2 * sides :]
    step = pl.program_id(0)
    for n in range(2):
        after_ref[n] = me_ref[n]

    @pl.when(step == 0)
    def _():
        out_acc[...] = jnp.zeros_like(out_acc)
        grad_acc[...] = jnp.zeros_like(grad_acc)

    out_acc[...] += dot32(att_ref[...], wo_ref[...])
    total = None
    for third, (g_third, w_ref) in enumerate(
        ((gq_ref, wq_ref), (gk_ref, wk_ref), (gv_ref, wv_ref))
    ):
        grad = g_third[...]
        part = dot32(grad, w_ref[...], NT)
        total = part if total is None else total + part
        gb_ref[third : third + 1] = jnp.sum(grad.astype(F32), 0, keepdims=True)
    grad_acc[...] += total

    @pl.when(step == pl.num_programs(0) - 1)
    def _():
        x = x_ref[...].astype(F32)
        g = g_ref[...].astype(F32)
        total = x + out_acc[...] + vector_row(bo_ref) + vector_row(bc_ref)
        for ref in feeds:
            total = total + ref[...].astype(F32)
        out_ref[...] = total.astype(BF16)
        unit, root = unit_rows(x)
        one = grad_acc[...]
        two = grads[0][...].astype(F32)
        for ref in grads[1:]:
            two = two + ref[...].astype(F32)
        down = one * vector_row(ga_ref) + two * vector_row(gf_ref)
        mean = jnp.mean(down, -1, keepdims=True)
        slope = jnp.mean(down * unit, -1, keepdims=True)
        gin_ref[...] = g + root * (down - mean - unit * slope)
        for r, rows in enumerate((one * unit, one, g, two * unit, two)):
            vec_ref[r : r + 1] = jnp.sum(rows, 0, keepdims=True)


def close_layer(x, g, vectors, gm, attended, weight, out_weight, feeds, grads, scalars, behind):
    rows, width = x.shape
    steps = 4
    cols = width // steps

    def third(t):
        return pl.BlockSpec((width, cols), lambda i: (0, t * steps + i))

    part = pl.BlockSpec((rows, cols), lambda i: (0, i))
    return pl.pallas_call(
        without(partial(close_kernel, sides=len(feeds)), 15 + 2 * len(feeds), len(behind)),
        grid=(steps,),
        out_shape=(
            shape_of((rows, width), BF16),
            shape_of((rows, width), F32),
            shape_of((5, width), F32),
            shape_of((3, width), F32),
            shape_of((2,), jnp.int32),
        ),
        in_specs=[
            fixed((rows, width)),
            fixed((rows, width)),
            *[fixed((width,))] * 4,
            part, part, part, part,
            third(0), third(1), third(2),
            pl.BlockSpec((cols, width), lambda i: (i, 0)),
            pl.BlockSpec(memory_space=pltpu.SMEM),
            *[
                pl.BlockSpec((rows, width), lambda i, n=n: (n, 0)) for _, n in (*feeds, *grads)
            ],
            *[pl.BlockSpec(memory_space=pl.ANY)] * len(behind),
        ],
        out_specs=(
            fixed((rows, width)),
            fixed((rows, width)),
            fixed((5, width)),
            pl.BlockSpec((3, cols), lambda i: (0, i)),
            pl.BlockSpec(memory_space=pltpu.SMEM),
        ),
        scratch_shapes=[pltpu.VMEM((rows, width), F32), pltpu.VMEM((rows, width), F32)],
        cost_estimate=cost(
            flops=8 * rows * width * width,
            bytes_accessed=8 * width * width + 24 * rows * width,
            transcendentals=0,
        ),
        compiler_params=pltpu.CompilerParams(vmem_limit_bytes=VMEM_LIMIT),
        name="close_layer",
    )(x, g, *vectors, *gm, attended, weight, weight, weight, out_weight, scalars, *[a for a, _ in (*feeds, *grads)], *behind)


def place_kernel(me_ref, own_ref, came_ref, merged_ref, dense_ref):
    half = dense_ref.shape[1] // 2
    for side, ref in enumerate((own_ref, came_ref)):
        at = ((me_ref[1] + side) % 2) * half
        for third, block in enumerate((0, 2, 1)):
            start = pl.multiple_of(third * 2 * half + at, half)
            value = ref[:, block * half : (block + 1) * half]
            merged_ref[:, pl.ds(start, half)] = value.astype(F32)
        dense_ref[:, pl.ds(pl.multiple_of(at, half), half)] = ref[:, 3 * half :].astype(F32)


def pair_swap(x):
    return lax.ppermute(x, "mlp", [(0, 1), (1, 0)])


def mlp_list(x, axis=0):
    if lax.axis_size("mlp") == 2:
        return [x, pair_swap(x)]
    return [lax.all_gather(x, "mlp", axis=axis, tiled=True)]


def after(value, *others):
    return lax.optimization_barrier((value, *others))[0]


def per_device(
    block_input,
    out_cotangent,
    attend_gain,
    attend_shift,
    query_key_value_weight,
    query_key_value_bias,
    attention_out_weight,
    attention_out_bias,
    feed_gain,
    feed_shift,
    expand_weight,
    expand_bias,
    contract_weight,
    contract_bias,
):
    seq_count, rows, width = block_input.shape
    members = lax.axis_size("seq")
    pairs = lax.axis_size("mlp")
    parts = members // HEADS
    own = width // members
    me = lax.axis_index("seq").astype(jnp.int32).reshape(1)
    pair_me = lax.axis_index("mlp")
    scalars = jnp.stack([me[0], pair_me.astype(jnp.int32)])
    inputs = block_input.reshape(rows, width)
    cot = out_cotangent.reshape(rows, width)

    outgoing, _, normed_two, table, one_t, turned = open_layer(
        inputs,
        cot,
        me * rows,
        (attend_gain, attend_shift, feed_gain, feed_shift),
        query_key_value_weight,
        query_key_value_bias,
        attention_out_weight,
        parts,
    )
    at_head = lax.all_to_all(outgoing, "seq", 0, 0, tiled=True)

    rows_list, cot_list = mlp_list(normed_two), mlp_list(cot)
    turned = mlp_list(turned, 1)
    one_t = mlp_list(one_t, 1)
    hidden, grad_pre, grad_hid_bias, *sides = feed(
        rows_list, cot_list, expand_weight, expand_bias, contract_weight
    )
    if pairs == 2:
        came = pair_swap(sides[2])
        feeds, grads = [(sides[0], 0), (came, 0)], [(sides[1], 0), (came, 1)]
    else:
        feeds, grads = (
            [(lax.psum_scatter(v, "mlp", scatter_dimension=0, tiled=True), 0)] for v in sides
        )
    slice_width = expand_weight.shape[1]
    block = min(512, slice_width)

    def runs(arrays, shape, index):
        if pairs == 2:
            return [(a, shape, lambda i, me: index(0, i, me)) for a in arrays]
        return [(arrays[0], shape, lambda i, me, m=m: index(m, i, me)) for m in range(pairs)]

    def sides_of(arrays, part=0):
        return runs(arrays, (width, rows), lambda m, i, me: (part, m))

    def ring_of(products, steps, block, stages):
        stages = ring_stages(stages)
        parts = weight_parts(scalars, products, steps, block, members, stages[0])
        return Ring(scalars, parts, stages)

    x_first, y_first = [(0,), (1,), (2,), (3,)], [(1,), (0,), (2,), (3,)]

    def feed_ring(part, b, stages):
        b_runs = [(b, (rows, block), lambda i, me, m=m: (m, i)) for m in range(pairs)]
        return ring_of([(sides_of(turned, part), b_runs)], slice_width // block, block, stages)

    ring_out = feed_ring(1, hidden, x_first)
    ring_hid = feed_ring(0, grad_pre, y_first)

    query_rows = rows // parts
    part = jnp.stack([me[0] % parts, me[0]]).astype(jnp.int32)
    from_first, head_grad, head_delta, probs, _ = forward_head(
        at_head,
        part,
        rows,
        query_rows,
        (*ring_out.sent, *ring_hid.sent, *[a for a, _ in (*feeds, *grads)], *turned, *one_t),
    )
    back_first = lax.all_to_all(from_first, "seq", 0, 0, tiled=True)
    from_second, after_second = backward_head(
        scalars, at_head, head_grad, head_delta, probs, rows, query_rows, ()
    )
    from_second = after(from_second, *ring_out.came, *ring_hid.came)
    back_second = lax.all_to_all(from_second, "seq", 0, 0, tiled=True)
    x_first, y_first = [(0,), (1,), (2, 3)], [(1,), (0,), (2, 3)]
    split = pairs == 2 and parts == 1
    share = width // pairs

    def pieces_of(arrays):
        stacked = jnp.stack([a.reshape(rows, pairs, share) for a in arrays], 2)
        stacked = jnp.transpose(stacked, (1, 0, 2, 3)).reshape(pairs, rows, len(arrays) * share)
        if pairs == 2:
            mine = lax.dynamic_index_in_dim(stacked, pair_me, 0, False)
            return [mine, pair_swap(lax.dynamic_index_in_dim(stacked, 1 - pair_me, 0, False))]
        got = lax.all_to_all(stacked, "mlp", 0, 0, tiled=True)
        return [got.reshape(pairs * rows, len(arrays) * share)]

    if split:

        attended, grad_v, sent, own_a, own_v = regroup_once(
            back_first, None, scalars, (from_second,)
        )
        came = pair_swap(sent)
        for ring in (ring_out, ring_hid):
            ring.hold(sent)
            ring.step()
        v_parts, d_parts, _ = weight_once(
            scalars,
            [*one_t, own_v, came, own_a, *cot_list],
            [
                ([((0, 1), (rows_run(2, 0, share), rows_run(3, width, share)), True)], (0,)),
                (
                    [((4, 3), (columns_run(5, share, None), columns_run(6, share, None)), False)],
                    (1,),
                ),
            ],
            width,
            share,
            members,
            (),
        )
        grad_q, grad_k, sent, own_qk = regroup_once(
            back_second, table, scalars, (*v_parts, *d_parts)
        )
        came = pair_swap(sent)
        qv_parts, kd_parts, weighed = weight_once(
            scalars,
            [*one_t, own_qk, came, *v_parts, *d_parts],
            [
                (
                    [
                        ((0, 1), (columns_run(2, share, n), columns_run(3, share, n)), False),
                        (4 + 2 * n, 5 + 2 * n),
                    ],
                    (n,),
                )
                for n in range(2)
            ],
            width,
            share,
            members,
            (),
        )
        ring_qv = Ring(scalars, qv_parts, x_first)
        ring_kd = Ring(scalars, kd_parts, y_first)
    else:
        for ring in (ring_out, ring_hid):
            ring.step()
        attended, grad_v, att_t = regroup(back_first, None, scalars, rows, query_rows, False)
        att_t = mlp_list(att_t, 1)
        grad_q, grad_k = regroup(back_second, table, scalars, rows, query_rows, False)
        pieces = [pieces_of([g]) for g in (grad_q, grad_v, grad_k)]
        q_runs, v_runs, k_runs = (
            runs(p, (rows, share), lambda m, i, me: (m, 0)) for p in pieces
        )
        cot_runs = runs(cot_list, (rows, share), lambda m, i, me: (m, me[1]))
        one = sides_of(one_t)
        ring_qv = ring_of([(one, q_runs), (one, v_runs)], 2, share, x_first)
        ring_kd = ring_of([(one, k_runs), (sides_of(att_t), cot_runs)], 2, share, y_first)

    ring_out.hold(*ring_kd.sent)
    ring_out.step(ring_hid)
    block_output, grad_input, vec, gm_bias, closed = close_layer(
        inputs,
        cot,
        (attend_gain, feed_gain, attention_out_bias, contract_bias),
        (grad_q, grad_k, grad_v),
        attended,
        query_key_value_weight,
        attention_out_weight,
        feeds,
        grads,
        scalars,
        ring_out.sent,
    )
    for ring in (ring_qv, ring_kd):
        ring.pass_on(closed[0])
    ring_out.came = [after(x, *ring_qv.sent, *ring_kd.sent) for x in ring_out.came]
    ring_out.pass_on(closed[0])

    bias_full = lax.dynamic_update_slice_in_dim(
        jnp.zeros((pairs * slice_width,), F32), grad_hid_bias[0], pair_me * slice_width, 0
    )
    vectors = [*[vec[r] for r in range(5)], gm_bias.reshape(-1), bias_full]
    packed = jnp.concatenate([v.reshape(members, pairs, -1) for v in vectors], -1)
    if pairs == 2:
        mine = lax.dynamic_index_in_dim(packed, pair_me, 1, False)
        other = lax.dynamic_index_in_dim(packed, 1 - pair_me, 1, False)
        packed = mine + pair_swap(after(other, *ring_out.sent))
    else:
        packed = lax.psum_scatter(packed, "mlp", scatter_dimension=1, tiled=False)
    ring_qv.step(ring_kd)
    packed = after(packed, *ring_qv.sent)
    packed = lax.all_to_all(packed, "seq", 0, 0, tiled=True)

    feed_total = ring_out.plain_total()
    out_weight = jnp.transpose(feed_total[:, :slice_width])
    hid_weight = feed_total[:, slice_width:]

    if pairs == 2:
        mine, other = ring_qv.total()
        packed = after(packed, other)
        merged, dense = vmem_call(
            place_kernel,
            [shape_of((own // pairs, 3 * width), F32), shape_of((own // pairs, width), F32)],
            scalars,
            [mine, pair_swap(other)],
            "place",
        )
    else:
        got = ring_qv.total([4 * share])[0].reshape(pairs, own // pairs, 4 * share)
        got = lax.all_to_all(got, "mlp", 0, 0, tiled=True)
        got = jnp.transpose(got.reshape(pairs, own // pairs, 4, share), (1, 2, 0, 3))
        merged = jnp.concatenate([got[:, n].reshape(-1, width) for n in (0, 2, 1)], -1)
        dense = got[:, 3].reshape(-1, width)
    packed = jnp.sum(packed, 0)
    outs, start = [], 0
    for v in vectors:
        size = v.shape[0] // (members * pairs)
        outs.append(lax.slice_in_dim(packed, start, start + size))
        start += size
    grad_gain_one, grad_shift_one, grad_dense_bias, grad_gain_two, grad_shift_two = outs[:5]
    grad_merged_bias, out_hid_bias = outs[5:]
    return (
        block_output.reshape(seq_count, rows, width),
        grad_input.reshape(seq_count, rows, width),
        grad_gain_one,
        grad_shift_one,
        merged,
        grad_merged_bias,
        dense,
        grad_dense_bias,
        grad_gain_two,
        grad_shift_two,
        hid_weight,
        out_hid_bias,
        out_weight,
        grad_dense_bias,
    )


def solution(mesh):
    in_specs = (
        P("mlp", "seq", None),
        P("mlp", "seq", None),
        P(),
        P(),
        P(),
        P(),
        P(),
        P(),
        P(),
        P(),
        P(None, "mlp"),
        P("mlp"),
        P("mlp", None),
        P(),
    )
    out_specs = (
        P("mlp", "seq", None),
        P("mlp", "seq", None),
        P(("seq", "mlp")),
        P(("seq", "mlp")),
        P(("seq", "mlp"), None),
        P(("seq", "mlp")),
        P(("seq", "mlp"), None),
        P(("seq", "mlp")),
        P(("seq", "mlp")),
        P(("seq", "mlp")),
        P("seq", "mlp"),
        P(("seq", "mlp")),
        P("mlp", "seq"),
        P(("seq", "mlp")),
    )
    return jax.shard_map(
        per_device, mesh=mesh, in_specs=in_specs, out_specs=out_specs, check_vma=False
    )
```
